32 devices in a mesh: dp: 8 (over z, y), mp: 4 (over x, core).
Axes of the slice: x: 2, y: 2, z: 4, core: 2. Of those that a mesh axis runs over, the one named last changes fastest.
Arguments:
- tokens: bfloat16 [8192, 768], P('dp'), may hold values from -6 to 6
- noise_field: bfloat16 [8192, 768], P('dp'), may hold values from -6 to 6
- codec_tokens: bfloat16 [16, 256, 768], P('dp'), may hold values from -6 to 6
- timesteps: int32 [16], P('dp'), may hold values from 0 to 999
- segments: int32 [16, 512], P('dp'), may hold values from 0 to 3, never falling along the last dimension, each value on 1 to 256 neighbouring positions
- cotangent: bfloat16 [8192, 768], P('dp'), may hold values from -6 to 6
- w_in: float32 [16, 768, 768], P(None, 'dp', 'mp'), may hold values from -0.14433757 to 0.14433757
- w_back: float32 [11, 768, 768], P(None, 'mp', 'dp'), may hold values from -0.4082483 to 0.4082483
- w_up: float32 [768, 3072], P('dp', 'mp'), may hold values from -0.21875 to 0.21875
- w_down: float32 [3072, 768], P('mp', 'dp'), may hold values from -0.109375 to 0.109375
- m_in: float32 [16, 768, 768], P(None, 'dp', 'mp'), may hold values from -256 to 256
- m_back: float32 [11, 768, 768], P(None, 'mp', 'dp'), may hold values from -256 to 256
- m_up: float32 [768, 3072], P('dp', 'mp'), may hold values from -256 to 256
- m_down: float32 [3072, 768], P('mp', 'dp'), may hold values from -256 to 256
- v_in: float32 [16, 768, 768], P(None, 'dp', 'mp'), may hold values from 2048 to 8192
- v_back: float32 [11, 768, 768], P(None, 'mp', 'dp'), may hold values from 2048 to 8192
- v_up: float32 [768, 3072], P('dp', 'mp'), may hold values from 2048 to 8192
- v_down: float32 [3072, 768], P('mp', 'dp'), may hold values from 2048 to 8192
- norm_params: float32 [10, 768], replicated, may hold values from -1.2 to 1.4
- norm_m: float32 [10, 768], replicated, may hold values from -256 to 256
- norm_v: float32 [10, 768], replicated, may hold values from 2048 to 8192
Outputs:
- out: bfloat16 [8192, 768], P('dp')
- grad_x: float32 [8192, 768], P('dp')
- new_w_in: float32 [16, 768, 768], P(None, 'dp', 'mp')
- new_w_back: float32 [11, 768, 768], P(None, 'mp', 'dp')
- new_w_up: float32 [768, 3072], P('dp', 'mp')
- new_w_down: float32 [3072, 768], P('mp', 'dp')
- new_m_in: float32 [16, 768, 768], P(None, 'dp', 'mp')
- new_m_back: float32 [11, 768, 768], P(None, 'mp', 'dp')
- new_m_up: float32 [768, 3072], P('dp', 'mp')
- new_m_down: float32 [3072, 768], P('mp', 'dp')
- new_v_in: float32 [16, 768, 768], P(None, 'dp', 'mp')
- new_v_back: float32 [11, 768, 768], P(None, 'mp', 'dp')
- new_v_up: float32 [768, 3072], P('dp', 'mp')
- new_v_down: float32 [3072, 768], P('mp', 'dp')
- new_norm_params: float32 [10, 768], replicated
- new_norm_m: float32 [10, 768], replicated
- new_norm_v: float32 [10, 768], replicated
- matrix_norms: float32 [2, 29], replicated
The draws below stay inside these ranges and needn't reach their ends.
Inputs may be any that keep to these rules, and one draw needn't show every extreme that they name: `segments`: along a sequence segment ids never fall; patches attend only within their segment; a segment holds at most 256 patches.
All inputs are finite; a program needn't handle non-finite values.
Results may differ from the reference program's by a relative error of at most 0.015.
Values may be sent and summed in bfloat16 or wider, within the bound.
A program may use at most 256 MiB of HBM per device.

```python
import math
from functools import partial
import jax
import jax.numpy as jnp
import numpy as np
from jax import lax

D = 768
HD = 64
FF = 3072
GROUPS = 32
FREQ = 8
TIME = 64
LEN = 512
CTOK = 256
TSTEPS = 1000
STEP = 5
SEQS = 16
TOKENS = 8192


def draw_w_in(key, part):
    sample = jax.random.truncated_normal(key, -4.0, 4.0, (16, D, D), jnp.float32)
    slice_index = jnp.arange(16)[:, None, None]
    slice_scale = jnp.where(slice_index >= 7, (9.0 * D) ** (-0.5), D ** (-0.5))
    return sample * slice_scale


def draw_w_back(key, part):
    sample = jax.random.truncated_normal(key, -4.0, 4.0, (11, D, D), jnp.float32)
    slice_index = jnp.arange(11)[:, None, None]
    slice_scale = jnp.where(slice_index < 2, (D // 8) ** (-0.5), (4.5 * D) ** (-0.5))
    return sample * slice_scale


def draw_norm_params(key, part):
    key_gain, key_shift = jax.random.split(key)
    gains_drawn = jax.random.uniform(key_gain, (10, D), jnp.float32, 0.6, 1.4)
    shifts_drawn = 0.3 * jax.random.truncated_normal(key_shift, -4.0, 4.0, (10, D), jnp.float32)
    row_index = jnp.arange(10)[:, None]
    return jnp.where(row_index % 2 == 0, gains_drawn, shifts_drawn)


def plant(entries, own_key, smallest, top_value):
    spot = [jax.random.randint(jax.random.fold_in(own_key, axis), (), 0, length) for axis, length in enumerate(entries.shape)]
    widest = entries.shape.index(max(entries.shape))
    next_to = spot[:widest] + [(spot[widest] + 1) % entries.shape[widest]] + spot[widest + 1:]
    return entries.at[tuple(spot)].set(smallest).at[tuple(next_to)].set(top_value)


def block_scale(stream_key, shape, pieces, least, top_value):
    gain = 1.0
    for dim, shards_of in pieces:
        draws = jax.random.uniform(jax.random.fold_in(jax.random.fold_in(stream_key, 6), dim), (shards_of,), jnp.float32, least / len(pieces), top_value / len(pieces))
        gain = gain * jnp.repeat(jnp.exp(draws), shape[dim] // shards_of).reshape((-1,) + (1,) * (len(shape) - 1 - dim))
    return gain


def length_profile(count, total, reach, slope):
    weights = [(1 << 20) // math.isqrt(grade ** slope) + 1 for grade in range(2, count + 1)]
    surplus, holding = total - reach - (count - 1), [1] * (count - 1)
    while surplus > 0:
        free = [i for i in range(count - 1) if holding[i] < reach]
        whole, budget = sum([weights[i] for i in free]), surplus
        for i in free:
            extra = min(reach - holding[i], max(1, budget * weights[i] // whole), surplus)
            holding[i] = holding[i] + extra
            surplus = surplus - extra
    return np.array([reach] + holding)


def uneven(rng, count, total, most, skew):
    if count == 2:
        one = jax.random.randint(rng, (), max(1, total - most), min(most, total - 1) + 1)
        return jnp.stack([one, total - one])
    sizes = jnp.asarray(length_profile(count, total, most, skew), jnp.int32)
    pairs = (count - 1) // 2
    giver, receiver = sizes[1:1 + 2 * pairs:2], sizes[2:2 + 2 * pairs:2]
    room = jnp.minimum(giver - 1, most - receiver)
    shifted = jax.random.randint(jax.random.fold_in(rng, 1), (pairs,), 0, 1 << 20) % (room + 1)
    sizes = sizes.at[1:1 + 2 * pairs:2].set(giver - shifted).at[2:2 + 2 * pairs:2].set(receiver + shifted)
    return sizes[jax.random.permutation(jax.random.fold_in(rng, 2), count)]


def normal_values(key, extent, width, most, cuts=(), kind=jnp.bfloat16):
    loudness = block_scale(key, extent, cuts, -0.22, 0.18) if cuts else 1.0
    entries = jax.random.normal(key, extent, jnp.float32) * width * loudness
    return jnp.minimum(jnp.maximum(entries, -most), most).astype(kind)


def setup_inputs(seed: int = 0) -> dict:
    key_of = jax.random.split(jax.random.key(seed), 22)
    return {
        "tokens": normal_values(key_of[0], (TOKENS, D), 1.0, 6.0, ((0, 8),)),
        "noise_field": normal_values(key_of[1], (TOKENS, D), 1.0, 6.0, ((0, 8),)),
        "codec_tokens": normal_values(key_of[2], (SEQS, CTOK, D), 1.0, 6.0, ((0, 8),)),
        "timesteps": plant(jax.random.randint(key_of[3], (SEQS,), 0, TSTEPS), jax.random.fold_in(key_of[3], 1), 0, TSTEPS - 1).astype(jnp.int32),
        "segments": jax.vmap(lambda own: jnp.searchsorted(jnp.cumsum(uneven(own, 4, LEN, LEN // 2, 0)), jnp.arange(LEN), side="right"))(jax.random.split(key_of[4], SEQS)).reshape((SEQS, LEN)).astype(jnp.int32),
        "cotangent": normal_values(key_of[5], (TOKENS, D), 1.0, 6.0, ((0, 8),)),
        "w_in": draw_w_in(jax.random.fold_in(key_of[21], 71), 0),
        "w_back": draw_w_back(jax.random.fold_in(key_of[21], 71), 0),
        "w_up": normal_values(key_of[8], (D, FF), D ** -0.5, 0.21875, ((0, 8), (1, 4)), jnp.float32),
        "w_down": normal_values(key_of[9], (FF, D), FF ** -0.5, 0.109375, ((0, 4), (1, 8)), jnp.float32),
        "m_in": normal_values(key_of[10], (16, D, D), ((TOKENS // 4) ** 0.5), 256.0, ((1, 8), (2, 4)), jnp.float32),
        "m_back": normal_values(key_of[11], (11, D, D), ((TOKENS // 4) ** 0.5), 256.0, ((1, 4), (2, 8)), jnp.float32),
        "m_up": normal_values(key_of[12], (D, FF), ((TOKENS // 4) ** 0.5), 256.0, ((0, 8), (1, 4)), jnp.float32),
        "m_down": normal_values(key_of[13], (FF, D), ((TOKENS // 4) ** 0.5), 256.0, ((0, 4), (1, 8)), jnp.float32),
        "v_in": jnp.clip(jnp.exp(math.log(8192.0) - 1.3862944 * jax.random.uniform(key_of[14], (16, D, D), jnp.float32) ** block_scale(key_of[14], (16, D, D), ((1, 8), (2, 4)), -0.2, 0.2)), 2048.0, 8192.0),
        "v_back": jnp.clip(jnp.exp(math.log(8192.0) - 1.3862944 * jax.random.uniform(key_of[15], (11, D, D), jnp.float32) ** block_scale(key_of[15], (11, D, D), ((1, 4), (2, 8)), -0.2, 0.2)), 2048.0, 8192.0),
        "v_up": jnp.clip(jnp.exp(math.log(8192.0) - 1.3862944 * jax.random.uniform(key_of[16], (D, FF), jnp.float32) ** block_scale(key_of[16], (D, FF), ((0, 8), (1, 4)), -0.2, 0.2)), 2048.0, 8192.0),
        "v_down": jnp.clip(jnp.exp(math.log(8192.0) - 1.3862944 * jax.random.uniform(key_of[17], (FF, D), jnp.float32) ** block_scale(key_of[17], (FF, D), ((0, 4), (1, 8)), -0.2, 0.2)), 2048.0, 8192.0),
        "norm_params": draw_norm_params(jax.random.fold_in(key_of[21], 71), 0),
        "norm_m": normal_values(key_of[19], (10, D), ((TOKENS // 4) ** 0.5), 256.0, (), jnp.float32),
        "norm_v": jnp.clip(jnp.exp(jax.random.uniform(key_of[20], (10, D), jnp.float32, math.log(2048.0), math.log(8192.0))), 2048.0, 8192.0),
    }


NORM_EPS = 1e-05
MOMENT_DECAY = 0.5
LEARN_RATE = 0.5
WEIGHT_DECAY = 0.01
ADAM_EPS = 1e-06
MASK_VALUE = -1e+30
HIGHEST_PRECISION = lax.Precision.HIGHEST

@jax.custom_vjp
def low(v):
    return lax.optimization_barrier(v.astype(jnp.bfloat16)).astype(jnp.float32)

@jax.custom_vjp
def low_back(v):
    return v

def low_keep(v):
    return (low(v), None)

def low_pass(kept, grad):
    return (grad,)

def back_keep(v):
    return (v, None)

def back_low(kept, grad):
    return (low(grad),)
low.defvjp(low_keep, low_pass)
low_back.defvjp(back_keep, back_low)

def layer_norm(value_tensor, gain_row, shift_row):
    centre = value_tensor - lax.optimization_barrier(jnp.mean(value_tensor, axis=-1, keepdims=True))
    spread = lax.optimization_barrier(jnp.mean(centre * centre, axis=-1, keepdims=True))
    return centre * lax.rsqrt(spread + NORM_EPS) * gain_row + shift_row

def group_norm(value_tensor, gain_row, shift_row, group_width):
    seqs_here, length, channels = value_tensor.shape
    grouped = value_tensor.reshape(seqs_here, length, channels // group_width, group_width)
    centre = grouped - lax.optimization_barrier(jnp.mean(grouped, axis=(1, 3), keepdims=True))
    spread = lax.optimization_barrier(jnp.mean(centre * centre, axis=(1, 3), keepdims=True))
    normed = (centre * lax.rsqrt(spread + NORM_EPS)).reshape(seqs_here, length, channels)
    return normed * gain_row + shift_row

def norm_silu(value_tensor, gain_row, shift_row, group_width):
    return jax.nn.silu(group_norm(value_tensor, gain_row, shift_row, group_width))

def time_embedding(timesteps, features):
    half_width = features // 2
    freq_rates = jnp.exp(-math.log(10000.0) * jnp.arange(half_width, dtype=jnp.float32) / half_width)
    angles = timesteps.astype(jnp.float32)[:, None] * freq_rates[None, :]
    return jnp.concatenate([jnp.sin(angles), jnp.cos(angles)], axis=1)

def matmul(value_tensor, weight_matrix):
    return jnp.einsum('qfw,wj->qfj', value_tensor, weight_matrix, precision=HIGHEST_PRECISION)

def conv_ref(grid_rows, tap_weights):
    seqs_here = grid_rows.shape[0]
    padded = jnp.pad(grid_rows.reshape(seqs_here, FREQ, TIME, -1), ((0, 0), (1, 1), (1, 1), (0, 0)))
    summed = jnp.zeros((seqs_here, FREQ * TIME, tap_weights.shape[2]), jnp.float32)
    for tap_index in range(9):
        row_off = tap_index // 3
        col_off = tap_index % 3
        window = padded[:, row_off:row_off + FREQ, col_off:col_off + TIME, :].reshape(seqs_here, FREQ * TIME, -1)
        summed = summed + matmul(window, tap_weights[tap_index])
    return summed

def attention_ref(queries, key_rows, value_rows, allowed, score_scale):
    seqs_here, query_count, channels = queries.shape
    key_count = key_rows.shape[1]
    heads_here = channels // HD
    query_heads = queries.reshape(seqs_here, query_count, heads_here, HD)
    key_heads = key_rows.reshape(seqs_here, key_count, heads_here, HD)
    value_heads = value_rows.reshape(seqs_here, key_count, heads_here, HD)
    scores = low_back(jnp.einsum('sqhd,skhd->shqk', query_heads, key_heads, precision=HIGHEST_PRECISION) * score_scale)
    if allowed is not None:
        scores = jnp.where(allowed[:, None], scores, MASK_VALUE)
    soft_low = low(jax.nn.softmax(scores, axis=-1))
    mixed_rows = jnp.einsum('shqk,skhd->sqhd', soft_low, value_heads, precision=HIGHEST_PRECISION)
    return mixed_rows.reshape(seqs_here, query_count, channels)

def block_forward(weights, inputs):
    in_low, back_low_w, up_low, down_low, gain_rows = weights
    resid_in, noise_rows, codec_rows, step_rows, segment_rows = inputs
    allowed = segment_rows[:, :, None] == segment_rows[:, None, :]
    score_scale = HD ** (-0.5)
    group_width = D // GROUPS
    normed_one = low(layer_norm(resid_in, gain_rows[0], gain_rows[1]))
    queries = low_back(low(matmul(normed_one, in_low[0])))
    key_rows = low_back(low(matmul(normed_one, in_low[1])))
    value_rows = low_back(low(matmul(normed_one, in_low[2])))
    mixed_rows = low_back(low(attention_ref(queries, key_rows, value_rows, allowed, score_scale)))
    resid_one = resid_in + low_back(matmul(mixed_rows, back_low_w[0]))
    normed_two = low(layer_norm(resid_one, gain_rows[2], gain_rows[3]))
    hidden_pre = low_back(matmul(normed_two, up_low))
    hidden = low(jax.nn.gelu(hidden_pre))
    resid_two = resid_one + low_back(matmul(hidden, down_low))
    noise_level = jnp.sqrt((step_rows.astype(jnp.float32) + 1.0) / TSTEPS)
    noisy = resid_two + noise_level[:, None, None] * noise_rows
    first_act = low(norm_silu(noisy, gain_rows[4], gain_rows[5], group_width))
    embed = low(jax.nn.silu(time_embedding(step_rows, D)))
    time_shift = jnp.einsum('sd,dc->sc', embed, in_low[3], precision=HIGHEST_PRECISION)
    conv_one = low_back(conv_ref(first_act, in_low[7:16]) + time_shift[:, None, :])
    second_act = low(norm_silu(conv_one, gain_rows[6], gain_rows[7], group_width))
    resid_three = noisy + low_back(conv_ref(second_act, back_low_w[2:11]))
    normed_three = low(layer_norm(resid_three, gain_rows[8], gain_rows[9]))
    cross_queries = low_back(low(matmul(normed_three, in_low[4])))
    cross_keys = low_back(low(matmul(codec_rows, in_low[5])))
    cross_values = low_back(low(matmul(codec_rows, in_low[6])))
    cross_mixed = low_back(low(attention_ref(cross_queries, cross_keys, cross_values, None, score_scale)))
    return resid_three + low_back(matmul(cross_mixed, back_low_w[1]))

def adam_update(master, grad_rows, first_moment, second_moment, decay_rate):
    first_new = MOMENT_DECAY * first_moment + (1.0 - MOMENT_DECAY) * grad_rows
    second_new = MOMENT_DECAY * second_moment + (1.0 - MOMENT_DECAY) * grad_rows * grad_rows
    correct = 1.0 - MOMENT_DECAY ** STEP
    update = first_new / correct / (jnp.sqrt(second_new / correct) + ADAM_EPS) + decay_rate * master
    return (first_new, second_new, update)

def reference(tokens, noise_field, codec_tokens, timesteps, segments, cotangent, w_in, w_back, w_up, w_down, m_in, m_back, m_up, m_down, v_in, v_back, v_up, v_down, norm_params, norm_m, norm_v):
    blocks = SEQS // 8
    noise_blocks = noise_field.astype(jnp.float32).reshape(blocks, 8, LEN, D)
    codec_blocks = codec_tokens.astype(jnp.float32).reshape(blocks, 8, CTOK, D)
    step_blocks = timesteps.reshape(blocks, 8)
    segment_blocks = segments.reshape(blocks, 8, LEN)

    def forward(resid_flat, in_master, back_master, up_master, down_master, gain_rows):
        weights = (low(in_master), low(back_master), low(up_master), low(down_master), gain_rows)
        inputs = (resid_flat.reshape(blocks, 8, LEN, D), noise_blocks, codec_blocks, step_blocks, segment_blocks)
        outputs = lax.map(jax.checkpoint(partial(block_forward, weights)), inputs)
        return outputs.reshape(TOKENS, D)
    primal, pull = jax.vjp(forward, tokens.astype(jnp.float32), w_in, w_back, w_up, w_down, norm_params)
    grad_x, grad_in, grad_back, grad_up, grad_down, grad_norm = pull(cotangent.astype(jnp.float32))
    m_in_new, v_in_new, upd_in = adam_update(w_in, grad_in, m_in, v_in, WEIGHT_DECAY)
    m_back_new, v_back_new, upd_back = adam_update(w_back, grad_back, m_back, v_back, WEIGHT_DECAY)
    m_up_new, v_up_new, upd_up = adam_update(w_up, grad_up, m_up, v_up, WEIGHT_DECAY)
    m_down_new, v_down_new, upd_down = adam_update(w_down, grad_down, m_down, v_down, WEIGHT_DECAY)
    weight_sq = jnp.concatenate([lax.optimization_barrier(jnp.sum(w_in * w_in, axis=(1, 2))), lax.optimization_barrier(jnp.sum(w_back * w_back, axis=(1, 2))), jnp.sum(w_up * w_up)[None], jnp.sum(w_down * w_down)[None]])
    update_sq = jnp.concatenate([lax.optimization_barrier(jnp.sum(upd_in * upd_in, axis=(1, 2))), lax.optimization_barrier(jnp.sum(upd_back * upd_back, axis=(1, 2))), jnp.sum(upd_up * upd_up)[None], jnp.sum(upd_down * upd_down)[None]])
    weight_len = jnp.sqrt(weight_sq)
    update_len = jnp.sqrt(update_sq)
    trust = weight_len / update_len
    new_in = w_in - LEARN_RATE * trust[0:16, None, None] * upd_in
    new_back = w_back - LEARN_RATE * trust[16:27, None, None] * upd_back
    new_up = w_up - LEARN_RATE * trust[27] * upd_up
    new_down = w_down - LEARN_RATE * trust[28] * upd_down
    norm_m_new, norm_v_new, upd_norm = adam_update(norm_params, grad_norm, norm_m, norm_v, 0.0)
    row_trust = jnp.sqrt(lax.optimization_barrier(jnp.sum(norm_params * norm_params, axis=1))) / jnp.sqrt(lax.optimization_barrier(jnp.sum(upd_norm * upd_norm, axis=1)))
    new_norm = norm_params - LEARN_RATE * row_trust[:, None] * upd_norm
    matrix_norms = jnp.stack([weight_len, update_len])
    return (primal.astype(jnp.bfloat16), grad_x, new_in, new_back, new_up, new_down, m_in_new, m_back_new, m_up_new, m_down_new, v_in_new, v_back_new, v_up_new, v_down_new, new_norm, norm_m_new, norm_v_new, matrix_norms)
```

```python
from functools import partial
import math

import jax
import jax.numpy as jnp
from jax import lax
from jax.sharding import PartitionSpec as P

HD = 64
GROUPS = 32
FREQ = 8
TIME = 64
TSTEPS = 1000
STEP = 5


NORM_EPS = 1e-05
MOMENT_DECAY = 0.5
LEARN_RATE = 0.5
WEIGHT_DECAY = 0.01
ADAM_EPS = 1e-06
MASK_VALUE = -1e30
HIGHEST_PRECISION = lax.Precision.HIGHEST


def layer_norm(value_tensor, gain_row, shift_row):
    centre = value_tensor - jnp.mean(value_tensor, axis=-1, keepdims=True)
    spread = jnp.mean(centre * centre, axis=-1, keepdims=True)
    return centre * lax.rsqrt(spread + NORM_EPS) * gain_row + shift_row


def group_norm(value_tensor, gain_row, shift_row, group_width):
    seqs_here, length, channels = value_tensor.shape
    grouped = value_tensor.reshape(seqs_here, length, channels // group_width, group_width)
    centre = grouped - jnp.mean(grouped, axis=(1, 3), keepdims=True)
    spread = jnp.mean(centre * centre, axis=(1, 3), keepdims=True)
    normed = (centre * lax.rsqrt(spread + NORM_EPS)).reshape(seqs_here, length, channels)
    return normed * gain_row + shift_row


def norm_silu(value_tensor, gain_row, shift_row, group_width):
    return jax.nn.silu(group_norm(value_tensor, gain_row, shift_row, group_width))


def time_embedding(timesteps, features):
    half_width = features // 2
    freq_rates = jnp.exp(
        -math.log(10000.0) * jnp.arange(half_width, dtype=jnp.float32) / half_width
    )
    angles = timesteps.astype(jnp.float32)[:, None] * freq_rates[None, :]
    return jnp.concatenate([jnp.sin(angles), jnp.cos(angles)], axis=1)


def flatten_rows(value_tensor):
    return value_tensor.reshape(-1, value_tensor.shape[-1])


def project(values_low, weight_matrix):
    summed = jnp.dot(flatten_rows(values_low), weight_matrix, preferred_element_type=jnp.float32)
    return summed.reshape(values_low.shape[0], values_low.shape[1], weight_matrix.shape[1])


def back_project(grad_low, weight_matrix):
    summed = jnp.einsum(
        "ne,ce->nc", flatten_rows(grad_low), weight_matrix, preferred_element_type=jnp.float32
    )
    return summed.reshape(grad_low.shape[0], grad_low.shape[1], weight_matrix.shape[0])


def weight_grad(left_low, right_low):
    return jnp.einsum(
        "nc,ne->ce",
        flatten_rows(left_low),
        flatten_rows(right_low),
        preferred_element_type=jnp.float32,
    )


def padded_grid(grid_rows):
    seqs_here = grid_rows.shape[0]
    return jnp.pad(grid_rows.reshape(seqs_here, FREQ, TIME, -1), ((0, 0), (1, 1), (1, 1), (0, 0)))


def grid_window(padded, tap_index):
    row_off = tap_index // 3
    col_off = tap_index % 3
    return padded[:, row_off : row_off + FREQ, col_off : col_off + TIME, :].reshape(
        -1, padded.shape[3]
    )


def conv_grid(grid_rows, tap_weights, backward):
    seqs_here = grid_rows.shape[0]
    padded = padded_grid(grid_rows)
    out_width = tap_weights.shape[1] if backward else tap_weights.shape[2]
    summed = jnp.zeros((seqs_here * FREQ * TIME, out_width), jnp.float32)
    for tap_index in range(9):
        window = grid_window(padded, tap_index)
        if backward:
            summed = summed + jnp.einsum(
                "nc,dc->nd", window, tap_weights[8 - tap_index], preferred_element_type=jnp.float32
            )
        else:
            summed = summed + jnp.dot(
                window, tap_weights[tap_index], preferred_element_type=jnp.float32
            )
    return summed.reshape(seqs_here, FREQ * TIME, out_width)


def conv_weight_grad(grid_low, grad_low):
    padded = padded_grid(grid_low)
    grad_flat = flatten_rows(grad_low)
    tap_grads = []
    for tap_index in range(9):
        window = grid_window(padded, tap_index)
        tap_grads.append(
            jnp.einsum("nc,ne->ce", window, grad_flat, preferred_element_type=jnp.float32)
        )
    return jnp.stack(tap_grads)


def split_heads(rows_low):
    return rows_low.reshape(rows_low.shape[0], rows_low.shape[1], rows_low.shape[2] // HD, HD)


def head_scores(queries, key_rows, allowed, score_scale):
    scores = (
        jnp.einsum(
            "sqhd,skhd->shqk",
            split_heads(queries),
            split_heads(key_rows),
            preferred_element_type=jnp.float32,
        )
        * score_scale
    )
    if allowed is not None:
        scores = jnp.where(allowed[:, None], scores, MASK_VALUE)
    return scores


def attend(queries, key_rows, value_rows, allowed, score_scale):
    scores = head_scores(queries, key_rows, allowed, score_scale)
    highest = jnp.max(scores, axis=-1, keepdims=True)
    raised = jnp.exp(scores - highest)
    totals = jnp.sum(raised, axis=-1, keepdims=True)
    soft_low = (raised / totals).astype(jnp.bfloat16)
    mixed_rows = jnp.einsum(
        "shqk,skhd->sqhd", soft_low, split_heads(value_rows), preferred_element_type=jnp.float32
    )
    return (mixed_rows.reshape(queries.shape), highest + jnp.log(totals))


def attend_back(queries, key_rows, value_rows, allowed, score_scale, log_total, grad_mixed):
    scores = head_scores(queries, key_rows, allowed, score_scale)
    soft = jnp.exp(scores - log_total)
    grad_heads = split_heads(grad_mixed)
    grad_soft = jnp.einsum(
        "sqhd,skhd->shqk", grad_heads, split_heads(value_rows), preferred_element_type=jnp.float32
    )
    grad_values = jnp.einsum(
        "shqk,sqhd->skhd", soft.astype(jnp.bfloat16), grad_heads, preferred_element_type=jnp.float32
    )
    row_dot = jnp.sum(soft * grad_soft, axis=-1, keepdims=True)
    grad_scores = (soft * (grad_soft - row_dot)).astype(jnp.bfloat16)
    grad_queries = (
        jnp.einsum(
            "shqk,skhd->sqhd",
            grad_scores,
            split_heads(key_rows),
            preferred_element_type=jnp.float32,
        )
        * score_scale
    )
    grad_keys = (
        jnp.einsum(
            "shqk,sqhd->skhd", grad_scores, split_heads(queries), preferred_element_type=jnp.float32
        )
        * score_scale
    )
    return (
        grad_queries.reshape(queries.shape).astype(jnp.bfloat16),
        grad_keys.reshape(key_rows.shape).astype(jnp.bfloat16),
        grad_values.reshape(value_rows.shape).astype(jnp.bfloat16),
    )


def tensor_parallel_sum(term_rows):
    return lax.psum(term_rows, "mp")


def matrix_squares(first_stack, second_stack, up_rows, down_rows):
    return jnp.concatenate(
        [
            jnp.sum(first_stack * first_stack, axis=(1, 2)),
            jnp.sum(second_stack * second_stack, axis=(1, 2)),
            jnp.sum(up_rows * up_rows)[None],
            jnp.sum(down_rows * down_rows)[None],
        ]
    )


def adam_update(master, grad_rows, first_moment, second_moment, decay_rate):
    first_new = MOMENT_DECAY * first_moment + (1.0 - MOMENT_DECAY) * grad_rows
    second_new = MOMENT_DECAY * second_moment + (1.0 - MOMENT_DECAY) * grad_rows * grad_rows
    correct = 1.0 - MOMENT_DECAY**STEP
    update = first_new / correct / (jnp.sqrt(second_new / correct) + ADAM_EPS) + decay_rate * master
    return (first_new, second_new, update)


def generic_device(
    tokens,
    noise_field,
    codec_tokens,
    timesteps,
    segments,
    cotangent,
    w_in,
    w_back,
    w_up,
    w_down,
    m_in,
    m_back,
    m_up,
    m_down,
    v_in,
    v_back,
    v_up,
    v_down,
    norm_params,
    norm_m,
    norm_v,
):
    seqs_here, length = segments.shape
    features = tokens.shape[1]
    chans_here = w_in.shape[2]
    group_width = features // GROUPS
    score_scale = HD ** (-0.5)
    channel_start = lax.axis_index("mp") * chans_here
    lead_device = (lax.axis_index("mp") == 0).astype(jnp.float32)
    weight_sq = matrix_squares(w_in, w_back, w_up, w_down)
    full_in, full_back, complete_up_weight, full_down = (
        lax.all_gather(w_in.astype(jnp.bfloat16), "dp", axis=1, tiled=True),
        lax.all_gather(w_back.astype(jnp.bfloat16), "dp", axis=2, tiled=True),
        lax.all_gather(w_up.astype(jnp.bfloat16), "dp", axis=0, tiled=True),
        lax.all_gather(w_down.astype(jnp.bfloat16), "dp", axis=1, tiled=True),
    )
    resid_in = tokens.astype(jnp.float32).reshape(seqs_here, length, features)
    allowed = segments[:, :, None] == segments[:, None, :]
    normed_one_low = layer_norm(resid_in, norm_params[0], norm_params[1]).astype(jnp.bfloat16)
    queries = project(normed_one_low, full_in[0]).astype(jnp.bfloat16)
    key_rows = project(normed_one_low, full_in[1]).astype(jnp.bfloat16)
    value_rows = project(normed_one_low, full_in[2]).astype(jnp.bfloat16)
    mixed_rows, log_self = attend(queries, key_rows, value_rows, allowed, score_scale)
    mixed_low = mixed_rows.astype(jnp.bfloat16)
    resid_one = resid_in + tensor_parallel_sum(project(mixed_low, full_back[0]))
    normed_two_low = layer_norm(resid_one, norm_params[2], norm_params[3]).astype(jnp.bfloat16)
    hidden_pre = project(normed_two_low, complete_up_weight)
    hidden_low = jax.nn.gelu(hidden_pre).astype(jnp.bfloat16)
    resid_two = resid_one + tensor_parallel_sum(project(hidden_low, full_down))
    noise_level = jnp.sqrt((timesteps.astype(jnp.float32) + 1.0) / TSTEPS)
    noisy = resid_two + noise_level[:, None, None] * noise_field.astype(jnp.float32).reshape(
        seqs_here, length, features
    )
    first_low = norm_silu(noisy, norm_params[4], norm_params[5], group_width).astype(jnp.bfloat16)
    embed_low = jax.nn.silu(time_embedding(timesteps, features)).astype(jnp.bfloat16)
    time_shift = jnp.dot(embed_low, full_in[3], preferred_element_type=jnp.float32)
    conv_one = conv_grid(first_low, full_in[7:16], False) + time_shift[:, None, :]
    gain_six = lax.dynamic_slice_in_dim(norm_params[6], channel_start, chans_here)
    shift_six = lax.dynamic_slice_in_dim(norm_params[7], channel_start, chans_here)
    second_low = norm_silu(conv_one, gain_six, shift_six, group_width).astype(jnp.bfloat16)
    resid_three = noisy + tensor_parallel_sum(conv_grid(second_low, full_back[2:11], False))
    normed_three_low = layer_norm(resid_three, norm_params[8], norm_params[9]).astype(jnp.bfloat16)
    cross_queries = project(normed_three_low, full_in[4]).astype(jnp.bfloat16)
    cross_keys = project(codec_tokens, full_in[5]).astype(jnp.bfloat16)
    cross_values = project(codec_tokens, full_in[6]).astype(jnp.bfloat16)
    cross_mixed, log_cross = attend(cross_queries, cross_keys, cross_values, None, score_scale)
    cross_low = cross_mixed.astype(jnp.bfloat16)
    result = resid_three + tensor_parallel_sum(project(cross_low, full_back[1]))
    out_low = result.astype(jnp.bfloat16)
    grad_out = cotangent.astype(jnp.float32).reshape(seqs_here, length, features)
    grad_cross_low = grad_out.astype(jnp.bfloat16)
    grad_w_co = weight_grad(cross_low, grad_cross_low)
    grad_cross_mixed = back_project(grad_cross_low, full_back[1]).astype(jnp.bfloat16)
    grad_cq, grad_ck, grad_cv = attend_back(
        cross_queries, cross_keys, cross_values, None, score_scale, log_cross, grad_cross_mixed
    )
    grad_w_cq = weight_grad(normed_three_low, grad_cq)
    grad_w_ck = weight_grad(codec_tokens, grad_ck)
    grad_w_cv = weight_grad(codec_tokens, grad_cv)
    grad_normed_three = tensor_parallel_sum(back_project(grad_cq, full_in[4]))
    pull_three = jax.vjp(layer_norm, resid_three, norm_params[8], norm_params[9])[1]
    grad_part, grad_gain_eight, grad_shift_eight = pull_three(grad_normed_three)
    grad_three = grad_out + grad_part
    grad_conv_low = grad_three.astype(jnp.bfloat16)
    grad_w_conv_two = conv_weight_grad(second_low, grad_conv_low)
    grad_second = conv_grid(grad_conv_low, full_back[2:11], True)
    gather_second_moment = jax.vjp(
        partial(norm_silu, group_width=group_width), conv_one, gain_six, shift_six
    )[1]
    grad_conv_one, grad_gain_six, grad_shift_six = gather_second_moment(grad_second)
    grad_conv_one_low = grad_conv_one.astype(jnp.bfloat16)
    grad_w_time = jnp.einsum(
        "sd,sc->dc",
        embed_low.astype(jnp.float32),
        jnp.sum(grad_conv_one_low.astype(jnp.float32), axis=1),
        precision=HIGHEST_PRECISION,
    )
    grad_w_conv_one = conv_weight_grad(first_low, grad_conv_one_low)
    grad_first = tensor_parallel_sum(conv_grid(grad_conv_one_low, full_in[7:16], True))
    gather_first_moment = jax.vjp(
        partial(norm_silu, group_width=group_width), noisy, norm_params[4], norm_params[5]
    )[1]
    grad_part, grad_gain_four, grad_shift_four = gather_first_moment(grad_first)
    grad_two = grad_three + grad_part
    grad_mlp_low = grad_two.astype(jnp.bfloat16)
    grad_w_down = weight_grad(hidden_low, grad_mlp_low)
    grad_hidden = back_project(grad_mlp_low, full_down)
    grad_pre_low = jax.vjp(jax.nn.gelu, hidden_pre)[1](grad_hidden)[0].astype(jnp.bfloat16)
    up_weight_gradient = weight_grad(normed_two_low, grad_pre_low)
    grad_normed_two = tensor_parallel_sum(back_project(grad_pre_low, complete_up_weight))
    pull_two = jax.vjp(layer_norm, resid_one, norm_params[2], norm_params[3])[1]
    grad_part, grad_gain_two, grad_shift_two = pull_two(grad_normed_two)
    grad_one = grad_two + grad_part
    grad_attn_low = grad_one.astype(jnp.bfloat16)
    grad_w_out = weight_grad(mixed_low, grad_attn_low)
    grad_mixed = back_project(grad_attn_low, full_back[0]).astype(jnp.bfloat16)
    grad_q, grad_k, grad_v = attend_back(
        queries, key_rows, value_rows, allowed, score_scale, log_self, grad_mixed
    )
    grad_w_q = weight_grad(normed_one_low, grad_q)
    grad_w_k = weight_grad(normed_one_low, grad_k)
    grad_w_v = weight_grad(normed_one_low, grad_v)
    grad_normed_one = tensor_parallel_sum(
        back_project(grad_q, full_in[0])
        + back_project(grad_k, full_in[1])
        + back_project(grad_v, full_in[2])
    )
    pull_one = jax.vjp(layer_norm, resid_in, norm_params[0], norm_params[1])[1]
    grad_part, grad_gain_zero, grad_shift_zero = pull_one(grad_normed_one)
    grad_input = grad_one + grad_part
    grad_in_stack = jnp.concatenate(
        [
            jnp.stack([grad_w_q, grad_w_k, grad_w_v, grad_w_time, grad_w_cq, grad_w_ck, grad_w_cv]),
            grad_w_conv_one,
        ]
    )
    grad_back_stack = jnp.concatenate([jnp.stack([grad_w_out, grad_w_co]), grad_w_conv_two])
    summed_in, summed_back, summed_up, summed_down = (
        lax.psum_scatter(grad_in_stack, "dp", scatter_dimension=1, tiled=True),
        lax.psum_scatter(grad_back_stack, "dp", scatter_dimension=2, tiled=True),
        lax.psum_scatter(up_weight_gradient, "dp", scatter_dimension=0, tiled=True),
        lax.psum_scatter(grad_w_down, "dp", scatter_dimension=1, tiled=True),
    )
    shared_rows = (
        jnp.stack(
            [
                grad_gain_zero,
                grad_shift_zero,
                grad_gain_two,
                grad_shift_two,
                grad_gain_four,
                grad_shift_four,
            ]
        )
        * lead_device
    )
    group_rows = lax.dynamic_update_slice(
        jnp.zeros((2, features), jnp.float32),
        jnp.stack([grad_gain_six, grad_shift_six]),
        (0, channel_start),
    )
    last_rows = jnp.stack([grad_gain_eight, grad_shift_eight]) * lead_device
    norm_grad = lax.psum(jnp.concatenate([shared_rows, group_rows, last_rows]), ("dp", "mp"))
    m_in_new, v_in_new, upd_in = adam_update(w_in, summed_in, m_in, v_in, WEIGHT_DECAY)
    m_back_new, v_back_new, upd_back = adam_update(
        w_back, summed_back, m_back, v_back, WEIGHT_DECAY
    )
    m_up_new, v_up_new, upd_up = adam_update(w_up, summed_up, m_up, v_up, WEIGHT_DECAY)
    m_down_new, v_down_new, upd_down = adam_update(
        w_down, summed_down, m_down, v_down, WEIGHT_DECAY
    )
    update_sq = matrix_squares(upd_in, upd_back, upd_up, upd_down)
    weight_total, update_total = lax.psum((weight_sq, update_sq), ("dp", "mp"))
    weight_len = jnp.sqrt(weight_total)
    update_len = jnp.sqrt(update_total)
    trust = weight_len / update_len
    new_in = w_in - LEARN_RATE * trust[0:16, None, None] * upd_in
    new_back = w_back - LEARN_RATE * trust[16:27, None, None] * upd_back
    new_up = w_up - LEARN_RATE * trust[27] * upd_up
    new_down = w_down - LEARN_RATE * trust[28] * upd_down
    norm_m_new, norm_v_new, upd_norm = adam_update(norm_params, norm_grad, norm_m, norm_v, 0.0)
    row_trust = jnp.sqrt(jnp.sum(norm_params * norm_params, axis=1)) / jnp.sqrt(
        jnp.sum(upd_norm * upd_norm, axis=1)
    )
    new_norm = norm_params - LEARN_RATE * row_trust[:, None] * upd_norm
    matrix_norms = jnp.stack([weight_len, update_len])
    out_rows = out_low.reshape(seqs_here * length, features)
    grad_rows = grad_input.reshape(seqs_here * length, features)
    return (
        out_rows,
        grad_rows,
        new_in,
        new_back,
        new_up,
        new_down,
        m_in_new,
        m_back_new,
        m_up_new,
        m_down_new,
        v_in_new,
        v_back_new,
        v_up_new,
        v_down_new,
        new_norm,
        norm_m_new,
        norm_v_new,
        matrix_norms,
    )


CORE_SWAP = [(i, i ^ 1) for i in range(4)]
X_SWAP = [(i, i ^ 2) for i in range(4)]
Y_SWAP = [(i, i ^ 1) for i in range(8)]
Z_TURN = [[(i, (i + 2 * k) % 8) for i in range(8)] for k in range(4)]
LOW = jnp.bfloat16
F32 = jnp.float32


def swap_core(v):
    return lax.ppermute(v, "mp", CORE_SWAP)


def swap_x(v):
    return lax.ppermute(v, "mp", X_SWAP)


def swap_y(v):
    return lax.ppermute(v, "dp", Y_SWAP)


def turn_z(v, k):
    return lax.ppermute(v, "dp", Z_TURN[k])


def by_parity(flag, own, other, axis):
    first = jnp.where(flag == 0, own, other)
    second = jnp.where(flag == 0, other, own)
    return jnp.stack([first, second], axis=axis)


def gather_line(piece, z):
    rows, cols = piece.shape
    buf = jnp.zeros((4, rows, cols), piece.dtype)
    for k in range(4):
        got = piece if k == 0 else turn_z(piece, k)
        buf = lax.dynamic_update_slice(buf, got[None], ((z - k) % 4, 0, 0))
    return buf


def gather_zyx(piece, z, y):
    line = gather_line(piece, z)
    plane = by_parity(y, line, swap_y(line), 1).reshape(-1, piece.shape[1])
    return plane, swap_x(plane)


def gather_zxy(piece, z, y):
    line = gather_line(piece, z)
    line_x = swap_x(line)
    own = by_parity(y, line, swap_y(line), 1).reshape(-1, piece.shape[1])
    other = by_parity(y, line_x, swap_y(line_x), 1).reshape(-1, piece.shape[1])
    return own, other


def pick(v, index, axis):
    return lax.dynamic_index_in_dim(v, index, axis, keepdims=False)


def scatter_line(rows4, z):
    sums = pick(rows4, z, 0)
    for k in range(1, 4):
        sent = pick(rows4, (z + k) % 4, 0).astype(LOW)
        sums = sums + turn_z(sent, k).astype(F32)
    return sums


def scatter_xyz(own, other, z, y):
    cols = own.shape[1]
    got = swap_x(other)
    plane = (own.astype(F32) + got.astype(F32)).reshape(4, 2, -1, cols)
    got_y = swap_y(pick(plane, 1 - y, 1).astype(LOW))
    return scatter_line(pick(plane, y, 1) + got_y.astype(F32), z)


def scatter_yxz(own, other, z, y):
    cols = own.shape[1]
    lines = []
    for part in (other, own):
        part = part.reshape(4, 2, -1, cols)
        got = swap_y(pick(part, 1 - y, 1))
        lines.append(pick(part, y, 1).astype(F32) + got.astype(F32))
    got_x = swap_x(lines[0].astype(LOW))
    return scatter_line(lines[1] + got_x.astype(F32), z)


def core_sum(partial_rows):
    low = partial_rows.astype(LOW)
    return low.astype(F32) + swap_core(low).astype(F32)


def ln_stats(v):
    centre = v - jnp.mean(v, axis=-1, keepdims=True)
    scale = lax.rsqrt(jnp.mean(centre * centre, axis=-1, keepdims=True) + NORM_EPS)
    return centre * scale, scale


def ln_back(v, gain, grad):
    hat, scale = ln_stats(v)
    pulled = grad * gain
    back = scale * (
        pulled
        - jnp.mean(pulled, axis=-1, keepdims=True)
        - hat * jnp.mean(pulled * hat, axis=-1, keepdims=True)
    )
    return back, jnp.sum(grad * hat, axis=0), jnp.sum(grad, axis=0)


def group_mean(row, width, count):
    means = jnp.mean(row.reshape(-1, width), axis=1, keepdims=True) / count
    return jnp.broadcast_to(means, (means.shape[0], width)).reshape(-1)


def gn_stats(v, width):
    rows = v.shape[0]
    centre = v - group_mean(jnp.sum(v, axis=0), width, rows)
    scale = lax.rsqrt(group_mean(jnp.sum(centre * centre, axis=0), width, rows) + NORM_EPS)
    return centre * scale, scale


def gn_silu(v, gain, shift, width):
    hat, _ = gn_stats(v, width)
    return jax.nn.silu(hat * gain + shift)


def gn_silu_back(v, gain, shift, width, grad):
    rows = v.shape[0]
    hat, scale = gn_stats(v, width)
    pre = hat * gain + shift
    gate = jax.nn.sigmoid(pre)
    grad_pre = grad * gate * (1.0 + pre * (1.0 - gate))
    grad_gain = jnp.sum(grad_pre * hat, axis=0)
    grad_shift = jnp.sum(grad_pre, axis=0)
    back = scale * (
        grad_pre * gain
        - group_mean(grad_shift * gain, width, rows)
        - hat * group_mean(grad_gain * gain, width, rows)
    )
    return back, grad_gain, grad_shift


def tap_shift(rows, tap, back):
    row_off, col_off = tap // 3 - 1, tap % 3 - 1
    if back:
        row_off, col_off = -row_off, -col_off
    grid = jnp.pad(rows.reshape(FREQ, TIME, -1), ((1, 1), (1, 1), (0, 0)))
    return grid[
        1 + row_off : 1 + row_off + FREQ, 1 + col_off : 1 + col_off + TIME
    ].reshape(rows.shape)


def tap_columns(rows, back):
    return jnp.concatenate([tap_shift(rows, tap, back) for tap in range(9)], axis=1)


def tap_sum(products, back):
    width = products.shape[1] // 9
    return sum(
        tap_shift(products[:, width * tap : width * (tap + 1)], tap, back) for tap in range(9)
    )


def mm(a, b):
    return lax.dot_general(a, b, (((1,), (0,)), ((), ())), preferred_element_type=F32)


def mm_nt(a, b):
    return lax.dot_general(a, b, (((1,), (1,)), ((), ())), preferred_element_type=F32)


def mm_tn(a, b):
    return lax.dot_general(a, b, (((0,), (0,)), ((), ())), preferred_element_type=F32)


def fast_device(
    tokens,
    noise_field,
    codec_tokens,
    timesteps,
    segments,
    cotangent,
    w_in,
    w_back,
    w_up,
    w_down,
    m_in,
    m_back,
    m_up,
    m_down,
    v_in,
    v_back,
    v_up,
    v_down,
    norm_params,
    norm_m,
    norm_v,
):
    length = segments.shape[1]
    features = tokens.shape[1]
    chans = w_in.shape[2]
    width = features // GROUPS
    score_scale = HD ** (-0.5)
    mp = lax.axis_index("mp")
    dp = lax.axis_index("dp")
    x, core, z, y = mp // 2, mp % 2, dp // 2, dp % 2
    lead = (core == 0).astype(F32)
    slices = [2 * x + core, 2 * (1 - x) + core]

    low_in = w_in.astype(LOW).transpose(1, 0, 2).reshape(w_in.shape[1], -1)
    low_back = w_back.astype(LOW).transpose(2, 0, 1).reshape(w_back.shape[2], -1)
    low_up = w_up.astype(LOW)
    low_down = w_down.astype(LOW).T
    n = chans
    piece_attn = jnp.concatenate([low_in[:, : 3 * n], low_back[:, :n]], axis=1)
    piece_mlp = jnp.concatenate([low_up, low_down], axis=1)
    piece_one = low_in[:, 7 * n :]
    piece_two = jnp.concatenate([low_back[:, 2 * n :], low_in[:, 3 * n : 4 * n]], axis=1)
    piece_cross = jnp.concatenate([low_in[:, 4 * n : 7 * n], low_back[:, n : 2 * n]], axis=1)
    w_attn = gather_zyx(piece_attn, z, y)
    w_mlp = gather_zxy(piece_mlp, z, y)
    w_one = gather_zyx(piece_one, z, y)
    w_two = gather_zxy(piece_two, z, y)
    w_cross = gather_zyx(piece_cross, z, y)
    weight_sq = matrix_squares(w_in, w_back, w_up, w_down)

    def own_rows(v):
        return lax.dynamic_slice_in_dim(v, x * length, length, 0)

    tok = own_rows(tokens).astype(F32)
    noise = own_rows(noise_field).astype(F32)
    cot = own_rows(cotangent)
    codec = pick(codec_tokens, x, 0)
    step = pick(timesteps, x, 0)
    seg = pick(segments, x, 0)
    allowed = (seg[:, None] == seg[None, :])[None]
    hid = w_up.shape[1]

    normed_one = ln_stats(tok)[0] * norm_params[0] + norm_params[1]
    normed_one = normed_one.astype(LOW)
    qkv = [mm(normed_one, w[:, : 3 * n]).astype(LOW) for w in w_attn]

    def join(parts, first):
        return jnp.concatenate([p[:, first * n : (first + 1) * n] for p in parts], axis=1)[None]

    queries, keys, values = join(qkv, 0), join(qkv, 1), join(qkv, 2)
    mixed, log_self = attend(queries, keys, values, allowed, score_scale)
    mixed = mixed.astype(LOW)[0]
    mixed = [mixed[:, :n], mixed[:, n:]]
    resid_one = tok + core_sum(sum(mm_nt(a, w[:, 3 * n :]) for a, w in zip(mixed, w_attn)))
    normed_two = (ln_stats(resid_one)[0] * norm_params[2] + norm_params[3]).astype(LOW)
    pre = [mm(normed_two, w[:, :hid]) for w in w_mlp]
    hidden = [jax.nn.gelu(p).astype(LOW) for p in pre]
    resid_two = resid_one + core_sum(sum(mm_nt(a, w[:, hid:]) for a, w in zip(hidden, w_mlp)))
    noise_level = jnp.sqrt((step.astype(F32) + 1.0) / TSTEPS)
    noisy = resid_two + noise_level * noise
    first = gn_silu(noisy, norm_params[4], norm_params[5], width).astype(LOW)
    embed = jax.nn.silu(time_embedding(step[None], features)).astype(LOW)
    gains = [lax.dynamic_slice_in_dim(norm_params[6], s * n, n) for s in slices]
    shifts = [lax.dynamic_slice_in_dim(norm_params[7], s * n, n) for s in slices]
    conv_one = [
        tap_sum(mm(first, w), False) + mm(embed, t[:, 9 * n :]) for w, t in zip(w_one, w_two)
    ]
    second = [gn_silu(v, g, b, width).astype(LOW) for v, g, b in zip(conv_one, gains, shifts)]
    second_taps = [tap_columns(v, False) for v in second]
    resid_three = noisy + core_sum(
        sum(mm_nt(a, w[:, : 9 * n]) for a, w in zip(second_taps, w_two))
    )
    normed_three = (ln_stats(resid_three)[0] * norm_params[8] + norm_params[9]).astype(LOW)
    cross_q = [mm(normed_three, w[:, :n]).astype(LOW) for w in w_cross]
    cross_kv = [mm(codec, w[:, n : 3 * n]).astype(LOW) for w in w_cross]
    cq, ck, cv = join(cross_q, 0), join(cross_kv, 0), join(cross_kv, 1)
    cross_mixed, log_cross = attend(cq, ck, cv, None, score_scale)
    cross_mixed = cross_mixed.astype(LOW)[0]
    cross_mixed = [cross_mixed[:, :n], cross_mixed[:, n:]]
    result = resid_three + core_sum(
        sum(mm_nt(a, w[:, 3 * n :]) for a, w in zip(cross_mixed, w_cross))
    )
    out_low = result.astype(LOW)
    out_rows = by_parity(x, out_low, swap_x(out_low), 0).reshape(-1, features)

    grad_out = cot.astype(F32)
    grad_co = [mm_tn(cot, a) for a in cross_mixed]
    grad_cm = jnp.concatenate([mm(cot, w[:, 3 * n :]).astype(LOW) for w in w_cross], axis=1)
    grad_cq, grad_ck, grad_cv = attend_back(
        cq, ck, cv, None, score_scale, log_cross, grad_cm[None]
    )

    def parts(v):
        return [v[0][:, :n], v[0][:, n:]]

    grad_cq = parts(grad_cq)
    grad_ckv = [
        jnp.concatenate([a, b], axis=1) for a, b in zip(parts(grad_ck), parts(grad_cv))
    ]
    d_cross = [
        jnp.concatenate([mm_tn(normed_three, q), mm_tn(codec, kv), o], axis=1).astype(LOW)
        for q, kv, o in zip(grad_cq, grad_ckv, grad_co)
    ]
    sum_cross = scatter_xyz(d_cross[0], d_cross[1], z, y)
    grad_n3 = core_sum(sum(mm_nt(g, w[:, :n]) for g, w in zip(grad_cq, w_cross)))
    part, gain_eight, shift_eight = ln_back(resid_three, norm_params[8], grad_n3)
    grad_three = grad_out + part
    grad_conv = grad_three.astype(LOW)
    d_two = [mm_tn(grad_conv, a) for a in second_taps]
    grad_second = [tap_sum(mm(grad_conv, w[:, : 9 * n]), True) for w in w_two]
    backs = [
        gn_silu_back(v, g, b, width, d)
        for v, g, b, d in zip(conv_one, gains, shifts, grad_second)
    ]
    grad_c1 = [b[0].astype(LOW) for b in backs]
    d_time = [
        embed[0].astype(F32)[:, None] * jnp.sum(g.astype(F32), axis=0)[None, :] for g in grad_c1
    ]
    d_two = [jnp.concatenate([a, b], axis=1).astype(LOW) for a, b in zip(d_two, d_time)]
    sum_two = scatter_yxz(d_two[0], d_two[1], z, y)
    c1_taps = [tap_columns(g, True) for g in grad_c1]
    d_one = [mm_tn(first, g).astype(LOW) for g in c1_taps]
    sum_one = scatter_xyz(d_one[0], d_one[1], z, y)
    grad_first = core_sum(sum(mm_nt(g, w) for g, w in zip(c1_taps, w_one)))
    part, gain_four, shift_four = gn_silu_back(
        noisy, norm_params[4], norm_params[5], width, grad_first
    )
    grad_two = grad_three + part
    grad_mlp = grad_two.astype(LOW)
    grad_hidden = [mm(grad_mlp, w[:, hid:]) for w in w_mlp]
    grad_pre = [
        jax.vjp(jax.nn.gelu, p)[1](g)[0].astype(LOW) for p, g in zip(pre, grad_hidden)
    ]
    d_mlp = [
        jnp.concatenate([mm_tn(normed_two, g), mm_tn(grad_mlp, a)], axis=1).astype(LOW)
        for g, a in zip(grad_pre, hidden)
    ]
    sum_mlp = scatter_yxz(d_mlp[0], d_mlp[1], z, y)
    grad_n2 = core_sum(sum(mm_nt(g, w[:, :hid]) for g, w in zip(grad_pre, w_mlp)))
    part, gain_two, shift_two = ln_back(resid_one, norm_params[2], grad_n2)
    grad_one = grad_two + part
    grad_attn = grad_one.astype(LOW)
    grad_o = [mm_tn(grad_attn, a) for a in mixed]
    grad_mixed = jnp.concatenate([mm(grad_attn, w[:, 3 * n :]).astype(LOW) for w in w_attn], axis=1)
    grad_q, grad_k, grad_v = attend_back(
        queries, keys, values, allowed, score_scale, log_self, grad_mixed[None]
    )
    grad_qkv = [
        jnp.concatenate(g, axis=1) for g in zip(parts(grad_q), parts(grad_k), parts(grad_v))
    ]
    d_attn = [
        jnp.concatenate([mm_tn(normed_one, g), o], axis=1).astype(LOW)
        for g, o in zip(grad_qkv, grad_o)
    ]
    sum_attn = scatter_xyz(d_attn[0], d_attn[1], z, y)
    grad_n1 = core_sum(sum(mm_nt(g, w[:, : 3 * n]) for g, w in zip(grad_qkv, w_attn)))
    part, gain_zero, shift_zero = ln_back(tok, norm_params[0], grad_n1)
    grad_x = (grad_one + part).astype(LOW)
    half = length // 2
    mine = lax.dynamic_slice_in_dim(grad_x, core * half, half, 0)
    got = swap_x(mine)
    other_x = by_parity(core, got, swap_core(got), 0).reshape(length, features)
    grad_rows = by_parity(x, grad_x, other_x, 0).reshape(-1, features).astype(F32)

    def unpack_in(v):
        return v.reshape(v.shape[0], -1, n).transpose(1, 0, 2)

    def unpack_back(v):
        return v.reshape(v.shape[0], -1, n).transpose(1, 2, 0)

    summed_in = unpack_in(
        jnp.concatenate(
            [sum_attn[:, : 3 * n], sum_two[:, 9 * n :], sum_cross[:, : 3 * n], sum_one], axis=1
        )
    )
    summed_back = unpack_back(
        jnp.concatenate([sum_attn[:, 3 * n :], sum_cross[:, 3 * n :], sum_two[:, : 9 * n]], axis=1)
    )
    summed_up = sum_mlp[:, :hid]
    summed_down = sum_mlp[:, hid:].T

    shared = jnp.stack([gain_zero, shift_zero, gain_two, shift_two, gain_four, shift_four]) * lead
    group_rows = jnp.zeros((2, features), F32)
    for s, b in zip(slices, backs):
        group_rows = lax.dynamic_update_slice(group_rows, jnp.stack([b[1], b[2]]), (0, s * n))
    last = jnp.stack([gain_eight, shift_eight]) * lead
    norm_grad = lax.psum(jnp.concatenate([shared, group_rows, last]), ("dp", "mp"))
    return finish(
        out_rows, grad_rows, weight_sq, (summed_in, summed_back, summed_up, summed_down),
        (w_in, w_back, w_up, w_down), (m_in, m_back, m_up, m_down), (v_in, v_back, v_up, v_down),
        norm_grad, norm_params, norm_m, norm_v,
    )


def finish(out_rows, grad_rows, weight_sq, grads, masters, moments, squares, norm_grad, norm_params, norm_m, norm_v):
    stepped = [
        adam_update(w, g, m, v, WEIGHT_DECAY)
        for w, g, m, v in zip(masters, grads, moments, squares)
    ]
    new_m = [s[0] for s in stepped]
    new_v = [s[1] for s in stepped]
    updates = [s[2] for s in stepped]
    update_sq = matrix_squares(*updates)
    weight_total, update_total = lax.psum((weight_sq, update_sq), ("dp", "mp"))
    weight_len = jnp.sqrt(weight_total)
    update_len = jnp.sqrt(update_total)
    trust = LEARN_RATE * (weight_len / update_len)
    scales = (trust[0:16, None, None], trust[16:27, None, None], trust[27], trust[28])
    new_w = [w - s * u for w, s, u in zip(masters, scales, updates)]
    norm_m_new, norm_v_new, upd_norm = adam_update(norm_params, norm_grad, norm_m, norm_v, 0.0)
    row_trust = jnp.sqrt(jnp.sum(norm_params * norm_params, axis=1)) / jnp.sqrt(
        jnp.sum(upd_norm * upd_norm, axis=1)
    )
    new_norm = norm_params - LEARN_RATE * row_trust[:, None] * upd_norm
    return (
        out_rows, grad_rows, *new_w, *new_m, *new_v, new_norm, norm_m_new, norm_v_new,
        jnp.stack([weight_len, update_len]),
    )


def solution(mesh):
    per_device = fast_device if dict(mesh.shape) == {"dp": 8, "mp": 4} else generic_device
    placed = (
        P("dp", None),
        P("dp", None),
        P("dp", None, None),
        P("dp"),
        P("dp", None),
        P("dp", None),
        P(None, "dp", "mp"),
        P(None, "mp", "dp"),
        P("dp", "mp"),
        P("mp", "dp"),
        P(None, "dp", "mp"),
        P(None, "mp", "dp"),
        P("dp", "mp"),
        P("mp", "dp"),
        P(None, "dp", "mp"),
        P(None, "mp", "dp"),
        P("dp", "mp"),
        P("mp", "dp"),
        P(),
        P(),
        P(),
    )
    return jax.shard_map(
        per_device,
        mesh=mesh,
        in_specs=placed,
        out_specs=(
            P("dp", None),
            P("dp", None),
            P(None, "dp", "mp"),
            P(None, "mp", "dp"),
            P("dp", "mp"),
            P("mp", "dp"),
            P(None, "dp", "mp"),
            P(None, "mp", "dp"),
            P("dp", "mp"),
            P("mp", "dp"),
            P(None, "dp", "mp"),
            P(None, "mp", "dp"),
            P("dp", "mp"),
            P("mp", "dp"),
            P(),
            P(),
            P(),
            P(),
        ),
        check_vma=False,
    )
```

```python
from functools import partial
import math

import jax
import jax.numpy as jnp
from jax import lax
from jax.experimental import pallas as pl
from jax.experimental.pallas import tpu as pltpu
from jax.sharding import PartitionSpec as P

HD = 64
GROUPS = 32
FREQ = 8
TIME = 64
TSTEPS = 1000
STEP = 5


NORM_EPS = 1e-05
MOMENT_DECAY = 0.5
LEARN_RATE = 0.5
WEIGHT_DECAY = 0.01
ADAM_EPS = 1e-06
MASK_VALUE = -1e30
HIGHEST_PRECISION = lax.Precision.HIGHEST


def layer_norm(value_tensor, gain_row, shift_row):
    centre = value_tensor - jnp.mean(value_tensor, axis=-1, keepdims=True)
    spread = jnp.mean(centre * centre, axis=-1, keepdims=True)
    return centre * lax.rsqrt(spread + NORM_EPS) * gain_row + shift_row


def group_norm(value_tensor, gain_row, shift_row, group_width):
    seqs_here, length, channels = value_tensor.shape
    grouped = value_tensor.reshape(seqs_here, length, channels // group_width, group_width)
    centre = grouped - jnp.mean(grouped, axis=(1, 3), keepdims=True)
    spread = jnp.mean(centre * centre, axis=(1, 3), keepdims=True)
    normed = (centre * lax.rsqrt(spread + NORM_EPS)).reshape(seqs_here, length, channels)
    return normed * gain_row + shift_row


def norm_silu(value_tensor, gain_row, shift_row, group_width):
    return jax.nn.silu(group_norm(value_tensor, gain_row, shift_row, group_width))


def time_embedding(timesteps, features):
    half_width = features // 2
    freq_rates = jnp.exp(
        -math.log(10000.0) * jnp.arange(half_width, dtype=jnp.float32) / half_width
    )
    angles = timesteps.astype(jnp.float32)[:, None] * freq_rates[None, :]
    return jnp.concatenate([jnp.sin(angles), jnp.cos(angles)], axis=1)


def flatten_rows(value_tensor):
    return value_tensor.reshape(-1, value_tensor.shape[-1])


def project(values_low, weight_matrix):
    summed = jnp.dot(flatten_rows(values_low), weight_matrix, preferred_element_type=jnp.float32)
    return summed.reshape(values_low.shape[0], values_low.shape[1], weight_matrix.shape[1])


def back_project(grad_low, weight_matrix):
    summed = jnp.einsum(
        "ne,ce->nc", flatten_rows(grad_low), weight_matrix, preferred_element_type=jnp.float32
    )
    return summed.reshape(grad_low.shape[0], grad_low.shape[1], weight_matrix.shape[0])


def weight_grad(left_low, right_low):
    return jnp.einsum(
        "nc,ne->ce",
        flatten_rows(left_low),
        flatten_rows(right_low),
        preferred_element_type=jnp.float32,
    )


def padded_grid(grid_rows):
    seqs_here = grid_rows.shape[0]
    return jnp.pad(grid_rows.reshape(seqs_here, FREQ, TIME, -1), ((0, 0), (1, 1), (1, 1), (0, 0)))


def grid_window(padded, tap_index):
    row_off = tap_index // 3
    col_off = tap_index % 3
    return padded[:, row_off : row_off + FREQ, col_off : col_off + TIME, :].reshape(
        -1, padded.shape[3]
    )


def conv_grid(grid_rows, tap_weights, backward):
    seqs_here = grid_rows.shape[0]
    padded = padded_grid(grid_rows)
    out_width = tap_weights.shape[1] if backward else tap_weights.shape[2]
    summed = jnp.zeros((seqs_here * FREQ * TIME, out_width), jnp.float32)
    for tap_index in range(9):
        window = grid_window(padded, tap_index)
        if backward:
            summed = summed + jnp.einsum(
                "nc,dc->nd", window, tap_weights[8 - tap_index], preferred_element_type=jnp.float32
            )
        else:
            summed = summed + jnp.dot(
                window, tap_weights[tap_index], preferred_element_type=jnp.float32
            )
    return summed.reshape(seqs_here, FREQ * TIME, out_width)


def conv_weight_grad(grid_low, grad_low):
    padded = padded_grid(grid_low)
    grad_flat = flatten_rows(grad_low)
    tap_grads = []
    for tap_index in range(9):
        window = grid_window(padded, tap_index)
        tap_grads.append(
            jnp.einsum("nc,ne->ce", window, grad_flat, preferred_element_type=jnp.float32)
        )
    return jnp.stack(tap_grads)


def split_heads(rows_low):
    return rows_low.reshape(rows_low.shape[0], rows_low.shape[1], rows_low.shape[2] // HD, HD)


def head_scores(queries, key_rows, allowed, score_scale):
    scores = (
        jnp.einsum(
            "sqhd,skhd->shqk",
            split_heads(queries),
            split_heads(key_rows),
            preferred_element_type=jnp.float32,
        )
        * score_scale
    )
    if allowed is not None:
        scores = jnp.where(allowed[:, None], scores, MASK_VALUE)
    return scores


def attend(queries, key_rows, value_rows, allowed, score_scale):
    scores = head_scores(queries, key_rows, allowed, score_scale)
    highest = jnp.max(scores, axis=-1, keepdims=True)
    raised = jnp.exp(scores - highest)
    totals = jnp.sum(raised, axis=-1, keepdims=True)
    soft_low = (raised / totals).astype(jnp.bfloat16)
    mixed_rows = jnp.einsum(
        "shqk,skhd->sqhd", soft_low, split_heads(value_rows), preferred_element_type=jnp.float32
    )
    return (mixed_rows.reshape(queries.shape), highest + jnp.log(totals))


def attend_back(queries, key_rows, value_rows, allowed, score_scale, log_total, grad_mixed):
    scores = head_scores(queries, key_rows, allowed, score_scale)
    soft = jnp.exp(scores - log_total)
    grad_heads = split_heads(grad_mixed)
    grad_soft = jnp.einsum(
        "sqhd,skhd->shqk", grad_heads, split_heads(value_rows), preferred_element_type=jnp.float32
    )
    grad_values = jnp.einsum(
        "shqk,sqhd->skhd", soft.astype(jnp.bfloat16), grad_heads, preferred_element_type=jnp.float32
    )
    row_dot = jnp.sum(soft * grad_soft, axis=-1, keepdims=True)
    grad_scores = (soft * (grad_soft - row_dot)).astype(jnp.bfloat16)
    grad_queries = (
        jnp.einsum(
            "shqk,skhd->sqhd",
            grad_scores,
            split_heads(key_rows),
            preferred_element_type=jnp.float32,
        )
        * score_scale
    )
    grad_keys = (
        jnp.einsum(
            "shqk,sqhd->skhd", grad_scores, split_heads(queries), preferred_element_type=jnp.float32
        )
        * score_scale
    )
    return (
        grad_queries.reshape(queries.shape).astype(jnp.bfloat16),
        grad_keys.reshape(key_rows.shape).astype(jnp.bfloat16),
        grad_values.reshape(value_rows.shape).astype(jnp.bfloat16),
    )


def tensor_parallel_sum(term_rows):
    return lax.psum(term_rows, "mp")


def matrix_squares(first_stack, second_stack, up_rows, down_rows):
    return jnp.concatenate(
        [
            jnp.sum(first_stack * first_stack, axis=(1, 2)),
            jnp.sum(second_stack * second_stack, axis=(1, 2)),
            jnp.sum(up_rows * up_rows)[None],
            jnp.sum(down_rows * down_rows)[None],
        ]
    )


def adam_update(master, grad_rows, first_moment, second_moment, decay_rate):
    first_new = MOMENT_DECAY * first_moment + (1.0 - MOMENT_DECAY) * grad_rows
    second_new = MOMENT_DECAY * second_moment + (1.0 - MOMENT_DECAY) * grad_rows * grad_rows
    correct = 1.0 - MOMENT_DECAY**STEP
    update = first_new / correct / (jnp.sqrt(second_new / correct) + ADAM_EPS) + decay_rate * master
    return (first_new, second_new, update)


def generic_device(
    tokens,
    noise_field,
    codec_tokens,
    timesteps,
    segments,
    cotangent,
    w_in,
    w_back,
    w_up,
    w_down,
    m_in,
    m_back,
    m_up,
    m_down,
    v_in,
    v_back,
    v_up,
    v_down,
    norm_params,
    norm_m,
    norm_v,
):
    seqs_here, length = segments.shape
    features = tokens.shape[1]
    chans_here = w_in.shape[2]
    group_width = features // GROUPS
    score_scale = HD ** (-0.5)
    channel_start = lax.axis_index("mp") * chans_here
    lead_device = (lax.axis_index("mp") == 0).astype(jnp.float32)
    weight_sq = matrix_squares(w_in, w_back, w_up, w_down)
    full_in, full_back, complete_up_weight, full_down = (
        lax.all_gather(w_in.astype(jnp.bfloat16), "dp", axis=1, tiled=True),
        lax.all_gather(w_back.astype(jnp.bfloat16), "dp", axis=2, tiled=True),
        lax.all_gather(w_up.astype(jnp.bfloat16), "dp", axis=0, tiled=True),
        lax.all_gather(w_down.astype(jnp.bfloat16), "dp", axis=1, tiled=True),
    )
    resid_in = tokens.astype(jnp.float32).reshape(seqs_here, length, features)
    allowed = segments[:, :, None] == segments[:, None, :]
    normed_one_low = layer_norm(resid_in, norm_params[0], norm_params[1]).astype(jnp.bfloat16)
    queries = project(normed_one_low, full_in[0]).astype(jnp.bfloat16)
    key_rows = project(normed_one_low, full_in[1]).astype(jnp.bfloat16)
    value_rows = project(normed_one_low, full_in[2]).astype(jnp.bfloat16)
    mixed_rows, log_self = attend(queries, key_rows, value_rows, allowed, score_scale)
    mixed_low = mixed_rows.astype(jnp.bfloat16)
    resid_one = resid_in + tensor_parallel_sum(project(mixed_low, full_back[0]))
    normed_two_low = layer_norm(resid_one, norm_params[2], norm_params[3]).astype(jnp.bfloat16)
    hidden_pre = project(normed_two_low, complete_up_weight)
    hidden_low = jax.nn.gelu(hidden_pre).astype(jnp.bfloat16)
    resid_two = resid_one + tensor_parallel_sum(project(hidden_low, full_down))
    noise_level = jnp.sqrt((timesteps.astype(jnp.float32) + 1.0) / TSTEPS)
    noisy = resid_two + noise_level[:, None, None] * noise_field.astype(jnp.float32).reshape(
        seqs_here, length, features
    )
    first_low = norm_silu(noisy, norm_params[4], norm_params[5], group_width).astype(jnp.bfloat16)
    embed_low = jax.nn.silu(time_embedding(timesteps, features)).astype(jnp.bfloat16)
    time_shift = jnp.dot(embed_low, full_in[3], preferred_element_type=jnp.float32)
    conv_one = conv_grid(first_low, full_in[7:16], False) + time_shift[:, None, :]
    gain_six = lax.dynamic_slice_in_dim(norm_params[6], channel_start, chans_here)
    shift_six = lax.dynamic_slice_in_dim(norm_params[7], channel_start, chans_here)
    second_low = norm_silu(conv_one, gain_six, shift_six, group_width).astype(jnp.bfloat16)
    resid_three = noisy + tensor_parallel_sum(conv_grid(second_low, full_back[2:11], False))
    normed_three_low = layer_norm(resid_three, norm_params[8], norm_params[9]).astype(jnp.bfloat16)
    cross_queries = project(normed_three_low, full_in[4]).astype(jnp.bfloat16)
    cross_keys = project(codec_tokens, full_in[5]).astype(jnp.bfloat16)
    cross_values = project(codec_tokens, full_in[6]).astype(jnp.bfloat16)
    cross_mixed, log_cross = attend(cross_queries, cross_keys, cross_values, None, score_scale)
    cross_low = cross_mixed.astype(jnp.bfloat16)
    result = resid_three + tensor_parallel_sum(project(cross_low, full_back[1]))
    out_low = result.astype(jnp.bfloat16)
    grad_out = cotangent.astype(jnp.float32).reshape(seqs_here, length, features)
    grad_cross_low = grad_out.astype(jnp.bfloat16)
    grad_w_co = weight_grad(cross_low, grad_cross_low)
    grad_cross_mixed = back_project(grad_cross_low, full_back[1]).astype(jnp.bfloat16)
    grad_cq, grad_ck, grad_cv = attend_back(
        cross_queries, cross_keys, cross_values, None, score_scale, log_cross, grad_cross_mixed
    )
    grad_w_cq = weight_grad(normed_three_low, grad_cq)
    grad_w_ck = weight_grad(codec_tokens, grad_ck)
    grad_w_cv = weight_grad(codec_tokens, grad_cv)
    grad_normed_three = tensor_parallel_sum(back_project(grad_cq, full_in[4]))
    pull_three = jax.vjp(layer_norm, resid_three, norm_params[8], norm_params[9])[1]
    grad_part, grad_gain_eight, grad_shift_eight = pull_three(grad_normed_three)
    grad_three = grad_out + grad_part
    grad_conv_low = grad_three.astype(jnp.bfloat16)
    grad_w_conv_two = conv_weight_grad(second_low, grad_conv_low)
    grad_second = conv_grid(grad_conv_low, full_back[2:11], True)
    gather_second_moment = jax.vjp(
        partial(norm_silu, group_width=group_width), conv_one, gain_six, shift_six
    )[1]
    grad_conv_one, grad_gain_six, grad_shift_six = gather_second_moment(grad_second)
    grad_conv_one_low = grad_conv_one.astype(jnp.bfloat16)
    grad_w_time = jnp.einsum(
        "sd,sc->dc",
        embed_low.astype(jnp.float32),
        jnp.sum(grad_conv_one_low.astype(jnp.float32), axis=1),
        precision=HIGHEST_PRECISION,
    )
    grad_w_conv_one = conv_weight_grad(first_low, grad_conv_one_low)
    grad_first = tensor_parallel_sum(conv_grid(grad_conv_one_low, full_in[7:16], True))
    gather_first_moment = jax.vjp(
        partial(norm_silu, group_width=group_width), noisy, norm_params[4], norm_params[5]
    )[1]
    grad_part, grad_gain_four, grad_shift_four = gather_first_moment(grad_first)
    grad_two = grad_three + grad_part
    grad_mlp_low = grad_two.astype(jnp.bfloat16)
    grad_w_down = weight_grad(hidden_low, grad_mlp_low)
    grad_hidden = back_project(grad_mlp_low, full_down)
    grad_pre_low = jax.vjp(jax.nn.gelu, hidden_pre)[1](grad_hidden)[0].astype(jnp.bfloat16)
    up_weight_gradient = weight_grad(normed_two_low, grad_pre_low)
    grad_normed_two = tensor_parallel_sum(back_project(grad_pre_low, complete_up_weight))
    pull_two = jax.vjp(layer_norm, resid_one, norm_params[2], norm_params[3])[1]
    grad_part, grad_gain_two, grad_shift_two = pull_two(grad_normed_two)
    grad_one = grad_two + grad_part
    grad_attn_low = grad_one.astype(jnp.bfloat16)
    grad_w_out = weight_grad(mixed_low, grad_attn_low)
    grad_mixed = back_project(grad_attn_low, full_back[0]).astype(jnp.bfloat16)
    grad_q, grad_k, grad_v = attend_back(
        queries, key_rows, value_rows, allowed, score_scale, log_self, grad_mixed
    )
    grad_w_q = weight_grad(normed_one_low, grad_q)
    grad_w_k = weight_grad(normed_one_low, grad_k)
    grad_w_v = weight_grad(normed_one_low, grad_v)
    grad_normed_one = tensor_parallel_sum(
        back_project(grad_q, full_in[0])
        + back_project(grad_k, full_in[1])
        + back_project(grad_v, full_in[2])
    )
    pull_one = jax.vjp(layer_norm, resid_in, norm_params[0], norm_params[1])[1]
    grad_part, grad_gain_zero, grad_shift_zero = pull_one(grad_normed_one)
    grad_input = grad_one + grad_part
    grad_in_stack = jnp.concatenate(
        [
            jnp.stack([grad_w_q, grad_w_k, grad_w_v, grad_w_time, grad_w_cq, grad_w_ck, grad_w_cv]),
            grad_w_conv_one,
        ]
    )
    grad_back_stack = jnp.concatenate([jnp.stack([grad_w_out, grad_w_co]), grad_w_conv_two])
    summed_in, summed_back, summed_up, summed_down = (
        lax.psum_scatter(grad_in_stack, "dp", scatter_dimension=1, tiled=True),
        lax.psum_scatter(grad_back_stack, "dp", scatter_dimension=2, tiled=True),
        lax.psum_scatter(up_weight_gradient, "dp", scatter_dimension=0, tiled=True),
        lax.psum_scatter(grad_w_down, "dp", scatter_dimension=1, tiled=True),
    )
    shared_rows = (
        jnp.stack(
            [
                grad_gain_zero,
                grad_shift_zero,
                grad_gain_two,
                grad_shift_two,
                grad_gain_four,
                grad_shift_four,
            ]
        )
        * lead_device
    )
    group_rows = lax.dynamic_update_slice(
        jnp.zeros((2, features), jnp.float32),
        jnp.stack([grad_gain_six, grad_shift_six]),
        (0, channel_start),
    )
    last_rows = jnp.stack([grad_gain_eight, grad_shift_eight]) * lead_device
    norm_grad = lax.psum(jnp.concatenate([shared_rows, group_rows, last_rows]), ("dp", "mp"))
    m_in_new, v_in_new, upd_in = adam_update(w_in, summed_in, m_in, v_in, WEIGHT_DECAY)
    m_back_new, v_back_new, upd_back = adam_update(
        w_back, summed_back, m_back, v_back, WEIGHT_DECAY
    )
    m_up_new, v_up_new, upd_up = adam_update(w_up, summed_up, m_up, v_up, WEIGHT_DECAY)
    m_down_new, v_down_new, upd_down = adam_update(
        w_down, summed_down, m_down, v_down, WEIGHT_DECAY
    )
    update_sq = matrix_squares(upd_in, upd_back, upd_up, upd_down)
    weight_total, update_total = lax.psum((weight_sq, update_sq), ("dp", "mp"))
    weight_len = jnp.sqrt(weight_total)
    update_len = jnp.sqrt(update_total)
    trust = weight_len / update_len
    new_in = w_in - LEARN_RATE * trust[0:16, None, None] * upd_in
    new_back = w_back - LEARN_RATE * trust[16:27, None, None] * upd_back
    new_up = w_up - LEARN_RATE * trust[27] * upd_up
    new_down = w_down - LEARN_RATE * trust[28] * upd_down
    norm_m_new, norm_v_new, upd_norm = adam_update(norm_params, norm_grad, norm_m, norm_v, 0.0)
    row_trust = jnp.sqrt(jnp.sum(norm_params * norm_params, axis=1)) / jnp.sqrt(
        jnp.sum(upd_norm * upd_norm, axis=1)
    )
    new_norm = norm_params - LEARN_RATE * row_trust[:, None] * upd_norm
    matrix_norms = jnp.stack([weight_len, update_len])
    out_rows = out_low.reshape(seqs_here * length, features)
    grad_rows = grad_input.reshape(seqs_here * length, features)
    return (
        out_rows,
        grad_rows,
        new_in,
        new_back,
        new_up,
        new_down,
        m_in_new,
        m_back_new,
        m_up_new,
        m_down_new,
        v_in_new,
        v_back_new,
        v_up_new,
        v_down_new,
        new_norm,
        norm_m_new,
        norm_v_new,
        matrix_norms,
    )


CORE_SWAP = [(i, i ^ 1) for i in range(4)]
X_SWAP = [(i, i ^ 2) for i in range(4)]
LOW = jnp.bfloat16
F32 = jnp.float32


def swap_core(v):
    return lax.ppermute(v, "mp", CORE_SWAP)


def swap_x(v):
    return lax.ppermute(v, "mp", X_SWAP)


def by_parity(flag, own, other, axis):
    first = jnp.where(flag == 0, own, other)
    second = jnp.where(flag == 0, other, own)
    return jnp.stack([first, second], axis=axis)


def pick(v, index, axis):
    return lax.dynamic_index_in_dim(v, index, axis, keepdims=False)


def ln_stats(v):
    centre = v - jnp.mean(v, axis=-1, keepdims=True)
    scale = lax.rsqrt(jnp.mean(centre * centre, axis=-1, keepdims=True) + NORM_EPS)
    return centre * scale, scale


def ln_back(v, gain, grad):
    hat, scale = ln_stats(v)
    pulled = grad * gain
    back = scale * (
        pulled
        - jnp.mean(pulled, axis=-1, keepdims=True)
        - hat * jnp.mean(pulled * hat, axis=-1, keepdims=True)
    )
    return back, jnp.sum(grad * hat, axis=0, keepdims=True), jnp.sum(grad, axis=0, keepdims=True)


def mm(a, b):
    return lax.dot_general(a, b, (((1,), (0,)), ((), ())), preferred_element_type=F32)


def mm_nt(a, b):
    return lax.dot_general(a, b, (((1,), (1,)), ((), ())), preferred_element_type=F32)


def mm_tn(a, b):
    return lax.dot_general(a, b, (((0,), (0,)), ((), ())), preferred_element_type=F32)


ANY = pl.ANY
VM = pltpu.VMEM
ROWS = 512
STEP_ROWS = 128


def spec_any():
    return pl.BlockSpec(memory_space=pl.ANY)


def spec_vm():
    return pl.BlockSpec(memory_space=pltpu.VMEM)


def run_kernel(body, name, ins, outs, scratch, hbm=(), flops=0):
    in_specs = [spec_any() if k in hbm else spec_vm() for k in range(len(ins))]
    moved = sum(v.size * v.dtype.itemsize for v in ins) + sum(
        math.prod(s) * jnp.dtype(t).itemsize for s, t in outs
    )
    return pl.pallas_call(
        body,
        name=name,
        in_specs=in_specs,
        out_specs=[spec_vm() for _ in outs],
        out_shape=[jax.ShapeDtypeStruct(s, t) for s, t in outs],
        scratch_shapes=scratch,
        compiler_params=pltpu.CompilerParams(vmem_limit_bytes=56 << 20),
        cost_estimate=pl.CostEstimate(flops=flops, bytes_accessed=moved, transcendentals=0),
    )(*ins)


def each_rows(fn, total=ROWS, step=STEP_ROWS):
    def body(k, carry):
        fn(pl.ds(pl.multiple_of(k * step, step), step))
        return carry

    lax.fori_loop(0, total // step, body, 0)


def start_copies(pairs, sems):
    copies = [pltpu.make_async_copy(a, b, sems.at[k]) for k, (a, b) in enumerate(pairs)]
    for c in copies:
        c.start()
    return copies


def group_mats(channels, width):
    count = channels // width
    r = lax.broadcasted_iota(jnp.int32, (channels, count), 0)
    c = lax.broadcasted_iota(jnp.int32, (channels, count), 1) * width
    down = ((r >= c) & (r < c + width)).astype(F32)
    r = lax.broadcasted_iota(jnp.int32, (count, channels), 1)
    c = lax.broadcasted_iota(jnp.int32, (count, channels), 0) * width
    up = ((r >= c) & (r < c + width)).astype(F32)
    return down, up


def exact_dot(a, b):
    return jnp.dot(a, b, precision=HIGHEST_PRECISION, preferred_element_type=F32)


def group_average(row, mats, width):
    wide = jnp.broadcast_to(row, (8, row.shape[1]))
    return exact_dot(exact_dot(wide, mats[0]) * (1.0 / (width * ROWS)), mats[1])[0:1]


def gelu_parts(v):
    k = math.sqrt(2.0 / math.pi)
    t = jnp.tanh(k * (v + 0.044715 * (v * v * v)))
    return t, 0.5 * v * (1.0 + t)


def gelu_slope(v, t):
    k = math.sqrt(2.0 / math.pi)
    return 0.5 * (1.0 + t) + 0.5 * v * (1.0 - t * t) * (k * (1.0 + 3 * 0.044715 * (v * v)))


def column_of(shape):
    return lax.broadcasted_iota(jnp.int32, shape, 0) % TIME


def from_left(v):
    return jnp.where(column_of(v.shape) == 0, 0.0, pltpu.roll(v, 1, 0))


def from_right(v):
    return jnp.where(column_of(v.shape) == TIME - 1, 0.0, pltpu.roll(v, v.shape[0] - 1, 0))


def softmax_heads(q, k, v, heads, score_scale, mask):
    mixed, logs = [], []
    for h in range(heads):
        s = mm_nt(q[:, HD * h : HD * (h + 1)], k[:, HD * h : HD * (h + 1)]) * score_scale
        if mask is not None:
            s = jnp.where(mask, s, MASK_VALUE)
        top = jnp.max(s, axis=1, keepdims=True)
        e = jnp.exp(s - top)
        total = jnp.sum(e, axis=1, keepdims=True)
        soft = (e * (1.0 / total)).astype(LOW)
        mixed.append(mm(soft, v[:, HD * h : HD * (h + 1)]))
        logs.append(top + jnp.log(total))
    return jnp.concatenate(mixed, axis=1).astype(LOW), logs


def softmax_heads_back(q, k, v, g, logs, heads, score_scale, mask):
    dq, dk, dv = [], [], []
    for h in range(heads):
        cols = slice(HD * h, HD * (h + 1))
        s = mm_nt(q[:, cols], k[:, cols]) * score_scale
        if mask is not None:
            s = jnp.where(mask, s, MASK_VALUE)
        soft = jnp.exp(s - logs[h])
        gs = mm_nt(g[:, cols], v[:, cols])
        dv.append(mm_tn(soft.astype(LOW), g[:, cols]))
        dot = jnp.sum(soft * gs, axis=1, keepdims=True)
        ds = (soft * (gs - dot)).astype(LOW)
        dq.append(mm(ds, k[:, cols]) * score_scale)
        dk.append(mm_tn(ds, q[:, cols]))
    return [jnp.concatenate(d, axis=1) for d in (dq, dk, dv)]


def attn_forward(seg_col, seg_row, tok, norms, w, n1, qkv, mixed, logs, part, wv, sems):
    n = mixed.shape[2]
    copies = start_copies([(w.at[0], wv.at[0]), (w.at[1], wv.at[1])], sems)

    def norm(r):
        hat, _ = ln_stats(tok[r, :].astype(F32))
        n1[r, :] = (hat * norms[0:1, :] + norms[1:2, :]).astype(LOW)

    each_rows(norm)
    for i in range(2):
        copies[i].wait()
        qkv[i] = mm(n1[...], wv[i, :, : 3 * n]).astype(LOW)

    def heads(r):
        mask = seg_col[r, :] == seg_row[...]
        found = []
        for i in range(2):
            got, logs_i = softmax_heads(
                qkv[i, r, 0:n], qkv[i, :, n : 2 * n], qkv[i, :, 2 * n : 3 * n],
                n // HD, HD ** (-0.5), mask,
            )
            mixed[i, r, :] = got
            found += logs_i
        logs[r, :] = jnp.concatenate(found, axis=1)

    each_rows(heads)
    total = mm_nt(mixed[0], wv[0, :, 3 * n :]) + mm_nt(mixed[1], wv[1, :, 3 * n :])
    part[...] = total.astype(LOW)


def mlp_forward(tok, own, other, norms, w, resid, n2, part, wv, acc, sems):
    hid = wv.shape[2] // 2
    copies = start_copies([(w.at[0], wv.at[0]), (w.at[1], wv.at[1])], sems)

    def norm(r):
        v = tok[r, :].astype(F32) + (own[r, :].astype(F32) + other[r, :].astype(F32))
        resid[r, :] = v
        hat, _ = ln_stats(v)
        n2[r, :] = (hat * norms[2:3, :] + norms[3:4, :]).astype(LOW)

    each_rows(norm)
    block = 256
    for i in range(2):
        copies[i].wait()
        for b in range(hid // block):
            pre = mm(n2[...], wv[i, :, block * b : block * (b + 1)])
            hidden = gelu_parts(pre)[1].astype(LOW)
            term = mm_nt(hidden, wv[i, :, hid + block * b : hid + block * (b + 1)])
            if i == 0 and b == 0:
                acc[...] = term
            else:
                acc[...] += term
    part[...] = acc[...].astype(LOW)


def conv_forward(
    level, resid, own, other, noise, norms, side, embed, w, u,
    noisy, first, conv, taps, part, pad, wv, uv, sems,
):
    n = conv.shape[2]
    width = noisy.shape[1] // GROUPS
    copies = start_copies(
        [(w.at[0], wv.at[0]), (w.at[1], wv.at[1]), (u.at[0], uv.at[0]), (u.at[1], uv.at[1])], sems
    )
    mats = group_mats(noisy.shape[1], width)
    mats_n = group_mats(n, width)
    pad[0:TIME, :] = jnp.zeros((TIME, pad.shape[1]), LOW)
    pad[TIME + ROWS :, :] = jnp.zeros((TIME, pad.shape[1]), LOW)

    def join(r):
        v = resid[r, :] + (own[r, :].astype(F32) + other[r, :].astype(F32))
        noisy[r, :] = v + level[...] * noise[r, :].astype(F32)

    each_rows(join)
    mean = group_average(jnp.sum(noisy[...], axis=0, keepdims=True), mats, width)
    centre = noisy[...] - mean
    var = group_average(jnp.sum(centre * centre, axis=0, keepdims=True), mats, width)
    scale = lax.rsqrt(var + NORM_EPS) * norms[4:5, :]

    def act(r):
        v = (noisy[r, :] - mean) * scale + norms[5:6, :]
        low = (v * jax.nn.sigmoid(v)).astype(LOW)
        first[r, :] = low

    each_rows(act)
    pad[TIME : TIME + ROWS, :] = first[...]
    for i in range(2):
        copies[i].wait()
        q = None
        for a in range(3):
            term = mm(pad[TIME * a : TIME * a + ROWS, :], wv[i, :, 3 * n * a : 3 * n * (a + 1)])
            q = term if q is None else q + term
        shift = mm(embed[...], wv[i, :, 9 * n : 10 * n])[0:1]
        c1 = from_left(q[:, :n]) + q[:, n : 2 * n] + from_right(q[:, 2 * n :]) + shift
        conv[i] = c1
        mean_n = group_average(jnp.sum(c1, axis=0, keepdims=True), mats_n, width)
        c1 = c1 - mean_n
        var_n = group_average(jnp.sum(c1 * c1, axis=0, keepdims=True), mats_n, width)
        v = c1 * lax.rsqrt(var_n + NORM_EPS) * side[i, 0:1, :] + side[i, 1:2, :]
        v = v * jax.nn.sigmoid(v)
        taps[i, 0:TIME, :] = jnp.zeros((TIME, 3 * n), LOW)
        taps[i, TIME + ROWS :, :] = jnp.zeros((TIME, 3 * n), LOW)
        taps[i, TIME : TIME + ROWS, :] = jnp.concatenate(
            [from_left(v), v, from_right(v)], axis=1
        ).astype(LOW)
    total = None
    for i in range(2):
        copies[2 + i].wait()
        for a in range(3):
            term = mm_nt(
                taps[i, TIME * a : TIME * a + ROWS, :], uv[i, :, 3 * n * a : 3 * n * (a + 1)]
            )
            total = term if total is None else total + term
    part[...] = total.astype(LOW)


def cross_forward(
    noisy, own, other, codec, norms, w, resid, n3, cq, ckv, mixed, logs, part, wv, sems
):
    n = mixed.shape[2]
    copies = start_copies([(w.at[0], wv.at[0]), (w.at[1], wv.at[1])], sems)

    def norm(r):
        v = noisy[r, :] + (own[r, :].astype(F32) + other[r, :].astype(F32))
        resid[r, :] = v
        hat, _ = ln_stats(v)
        n3[r, :] = (hat * norms[8:9, :] + norms[9:10, :]).astype(LOW)

    each_rows(norm)
    for i in range(2):
        copies[i].wait()
        cq[i] = mm(n3[...], wv[i, :, :n]).astype(LOW)
        ckv[i] = mm(codec[...], wv[i, :, n : 3 * n]).astype(LOW)

    def heads(r):
        found = []
        for i in range(2):
            got, logs_i = softmax_heads(
                cq[i, r, :], ckv[i, :, :n], ckv[i, :, n:], n // HD, HD ** (-0.5), None
            )
            mixed[i, r, :] = got
            found += logs_i
        logs[r, :] = jnp.concatenate(found, axis=1)

    each_rows(heads)
    total = mm_nt(mixed[0], wv[0, :, 3 * n :]) + mm_nt(mixed[1], wv[1, :, 3 * n :])
    part[...] = total.astype(LOW)


def cross_backward(
    cot, n3, codec, cq, ckv, mixed, logs, w, d, part, wv, gm, dq, dkv, sems
):
    n = mixed.shape[2]
    copies = start_copies([(w.at[0], wv.at[0]), (w.at[1], wv.at[1])], sems)
    for i in (1, 0):
        d[i, :, 3 * n :] = mm_tn(cot[...], mixed[i]).astype(LOW)
    for i in range(2):
        copies[i].wait()
        gm[i] = mm(cot[...], wv[i, :, 3 * n :]).astype(LOW)
    dkv[...] = jnp.zeros(dkv.shape, F32)

    def heads(r):
        for i in range(2):
            per = n // HD
            rows_logs = [logs[r, per * i + h : per * i + h + 1] for h in range(per)]
            gq, gk, gv = softmax_heads_back(
                cq[i, r, :], ckv[i, :, :n], ckv[i, :, n:], gm[i, r, :], rows_logs,
                per, HD ** (-0.5), None,
            )
            dq[i, r, :] = gq.astype(LOW)
            dkv[i] += jnp.concatenate([gk, gv], axis=1)

    each_rows(heads)
    total = None
    for i in (1, 0):
        low_kv = jnp.concatenate(
            [dkv[i, :, :n] * (HD ** (-0.5)), dkv[i, :, n:]], axis=1
        ).astype(LOW)
        d[i, :, :n] = mm_tn(n3[...], dq[i]).astype(LOW)
        d[i, :, n : 3 * n] = mm_tn(codec[...], low_kv).astype(LOW)
        term = mm_nt(dq[i], wv[i, :, :n])
        total = term if total is None else total + term
    part[...] = total.astype(LOW)


def conv_two_backward(
    resid, own, other, cot, norms, side, conv, taps, u,
    grad3, d, tapsg, ln_rows, gn_rows, gsum, pad, gl, uv, sems,
):
    n = conv.shape[2]
    width = resid.shape[1] // GROUPS
    mats_n = group_mats(n, width)
    copies = start_copies([(u.at[0], uv.at[0]), (u.at[1], uv.at[1])], sems)
    pad[0:TIME, :] = jnp.zeros((TIME, pad.shape[1]), LOW)
    pad[TIME + ROWS :, :] = jnp.zeros((TIME, pad.shape[1]), LOW)
    ln_rows[...] = jnp.zeros(ln_rows.shape, F32)

    def pull(r):
        g = own[r, :].astype(F32) + other[r, :].astype(F32)
        back, gain, shift = ln_back(resid[r, :], norms[8:9, :], g)
        v = cot[r, :].astype(F32) + back
        grad3[r, :] = v
        gl[r, :] = v.astype(LOW)
        ln_rows[0:1, :] += gain
        ln_rows[1:2, :] += shift

    each_rows(pull)
    pad[TIME : TIME + ROWS, :] = gl[...]
    for i in (1, 0):
        for a in range(3):
            d[i, :, 3 * n * a : 3 * n * (a + 1)] = mm_tn(
                gl[...], taps[i, TIME * a : TIME * a + ROWS, :]
            ).astype(LOW)
    for i in range(2):
        copies[i].wait()
        q = None
        for a in range(3):
            term = mm(
                pad[TIME * (2 - a) : TIME * (2 - a) + ROWS, :],
                uv[i, :, 3 * n * a : 3 * n * (a + 1)],
            )
            q = term if q is None else q + term
        grad = from_right(q[:, :n]) + q[:, n : 2 * n] + from_left(q[:, 2 * n :])
        c1 = conv[i]
        c1 = c1 - group_average(jnp.sum(c1, axis=0, keepdims=True), mats_n, width)
        var_n = group_average(jnp.sum(c1 * c1, axis=0, keepdims=True), mats_n, width)
        scale = lax.rsqrt(var_n + NORM_EPS)
        hat = c1 * scale
        gain = side[i, 0:1, :]
        pre = hat * gain + side[i, 1:2, :]
        gate = jax.nn.sigmoid(pre)
        grad = grad * gate * (1.0 + pre * (1.0 - gate))
        d_gain = jnp.sum(grad * hat, axis=0, keepdims=True)
        d_shift = jnp.sum(grad, axis=0, keepdims=True)
        gn_rows[i] = jnp.concatenate([d_gain, d_shift], axis=0)
        back = scale * (
            grad * gain
            - group_average(d_shift * gain, mats_n, width)
            - hat * group_average(d_gain * gain, mats_n, width)
        )
        back = back.astype(LOW).astype(F32)
        gsum[i : i + 1, :] = jnp.sum(back, axis=0, keepdims=True)
        tapsg[i, 0:TIME, :] = jnp.zeros((TIME, 3 * n), LOW)
        tapsg[i, TIME + ROWS :, :] = jnp.zeros((TIME, 3 * n), LOW)
        tapsg[i, TIME : TIME + ROWS, :] = jnp.concatenate(
            [from_right(back), back, from_left(back)], axis=1
        ).astype(LOW)


def conv_one_backward(first, tapsg, gsum, embed_col, w, d, part, wv, sems):
    n = gsum.shape[1]
    copies = start_copies([(w.at[0], wv.at[0]), (w.at[1], wv.at[1])], sems)
    for i in (1, 0):
        for a in range(3):
            d[i, :, 3 * n * a : 3 * n * (a + 1)] = mm_tn(
                first[...], tapsg[i, TIME * (2 - a) : TIME * (2 - a) + ROWS, :]
            ).astype(LOW)
        d[i, :, 9 * n :] = (embed_col[...] * gsum[i : i + 1, :]).astype(LOW)
    total = None
    for i in range(2):
        copies[i].wait()
        for a in range(3):
            term = mm_nt(
                tapsg[i, TIME * (2 - a) : TIME * (2 - a) + ROWS, :],
                wv[i, :, 3 * n * a : 3 * n * (a + 1)],
            )
            total = term if total is None else total + term
    part[...] = total.astype(LOW)


def mlp_backward(
    noisy, own, other, grad3, norms, n2, w, grad2, d, part, gn_rows, wv, gl, hb, acc, sems
):
    hid = wv.shape[2] // 2
    width = noisy.shape[1] // GROUPS
    mats = group_mats(noisy.shape[1], width)
    copies = start_copies([(w.at[0], wv.at[0]), (w.at[1], wv.at[1])], sems)
    mean = group_average(jnp.sum(noisy[...], axis=0, keepdims=True), mats, width)
    centre = noisy[...] - mean
    var = group_average(jnp.sum(centre * centre, axis=0, keepdims=True), mats, width)
    scale = lax.rsqrt(var + NORM_EPS)
    gain, shift = norms[4:5, :], norms[5:6, :]
    gn_rows[...] = jnp.zeros(gn_rows.shape, F32)

    def through_silu(r):
        hat = (noisy[r, :] - mean) * scale
        pre = hat * gain + shift
        gate = jax.nn.sigmoid(pre)
        g = own[r, :].astype(F32) + other[r, :].astype(F32)
        g = g * gate * (1.0 + pre * (1.0 - gate))
        acc[r, :] = g
        gn_rows[0:1, :] += jnp.sum(g * hat, axis=0, keepdims=True)
        gn_rows[1:2, :] += jnp.sum(g, axis=0, keepdims=True)

    each_rows(through_silu)
    mean_shift = group_average(gn_rows[1:2, :] * gain, mats, width)
    mean_gain = group_average(gn_rows[0:1, :] * gain, mats, width)

    def pull(r):
        hat = (noisy[r, :] - mean) * scale
        v = grad3[r, :] + scale * (acc[r, :] * gain - mean_shift - hat * mean_gain)
        grad2[r, :] = v
        gl[r, :] = v.astype(LOW)

    each_rows(pull)
    block = 256
    started = False
    copies[0].wait()
    copies[1].wait()
    for i in (1, 0):
        for b in range(hid // block):
            up = slice(block * b, block * (b + 1))
            down = slice(hid + block * b, hid + block * (b + 1))
            pre = mm(n2[...], wv[i, :, up])
            t, hidden = gelu_parts(pre)
            slope = gelu_slope(pre, t)
            d[i, :, down] = mm_tn(gl[...], hidden.astype(LOW)).astype(LOW)
            hb[...] = (mm(gl[...], wv[i, :, down]) * slope).astype(LOW)
            d[i, :, up] = mm_tn(n2[...], hb[...]).astype(LOW)
            term = mm_nt(hb[...], wv[i, :, up])
            if started:
                acc[...] += term
            else:
                acc[...] = term
                started = True
    part[...] = acc[...].astype(LOW)


def attn_backward(
    seg_col, seg_row, resid, own, other, grad2, norms, n1, qkv, mixed, logs, w,
    grad1, d, part, ln_rows, wv, gl, gm, dqkv, dkv, sems,
):
    n = mixed.shape[2]
    copies = start_copies([(w.at[0], wv.at[0]), (w.at[1], wv.at[1])], sems)
    ln_rows[...] = jnp.zeros(ln_rows.shape, F32)

    def pull(r):
        g = own[r, :].astype(F32) + other[r, :].astype(F32)
        back, gain, shift = ln_back(resid[r, :], norms[2:3, :], g)
        v = grad2[r, :] + back
        grad1[r, :] = v
        gl[r, :] = v.astype(LOW)
        ln_rows[0:1, :] += gain
        ln_rows[1:2, :] += shift

    each_rows(pull)
    for i in range(2):
        d[i, :, 3 * n :] = mm_tn(gl[...], mixed[i]).astype(LOW)
        copies[i].wait()
        gm[i] = mm(gl[...], wv[i, :, 3 * n :]).astype(LOW)
    dkv[...] = jnp.zeros(dkv.shape, F32)

    def heads(r):
        mask = seg_col[r, :] == seg_row[...]
        for i in range(2):
            per = n // HD
            rows_logs = [logs[r, per * i + h : per * i + h + 1] for h in range(per)]
            gq, gk, gv = softmax_heads_back(
                qkv[i, r, :n], qkv[i, :, n : 2 * n], qkv[i, :, 2 * n :], gm[i, r, :], rows_logs,
                per, HD ** (-0.5), mask,
            )
            dqkv[i, r, :n] = gq.astype(LOW)
            dkv[i] += jnp.concatenate([gk, gv], axis=1)

    each_rows(heads)
    total = None
    for i in (1, 0):
        dqkv[i, :, n:] = jnp.concatenate(
            [dkv[i, :, :n] * (HD ** (-0.5)), dkv[i, :, n:]], axis=1
        ).astype(LOW)
        d[i, :, : 3 * n] = mm_tn(n1[...], dqkv[i]).astype(LOW)
        term = mm_nt(dqkv[i], wv[i, :, : 3 * n])
        total = term if total is None else total + term
    part[...] = total.astype(LOW)


def input_backward(tok, own, other, grad1, norms, grad_x, ln_rows):
    ln_rows[...] = jnp.zeros(ln_rows.shape, F32)

    def pull(r):
        g = own[r, :].astype(F32) + other[r, :].astype(F32)
        back, gain, shift = ln_back(tok[r, :].astype(F32), norms[0:1, :], g)
        grad_x[r, :] = (grad1[r, :] + back).astype(LOW)
        ln_rows[0:1, :] += gain
        ln_rows[1:2, :] += shift

    each_rows(pull)


MESH_IDS = pl.DeviceIdType.MESH


def place():
    mp = lax.axis_index("mp")
    dp = lax.axis_index("dp")
    return mp // 2, mp % 2, dp // 2, dp % 2


def device(x, core, z, y):
    return (2 * z + y, 2 * x + core)


def meet(peers):
    barrier = pltpu.get_barrier_semaphore()
    for peer in peers:
        pl.semaphore_signal(barrier, inc=1, device_id=peer, device_id_type=MESH_IDS)
    pl.semaphore_wait(barrier, len(peers))


def chip_peers():
    x, core, z, y = place()
    along_z = [device(x, core, (z + k) % 4, y) for k in range(1, 4)]
    return device(1 - x, core, z, y), device(x, core, z, 1 - y), along_z


class Sender:
    def __init__(self, send, recv):
        self.send, self.recv, self.used = send, recv, 0

    def start(self, src, dst, peer):
        k = self.used
        self.used += 1
        copy = pltpu.make_async_remote_copy(
            src_ref=src, dst_ref=dst, send_sem=self.send.at[k], recv_sem=self.recv.at[k],
            device_id=peer, device_id_type=MESH_IDS,
        )
        copy.start()
        return copy


def gather_body(count, *refs):
    pieces, outs, (own_sem, send, recv) = refs[:count], refs[count : 2 * count], refs[2 * count :]
    x, core, z, y = place()
    to_x, to_y, to_z = chip_peers()
    net = Sender(send, recv)
    local = [
        pltpu.make_async_copy(pieces[g], outs[g].at[0, z, y], own_sem.at[g]) for g in range(count)
    ]
    for c in local:
        c.start()
    meet([to_x, to_y, *to_z])

    def send_line(g):
        return [net.start(pieces[g], outs[g].at[0, z, y], peer) for peer in to_z]

    def send_planes(g):
        line = outs[g].at[0, :, y]
        return (
            net.start(line, outs[g].at[1, :, y], to_x),
            net.start(line, outs[g].at[0, :, y], to_y),
        )

    def send_corners(g):
        return (
            net.start(outs[g].at[0, 0:2, 1 - y], outs[g].at[1, 0:2, 1 - y], to_x),
            net.start(outs[g].at[1, 2:4, y], outs[g].at[1, 2:4, y], to_y),
        )

    last = count - 1
    src = pieces[last]
    lines = {0: send_line(0)}
    early_x = net.start(src, outs[last].at[1, z, y], to_x)
    early_y = net.start(src, outs[last].at[0, z, y], to_y)
    planes, corners, done = {}, {}, [early_x, early_y]
    for g in range(last):
        for c in lines[g]:
            c.wait_recv()
        local[g].wait()
        planes[g] = send_planes(g)
        if g + 1 < last:
            lines[g + 1] = send_line(g + 1)
        if g == 0:
            early_x.wait_recv()
            late = net.start(outs[last].at[1, z, y], outs[last].at[1, z, y], to_y)
        if g == 1:
            early_y.wait_recv()
            late.wait_recv()
            local[last].wait()
            block = outs[last].at[:, z]
            far = [net.start(block, outs[last].at[:, z], peer) for peer in to_z]
        if g >= 1:
            for c in planes[g - 1]:
                c.wait_recv()
            corners[g - 1] = send_corners(g - 1)
    for c in planes[last - 1]:
        c.wait_recv()
    corners[last - 1] = send_corners(last - 1)
    for g in range(last):
        for c in corners[g]:
            c.wait_recv()
    for c in far:
        c.wait_recv()
    for c in [*done, late, *far]:
        c.wait_send()
    for g in range(last):
        for c in [*lines[g], *planes[g], *corners[g]]:
            c.wait_send()


def gather_all(pieces):
    count = len(pieces)
    copies = (count - 1) * 7 + 6
    return pl.pallas_call(
        partial(gather_body, count),
        name="gather_weights",
        in_specs=[spec_any() for _ in pieces],
        out_specs=[spec_any() for _ in pieces],
        out_shape=[jax.ShapeDtypeStruct((2, 4, 2, *p.shape), LOW) for p in pieces],
        scratch_shapes=[
            pltpu.SemaphoreType.DMA((count,)), pltpu.SemaphoreType.DMA((copies,)),
            pltpu.SemaphoreType.DMA((copies,)),
        ],
        compiler_params=pltpu.CompilerParams(collective_id=0, has_side_effects=True),
    )(*pieces)


def add_rows(target, terms, step=16):
    def body(k, carry):
        r = pl.ds(pl.multiple_of(k * step, step), step)
        total = terms[0][r, :].astype(F32)
        for t in terms[1:]:
            total = total + t[r, :].astype(F32)
        target[r, :] = total.astype(target.dtype)
        return carry

    lax.fori_loop(0, target.shape[0] // step, body, 0)


def scatter_body(count, *refs):
    last = count - 1
    grads, outs, refs = refs[:count], refs[count : 2 * count], refs[2 * count :]
    bufs, refs = refs[: 5 * last], refs[5 * last :]
    far_buf, mid_buf, side_buf, send, recv = refs
    x, core, z, y = place()
    to_x, to_y, to_z = chip_peers()
    net = Sender(send, recv)
    meet([to_x, to_y, *to_z])
    far = [
        net.start(grads[last].at[:, (z + k) % 4], far_buf.at[k - 1], to_z[k - 1])
        for k in range(1, 4)
    ]
    first, second, ends = {}, {}, {}
    order = list(range(last))[::-1]

    def send_raw(g):
        cx, cy, lx, ly = bufs[5 * g : 5 * g + 4]
        first[g] = (
            net.start(grads[g].at[1, 0:2, 1 - y], cx, to_x),
            net.start(grads[g].at[1, 2:4, 1 - y], cy, to_y),
            net.start(grads[g].at[1, 0:2, y], lx.at[0:2], to_x),
            net.start(grads[g].at[0, 2:4, 1 - y], ly.at[2:4], to_y),
        )

    def fold_corners(g):
        cx, cy, lx, ly = bufs[5 * g : 5 * g + 4]
        first[g][0].wait_recv()
        for k in range(2):
            add_rows(cx.at[k], [cx.at[k], grads[g].at[0, k, 1 - y]])
        to_line = net.start(cx, ly.at[0:2], to_y)
        first[g][1].wait_recv()
        for k in range(2):
            add_rows(cy.at[k], [cy.at[k], grads[g].at[1, 2 + k, y]])
        second[g] = (to_line, net.start(cy, lx.at[2:4], to_x))

    def fold_lines(g):
        lx, ly, zb = bufs[5 * g + 2 : 5 * g + 5]
        for c in (first[g][2], first[g][3], *second[g]):
            c.wait_recv()
        for k in range(4):
            add_rows(lx.at[k], [lx.at[k], ly.at[k], grads[g].at[0, k, y]])
        ends[g] = [
            net.start(lx.at[(z + k) % 4], zb.at[k - 1], to_z[k - 1]) for k in range(1, 4)
        ]

    def finish_group(g):
        lx, zb = bufs[5 * g + 2], bufs[5 * g + 4]
        for c in ends[g]:
            c.wait_recv()
        add_rows(outs[g], [lx.at[z], zb.at[0], zb.at[1], zb.at[2]])

    send_raw(order[0])
    for c in far:
        c.wait_recv()
    for i in range(2):
        for j in range(2):
            add_rows(
                mid_buf.at[i, j], [grads[last].at[i, z, j], *(far_buf.at[k, i, j] for k in range(3))]
            )
    half = net.start(mid_buf.at[:, 1 - y], side_buf.at[0:2], to_y)
    for pos, g in enumerate(order):
        fold_corners(g)
        if pos + 1 < last:
            send_raw(order[pos + 1])
        if pos == 0:
            half.wait_recv()
            for i in (1, 0):
                add_rows(mid_buf.at[i, y], [mid_buf.at[i, y], side_buf.at[i]])
            tail = net.start(mid_buf.at[1, y], side_buf.at[2], to_x)
        fold_lines(g)
        if pos >= 1:
            finish_group(order[pos - 1])
    tail.wait_recv()
    add_rows(outs[last], [mid_buf.at[0, y], side_buf.at[2]])
    finish_group(order[-1])
    for c in [*far, half, tail]:
        c.wait_send()
    for g in range(last):
        for c in [*first[g], *second[g], *ends[g]]:
            c.wait_send()


def scatter_all(grads):
    count = len(grads)
    rows = grads[0].shape[3]
    widths = [g.shape[4] for g in grads]
    copies = (count - 1) * 9 + 5
    scratch = []
    for w in widths[:-1]:
        scratch += [VM((k, rows, w), LOW) for k in (2, 2, 4, 4, 3)]
    w = widths[-1]
    scratch += [VM((3, 2, 2, rows, w), LOW), VM((2, 2, rows, w), LOW), VM((3, rows, w), LOW)]
    return pl.pallas_call(
        partial(scatter_body, count),
        name="scatter_grads",
        in_specs=[spec_vm() for _ in grads],
        out_specs=[spec_vm() for _ in grads],
        out_shape=[jax.ShapeDtypeStruct((rows, w), F32) for w in widths],
        scratch_shapes=[
            *scratch, pltpu.SemaphoreType.DMA((copies,)), pltpu.SemaphoreType.DMA((copies,)),
        ],
        compiler_params=pltpu.CompilerParams(
            collective_id=1, has_side_effects=True, vmem_limit_bytes=60 << 20
        ),
    )(*grads)


def fast_device(
    tokens,
    noise_field,
    codec_tokens,
    timesteps,
    segments,
    cotangent,
    w_in,
    w_back,
    w_up,
    w_down,
    m_in,
    m_back,
    m_up,
    m_down,
    v_in,
    v_back,
    v_up,
    v_down,
    norm_params,
    norm_m,
    norm_v,
):
    length = segments.shape[1]
    features = tokens.shape[1]
    n = w_in.shape[2]
    hid = w_up.shape[1]
    heads = 2 * n // HD
    mp = lax.axis_index("mp")
    dp = lax.axis_index("dp")
    x, core, z, y = mp // 2, mp % 2, dp // 2, dp % 2
    lead = (core == 0).astype(F32)
    slices = [2 * x + core, 2 * (1 - x) + core]

    low_in = w_in.astype(LOW).transpose(1, 0, 2).reshape(w_in.shape[1], -1)
    low_back = w_back.astype(LOW).transpose(2, 0, 1).reshape(w_back.shape[2], -1)
    low_up = w_up.astype(LOW)
    low_down = w_down.astype(LOW).T
    piece_attn = jnp.concatenate([low_in[:, : 3 * n], low_back[:, :n]], axis=1)
    piece_mlp = jnp.concatenate([low_up, low_down], axis=1)
    piece_one = jnp.concatenate([low_in[:, 7 * n :], low_in[:, 3 * n : 4 * n]], axis=1)
    piece_two = low_back[:, 2 * n :]
    piece_cross = jnp.concatenate([low_in[:, 4 * n : 7 * n], low_back[:, n : 2 * n]], axis=1)
    gathered = gather_all([piece_attn, piece_mlp, piece_one, piece_two, piece_cross])
    w_attn, w_mlp, w_one, w_two, w_cross = [
        w.reshape(2, features, -1) for w in gathered
    ]
    weight_sq = matrix_squares(w_in, w_back, w_up, w_down)

    def own_rows(v):
        return lax.dynamic_slice_in_dim(v, x * length, length, 0)

    tok = own_rows(tokens)
    noise = own_rows(noise_field)
    cot = own_rows(cotangent)
    codec = pick(codec_tokens, x, 0)
    step = pick(timesteps, x, 0)
    seg = pick(segments, x, 0)
    seg_col, seg_row = seg[:, None], seg[None, :]
    noise_level = jnp.sqrt((step.astype(F32) + 1.0) / TSTEPS).reshape(1, 1)
    embed = jax.nn.silu(time_embedding(step[None], features)).astype(LOW)
    embed_rows = jnp.broadcast_to(embed, (8, features))
    embed_col = embed.astype(F32).reshape(features, 1)
    side = jnp.stack(
        [lax.dynamic_slice(norm_params, (6, s * n), (2, n)) for s in slices]
    )
    full = (length, features)
    square = (features, 4 * n)
    sem = pltpu.SemaphoreType.DMA
    norms = norm_params

    n1, qkv, mixed, logs, part = run_kernel(
        attn_forward, "attn_forward",
        [seg_col, seg_row, tok, norms, w_attn],
        [(full, LOW), ((2, length, 3 * n), LOW), ((2, length, n), LOW), ((length, heads), F32), (full, LOW)],
        [VM((2, *square), LOW), sem((2,))], hbm=(4,), flops=4 * 10**9,
    )
    resid_one, n2, part_two = run_kernel(
        mlp_forward, "mlp_forward",
        [tok, part, swap_core(part), norms, w_mlp],
        [(full, F32), (full, LOW), (full, LOW)],
        [VM((2, features, 2 * hid), LOW), VM(full, F32), sem((2,))], hbm=(4,), flops=3 * 10**9,
    )
    tall = length + 2 * TIME
    noisy, first, conv, taps, part = run_kernel(
        conv_forward, "conv_forward",
        [noise_level, resid_one, part_two, swap_core(part_two), noise, norms, side, embed_rows, w_one, w_two],
        [(full, F32), (full, LOW), ((2, length, n), F32), ((2, tall, 3 * n), LOW), (full, LOW)],
        [
            VM((tall, features), LOW), VM((2, features, 10 * n), LOW), VM((2, features, 9 * n), LOW),
            sem((4,)),
        ],
        hbm=(8, 9), flops=7 * 10**9,
    )
    resid_three, n3, cq, ckv, cross, logs_c, part = run_kernel(
        cross_forward, "cross_forward",
        [noisy, part, swap_core(part), codec, norms, w_cross],
        [
            (full, F32), (full, LOW), ((2, length, n), LOW), ((2, codec.shape[0], 2 * n), LOW),
            ((2, length, n), LOW), ((length, heads), F32), (full, LOW),
        ],
        [VM((2, *square), LOW), sem((2,))], hbm=(5,), flops=2 * 10**9,
    )
    result = resid_three + (part.astype(F32) + swap_core(part).astype(F32))
    out_low = result.astype(LOW)
    out_rows = by_parity(x, out_low, swap_x(out_low), 0).reshape(-1, features)

    d, part = run_kernel(
        cross_backward, "cross_backward",
        [cot, n3, codec, cq, ckv, cross, logs_c, w_cross],
        [((2, *square), LOW), (full, LOW)],
        [
            VM((2, *square), LOW), VM((2, length, n), LOW), VM((2, length, n), LOW),
            VM((2, codec.shape[0], 2 * n), F32), sem((2,)),
        ],
        hbm=(7,), flops=4 * 10**9,
    )
    d_cross = d
    wide = (features, 9 * n)
    grad_three, d, tapsg, ln_eight, gn_six, gsum = run_kernel(
        conv_two_backward, "conv_two_backward",
        [resid_three, part, swap_core(part), cot, norms, side, conv, taps, w_two],
        [
            (full, F32), ((2, *wide), LOW), ((2, tall, 3 * n), LOW), ((2, features), F32),
            ((2, 2, n), F32), ((2, n), F32),
        ],
        [VM((tall, features), LOW), VM(full, LOW), VM((2, *wide), LOW), sem((2,))],
        hbm=(8,), flops=6 * 10**9,
    )
    d_two = d
    wider = (features, 10 * n)
    d, part = run_kernel(
        conv_one_backward, "conv_one_backward",
        [first, tapsg, gsum, embed_col, w_one],
        [((2, *wider), LOW), (full, LOW)],
        [VM((2, *wider), LOW), sem((2,))], hbm=(4,), flops=6 * 10**9,
    )
    d_one = d
    double = (features, 2 * hid)
    grad_two, d, part, gn_four = run_kernel(
        mlp_backward, "mlp_backward",
        [noisy, part, swap_core(part), grad_three, norms, n2, w_mlp],
        [(full, F32), ((2, *double), LOW), (full, LOW), ((2, features), F32)],
        [VM((2, *double), LOW), VM(full, LOW), VM((length, 256), LOW), VM(full, F32), sem((2,))],
        hbm=(6,), flops=7 * 10**9,
    )
    d_mlp = d
    grad_one, d, part, ln_two = run_kernel(
        attn_backward, "attn_backward",
        [seg_col, seg_row, resid_one, part, swap_core(part), grad_two, norms, n1, qkv, mixed, logs, w_attn],
        [(full, F32), ((2, *square), LOW), (full, LOW), ((2, features), F32)],
        [
            VM((2, *square), LOW), VM(full, LOW), VM((2, length, n), LOW), VM((2, length, 3 * n), LOW),
            VM((2, length, 2 * n), F32), sem((2,)),
        ],
        hbm=(11,), flops=8 * 10**9,
    )
    d_attn = d
    grad_x, ln_zero = run_kernel(
        input_backward, "input_backward",
        [tok, part, swap_core(part), grad_one, norms],
        [(full, LOW), ((2, features), F32)], [],
    )
    sums = scatter_all(
        [v.reshape(2, 4, 2, -1, v.shape[2]) for v in (d_attn, d_mlp, d_one, d_two, d_cross)]
    )
    sum_attn, sum_mlp, sum_one, sum_two, sum_cross = sums
    half = length // 2
    mine = lax.dynamic_slice_in_dim(grad_x, core * half, half, 0)
    got = swap_x(mine)
    other_x = by_parity(core, got, swap_core(got), 0).reshape(length, features)
    grad_rows = by_parity(x, grad_x, other_x, 0).reshape(-1, features).astype(F32)

    def unpack_in(v):
        return v.reshape(v.shape[0], -1, n).transpose(1, 0, 2)

    def unpack_back(v):
        return v.reshape(v.shape[0], -1, n).transpose(1, 2, 0)

    summed_in = unpack_in(
        jnp.concatenate(
            [sum_attn[:, : 3 * n], sum_one[:, 9 * n :], sum_cross[:, : 3 * n], sum_one[:, : 9 * n]],
            axis=1,
        )
    )
    summed_back = unpack_back(
        jnp.concatenate([sum_attn[:, 3 * n :], sum_cross[:, 3 * n :], sum_two], axis=1)
    )
    summed_up = sum_mlp[:, :hid]
    summed_down = sum_mlp[:, hid:].T

    group_rows = jnp.zeros((2, features), F32)
    for i, s in enumerate(slices):
        group_rows = lax.dynamic_update_slice(group_rows, gn_six[i], (0, s * n))
    norm_grad = lax.psum(
        jnp.concatenate(
            [ln_zero * lead, ln_two * lead, gn_four * lead, group_rows, ln_eight * lead]
        ),
        ("dp", "mp"),
    )
    return finish(
        out_rows, grad_rows, weight_sq, (summed_in, summed_back, summed_up, summed_down),
        (w_in, w_back, w_up, w_down), (m_in, m_back, m_up, m_down), (v_in, v_back, v_up, v_down),
        norm_grad, norm_params, norm_m, norm_v,
    )


def finish(out_rows, grad_rows, weight_sq, grads, masters, moments, squares, norm_grad, norm_params, norm_m, norm_v):
    stepped = [
        adam_update(w, g, m, v, WEIGHT_DECAY)
        for w, g, m, v in zip(masters, grads, moments, squares)
    ]
    new_m = [s[0] for s in stepped]
    new_v = [s[1] for s in stepped]
    updates = [s[2] for s in stepped]
    update_sq = matrix_squares(*updates)
    weight_total, update_total = lax.psum((weight_sq, update_sq), ("dp", "mp"))
    weight_len = jnp.sqrt(weight_total)
    update_len = jnp.sqrt(update_total)
    trust = LEARN_RATE * (weight_len / update_len)
    scales = (trust[0:16, None, None], trust[16:27, None, None], trust[27], trust[28])
    new_w = [w - s * u for w, s, u in zip(masters, scales, updates)]
    norm_m_new, norm_v_new, upd_norm = adam_update(norm_params, norm_grad, norm_m, norm_v, 0.0)
    row_trust = jnp.sqrt(jnp.sum(norm_params * norm_params, axis=1)) / jnp.sqrt(
        jnp.sum(upd_norm * upd_norm, axis=1)
    )
    new_norm = norm_params - LEARN_RATE * row_trust[:, None] * upd_norm
    return (
        out_rows, grad_rows, *new_w, *new_m, *new_v, new_norm, norm_m_new, norm_v_new,
        jnp.stack([weight_len, update_len]),
    )


def solution(mesh):
    per_device = fast_device if dict(mesh.shape) == {"dp": 8, "mp": 4} else generic_device
    placed = (
        P("dp", None),
        P("dp", None),
        P("dp", None, None),
        P("dp"),
        P("dp", None),
        P("dp", None),
        P(None, "dp", "mp"),
        P(None, "mp", "dp"),
        P("dp", "mp"),
        P("mp", "dp"),
        P(None, "dp", "mp"),
        P(None, "mp", "dp"),
        P("dp", "mp"),
        P("mp", "dp"),
        P(None, "dp", "mp"),
        P(None, "mp", "dp"),
        P("dp", "mp"),
        P("mp", "dp"),
        P(),
        P(),
        P(),
    )
    return jax.shard_map(
        per_device,
        mesh=mesh,
        in_specs=placed,
        out_specs=(
            P("dp", None),
            P("dp", None),
            P(None, "dp", "mp"),
            P(None, "mp", "dp"),
            P("dp", "mp"),
            P("mp", "dp"),
            P(None, "dp", "mp"),
            P(None, "mp", "dp"),
            P("dp", "mp"),
            P("mp", "dp"),
            P(None, "dp", "mp"),
            P(None, "mp", "dp"),
            P("dp", "mp"),
            P("mp", "dp"),
            P(),
            P(),
            P(),
            P(),
        ),
        check_vma=False,
    )
```

```python
from functools import partial
import math

import jax
import jax.numpy as jnp
from jax import lax
from jax.experimental import pallas as pl
from jax.experimental.pallas import tpu as pltpu
from jax.sharding import PartitionSpec as P

HD = 64
GROUPS = 32
FREQ = 8
TIME = 64
TSTEPS = 1000
STEP = 5


NORM_EPS = 1e-05
MOMENT_DECAY = 0.5
LEARN_RATE = 0.5
WEIGHT_DECAY = 0.01
ADAM_EPS = 1e-06
MASK_VALUE = -1e30
HIGHEST_PRECISION = lax.Precision.HIGHEST


def layer_norm(value_tensor, gain_row, shift_row):
    centre = value_tensor - jnp.mean(value_tensor, axis=-1, keepdims=True)
    spread = jnp.mean(centre * centre, axis=-1, keepdims=True)
    return centre * lax.rsqrt(spread + NORM_EPS) * gain_row + shift_row


def group_norm(value_tensor, gain_row, shift_row, group_width):
    seqs_here, length, channels = value_tensor.shape
    grouped = value_tensor.reshape(seqs_here, length, channels // group_width, group_width)
    centre = grouped - jnp.mean(grouped, axis=(1, 3), keepdims=True)
    spread = jnp.mean(centre * centre, axis=(1, 3), keepdims=True)
    normed = (centre * lax.rsqrt(spread + NORM_EPS)).reshape(seqs_here, length, channels)
    return normed * gain_row + shift_row


def norm_silu(value_tensor, gain_row, shift_row, group_width):
    return jax.nn.silu(group_norm(value_tensor, gain_row, shift_row, group_width))


def time_embedding(timesteps, features):
    half_width = features // 2
    freq_rates = jnp.exp(
        -math.log(10000.0) * jnp.arange(half_width, dtype=jnp.float32) / half_width
    )
    angles = timesteps.astype(jnp.float32)[:, None] * freq_rates[None, :]
    return jnp.concatenate([jnp.sin(angles), jnp.cos(angles)], axis=1)


def flatten_rows(value_tensor):
    return value_tensor.reshape(-1, value_tensor.shape[-1])


def project(values_low, weight_matrix):
    summed = jnp.dot(flatten_rows(values_low), weight_matrix, preferred_element_type=jnp.float32)
    return summed.reshape(values_low.shape[0], values_low.shape[1], weight_matrix.shape[1])


def back_project(grad_low, weight_matrix):
    summed = jnp.einsum(
        "ne,ce->nc", flatten_rows(grad_low), weight_matrix, preferred_element_type=jnp.float32
    )
    return summed.reshape(grad_low.shape[0], grad_low.shape[1], weight_matrix.shape[0])


def weight_grad(left_low, right_low):
    return jnp.einsum(
        "nc,ne->ce",
        flatten_rows(left_low),
        flatten_rows(right_low),
        preferred_element_type=jnp.float32,
    )


def padded_grid(grid_rows):
    seqs_here = grid_rows.shape[0]
    return jnp.pad(grid_rows.reshape(seqs_here, FREQ, TIME, -1), ((0, 0), (1, 1), (1, 1), (0, 0)))


def grid_window(padded, tap_index):
    row_off = tap_index // 3
    col_off = tap_index % 3
    return padded[:, row_off : row_off + FREQ, col_off : col_off + TIME, :].reshape(
        -1, padded.shape[3]
    )


def conv_grid(grid_rows, tap_weights, backward):
    seqs_here = grid_rows.shape[0]
    padded = padded_grid(grid_rows)
    out_width = tap_weights.shape[1] if backward else tap_weights.shape[2]
    summed = jnp.zeros((seqs_here * FREQ * TIME, out_width), jnp.float32)
    for tap_index in range(9):
        window = grid_window(padded, tap_index)
        if backward:
            summed = summed + jnp.einsum(
                "nc,dc->nd", window, tap_weights[8 - tap_index], preferred_element_type=jnp.float32
            )
        else:
            summed = summed + jnp.dot(
                window, tap_weights[tap_index], preferred_element_type=jnp.float32
            )
    return summed.reshape(seqs_here, FREQ * TIME, out_width)


def conv_weight_grad(grid_low, grad_low):
    padded = padded_grid(grid_low)
    grad_flat = flatten_rows(grad_low)
    tap_grads = []
    for tap_index in range(9):
        window = grid_window(padded, tap_index)
        tap_grads.append(
            jnp.einsum("nc,ne->ce", window, grad_flat, preferred_element_type=jnp.float32)
        )
    return jnp.stack(tap_grads)


def split_heads(rows_low):
    return rows_low.reshape(rows_low.shape[0], rows_low.shape[1], rows_low.shape[2] // HD, HD)


def head_scores(queries, key_rows, allowed, score_scale):
    scores = (
        jnp.einsum(
            "sqhd,skhd->shqk",
            split_heads(queries),
            split_heads(key_rows),
            preferred_element_type=jnp.float32,
        )
        * score_scale
    )
    if allowed is not None:
        scores = jnp.where(allowed[:, None], scores, MASK_VALUE)
    return scores


def attend(queries, key_rows, value_rows, allowed, score_scale):
    scores = head_scores(queries, key_rows, allowed, score_scale)
    highest = jnp.max(scores, axis=-1, keepdims=True)
    raised = jnp.exp(scores - highest)
    totals = jnp.sum(raised, axis=-1, keepdims=True)
    soft_low = (raised / totals).astype(jnp.bfloat16)
    mixed_rows = jnp.einsum(
        "shqk,skhd->sqhd", soft_low, split_heads(value_rows), preferred_element_type=jnp.float32
    )
    return (mixed_rows.reshape(queries.shape), highest + jnp.log(totals))


def attend_back(queries, key_rows, value_rows, allowed, score_scale, log_total, grad_mixed):
    scores = head_scores(queries, key_rows, allowed, score_scale)
    soft = jnp.exp(scores - log_total)
    grad_heads = split_heads(grad_mixed)
    grad_soft = jnp.einsum(
        "sqhd,skhd->shqk", grad_heads, split_heads(value_rows), preferred_element_type=jnp.float32
    )
    grad_values = jnp.einsum(
        "shqk,sqhd->skhd", soft.astype(jnp.bfloat16), grad_heads, preferred_element_type=jnp.float32
    )
    row_dot = jnp.sum(soft * grad_soft, axis=-1, keepdims=True)
    grad_scores = (soft * (grad_soft - row_dot)).astype(jnp.bfloat16)
    grad_queries = (
        jnp.einsum(
            "shqk,skhd->sqhd",
            grad_scores,
            split_heads(key_rows),
            preferred_element_type=jnp.float32,
        )
        * score_scale
    )
    grad_keys = (
        jnp.einsum(
            "shqk,sqhd->skhd", grad_scores, split_heads(queries), preferred_element_type=jnp.float32
        )
        * score_scale
    )
    return (
        grad_queries.reshape(queries.shape).astype(jnp.bfloat16),
        grad_keys.reshape(key_rows.shape).astype(jnp.bfloat16),
        grad_values.reshape(value_rows.shape).astype(jnp.bfloat16),
    )


def tensor_parallel_sum(term_rows):
    return lax.psum(term_rows, "mp")


def matrix_squares(first_stack, second_stack, up_rows, down_rows):
    return jnp.concatenate(
        [
            jnp.sum(first_stack * first_stack, axis=(1, 2)),
            jnp.sum(second_stack * second_stack, axis=(1, 2)),
            jnp.sum(up_rows * up_rows)[None],
            jnp.sum(down_rows * down_rows)[None],
        ]
    )


def adam_update(master, grad_rows, first_moment, second_moment, decay_rate):
    first_new = MOMENT_DECAY * first_moment + (1.0 - MOMENT_DECAY) * grad_rows
    second_new = MOMENT_DECAY * second_moment + (1.0 - MOMENT_DECAY) * grad_rows * grad_rows
    correct = 1.0 - MOMENT_DECAY**STEP
    update = first_new / correct / (jnp.sqrt(second_new / correct) + ADAM_EPS) + decay_rate * master
    return (first_new, second_new, update)


def generic_device(
    tokens,
    noise_field,
    codec_tokens,
    timesteps,
    segments,
    cotangent,
    w_in,
    w_back,
    w_up,
    w_down,
    m_in,
    m_back,
    m_up,
    m_down,
    v_in,
    v_back,
    v_up,
    v_down,
    norm_params,
    norm_m,
    norm_v,
):
    seqs_here, length = segments.shape
    features = tokens.shape[1]
    chans_here = w_in.shape[2]
    group_width = features // GROUPS
    score_scale = HD ** (-0.5)
    channel_start = lax.axis_index("mp") * chans_here
    lead_device = (lax.axis_index("mp") == 0).astype(jnp.float32)
    weight_sq = matrix_squares(w_in, w_back, w_up, w_down)
    full_in, full_back, complete_up_weight, full_down = (
        lax.all_gather(w_in.astype(jnp.bfloat16), "dp", axis=1, tiled=True),
        lax.all_gather(w_back.astype(jnp.bfloat16), "dp", axis=2, tiled=True),
        lax.all_gather(w_up.astype(jnp.bfloat16), "dp", axis=0, tiled=True),
        lax.all_gather(w_down.astype(jnp.bfloat16), "dp", axis=1, tiled=True),
    )
    resid_in = tokens.astype(jnp.float32).reshape(seqs_here, length, features)
    allowed = segments[:, :, None] == segments[:, None, :]
    normed_one_low = layer_norm(resid_in, norm_params[0], norm_params[1]).astype(jnp.bfloat16)
    queries = project(normed_one_low, full_in[0]).astype(jnp.bfloat16)
    key_rows = project(normed_one_low, full_in[1]).astype(jnp.bfloat16)
    value_rows = project(normed_one_low, full_in[2]).astype(jnp.bfloat16)
    mixed_rows, log_self = attend(queries, key_rows, value_rows, allowed, score_scale)
    mixed_low = mixed_rows.astype(jnp.bfloat16)
    resid_one = resid_in + tensor_parallel_sum(project(mixed_low, full_back[0]))
    normed_two_low = layer_norm(resid_one, norm_params[2], norm_params[3]).astype(jnp.bfloat16)
    hidden_pre = project(normed_two_low, complete_up_weight)
    hidden_low = jax.nn.gelu(hidden_pre).astype(jnp.bfloat16)
    resid_two = resid_one + tensor_parallel_sum(project(hidden_low, full_down))
    noise_level = jnp.sqrt((timesteps.astype(jnp.float32) + 1.0) / TSTEPS)
    noisy = resid_two + noise_level[:, None, None] * noise_field.astype(jnp.float32).reshape(
        seqs_here, length, features
    )
    first_low = norm_silu(noisy, norm_params[4], norm_params[5], group_width).astype(jnp.bfloat16)
    embed_low = jax.nn.silu(time_embedding(timesteps, features)).astype(jnp.bfloat16)
    time_shift = jnp.dot(embed_low, full_in[3], preferred_element_type=jnp.float32)
    conv_one = conv_grid(first_low, full_in[7:16], False) + time_shift[:, None, :]
    gain_six = lax.dynamic_slice_in_dim(norm_params[6], channel_start, chans_here)
    shift_six = lax.dynamic_slice_in_dim(norm_params[7], channel_start, chans_here)
    second_low = norm_silu(conv_one, gain_six, shift_six, group_width).astype(jnp.bfloat16)
    resid_three = noisy + tensor_parallel_sum(conv_grid(second_low, full_back[2:11], False))
    normed_three_low = layer_norm(resid_three, norm_params[8], norm_params[9]).astype(jnp.bfloat16)
    cross_queries = project(normed_three_low, full_in[4]).astype(jnp.bfloat16)
    cross_keys = project(codec_tokens, full_in[5]).astype(jnp.bfloat16)
    cross_values = project(codec_tokens, full_in[6]).astype(jnp.bfloat16)
    cross_mixed, log_cross = attend(cross_queries, cross_keys, cross_values, None, score_scale)
    cross_low = cross_mixed.astype(jnp.bfloat16)
    result = resid_three + tensor_parallel_sum(project(cross_low, full_back[1]))
    out_low = result.astype(jnp.bfloat16)
    grad_out = cotangent.astype(jnp.float32).reshape(seqs_here, length, features)
    grad_cross_low = grad_out.astype(jnp.bfloat16)
    grad_w_co = weight_grad(cross_low, grad_cross_low)
    grad_cross_mixed = back_project(grad_cross_low, full_back[1]).astype(jnp.bfloat16)
    grad_cq, grad_ck, grad_cv = attend_back(
        cross_queries, cross_keys, cross_values, None, score_scale, log_cross, grad_cross_mixed
    )
    grad_w_cq = weight_grad(normed_three_low, grad_cq)
    grad_w_ck = weight_grad(codec_tokens, grad_ck)
    grad_w_cv = weight_grad(codec_tokens, grad_cv)
    grad_normed_three = tensor_parallel_sum(back_project(grad_cq, full_in[4]))
    pull_three = jax.vjp(layer_norm, resid_three, norm_params[8], norm_params[9])[1]
    grad_part, grad_gain_eight, grad_shift_eight = pull_three(grad_normed_three)
    grad_three = grad_out + grad_part
    grad_conv_low = grad_three.astype(jnp.bfloat16)
    grad_w_conv_two = conv_weight_grad(second_low, grad_conv_low)
    grad_second = conv_grid(grad_conv_low, full_back[2:11], True)
    gather_second_moment = jax.vjp(
        partial(norm_silu, group_width=group_width), conv_one, gain_six, shift_six
    )[1]
    grad_conv_one, grad_gain_six, grad_shift_six = gather_second_moment(grad_second)
    grad_conv_one_low = grad_conv_one.astype(jnp.bfloat16)
    grad_w_time = jnp.einsum(
        "sd,sc->dc",
        embed_low.astype(jnp.float32),
        jnp.sum(grad_conv_one_low.astype(jnp.float32), axis=1),
        precision=HIGHEST_PRECISION,
    )
    grad_w_conv_one = conv_weight_grad(first_low, grad_conv_one_low)
    grad_first = tensor_parallel_sum(conv_grid(grad_conv_one_low, full_in[7:16], True))
    gather_first_moment = jax.vjp(
        partial(norm_silu, group_width=group_width), noisy, norm_params[4], norm_params[5]
    )[1]
    grad_part, grad_gain_four, grad_shift_four = gather_first_moment(grad_first)
    grad_two = grad_three + grad_part
    grad_mlp_low = grad_two.astype(jnp.bfloat16)
    grad_w_down = weight_grad(hidden_low, grad_mlp_low)
    grad_hidden = back_project(grad_mlp_low, full_down)
    grad_pre_low = jax.vjp(jax.nn.gelu, hidden_pre)[1](grad_hidden)[0].astype(jnp.bfloat16)
    up_weight_gradient = weight_grad(normed_two_low, grad_pre_low)
    grad_normed_two = tensor_parallel_sum(back_project(grad_pre_low, complete_up_weight))
    pull_two = jax.vjp(layer_norm, resid_one, norm_params[2], norm_params[3])[1]
    grad_part, grad_gain_two, grad_shift_two = pull_two(grad_normed_two)
    grad_one = grad_two + grad_part
    grad_attn_low = grad_one.astype(jnp.bfloat16)
    grad_w_out = weight_grad(mixed_low, grad_attn_low)
    grad_mixed = back_project(grad_attn_low, full_back[0]).astype(jnp.bfloat16)
    grad_q, grad_k, grad_v = attend_back(
        queries, key_rows, value_rows, allowed, score_scale, log_self, grad_mixed
    )
    grad_w_q = weight_grad(normed_one_low, grad_q)
    grad_w_k = weight_grad(normed_one_low, grad_k)
    grad_w_v = weight_grad(normed_one_low, grad_v)
    grad_normed_one = tensor_parallel_sum(
        back_project(grad_q, full_in[0])
        + back_project(grad_k, full_in[1])
        + back_project(grad_v, full_in[2])
    )
    pull_one = jax.vjp(layer_norm, resid_in, norm_params[0], norm_params[1])[1]
    grad_part, grad_gain_zero, grad_shift_zero = pull_one(grad_normed_one)
    grad_input = grad_one + grad_part
    grad_in_stack = jnp.concatenate(
        [
            jnp.stack([grad_w_q, grad_w_k, grad_w_v, grad_w_time, grad_w_cq, grad_w_ck, grad_w_cv]),
            grad_w_conv_one,
        ]
    )
    grad_back_stack = jnp.concatenate([jnp.stack([grad_w_out, grad_w_co]), grad_w_conv_two])
    summed_in, summed_back, summed_up, summed_down = (
        lax.psum_scatter(grad_in_stack, "dp", scatter_dimension=1, tiled=True),
        lax.psum_scatter(grad_back_stack, "dp", scatter_dimension=2, tiled=True),
        lax.psum_scatter(up_weight_gradient, "dp", scatter_dimension=0, tiled=True),
        lax.psum_scatter(grad_w_down, "dp", scatter_dimension=1, tiled=True),
    )
    shared_rows = (
        jnp.stack(
            [
                grad_gain_zero,
                grad_shift_zero,
                grad_gain_two,
                grad_shift_two,
                grad_gain_four,
                grad_shift_four,
            ]
        )
        * lead_device
    )
    group_rows = lax.dynamic_update_slice(
        jnp.zeros((2, features), jnp.float32),
        jnp.stack([grad_gain_six, grad_shift_six]),
        (0, channel_start),
    )
    last_rows = jnp.stack([grad_gain_eight, grad_shift_eight]) * lead_device
    norm_grad = lax.psum(jnp.concatenate([shared_rows, group_rows, last_rows]), ("dp", "mp"))
    m_in_new, v_in_new, upd_in = adam_update(w_in, summed_in, m_in, v_in, WEIGHT_DECAY)
    m_back_new, v_back_new, upd_back = adam_update(
        w_back, summed_back, m_back, v_back, WEIGHT_DECAY
    )
    m_up_new, v_up_new, upd_up = adam_update(w_up, summed_up, m_up, v_up, WEIGHT_DECAY)
    m_down_new, v_down_new, upd_down = adam_update(
        w_down, summed_down, m_down, v_down, WEIGHT_DECAY
    )
    update_sq = matrix_squares(upd_in, upd_back, upd_up, upd_down)
    weight_total, update_total = lax.psum((weight_sq, update_sq), ("dp", "mp"))
    weight_len = jnp.sqrt(weight_total)
    update_len = jnp.sqrt(update_total)
    trust = weight_len / update_len
    new_in = w_in - LEARN_RATE * trust[0:16, None, None] * upd_in
    new_back = w_back - LEARN_RATE * trust[16:27, None, None] * upd_back
    new_up = w_up - LEARN_RATE * trust[27] * upd_up
    new_down = w_down - LEARN_RATE * trust[28] * upd_down
    norm_m_new, norm_v_new, upd_norm = adam_update(norm_params, norm_grad, norm_m, norm_v, 0.0)
    row_trust = jnp.sqrt(jnp.sum(norm_params * norm_params, axis=1)) / jnp.sqrt(
        jnp.sum(upd_norm * upd_norm, axis=1)
    )
    new_norm = norm_params - LEARN_RATE * row_trust[:, None] * upd_norm
    matrix_norms = jnp.stack([weight_len, update_len])
    out_rows = out_low.reshape(seqs_here * length, features)
    grad_rows = grad_input.reshape(seqs_here * length, features)
    return (
        out_rows,
        grad_rows,
        new_in,
        new_back,
        new_up,
        new_down,
        m_in_new,
        m_back_new,
        m_up_new,
        m_down_new,
        v_in_new,
        v_back_new,
        v_up_new,
        v_down_new,
        new_norm,
        norm_m_new,
        norm_v_new,
        matrix_norms,
    )


CORE_SWAP = [(i, i ^ 1) for i in range(4)]
X_SWAP = [(i, i ^ 2) for i in range(4)]
LOW = jnp.bfloat16
F32 = jnp.float32


def swap_core(v):
    return lax.ppermute(v, "mp", CORE_SWAP)


def swap_x(v):
    return lax.ppermute(v, "mp", X_SWAP)


def by_parity(flag, own, other, axis):
    first = jnp.where(flag == 0, own, other)
    second = jnp.where(flag == 0, other, own)
    return jnp.stack([first, second], axis=axis)


def pick(v, index, axis):
    return lax.dynamic_index_in_dim(v, index, axis, keepdims=False)


def ln_stats(v):
    centre = v - jnp.mean(v, axis=-1, keepdims=True)
    scale = lax.rsqrt(jnp.mean(centre * centre, axis=-1, keepdims=True) + NORM_EPS)
    return centre * scale, scale


def ln_back(v, gain, grad):
    hat, scale = ln_stats(v)
    pulled = grad * gain
    back = scale * (
        pulled
        - jnp.mean(pulled, axis=-1, keepdims=True)
        - hat * jnp.mean(pulled * hat, axis=-1, keepdims=True)
    )
    return back, jnp.sum(grad * hat, axis=0, keepdims=True), jnp.sum(grad, axis=0, keepdims=True)


def mm(a, b):
    return lax.dot_general(a, b, (((1,), (0,)), ((), ())), preferred_element_type=F32)


def mm_nt(a, b):
    return lax.dot_general(a, b, (((1,), (1,)), ((), ())), preferred_element_type=F32)


def mm_tn(a, b):
    return lax.dot_general(a, b, (((0,), (0,)), ((), ())), preferred_element_type=F32)


ANY = pl.ANY
VM = pltpu.VMEM
ROWS = 512
STEP_ROWS = 128


def spec_any():
    return pl.BlockSpec(memory_space=pl.ANY)


def spec_vm():
    return pl.BlockSpec(memory_space=pltpu.VMEM)


def run_kernel(body, name, ins, outs, scratch, hbm=(), flops=0):
    in_specs = [spec_any() if k in hbm else spec_vm() for k in range(len(ins))]
    moved = sum(v.size * v.dtype.itemsize for v in ins) + sum(
        math.prod(s) * jnp.dtype(t).itemsize for s, t in outs
    )
    return pl.pallas_call(
        body,
        name=name,
        in_specs=in_specs,
        out_specs=[spec_vm() for _ in outs],
        out_shape=[jax.ShapeDtypeStruct(s, t) for s, t in outs],
        scratch_shapes=scratch,
        compiler_params=pltpu.CompilerParams(vmem_limit_bytes=56 << 20),
        cost_estimate=pl.CostEstimate(flops=flops, bytes_accessed=moved, transcendentals=0),
    )(*ins)


def each_rows(fn, total=ROWS, step=STEP_ROWS):
    def body(k, carry):
        fn(pl.ds(pl.multiple_of(k * step, step), step))
        return carry

    lax.fori_loop(0, total // step, body, 0)


def start_copies(pairs, sems):
    copies = [pltpu.make_async_copy(a, b, sems.at[k]) for k, (a, b) in enumerate(pairs)]
    for c in copies:
        c.start()
    return copies


def group_mats(channels, width):
    count = channels // width
    r = lax.broadcasted_iota(jnp.int32, (channels, count), 0)
    c = lax.broadcasted_iota(jnp.int32, (channels, count), 1) * width
    down = ((r >= c) & (r < c + width)).astype(F32)
    r = lax.broadcasted_iota(jnp.int32, (count, channels), 1)
    c = lax.broadcasted_iota(jnp.int32, (count, channels), 0) * width
    up = ((r >= c) & (r < c + width)).astype(F32)
    return down, up


def exact_dot(a, b):
    return jnp.dot(a, b, precision=HIGHEST_PRECISION, preferred_element_type=F32)


def group_average(row, mats, width):
    wide = jnp.broadcast_to(row, (8, row.shape[1]))
    return exact_dot(exact_dot(wide, mats[0]) * (1.0 / (width * ROWS)), mats[1])[0:1]


def gelu_parts(v):
    k = math.sqrt(2.0 / math.pi)
    t = jnp.tanh(k * (v + 0.044715 * (v * v * v)))
    return t, 0.5 * v * (1.0 + t)


def gelu_slope(v, t):
    k = math.sqrt(2.0 / math.pi)
    return 0.5 * (1.0 + t) + 0.5 * v * (1.0 - t * t) * (k * (1.0 + 3 * 0.044715 * (v * v)))


def column_of(shape):
    return lax.broadcasted_iota(jnp.int32, shape, 0) % TIME


def from_left(v):
    return jnp.where(column_of(v.shape) == 0, 0.0, pltpu.roll(v, 1, 0))


def from_right(v):
    return jnp.where(column_of(v.shape) == TIME - 1, 0.0, pltpu.roll(v, v.shape[0] - 1, 0))


def softmax_heads(q, k, v, heads, score_scale, mask):
    mixed, logs = [], []
    for h in range(heads):
        s = mm_nt(q[:, HD * h : HD * (h + 1)], k[:, HD * h : HD * (h + 1)]) * score_scale
        if mask is not None:
            s = jnp.where(mask, s, MASK_VALUE)
        top = jnp.max(s, axis=1, keepdims=True)
        e = jnp.exp(s - top)
        total = jnp.sum(e, axis=1, keepdims=True)
        soft = (e * (1.0 / total)).astype(LOW)
        mixed.append(mm(soft, v[:, HD * h : HD * (h + 1)]))
        logs.append(top + jnp.log(total))
    return jnp.concatenate(mixed, axis=1).astype(LOW), logs


def softmax_heads_back(q, k, v, g, logs, heads, score_scale, mask):
    dq, dk, dv = [], [], []
    for h in range(heads):
        cols = slice(HD * h, HD * (h + 1))
        s = mm_nt(q[:, cols], k[:, cols]) * score_scale
        if mask is not None:
            s = jnp.where(mask, s, MASK_VALUE)
        soft = jnp.exp(s - logs[h])
        gs = mm_nt(g[:, cols], v[:, cols])
        dv.append(mm_tn(soft.astype(LOW), g[:, cols]))
        dot = jnp.sum(soft * gs, axis=1, keepdims=True)
        ds = (soft * (gs - dot)).astype(LOW)
        dq.append(mm(ds, k[:, cols]) * score_scale)
        dk.append(mm_tn(ds, q[:, cols]))
    return [jnp.concatenate(d, axis=1) for d in (dq, dk, dv)]


def cross_backward(
    cot, n3, codec, cq, ckv, mixed, logs, w, d, part, wv, gm, dq, dkv, sems
):
    n = mixed.shape[2]
    copies = start_copies([(w.at[0], wv.at[0]), (w.at[1], wv.at[1])], sems)
    for i in (1, 0):
        d[i, :, 3 * n :] = mm_tn(cot[...], mixed[i]).astype(LOW)
    for i in range(2):
        copies[i].wait()
        gm[i] = mm(cot[...], wv[i, :, 3 * n :]).astype(LOW)
    dkv[...] = jnp.zeros(dkv.shape, F32)

    def heads(r):
        for i in range(2):
            per = n // HD
            rows_logs = [logs[r, per * i + h : per * i + h + 1] for h in range(per)]
            gq, gk, gv = softmax_heads_back(
                cq[i, r, :], ckv[i, :, :n], ckv[i, :, n:], gm[i, r, :], rows_logs,
                per, HD ** (-0.5), None,
            )
            dq[i, r, :] = gq.astype(LOW)
            dkv[i] += jnp.concatenate([gk, gv], axis=1)

    each_rows(heads)
    total = None
    for i in (1, 0):
        low_kv = jnp.concatenate(
            [dkv[i, :, :n] * (HD ** (-0.5)), dkv[i, :, n:]], axis=1
        ).astype(LOW)
        d[i, :, :n] = mm_tn(n3[...], dq[i]).astype(LOW)
        d[i, :, n : 3 * n] = mm_tn(codec[...], low_kv).astype(LOW)
        term = mm_nt(dq[i], wv[i, :, :n])
        total = term if total is None else total + term
    part[...] = total.astype(LOW)


def conv_two_backward(
    resid, own, other, cot, norms, side, conv, taps, u,
    grad3, d, tapsg, ln_rows, gn_rows, gsum, pad, gl, uv, sems,
):
    n = conv.shape[2]
    width = resid.shape[1] // GROUPS
    mats_n = group_mats(n, width)
    copies = start_copies([(u.at[0], uv.at[0]), (u.at[1], uv.at[1])], sems)
    pad[0:TIME, :] = jnp.zeros((TIME, pad.shape[1]), LOW)
    pad[TIME + ROWS :, :] = jnp.zeros((TIME, pad.shape[1]), LOW)
    ln_rows[...] = jnp.zeros(ln_rows.shape, F32)

    def pull(r):
        g = own[r, :].astype(F32) + other[r, :].astype(F32)
        back, gain, shift = ln_back(resid[r, :], norms[8:9, :], g)
        v = cot[r, :].astype(F32) + back
        grad3[r, :] = v
        gl[r, :] = v.astype(LOW)
        ln_rows[0:1, :] += gain
        ln_rows[1:2, :] += shift

    each_rows(pull)
    pad[TIME : TIME + ROWS, :] = gl[...]
    for i in (1, 0):
        for a in range(3):
            d[i, :, 3 * n * a : 3 * n * (a + 1)] = mm_tn(
                gl[...], taps[i, TIME * a : TIME * a + ROWS, :]
            ).astype(LOW)
    for i in range(2):
        copies[i].wait()
        q = None
        for a in range(3):
            term = mm(
                pad[TIME * (2 - a) : TIME * (2 - a) + ROWS, :],
                uv[i, :, 3 * n * a : 3 * n * (a + 1)],
            )
            q = term if q is None else q + term
        grad = from_right(q[:, :n]) + q[:, n : 2 * n] + from_left(q[:, 2 * n :])
        c1 = conv[i]
        c1 = c1 - group_average(jnp.sum(c1, axis=0, keepdims=True), mats_n, width)
        var_n = group_average(jnp.sum(c1 * c1, axis=0, keepdims=True), mats_n, width)
        scale = lax.rsqrt(var_n + NORM_EPS)
        hat = c1 * scale
        gain = side[i, 0:1, :]
        pre = hat * gain + side[i, 1:2, :]
        gate = jax.nn.sigmoid(pre)
        grad = grad * gate * (1.0 + pre * (1.0 - gate))
        d_gain = jnp.sum(grad * hat, axis=0, keepdims=True)
        d_shift = jnp.sum(grad, axis=0, keepdims=True)
        gn_rows[i] = jnp.concatenate([d_gain, d_shift], axis=0)
        back = scale * (
            grad * gain
            - group_average(d_shift * gain, mats_n, width)
            - hat * group_average(d_gain * gain, mats_n, width)
        )
        back = back.astype(LOW).astype(F32)
        gsum[i : i + 1, :] = jnp.sum(back, axis=0, keepdims=True)
        tapsg[i, 0:TIME, :] = jnp.zeros((TIME, 3 * n), LOW)
        tapsg[i, TIME + ROWS :, :] = jnp.zeros((TIME, 3 * n), LOW)
        tapsg[i, TIME : TIME + ROWS, :] = jnp.concatenate(
            [from_right(back), back, from_left(back)], axis=1
        ).astype(LOW)


def conv_one_backward(first, tapsg, gsum, embed_col, w, d, part, wv, sems):
    n = gsum.shape[1]
    copies = start_copies([(w.at[0], wv.at[0]), (w.at[1], wv.at[1])], sems)
    for i in (1, 0):
        for a in range(3):
            d[i, :, 3 * n * a : 3 * n * (a + 1)] = mm_tn(
                first[...], tapsg[i, TIME * (2 - a) : TIME * (2 - a) + ROWS, :]
            ).astype(LOW)
        d[i, :, 9 * n :] = (embed_col[...] * gsum[i : i + 1, :]).astype(LOW)
    total = None
    for i in range(2):
        copies[i].wait()
        for a in range(3):
            term = mm_nt(
                tapsg[i, TIME * (2 - a) : TIME * (2 - a) + ROWS, :],
                wv[i, :, 3 * n * a : 3 * n * (a + 1)],
            )
            total = term if total is None else total + term
    part[...] = total.astype(LOW)


def mlp_backward(
    noisy, own, other, grad3, norms, n2, w, grad2, d, part, gn_rows, wv, gl, hb, acc, sems
):
    hid = wv.shape[2] // 2
    width = noisy.shape[1] // GROUPS
    mats = group_mats(noisy.shape[1], width)
    copies = start_copies([(w.at[0], wv.at[0]), (w.at[1], wv.at[1])], sems)
    mean = group_average(jnp.sum(noisy[...], axis=0, keepdims=True), mats, width)
    centre = noisy[...] - mean
    var = group_average(jnp.sum(centre * centre, axis=0, keepdims=True), mats, width)
    scale = lax.rsqrt(var + NORM_EPS)
    gain, shift = norms[4:5, :], norms[5:6, :]
    gn_rows[...] = jnp.zeros(gn_rows.shape, F32)

    def through_silu(r):
        hat = (noisy[r, :] - mean) * scale
        pre = hat * gain + shift
        gate = jax.nn.sigmoid(pre)
        g = own[r, :].astype(F32) + other[r, :].astype(F32)
        g = g * gate * (1.0 + pre * (1.0 - gate))
        acc[r, :] = g
        gn_rows[0:1, :] += jnp.sum(g * hat, axis=0, keepdims=True)
        gn_rows[1:2, :] += jnp.sum(g, axis=0, keepdims=True)

    each_rows(through_silu)
    mean_shift = group_average(gn_rows[1:2, :] * gain, mats, width)
    mean_gain = group_average(gn_rows[0:1, :] * gain, mats, width)

    def pull(r):
        hat = (noisy[r, :] - mean) * scale
        v = grad3[r, :] + scale * (acc[r, :] * gain - mean_shift - hat * mean_gain)
        grad2[r, :] = v
        gl[r, :] = v.astype(LOW)

    each_rows(pull)
    block = 256
    started = False
    copies[0].wait()
    copies[1].wait()
    for i in (1, 0):
        for b in range(hid // block):
            up = slice(block * b, block * (b + 1))
            down = slice(hid + block * b, hid + block * (b + 1))
            pre = mm(n2[...], wv[i, :, up])
            t, hidden = gelu_parts(pre)
            slope = gelu_slope(pre, t)
            d[i, :, down] = mm_tn(gl[...], hidden.astype(LOW)).astype(LOW)
            hb[...] = (mm(gl[...], wv[i, :, down]) * slope).astype(LOW)
            d[i, :, up] = mm_tn(n2[...], hb[...]).astype(LOW)
            term = mm_nt(hb[...], wv[i, :, up])
            if started:
                acc[...] += term
            else:
                acc[...] = term
                started = True
    part[...] = acc[...].astype(LOW)


def attn_backward(
    seg_col, seg_row, resid, own, other, grad2, norms, n1, qkv, mixed, logs, w,
    grad1, d, part, ln_rows, wv, gl, gm, dqkv, dkv, sems,
):
    n = mixed.shape[2]
    copies = start_copies([(w.at[0], wv.at[0]), (w.at[1], wv.at[1])], sems)
    ln_rows[...] = jnp.zeros(ln_rows.shape, F32)

    def pull(r):
        g = own[r, :].astype(F32) + other[r, :].astype(F32)
        back, gain, shift = ln_back(resid[r, :], norms[2:3, :], g)
        v = grad2[r, :] + back
        grad1[r, :] = v
        gl[r, :] = v.astype(LOW)
        ln_rows[0:1, :] += gain
        ln_rows[1:2, :] += shift

    each_rows(pull)
    for i in range(2):
        d[i, :, 3 * n :] = mm_tn(gl[...], mixed[i]).astype(LOW)
        copies[i].wait()
        gm[i] = mm(gl[...], wv[i, :, 3 * n :]).astype(LOW)
    dkv[...] = jnp.zeros(dkv.shape, F32)

    def heads(r):
        mask = seg_col[r, :] == seg_row[...]
        for i in range(2):
            per = n // HD
            rows_logs = [logs[r, per * i + h : per * i + h + 1] for h in range(per)]
            gq, gk, gv = softmax_heads_back(
                qkv[i, r, :n], qkv[i, :, n : 2 * n], qkv[i, :, 2 * n :], gm[i, r, :], rows_logs,
                per, HD ** (-0.5), mask,
            )
            dqkv[i, r, :n] = gq.astype(LOW)
            dkv[i] += jnp.concatenate([gk, gv], axis=1)

    each_rows(heads)
    total = None
    for i in (1, 0):
        dqkv[i, :, n:] = jnp.concatenate(
            [dkv[i, :, :n] * (HD ** (-0.5)), dkv[i, :, n:]], axis=1
        ).astype(LOW)
        d[i, :, : 3 * n] = mm_tn(n1[...], dqkv[i]).astype(LOW)
        term = mm_nt(dqkv[i], wv[i, :, : 3 * n])
        total = term if total is None else total + term
    part[...] = total.astype(LOW)


def input_backward(tok, own, other, grad1, norms, grad_x, ln_rows):
    ln_rows[...] = jnp.zeros(ln_rows.shape, F32)

    def pull(r):
        g = own[r, :].astype(F32) + other[r, :].astype(F32)
        back, gain, shift = ln_back(tok[r, :].astype(F32), norms[0:1, :], g)
        grad_x[r, :] = (grad1[r, :] + back).astype(LOW)
        ln_rows[0:1, :] += gain
        ln_rows[1:2, :] += shift

    each_rows(pull)


MESH_IDS = pl.DeviceIdType.MESH


def place():
    mp = lax.axis_index("mp")
    dp = lax.axis_index("dp")
    return mp // 2, mp % 2, dp // 2, dp % 2


def device(x, core, z, y):
    return (2 * z + y, 2 * x + core)


def meet(peers):
    barrier = pltpu.get_barrier_semaphore()
    for peer in peers:
        pl.semaphore_signal(barrier, inc=1, device_id=peer, device_id_type=MESH_IDS)
    pl.semaphore_wait(barrier, len(peers))


def chip_peers():
    x, core, z, y = place()
    along_z = [device(x, core, (z + k) % 4, y) for k in range(1, 4)]
    return device(1 - x, core, z, y), device(x, core, z, 1 - y), along_z


class Sender:
    def __init__(self, send, recv):
        self.send, self.recv, self.made = send, recv, []

    def start(self, src, dst, peer):
        k = len(self.made)
        copy = pltpu.make_async_remote_copy(
            src_ref=src, dst_ref=dst, send_sem=self.send.at[k], recv_sem=self.recv.at[k],
            device_id=peer, device_id_type=MESH_IDS,
        )
        copy.start()
        self.made.append(copy)
        return copy

    def close(self):
        for copy in self.made:
            copy.wait_send()


def pack_piece(g, w_in, w_back, w_up, w_down, piece):
    n = w_in.shape[2]
    if g == 1:
        hid = w_up.shape[1]
        piece[:, :hid] = w_up[...].astype(LOW)
        piece[:, hid:] = w_down[...].astype(LOW)
        return
    ins, backs = GROUPS_OF[g]
    cols = [w_in[j] for j in ins] + [w_back[j].T for j in backs]
    for k in range(0, len(cols), 2):
        pair = cols[k : k + 2]
        both = pair[0] if len(pair) == 1 else jnp.concatenate(pair, axis=1)
        piece[:, n * k : n * (k + len(pair))] = both.astype(LOW)


GROUPS_OF = {
    0: ([0, 1, 2], [0]),
    2: ([*range(7, 16), 3], []),
    3: ([], [*range(2, 11)]),
    4: ([4, 5, 6], [1]),
}


def row_of(values):
    lane = lax.broadcasted_iota(jnp.int32, (1, 128), 1)
    row = jnp.zeros((1, 128), F32)
    for j, v in enumerate(values):
        row = row + jnp.where(lane == j, v, 0.0)
    return row


def square_sum(v):
    return jnp.sum(jnp.sum(v * v, axis=1, keepdims=True), axis=0, keepdims=True)


class Gather:
    def __init__(self, pieces, outs, net):
        self.pieces, self.outs, self.net = pieces, outs, net
        self.x, self.core, self.z, self.y = place()
        self.to_x, self.to_y, self.to_z = chip_peers()
        self.lines, self.planes, self.corners = {}, {}, {}

    def line(self, g):
        self.lines[g] = [
            self.net.start(self.pieces[g], self.outs[g].at[0, self.z, self.y], peer)
            for peer in self.to_z
        ]

    def own(self, g):
        z, y, out = self.z, self.y, self.outs[g]
        self.planes[g] = [
            self.net.start(self.pieces[g], out.at[1, z, y], self.to_x),
            self.net.start(self.pieces[g], out.at[0, z, y], self.to_y),
        ]

    def spread(self, g, k):
        self.lines[g][k - 1].wait_recv()
        src = self.outs[g].at[0, (self.z - k) % 4, self.y]
        dst = self.outs[g].at[1, (self.z - k) % 4, self.y]
        self.planes[g] += [self.net.start(src, dst, self.to_x), self.net.start(src, src, self.to_y)]

    def turn(self, g):
        for c in self.planes[g]:
            c.wait_recv()
        out, y = self.outs[g], self.y
        self.corners[g] = [
            self.net.start(out.at[0, 0:2, 1 - y], out.at[1, 0:2, 1 - y], self.to_x),
            self.net.start(out.at[1, 2:4, y], out.at[1, 2:4, y], self.to_y),
        ]

    def ready(self, g):
        for c in self.corners[g]:
            c.wait_recv()

    def early(self, g):
        z, y, out = self.z, self.y, self.outs[g]
        self.first = [
            self.net.start(self.pieces[g], out.at[1, z, y], self.to_x),
            self.net.start(self.pieces[g], out.at[0, z, y], self.to_y),
        ]

    def late(self, g):
        self.first[0].wait_recv()
        src = self.outs[g].at[1, self.z, self.y]
        self.first.append(self.net.start(src, src, self.to_y))

    def far(self, g):
        self.first[1].wait_recv()
        self.first[2].wait_recv()
        block = self.outs[g].at[:, self.z]
        self.corners[g] = [self.net.start(block, block, peer) for peer in self.to_z]


def matrix_of(ref, i, first, last):
    block = ref[i, :, :, :, first:last]
    return block.reshape(-1, last - first)


def forward_body(
    w_in, w_back, w_up, w_down, seg_col, seg_row, norms, side, embed, level, tokens, noises, codecs,
    g0, g1, g2, g3, g4, sq, n1_o, qkv_o, mixed_o, logs_o, resid_o, n2_o, noisy_o, first_o, conv_o,
    taps_o, resid3_o, n3_o, cq_o, ckv_o, cross_o, logs_c_o, out_o,
    p0, p1, p2, p3, p4, v0, v1, v2, v3, v4, tok, noise, codec, n1, qkv, mixed, logs, resid, n2,
    noisy, first, conv, taps, resid3, n3, cq, ckv, cross, logs_c, out, pad, acc, sent, got,
    in_sem, out_sem, own_sem, send, recv,
):
    pieces, held, kept = (p0, p1, p2, p3, p4), (v0, v1, v2, v3, v4), (g0, g1, g2, g3, g4)
    n = mixed.shape[2]
    hid = w_up.shape[1]
    features = norms.shape[1]
    width = features // GROUPS
    heads = n // HD
    score_scale = HD ** (-0.5)
    net = Sender(send, recv)
    run = Gather(pieces, held, net)
    x, core, z, y = place()
    sibling = device(x, 1 - core, z, y)
    loads = [
        pltpu.make_async_copy(tokens.at[pl.ds(pl.multiple_of(x * ROWS, ROWS), ROWS), :], tok, in_sem.at[0]),
        pltpu.make_async_copy(noises.at[pl.ds(pl.multiple_of(x * ROWS, ROWS), ROWS), :], noise, in_sem.at[1]),
        pltpu.make_async_copy(codecs.at[x], codec, in_sem.at[2]),
    ]
    for c in loads:
        c.start()
    stores = []

    def store(src, dst):
        copy = pltpu.make_async_copy(src, dst, out_sem.at[len(stores)])
        copy.start()
        stores.append(copy)

    def pack(g):
        pack_piece(g, w_in, w_back, w_up, w_down, pieces[g])
        copy = pltpu.make_async_copy(pieces[g], held[g].at[0, z, y], own_sem.at[g])
        copy.start()
        return copy

    def exchange(k, total):
        sent[k] = total.astype(LOW)
        return net.start(sent.at[k], got.at[k], sibling)

    def joined(k, r):
        return sent[k, r, :].astype(F32) + got[k, r, :].astype(F32)

    local = [pack(0)]
    meet([run.to_x, run.to_y, *run.to_z, sibling])
    run.line(0)
    run.own(0)
    local.append(pack(1))
    run.own(1)
    local += [pack(2), pack(3), pack(4)]
    run.early(4)
    loads[0].wait()

    def norm_one(r):
        hat, _ = ln_stats(tok[r, :].astype(F32))
        n1[r, :] = (hat * norms[0:1, :] + norms[1:2, :]).astype(LOW)

    each_rows(norm_one)
    store(n1, n1_o)
    run.spread(0, 1)
    run.line(1)
    run.spread(0, 2)
    run.spread(0, 3)
    run.own(2)
    sq[...] = row_of(
        [square_sum(w_in[j]) for j in range(16)] + [square_sum(w_back[j]) for j in range(11)]
        + [square_sum(w_up[...]), square_sum(w_down[...])]
    )
    run.turn(0)
    run.late(4)
    local[0].wait()
    run.ready(0)
    store(v0, g0)
    for i in range(2):
        qkv[i] = mm(n1[...], matrix_of(v0, i, 0, 3 * n)).astype(LOW)
    store(qkv, qkv_o)
    run.spread(1, 1)
    run.line(2)
    run.spread(1, 2)
    run.spread(1, 3)
    run.own(3)

    def self_heads(r):
        mask = seg_col[r, :] == seg_row[...]
        found = []
        for i in range(2):
            part, logs_i = softmax_heads(
                qkv[i, r, 0:n], qkv[i, :, n : 2 * n], qkv[i, :, 2 * n : 3 * n], heads, score_scale, mask
            )
            mixed[i, r, :] = part
            found += logs_i
        logs[r, :] = jnp.concatenate(found, axis=1)

    each_rows(self_heads)
    swap = exchange(
        0,
        mm_nt(mixed[0], matrix_of(v0, 0, 3 * n, 4 * n)) + mm_nt(mixed[1], matrix_of(v0, 1, 3 * n, 4 * n)),
    )
    store(mixed, mixed_o)
    store(logs, logs_o)
    run.turn(1)
    swap.wait_recv()

    def norm_two(r):
        v = tok[r, :].astype(F32) + joined(0, r)
        resid[r, :] = v
        hat, _ = ln_stats(v)
        n2[r, :] = (hat * norms[2:3, :] + norms[3:4, :]).astype(LOW)

    each_rows(norm_two)
    store(resid, resid_o)
    store(n2, n2_o)
    run.spread(2, 1)
    run.line(3)
    run.spread(2, 2)
    run.spread(2, 3)
    local[1].wait()
    run.ready(1)
    store(v1, g1)
    block = 256
    for i in range(2):
        for b in range(hid // block):
            pre = mm(n2[...], matrix_of(v1, i, block * b, block * (b + 1)))
            low = gelu_parts(pre)[1].astype(LOW)
            term = mm_nt(low, matrix_of(v1, i, hid + block * b, hid + block * (b + 1)))
            if i == 0 and b == 0:
                acc[...] = term
            else:
                acc[...] += term
    swap = exchange(1, acc[...])
    run.turn(2)
    loads[1].wait()
    swap.wait_recv()

    def add_noise(r):
        noisy[r, :] = resid[r, :] + joined(1, r) + level[...] * noise[r, :].astype(F32)

    each_rows(add_noise)
    store(noisy, noisy_o)
    mats = group_mats(features, width)
    mats_n = group_mats(n, width)
    mean = group_average(jnp.sum(noisy[...], axis=0, keepdims=True), mats, width)
    centre = noisy[...] - mean
    var = group_average(jnp.sum(centre * centre, axis=0, keepdims=True), mats, width)
    scale = lax.rsqrt(var + NORM_EPS) * norms[4:5, :]
    pad[0:TIME, :] = jnp.zeros((TIME, features), LOW)
    pad[TIME + ROWS :, :] = jnp.zeros((TIME, features), LOW)

    def act(r):
        v = (noisy[r, :] - mean) * scale + norms[5:6, :]
        first[r, :] = (v * jax.nn.sigmoid(v)).astype(LOW)

    each_rows(act)
    pad[TIME : TIME + ROWS, :] = first[...]
    store(first, first_o)
    run.spread(3, 1)
    run.spread(3, 2)
    run.spread(3, 3)
    local[4].wait()
    run.far(4)
    local[2].wait()
    run.ready(2)
    store(v2, g2)
    for i in range(2):
        q = None
        for a in range(3):
            term = mm(
                pad[TIME * a : TIME * a + ROWS, :], matrix_of(v2, i, 3 * n * a, 3 * n * (a + 1))
            )
            q = term if q is None else q + term
        shift = mm(embed[...], matrix_of(v2, i, 9 * n, 10 * n))[0:1]
        c1 = from_left(q[:, :n]) + q[:, n : 2 * n] + from_right(q[:, 2 * n :]) + shift
        conv[i] = c1
        c1 = c1 - group_average(jnp.sum(c1, axis=0, keepdims=True), mats_n, width)
        var_n = group_average(jnp.sum(c1 * c1, axis=0, keepdims=True), mats_n, width)
        v = c1 * lax.rsqrt(var_n + NORM_EPS) * side[i, 0:1, :] + side[i, 1:2, :]
        v = v * jax.nn.sigmoid(v)
        taps[i, 0:TIME, :] = jnp.zeros((TIME, 3 * n), LOW)
        taps[i, TIME + ROWS :, :] = jnp.zeros((TIME, 3 * n), LOW)
        taps[i, TIME : TIME + ROWS, :] = jnp.concatenate(
            [from_left(v), v, from_right(v)], axis=1
        ).astype(LOW)
    store(conv, conv_o)
    store(taps, taps_o)
    run.turn(3)
    local[3].wait()
    run.ready(3)
    store(v3, g3)
    total = None
    for i in range(2):
        for a in range(3):
            term = mm_nt(
                taps[i, TIME * a : TIME * a + ROWS, :], matrix_of(v3, i, 3 * n * a, 3 * n * (a + 1))
            )
            total = term if total is None else total + term
    swap = exchange(2, total)
    loads[2].wait()
    run.ready(4)
    store(v4, g4)
    for i in range(2):
        ckv[i] = mm(codec[...], matrix_of(v4, i, n, 3 * n)).astype(LOW)
    store(ckv, ckv_o)
    swap.wait_recv()

    def norm_three(r):
        v = noisy[r, :] + joined(2, r)
        resid3[r, :] = v
        hat, _ = ln_stats(v)
        n3[r, :] = (hat * norms[8:9, :] + norms[9:10, :]).astype(LOW)

    each_rows(norm_three)
    store(resid3, resid3_o)
    store(n3, n3_o)
    for i in range(2):
        cq[i] = mm(n3[...], matrix_of(v4, i, 0, n)).astype(LOW)
    store(cq, cq_o)

    def cross_heads(r):
        found = []
        for i in range(2):
            part, logs_i = softmax_heads(
                cq[i, r, :], ckv[i, :, :n], ckv[i, :, n:], heads, score_scale, None
            )
            cross[i, r, :] = part
            found += logs_i
        logs_c[r, :] = jnp.concatenate(found, axis=1)

    each_rows(cross_heads)
    swap = exchange(
        3,
        mm_nt(cross[0], matrix_of(v4, 0, 3 * n, 4 * n)) + mm_nt(cross[1], matrix_of(v4, 1, 3 * n, 4 * n)),
    )
    store(cross, cross_o)
    store(logs_c, logs_c_o)
    swap.wait_recv()

    def finish_rows(r):
        out[r, :] = (resid3[r, :] + joined(3, r)).astype(LOW)

    each_rows(finish_rows)
    store(out, out_o)
    for c in stores:
        c.wait()
    net.close()


def forward_all(w_in, w_back, w_up, w_down, seg_col, seg_row, norms, side, embed, level, tokens, noises, codecs):
    n, hid = w_in.shape[2], w_up.shape[1]
    rows, features = w_in.shape[1], norms.shape[1]
    heads = 2 * n // HD
    ctok = codecs.shape[1]
    widths = [4 * n, 2 * hid, 10 * n, 9 * n, 4 * n]
    full = (ROWS, features)
    tall = ROWS + 2 * TIME
    kept = [
        (full, LOW), ((2, ROWS, 3 * n), LOW), ((2, ROWS, n), LOW), ((ROWS, heads), F32), (full, F32),
        (full, LOW), (full, F32), (full, LOW), ((2, ROWS, n), F32), ((2, tall, 3 * n), LOW),
        (full, F32), (full, LOW), ((2, ROWS, n), LOW), ((2, ctok, 2 * n), LOW), ((2, ROWS, n), LOW),
        ((ROWS, heads), F32), (full, LOW),
    ]
    groups = [(2, 4, 2, rows, w) for w in widths]
    dma = pltpu.SemaphoreType.DMA
    copies = 4 * 13 + 6 + 4
    res = pl.pallas_call(
        forward_body,
        name="forward",
        in_specs=[spec_vm() for _ in range(10)] + [spec_any() for _ in range(3)],
        out_specs=[spec_any() for _ in groups] + [spec_vm()] + [spec_any() for _ in kept],
        out_shape=[jax.ShapeDtypeStruct(s, LOW) for s in groups]
        + [jax.ShapeDtypeStruct((1, 128), F32)]
        + [jax.ShapeDtypeStruct(s, t) for s, t in kept],
        scratch_shapes=[
            *[VM((rows, w), LOW) for w in widths], *[VM(s, LOW) for s in groups],
            VM(full, LOW), VM(full, LOW), VM((ctok, features), LOW), *[VM(s, t) for s, t in kept],
            VM((tall, features), LOW), VM(full, F32), VM((4, *full), LOW), VM((4, *full), LOW),
            dma((3,)), dma((22,)), dma((5,)), dma((copies,)), dma((copies,)),
        ],
        compiler_params=pltpu.CompilerParams(
            collective_id=0, has_side_effects=True, vmem_limit_bytes=62 << 20
        ),
    )(w_in, w_back, w_up, w_down, seg_col, seg_row, norms, side, embed, level, tokens, noises, codecs)
    return res[:5], res[5], res[6:]


def add_rows(target, terms, step=16):
    def body(k, carry):
        r = pl.ds(pl.multiple_of(k * step, step), step)
        total = terms[0][r, :].astype(F32)
        for t in terms[1:]:
            total = total + t[r, :].astype(F32)
        target[r, :] = total.astype(target.dtype)
        return carry

    lax.fori_loop(0, target.shape[0] // step, body, 0)


def scatter_body(count, *refs):
    last = count - 1
    grads, outs, refs = refs[:count], refs[count : 2 * count], refs[2 * count :]
    bufs, refs = refs[: 5 * last], refs[5 * last :]
    far_buf, mid_buf, side_buf, send, recv = refs
    x, core, z, y = place()
    to_x, to_y, to_z = chip_peers()
    net = Sender(send, recv)
    meet([to_x, to_y, *to_z])
    far = [
        net.start(grads[last].at[:, (z + k) % 4], far_buf.at[k - 1], to_z[k - 1])
        for k in range(1, 4)
    ]
    first, second, ends = {}, {}, {}
    order = list(range(last))[::-1]

    def send_raw(g):
        cx, cy, lx, ly = bufs[5 * g : 5 * g + 4]
        first[g] = (
            net.start(grads[g].at[1, 0:2, 1 - y], cx, to_x),
            net.start(grads[g].at[1, 2:4, 1 - y], cy, to_y),
            net.start(grads[g].at[1, 0:2, y], lx.at[0:2], to_x),
            net.start(grads[g].at[0, 2:4, 1 - y], ly.at[2:4], to_y),
        )

    def fold_corners(g):
        cx, cy, lx, ly = bufs[5 * g : 5 * g + 4]
        first[g][0].wait_recv()
        for k in range(2):
            add_rows(cx.at[k], [cx.at[k], grads[g].at[0, k, 1 - y]])
        to_line = net.start(cx, ly.at[0:2], to_y)
        first[g][1].wait_recv()
        for k in range(2):
            add_rows(cy.at[k], [cy.at[k], grads[g].at[1, 2 + k, y]])
        second[g] = (to_line, net.start(cy, lx.at[2:4], to_x))

    def fold_lines(g):
        lx, ly, zb = bufs[5 * g + 2 : 5 * g + 5]
        for c in (first[g][2], first[g][3], *second[g]):
            c.wait_recv()
        for k in range(4):
            add_rows(lx.at[k], [lx.at[k], ly.at[k], grads[g].at[0, k, y]])
        ends[g] = [
            net.start(lx.at[(z + k) % 4], zb.at[k - 1], to_z[k - 1]) for k in range(1, 4)
        ]

    def finish_group(g):
        lx, zb = bufs[5 * g + 2], bufs[5 * g + 4]
        for c in ends[g]:
            c.wait_recv()
        add_rows(outs[g], [lx.at[z], zb.at[0], zb.at[1], zb.at[2]])

    send_raw(order[0])
    for c in far:
        c.wait_recv()
    for i in range(2):
        for j in range(2):
            add_rows(
                mid_buf.at[i, j], [grads[last].at[i, z, j], *(far_buf.at[k, i, j] for k in range(3))]
            )
    half = net.start(mid_buf.at[:, 1 - y], side_buf.at[0:2], to_y)
    for pos, g in enumerate(order):
        fold_corners(g)
        if pos + 1 < last:
            send_raw(order[pos + 1])
        if pos == 0:
            half.wait_recv()
            for i in (1, 0):
                add_rows(mid_buf.at[i, y], [mid_buf.at[i, y], side_buf.at[i]])
            tail = net.start(mid_buf.at[1, y], side_buf.at[2], to_x)
        fold_lines(g)
        if pos >= 1:
            finish_group(order[pos - 1])
    tail.wait_recv()
    add_rows(outs[last], [mid_buf.at[0, y], side_buf.at[2]])
    finish_group(order[-1])
    for c in [*far, half, tail]:
        c.wait_send()
    for g in range(last):
        for c in [*first[g], *second[g], *ends[g]]:
            c.wait_send()


def scatter_all(grads):
    count = len(grads)
    rows = grads[0].shape[3]
    widths = [g.shape[4] for g in grads]
    copies = (count - 1) * 9 + 5
    scratch = []
    for w in widths[:-1]:
        scratch += [VM((k, rows, w), LOW) for k in (2, 2, 4, 4, 3)]
    w = widths[-1]
    scratch += [VM((3, 2, 2, rows, w), LOW), VM((2, 2, rows, w), LOW), VM((3, rows, w), LOW)]
    return pl.pallas_call(
        partial(scatter_body, count),
        name="scatter_grads",
        in_specs=[spec_vm() for _ in grads],
        out_specs=[spec_vm() for _ in grads],
        out_shape=[jax.ShapeDtypeStruct((rows, w), F32) for w in widths],
        scratch_shapes=[
            *scratch, pltpu.SemaphoreType.DMA((copies,)), pltpu.SemaphoreType.DMA((copies,)),
        ],
        compiler_params=pltpu.CompilerParams(
            collective_id=1, has_side_effects=True, vmem_limit_bytes=60 << 20
        ),
    )(*grads)


def adam_rows(w, g, m, v, decay_rate):
    m_new = MOMENT_DECAY * m + (1.0 - MOMENT_DECAY) * g
    v_new = MOMENT_DECAY * v + (1.0 - MOMENT_DECAY) * g * g
    correct = 1.0 - MOMENT_DECAY**STEP
    update = m_new / correct / (jnp.sqrt(v_new / correct) + ADAM_EPS) + decay_rate * w
    return m_new, v_new, update


def moments_body(*refs):
    sums, refs = refs[:5], refs[5:]
    w_in, w_back, w_up, w_down, m_in, m_back, m_up, m_down, v_in, v_back, v_up, v_down = refs[:12]
    nm_in, nm_back, nm_up, nm_down, nv_in, nv_back, nv_up, nv_down = refs[12:20]
    u_in, u_back, u_up, u_down, usq = refs[20:]
    n = w_in.shape[2]
    squares = [None] * 29

    def place_in(j, g):
        m, v, u = adam_rows(w_in[j], g, m_in[j], v_in[j], WEIGHT_DECAY)
        nm_in[j], nv_in[j], u_in[j] = m, v, u
        squares[j] = square_sum(u)

    def place_back(j, g):
        m, v, u = adam_rows(w_back[j], g.T, m_back[j], v_back[j], WEIGHT_DECAY)
        nm_back[j], nv_back[j], u_back[j] = m, v, u
        squares[16 + j] = square_sum(u)

    for g, (ins, backs) in GROUPS_OF.items():
        for k, j in enumerate(ins):
            place_in(j, sums[g][:, n * k : n * (k + 1)])
        for k, j in enumerate(backs, len(ins)):
            place_back(j, sums[g][:, n * k : n * (k + 1)])
    hid = w_up.shape[1]
    m, v, u = adam_rows(w_up[...], sums[1][:, :hid], m_up[...], v_up[...], WEIGHT_DECAY)
    nm_up[...], nv_up[...], u_up[...] = m, v, u
    squares[27] = square_sum(u)
    m, v, u = adam_rows(w_down[...], sums[1][:, hid:], m_down[...], v_down[...], WEIGHT_DECAY)
    nm_down[...], nv_down[...], u_down[...] = m, v, u
    squares[28] = square_sum(u)
    usq[...] = row_of(squares)


def totals_body(rows, sq, usq, out, ring, ring_b, send, recv):
    mp, dp = lax.axis_index("mp"), lax.axis_index("dp")
    dp_peers = [((dp + k) % 8, mp) for k in range(1, 8)]
    mp_peers = [(dp, (mp + k) % 4) for k in range(1, 4)]
    ring[dp] = jnp.zeros(ring.shape[1:], F32)
    ring[dp, 0:10, :] = rows[...]
    ring[dp, 10:11, 0:128] = sq[...]
    ring[dp, 11:12, 0:128] = usq[...]
    meet(dp_peers + mp_peers)
    net = Sender(send, recv)
    copies = [net.start(ring.at[dp], ring.at[dp], p) for p in dp_peers]
    for c in copies:
        c.wait_recv()
    total = ring[0]
    for k in range(1, 8):
        total = total + ring[k]
    ring_b[mp] = total
    copies = [net.start(ring_b.at[mp], ring_b.at[mp], p) for p in mp_peers]
    for c in copies:
        c.wait_recv()
    out[...] = ring_b[0] + ring_b[1] + ring_b[2] + ring_b[3]
    net.close()


def apply_body(total, w_in, w_back, w_up, w_down, u_in, u_back, u_up, u_down, norms, norm_m, norm_v, *outs):
    nw_in, nw_back, nw_up, nw_down, new_norm, new_nm, new_nv, lens = outs
    both = jnp.sqrt(total[10:12, 0:128])
    lens[...] = both[:, 0:29]
    trust = LEARN_RATE * (both[0:1, :] / jnp.where(both[1:2, :] == 0.0, 1.0, both[1:2, :]))
    lane = lax.broadcasted_iota(jnp.int32, (1, 128), 1)

    def trust_of(j):
        return jnp.sum(jnp.where(lane == j, trust, 0.0), axis=1, keepdims=True)

    for j in range(16):
        nw_in[j] = w_in[j] - trust_of(j) * u_in[j]
    for j in range(11):
        nw_back[j] = w_back[j] - trust_of(16 + j) * u_back[j]
    nw_up[...] = w_up[...] - trust_of(27) * u_up[...]
    nw_down[...] = w_down[...] - trust_of(28) * u_down[...]
    m, v, u = adam_rows(norms[...], total[0:10, :], norm_m[...], norm_v[...], 0.0)
    w = norms[...]
    row_trust = jnp.sqrt(jnp.sum(w * w, axis=1, keepdims=True)) / jnp.sqrt(
        jnp.sum(u * u, axis=1, keepdims=True)
    )
    new_norm[...] = w - LEARN_RATE * row_trust * u
    new_nm[...] = m
    new_nv[...] = v


def lamb_all(sums, sq, rows, masters, moments, squares, norms, norm_m, norm_v):
    shapes = [(v.shape, F32) for v in masters]
    *mvu, usq = run_kernel(
        moments_body, "lamb_moments", [*sums, *masters, *moments, *squares],
        [*shapes, *shapes, *shapes, ((1, 128), F32)], [],
    )
    dma = pltpu.SemaphoreType.DMA
    wide = norms.shape[1]
    total = pl.pallas_call(
        totals_body,
        name="norm_totals",
        in_specs=[spec_vm() for _ in range(3)],
        out_specs=spec_vm(),
        out_shape=jax.ShapeDtypeStruct((16, wide), F32),
        scratch_shapes=[VM((8, 16, wide), F32), VM((4, 16, wide), F32), dma((10,)), dma((10,))],
        compiler_params=pltpu.CompilerParams(collective_id=2, has_side_effects=True),
    )(rows, sq, usq)
    *weights, new_norm, new_nm, new_nv, lens = run_kernel(
        apply_body, "lamb_apply", [total, *masters, *mvu[8:], norms, norm_m, norm_v],
        [*shapes, *[(norms.shape, F32)] * 3, ((2, 29), F32)], [],
    )
    return (*weights, *mvu[:8], new_norm, new_nm, new_nv, lens)


def fast_device(
    tokens,
    noise_field,
    codec_tokens,
    timesteps,
    segments,
    cotangent,
    w_in,
    w_back,
    w_up,
    w_down,
    m_in,
    m_back,
    m_up,
    m_down,
    v_in,
    v_back,
    v_up,
    v_down,
    norm_params,
    norm_m,
    norm_v,
):
    length = segments.shape[1]
    features = tokens.shape[1]
    n = w_in.shape[2]
    hid = w_up.shape[1]
    mp = lax.axis_index("mp")
    dp = lax.axis_index("dp")
    x, core, z, y = mp // 2, mp % 2, dp // 2, dp % 2
    lead = (core == 0).astype(F32)
    slices = [2 * x + core, 2 * (1 - x) + core]

    def own_rows(v):
        return lax.dynamic_slice_in_dim(v, x * length, length, 0)

    tok = own_rows(tokens)
    cot = own_rows(cotangent)
    codec = pick(codec_tokens, x, 0)
    step = pick(timesteps, x, 0)
    seg = pick(segments, x, 0)
    seg_col, seg_row = seg[:, None], seg[None, :]
    noise_level = jnp.sqrt((step.astype(F32) + 1.0) / TSTEPS).reshape(1, 1)
    embed = jax.nn.silu(time_embedding(step[None], features)).astype(LOW)
    embed_rows = jnp.broadcast_to(embed, (8, features))
    embed_col = embed.astype(F32).reshape(features, 1)
    side = jnp.stack(
        [lax.dynamic_slice(norm_params, (6, s * n), (2, n)) for s in slices]
    )
    full = (length, features)
    square = (features, 4 * n)
    sem = pltpu.SemaphoreType.DMA
    norms = norm_params

    gathered, weight_sq, kept = forward_all(
        w_in, w_back, w_up, w_down.T, seg_col, seg_row, norms, side, embed_rows, noise_level,
        tokens, noise_field, codec_tokens,
    )
    w_attn, w_mlp, w_one, w_two, w_cross = [w.reshape(2, features, -1) for w in gathered]
    n1, qkv, mixed, logs, resid_one, n2, noisy, first, conv, taps = kept[:10]
    resid_three, n3, cq, ckv, cross, logs_c, out_low = kept[10:]
    tall = length + 2 * TIME
    out_rows = by_parity(x, out_low, swap_x(out_low), 0).reshape(-1, features)

    d, part = run_kernel(
        cross_backward, "cross_backward",
        [cot, n3, codec, cq, ckv, cross, logs_c, w_cross],
        [((2, *square), LOW), (full, LOW)],
        [
            VM((2, *square), LOW), VM((2, length, n), LOW), VM((2, length, n), LOW),
            VM((2, codec.shape[0], 2 * n), F32), sem((2,)),
        ],
        hbm=(7,), flops=4 * 10**9,
    )
    d_cross = d
    wide = (features, 9 * n)
    grad_three, d, tapsg, ln_eight, gn_six, gsum = run_kernel(
        conv_two_backward, "conv_two_backward",
        [resid_three, part, swap_core(part), cot, norms, side, conv, taps, w_two],
        [
            (full, F32), ((2, *wide), LOW), ((2, tall, 3 * n), LOW), ((2, features), F32),
            ((2, 2, n), F32), ((2, n), F32),
        ],
        [VM((tall, features), LOW), VM(full, LOW), VM((2, *wide), LOW), sem((2,))],
        hbm=(8,), flops=6 * 10**9,
    )
    d_two = d
    wider = (features, 10 * n)
    d, part = run_kernel(
        conv_one_backward, "conv_one_backward",
        [first, tapsg, gsum, embed_col, w_one],
        [((2, *wider), LOW), (full, LOW)],
        [VM((2, *wider), LOW), sem((2,))], hbm=(4,), flops=6 * 10**9,
    )
    d_one = d
    double = (features, 2 * hid)
    grad_two, d, part, gn_four = run_kernel(
        mlp_backward, "mlp_backward",
        [noisy, part, swap_core(part), grad_three, norms, n2, w_mlp],
        [(full, F32), ((2, *double), LOW), (full, LOW), ((2, features), F32)],
        [VM((2, *double), LOW), VM(full, LOW), VM((length, 256), LOW), VM(full, F32), sem((2,))],
        hbm=(6,), flops=7 * 10**9,
    )
    d_mlp = d
    grad_one, d, part, ln_two = run_kernel(
        attn_backward, "attn_backward",
        [seg_col, seg_row, resid_one, part, swap_core(part), grad_two, norms, n1, qkv, mixed, logs, w_attn],
        [(full, F32), ((2, *square), LOW), (full, LOW), ((2, features), F32)],
        [
            VM((2, *square), LOW), VM(full, LOW), VM((2, length, n), LOW), VM((2, length, 3 * n), LOW),
            VM((2, length, 2 * n), F32), sem((2,)),
        ],
        hbm=(11,), flops=8 * 10**9,
    )
    d_attn = d
    grad_x, ln_zero = run_kernel(
        input_backward, "input_backward",
        [tok, part, swap_core(part), grad_one, norms],
        [(full, LOW), ((2, features), F32)], [],
    )
    sums = scatter_all(
        [v.reshape(2, 4, 2, -1, v.shape[2]) for v in (d_attn, d_mlp, d_one, d_two, d_cross)]
    )
    half = length // 2
    mine = lax.dynamic_slice_in_dim(grad_x, core * half, half, 0)
    got = swap_x(mine)
    other_x = by_parity(core, got, swap_core(got), 0).reshape(length, features)
    grad_rows = by_parity(x, grad_x, other_x, 0).reshape(-1, features).astype(F32)

    group_rows = jnp.zeros((2, features), F32)
    for i, s in enumerate(slices):
        group_rows = lax.dynamic_update_slice(group_rows, gn_six[i], (0, s * n))
    rows = jnp.concatenate(
        [ln_zero * lead, ln_two * lead, gn_four * lead, group_rows, ln_eight * lead]
    )
    stepped = lamb_all(
        sums, weight_sq, rows, (w_in, w_back, w_up, w_down.T), (m_in, m_back, m_up, m_down.T),
        (v_in, v_back, v_up, v_down.T), norm_params, norm_m, norm_v,
    )
    stepped = [v.T if k in (3, 7, 11) else v for k, v in enumerate(stepped)]
    return (out_rows, grad_rows, *stepped)


def solution(mesh):
    per_device = fast_device if dict(mesh.shape) == {"dp": 8, "mp": 4} else generic_device
    placed = (
        P("dp", None),
        P("dp", None),
        P("dp", None, None),
        P("dp"),
        P("dp", None),
        P("dp", None),
        P(None, "dp", "mp"),
        P(None, "mp", "dp"),
        P("dp", "mp"),
        P("mp", "dp"),
        P(None, "dp", "mp"),
        P(None, "mp", "dp"),
        P("dp", "mp"),
        P("mp", "dp"),
        P(None, "dp", "mp"),
        P(None, "mp", "dp"),
        P("dp", "mp"),
        P("mp", "dp"),
        P(),
        P(),
        P(),
    )
    return jax.shard_map(
        per_device,
        mesh=mesh,
        in_specs=placed,
        out_specs=(
            P("dp", None),
            P("dp", None),
            P(None, "dp", "mp"),
            P(None, "mp", "dp"),
            P("dp", "mp"),
            P("mp", "dp"),
            P(None, "dp", "mp"),
            P(None, "mp", "dp"),
            P("dp", "mp"),
            P("mp", "dp"),
            P(None, "dp", "mp"),
            P(None, "mp", "dp"),
            P("dp", "mp"),
            P("mp", "dp"),
            P(),
            P(),
            P(),
            P(),
        ),
        check_vma=False,
    )
```

```python
from functools import partial
import math

import jax
import jax.numpy as jnp
from jax import lax
from jax.experimental import pallas as pl
from jax.experimental.pallas import tpu as pltpu
from jax.sharding import PartitionSpec as P

HD = 64
GROUPS = 32
FREQ = 8
TIME = 64
TSTEPS = 1000
STEP = 5


NORM_EPS = 1e-05
MOMENT_DECAY = 0.5
LEARN_RATE = 0.5
WEIGHT_DECAY = 0.01
ADAM_EPS = 1e-06
MASK_VALUE = -1e30
HIGHEST_PRECISION = lax.Precision.HIGHEST


def layer_norm(value_tensor, gain_row, shift_row):
    centre = value_tensor - jnp.mean(value_tensor, axis=-1, keepdims=True)
    spread = jnp.mean(centre * centre, axis=-1, keepdims=True)
    return centre * lax.rsqrt(spread + NORM_EPS) * gain_row + shift_row


def group_norm(value_tensor, gain_row, shift_row, group_width):
    seqs_here, length, channels = value_tensor.shape
    grouped = value_tensor.reshape(seqs_here, length, channels // group_width, group_width)
    centre = grouped - jnp.mean(grouped, axis=(1, 3), keepdims=True)
    spread = jnp.mean(centre * centre, axis=(1, 3), keepdims=True)
    normed = (centre * lax.rsqrt(spread + NORM_EPS)).reshape(seqs_here, length, channels)
    return normed * gain_row + shift_row


def norm_silu(value_tensor, gain_row, shift_row, group_width):
    return jax.nn.silu(group_norm(value_tensor, gain_row, shift_row, group_width))


def time_embedding(timesteps, features):
    half_width = features // 2
    freq_rates = jnp.exp(
        -math.log(10000.0) * jnp.arange(half_width, dtype=jnp.float32) / half_width
    )
    angles = timesteps.astype(jnp.float32)[:, None] * freq_rates[None, :]
    return jnp.concatenate([jnp.sin(angles), jnp.cos(angles)], axis=1)


def flatten_rows(value_tensor):
    return value_tensor.reshape(-1, value_tensor.shape[-1])


def project(values_low, weight_matrix):
    summed = jnp.dot(flatten_rows(values_low), weight_matrix, preferred_element_type=jnp.float32)
    return summed.reshape(values_low.shape[0], values_low.shape[1], weight_matrix.shape[1])


def back_project(grad_low, weight_matrix):
    summed = jnp.einsum(
        "ne,ce->nc", flatten_rows(grad_low), weight_matrix, preferred_element_type=jnp.float32
    )
    return summed.reshape(grad_low.shape[0], grad_low.shape[1], weight_matrix.shape[0])


def weight_grad(left_low, right_low):
    return jnp.einsum(
        "nc,ne->ce",
        flatten_rows(left_low),
        flatten_rows(right_low),
        preferred_element_type=jnp.float32,
    )


def padded_grid(grid_rows):
    seqs_here = grid_rows.shape[0]
    return jnp.pad(grid_rows.reshape(seqs_here, FREQ, TIME, -1), ((0, 0), (1, 1), (1, 1), (0, 0)))


def grid_window(padded, tap_index):
    row_off = tap_index // 3
    col_off = tap_index % 3
    return padded[:, row_off : row_off + FREQ, col_off : col_off + TIME, :].reshape(
        -1, padded.shape[3]
    )


def conv_grid(grid_rows, tap_weights, backward):
    seqs_here = grid_rows.shape[0]
    padded = padded_grid(grid_rows)
    out_width = tap_weights.shape[1] if backward else tap_weights.shape[2]
    summed = jnp.zeros((seqs_here * FREQ * TIME, out_width), jnp.float32)
    for tap_index in range(9):
        window = grid_window(padded, tap_index)
        if backward:
            summed = summed + jnp.einsum(
                "nc,dc->nd", window, tap_weights[8 - tap_index], preferred_element_type=jnp.float32
            )
        else:
            summed = summed + jnp.dot(
                window, tap_weights[tap_index], preferred_element_type=jnp.float32
            )
    return summed.reshape(seqs_here, FREQ * TIME, out_width)


def conv_weight_grad(grid_low, grad_low):
    padded = padded_grid(grid_low)
    grad_flat = flatten_rows(grad_low)
    tap_grads = []
    for tap_index in range(9):
        window = grid_window(padded, tap_index)
        tap_grads.append(
            jnp.einsum("nc,ne->ce", window, grad_flat, preferred_element_type=jnp.float32)
        )
    return jnp.stack(tap_grads)


def split_heads(rows_low):
    return rows_low.reshape(rows_low.shape[0], rows_low.shape[1], rows_low.shape[2] // HD, HD)


def head_scores(queries, key_rows, allowed, score_scale):
    scores = (
        jnp.einsum(
            "sqhd,skhd->shqk",
            split_heads(queries),
            split_heads(key_rows),
            preferred_element_type=jnp.float32,
        )
        * score_scale
    )
    if allowed is not None:
        scores = jnp.where(allowed[:, None], scores, MASK_VALUE)
    return scores


def attend(queries, key_rows, value_rows, allowed, score_scale):
    scores = head_scores(queries, key_rows, allowed, score_scale)
    highest = jnp.max(scores, axis=-1, keepdims=True)
    raised = jnp.exp(scores - highest)
    totals = jnp.sum(raised, axis=-1, keepdims=True)
    soft_low = (raised / totals).astype(jnp.bfloat16)
    mixed_rows = jnp.einsum(
        "shqk,skhd->sqhd", soft_low, split_heads(value_rows), preferred_element_type=jnp.float32
    )
    return (mixed_rows.reshape(queries.shape), highest + jnp.log(totals))


def attend_back(queries, key_rows, value_rows, allowed, score_scale, log_total, grad_mixed):
    scores = head_scores(queries, key_rows, allowed, score_scale)
    soft = jnp.exp(scores - log_total)
    grad_heads = split_heads(grad_mixed)
    grad_soft = jnp.einsum(
        "sqhd,skhd->shqk", grad_heads, split_heads(value_rows), preferred_element_type=jnp.float32
    )
    grad_values = jnp.einsum(
        "shqk,sqhd->skhd", soft.astype(jnp.bfloat16), grad_heads, preferred_element_type=jnp.float32
    )
    row_dot = jnp.sum(soft * grad_soft, axis=-1, keepdims=True)
    grad_scores = (soft * (grad_soft - row_dot)).astype(jnp.bfloat16)
    grad_queries = (
        jnp.einsum(
            "shqk,skhd->sqhd",
            grad_scores,
            split_heads(key_rows),
            preferred_element_type=jnp.float32,
        )
        * score_scale
    )
    grad_keys = (
        jnp.einsum(
            "shqk,sqhd->skhd", grad_scores, split_heads(queries), preferred_element_type=jnp.float32
        )
        * score_scale
    )
    return (
        grad_queries.reshape(queries.shape).astype(jnp.bfloat16),
        grad_keys.reshape(key_rows.shape).astype(jnp.bfloat16),
        grad_values.reshape(value_rows.shape).astype(jnp.bfloat16),
    )


def tensor_parallel_sum(term_rows):
    return lax.psum(term_rows, "mp")


def matrix_squares(first_stack, second_stack, up_rows, down_rows):
    return jnp.concatenate(
        [
            jnp.sum(first_stack * first_stack, axis=(1, 2)),
            jnp.sum(second_stack * second_stack, axis=(1, 2)),
            jnp.sum(up_rows * up_rows)[None],
            jnp.sum(down_rows * down_rows)[None],
        ]
    )


def adam_update(master, grad_rows, first_moment, second_moment, decay_rate):
    first_new = MOMENT_DECAY * first_moment + (1.0 - MOMENT_DECAY) * grad_rows
    second_new = MOMENT_DECAY * second_moment + (1.0 - MOMENT_DECAY) * grad_rows * grad_rows
    correct = 1.0 - MOMENT_DECAY**STEP
    update = first_new / correct / (jnp.sqrt(second_new / correct) + ADAM_EPS) + decay_rate * master
    return (first_new, second_new, update)


def generic_device(
    tokens,
    noise_field,
    codec_tokens,
    timesteps,
    segments,
    cotangent,
    w_in,
    w_back,
    w_up,
    w_down,
    m_in,
    m_back,
    m_up,
    m_down,
    v_in,
    v_back,
    v_up,
    v_down,
    norm_params,
    norm_m,
    norm_v,
):
    seqs_here, length = segments.shape
    features = tokens.shape[1]
    chans_here = w_in.shape[2]
    group_width = features // GROUPS
    score_scale = HD ** (-0.5)
    channel_start = lax.axis_index("mp") * chans_here
    lead_device = (lax.axis_index("mp") == 0).astype(jnp.float32)
    weight_sq = matrix_squares(w_in, w_back, w_up, w_down)
    full_in, full_back, complete_up_weight, full_down = (
        lax.all_gather(w_in.astype(jnp.bfloat16), "dp", axis=1, tiled=True),
        lax.all_gather(w_back.astype(jnp.bfloat16), "dp", axis=2, tiled=True),
        lax.all_gather(w_up.astype(jnp.bfloat16), "dp", axis=0, tiled=True),
        lax.all_gather(w_down.astype(jnp.bfloat16), "dp", axis=1, tiled=True),
    )
    resid_in = tokens.astype(jnp.float32).reshape(seqs_here, length, features)
    allowed = segments[:, :, None] == segments[:, None, :]
    normed_one_low = layer_norm(resid_in, norm_params[0], norm_params[1]).astype(jnp.bfloat16)
    queries = project(normed_one_low, full_in[0]).astype(jnp.bfloat16)
    key_rows = project(normed_one_low, full_in[1]).astype(jnp.bfloat16)
    value_rows = project(normed_one_low, full_in[2]).astype(jnp.bfloat16)
    mixed_rows, log_self = attend(queries, key_rows, value_rows, allowed, score_scale)
    mixed_low = mixed_rows.astype(jnp.bfloat16)
    resid_one = resid_in + tensor_parallel_sum(project(mixed_low, full_back[0]))
    normed_two_low = layer_norm(resid_one, norm_params[2], norm_params[3]).astype(jnp.bfloat16)
    hidden_pre = project(normed_two_low, complete_up_weight)
    hidden_low = jax.nn.gelu(hidden_pre).astype(jnp.bfloat16)
    resid_two = resid_one + tensor_parallel_sum(project(hidden_low, full_down))
    noise_level = jnp.sqrt((timesteps.astype(jnp.float32) + 1.0) / TSTEPS)
    noisy = resid_two + noise_level[:, None, None] * noise_field.astype(jnp.float32).reshape(
        seqs_here, length, features
    )
    first_low = norm_silu(noisy, norm_params[4], norm_params[5], group_width).astype(jnp.bfloat16)
    embed_low = jax.nn.silu(time_embedding(timesteps, features)).astype(jnp.bfloat16)
    time_shift = jnp.dot(embed_low, full_in[3], preferred_element_type=jnp.float32)
    conv_one = conv_grid(first_low, full_in[7:16], False) + time_shift[:, None, :]
    gain_six = lax.dynamic_slice_in_dim(norm_params[6], channel_start, chans_here)
    shift_six = lax.dynamic_slice_in_dim(norm_params[7], channel_start, chans_here)
    second_low = norm_silu(conv_one, gain_six, shift_six, group_width).astype(jnp.bfloat16)
    resid_three = noisy + tensor_parallel_sum(conv_grid(second_low, full_back[2:11], False))
    normed_three_low = layer_norm(resid_three, norm_params[8], norm_params[9]).astype(jnp.bfloat16)
    cross_queries = project(normed_three_low, full_in[4]).astype(jnp.bfloat16)
    cross_keys = project(codec_tokens, full_in[5]).astype(jnp.bfloat16)
    cross_values = project(codec_tokens, full_in[6]).astype(jnp.bfloat16)
    cross_mixed, log_cross = attend(cross_queries, cross_keys, cross_values, None, score_scale)
    cross_low = cross_mixed.astype(jnp.bfloat16)
    result = resid_three + tensor_parallel_sum(project(cross_low, full_back[1]))
    out_low = result.astype(jnp.bfloat16)
    grad_out = cotangent.astype(jnp.float32).reshape(seqs_here, length, features)
    grad_cross_low = grad_out.astype(jnp.bfloat16)
    grad_w_co = weight_grad(cross_low, grad_cross_low)
    grad_cross_mixed = back_project(grad_cross_low, full_back[1]).astype(jnp.bfloat16)
    grad_cq, grad_ck, grad_cv = attend_back(
        cross_queries, cross_keys, cross_values, None, score_scale, log_cross, grad_cross_mixed
    )
    grad_w_cq = weight_grad(normed_three_low, grad_cq)
    grad_w_ck = weight_grad(codec_tokens, grad_ck)
    grad_w_cv = weight_grad(codec_tokens, grad_cv)
    grad_normed_three = tensor_parallel_sum(back_project(grad_cq, full_in[4]))
    pull_three = jax.vjp(layer_norm, resid_three, norm_params[8], norm_params[9])[1]
    grad_part, grad_gain_eight, grad_shift_eight = pull_three(grad_normed_three)
    grad_three = grad_out + grad_part
    grad_conv_low = grad_three.astype(jnp.bfloat16)
    grad_w_conv_two = conv_weight_grad(second_low, grad_conv_low)
    grad_second = conv_grid(grad_conv_low, full_back[2:11], True)
    gather_second_moment = jax.vjp(
        partial(norm_silu, group_width=group_width), conv_one, gain_six, shift_six
    )[1]
    grad_conv_one, grad_gain_six, grad_shift_six = gather_second_moment(grad_second)
    grad_conv_one_low = grad_conv_one.astype(jnp.bfloat16)
    grad_w_time = jnp.einsum(
        "sd,sc->dc",
        embed_low.astype(jnp.float32),
        jnp.sum(grad_conv_one_low.astype(jnp.float32), axis=1),
        precision=HIGHEST_PRECISION,
    )
    grad_w_conv_one = conv_weight_grad(first_low, grad_conv_one_low)
    grad_first = tensor_parallel_sum(conv_grid(grad_conv_one_low, full_in[7:16], True))
    gather_first_moment = jax.vjp(
        partial(norm_silu, group_width=group_width), noisy, norm_params[4], norm_params[5]
    )[1]
    grad_part, grad_gain_four, grad_shift_four = gather_first_moment(grad_first)
    grad_two = grad_three + grad_part
    grad_mlp_low = grad_two.astype(jnp.bfloat16)
    grad_w_down = weight_grad(hidden_low, grad_mlp_low)
    grad_hidden = back_project(grad_mlp_low, full_down)
    grad_pre_low = jax.vjp(jax.nn.gelu, hidden_pre)[1](grad_hidden)[0].astype(jnp.bfloat16)
    up_weight_gradient = weight_grad(normed_two_low, grad_pre_low)
    grad_normed_two = tensor_parallel_sum(back_project(grad_pre_low, complete_up_weight))
    pull_two = jax.vjp(layer_norm, resid_one, norm_params[2], norm_params[3])[1]
    grad_part, grad_gain_two, grad_shift_two = pull_two(grad_normed_two)
    grad_one = grad_two + grad_part
    grad_attn_low = grad_one.astype(jnp.bfloat16)
    grad_w_out = weight_grad(mixed_low, grad_attn_low)
    grad_mixed = back_project(grad_attn_low, full_back[0]).astype(jnp.bfloat16)
    grad_q, grad_k, grad_v = attend_back(
        queries, key_rows, value_rows, allowed, score_scale, log_self, grad_mixed
    )
    grad_w_q = weight_grad(normed_one_low, grad_q)
    grad_w_k = weight_grad(normed_one_low, grad_k)
    grad_w_v = weight_grad(normed_one_low, grad_v)
    grad_normed_one = tensor_parallel_sum(
        back_project(grad_q, full_in[0])
        + back_project(grad_k, full_in[1])
        + back_project(grad_v, full_in[2])
    )
    pull_one = jax.vjp(layer_norm, resid_in, norm_params[0], norm_params[1])[1]
    grad_part, grad_gain_zero, grad_shift_zero = pull_one(grad_normed_one)
    grad_input = grad_one + grad_part
    grad_in_stack = jnp.concatenate(
        [
            jnp.stack([grad_w_q, grad_w_k, grad_w_v, grad_w_time, grad_w_cq, grad_w_ck, grad_w_cv]),
            grad_w_conv_one,
        ]
    )
    grad_back_stack = jnp.concatenate([jnp.stack([grad_w_out, grad_w_co]), grad_w_conv_two])
    summed_in, summed_back, summed_up, summed_down = (
        lax.psum_scatter(grad_in_stack, "dp", scatter_dimension=1, tiled=True),
        lax.psum_scatter(grad_back_stack, "dp", scatter_dimension=2, tiled=True),
        lax.psum_scatter(up_weight_gradient, "dp", scatter_dimension=0, tiled=True),
        lax.psum_scatter(grad_w_down, "dp", scatter_dimension=1, tiled=True),
    )
    shared_rows = (
        jnp.stack(
            [
                grad_gain_zero,
                grad_shift_zero,
                grad_gain_two,
                grad_shift_two,
                grad_gain_four,
                grad_shift_four,
            ]
        )
        * lead_device
    )
    group_rows = lax.dynamic_update_slice(
        jnp.zeros((2, features), jnp.float32),
        jnp.stack([grad_gain_six, grad_shift_six]),
        (0, channel_start),
    )
    last_rows = jnp.stack([grad_gain_eight, grad_shift_eight]) * lead_device
    norm_grad = lax.psum(jnp.concatenate([shared_rows, group_rows, last_rows]), ("dp", "mp"))
    m_in_new, v_in_new, upd_in = adam_update(w_in, summed_in, m_in, v_in, WEIGHT_DECAY)
    m_back_new, v_back_new, upd_back = adam_update(
        w_back, summed_back, m_back, v_back, WEIGHT_DECAY
    )
    m_up_new, v_up_new, upd_up = adam_update(w_up, summed_up, m_up, v_up, WEIGHT_DECAY)
    m_down_new, v_down_new, upd_down = adam_update(
        w_down, summed_down, m_down, v_down, WEIGHT_DECAY
    )
    update_sq = matrix_squares(upd_in, upd_back, upd_up, upd_down)
    weight_total, update_total = lax.psum((weight_sq, update_sq), ("dp", "mp"))
    weight_len = jnp.sqrt(weight_total)
    update_len = jnp.sqrt(update_total)
    trust = weight_len / update_len
    new_in = w_in - LEARN_RATE * trust[0:16, None, None] * upd_in
    new_back = w_back - LEARN_RATE * trust[16:27, None, None] * upd_back
    new_up = w_up - LEARN_RATE * trust[27] * upd_up
    new_down = w_down - LEARN_RATE * trust[28] * upd_down
    norm_m_new, norm_v_new, upd_norm = adam_update(norm_params, norm_grad, norm_m, norm_v, 0.0)
    row_trust = jnp.sqrt(jnp.sum(norm_params * norm_params, axis=1)) / jnp.sqrt(
        jnp.sum(upd_norm * upd_norm, axis=1)
    )
    new_norm = norm_params - LEARN_RATE * row_trust[:, None] * upd_norm
    matrix_norms = jnp.stack([weight_len, update_len])
    out_rows = out_low.reshape(seqs_here * length, features)
    grad_rows = grad_input.reshape(seqs_here * length, features)
    return (
        out_rows,
        grad_rows,
        new_in,
        new_back,
        new_up,
        new_down,
        m_in_new,
        m_back_new,
        m_up_new,
        m_down_new,
        v_in_new,
        v_back_new,
        v_up_new,
        v_down_new,
        new_norm,
        norm_m_new,
        norm_v_new,
        matrix_norms,
    )


CORE_SWAP = [(i, i ^ 1) for i in range(4)]
X_SWAP = [(i, i ^ 2) for i in range(4)]
LOW = jnp.bfloat16
F32 = jnp.float32


def swap_core(v):
    return lax.ppermute(v, "mp", CORE_SWAP)


def swap_x(v):
    return lax.ppermute(v, "mp", X_SWAP)


def by_parity(flag, own, other, axis):
    first = jnp.where(flag == 0, own, other)
    second = jnp.where(flag == 0, other, own)
    return jnp.stack([first, second], axis=axis)


def pick(v, index, axis):
    return lax.dynamic_index_in_dim(v, index, axis, keepdims=False)


def ln_stats(v):
    centre = v - jnp.mean(v, axis=-1, keepdims=True)
    scale = lax.rsqrt(jnp.mean(centre * centre, axis=-1, keepdims=True) + NORM_EPS)
    return centre * scale, scale


def ln_back(v, gain, grad):
    hat, scale = ln_stats(v)
    pulled = grad * gain
    back = scale * (
        pulled
        - jnp.mean(pulled, axis=-1, keepdims=True)
        - hat * jnp.mean(pulled * hat, axis=-1, keepdims=True)
    )
    return back, jnp.sum(grad * hat, axis=0, keepdims=True), jnp.sum(grad, axis=0, keepdims=True)


def mm(a, b):
    return lax.dot_general(a, b, (((1,), (0,)), ((), ())), preferred_element_type=F32)


def mm_nt(a, b):
    return lax.dot_general(a, b, (((1,), (1,)), ((), ())), preferred_element_type=F32)


def mm_tn(a, b):
    return lax.dot_general(a, b, (((0,), (0,)), ((), ())), preferred_element_type=F32)


ANY = pl.ANY
VM = pltpu.VMEM
ROWS = 512
STEP_ROWS = 128


def spec_any():
    return pl.BlockSpec(memory_space=pl.ANY)


def spec_vm():
    return pl.BlockSpec(memory_space=pltpu.VMEM)


def run_kernel(body, name, ins, outs, scratch, hbm=(), flops=0):
    in_specs = [spec_any() if k in hbm else spec_vm() for k in range(len(ins))]
    moved = sum(v.size * v.dtype.itemsize for v in ins) + sum(
        math.prod(s) * jnp.dtype(t).itemsize for s, t in outs
    )
    return pl.pallas_call(
        body,
        name=name,
        in_specs=in_specs,
        out_specs=[spec_vm() for _ in outs],
        out_shape=[jax.ShapeDtypeStruct(s, t) for s, t in outs],
        scratch_shapes=scratch,
        compiler_params=pltpu.CompilerParams(vmem_limit_bytes=56 << 20),
        cost_estimate=pl.CostEstimate(flops=flops, bytes_accessed=moved, transcendentals=0),
    )(*ins)


def each_rows(fn, total=ROWS, step=STEP_ROWS):
    def body(k, carry):
        fn(pl.ds(pl.multiple_of(k * step, step), step))
        return carry

    lax.fori_loop(0, total // step, body, 0)


def start_copies(pairs, sems):
    copies = [pltpu.make_async_copy(a, b, sems.at[k]) for k, (a, b) in enumerate(pairs)]
    for c in copies:
        c.start()
    return copies


def group_mats(channels, width):
    count = channels // width
    r = lax.broadcasted_iota(jnp.int32, (channels, count), 0)
    c = lax.broadcasted_iota(jnp.int32, (channels, count), 1) * width
    down = ((r >= c) & (r < c + width)).astype(F32)
    r = lax.broadcasted_iota(jnp.int32, (count, channels), 1)
    c = lax.broadcasted_iota(jnp.int32, (count, channels), 0) * width
    up = ((r >= c) & (r < c + width)).astype(F32)
    return down, up


def exact_dot(a, b):
    return jnp.dot(a, b, precision=HIGHEST_PRECISION, preferred_element_type=F32)


def group_average(row, mats, width):
    wide = jnp.broadcast_to(row, (8, row.shape[1]))
    return exact_dot(exact_dot(wide, mats[0]) * (1.0 / (width * ROWS)), mats[1])[0:1]


def gelu_parts(v):
    k = math.sqrt(2.0 / math.pi)
    t = jnp.tanh(k * (v + 0.044715 * (v * v * v)))
    return t, 0.5 * v * (1.0 + t)


def gelu_slope(v, t):
    k = math.sqrt(2.0 / math.pi)
    return 0.5 * (1.0 + t) + 0.5 * v * (1.0 - t * t) * (k * (1.0 + 3 * 0.044715 * (v * v)))


def column_of(shape):
    return lax.broadcasted_iota(jnp.int32, shape, 0) % TIME


def from_left(v):
    return jnp.where(column_of(v.shape) == 0, 0.0, pltpu.roll(v, 1, 0))


def from_right(v):
    return jnp.where(column_of(v.shape) == TIME - 1, 0.0, pltpu.roll(v, v.shape[0] - 1, 0))


def softmax_heads(q, k, v, heads, score_scale, mask):
    mixed, logs = [], []
    for h in range(heads):
        s = mm_nt(q[:, HD * h : HD * (h + 1)], k[:, HD * h : HD * (h + 1)]) * score_scale
        if mask is not None:
            s = jnp.where(mask, s, MASK_VALUE)
        top = jnp.max(s, axis=1, keepdims=True)
        e = jnp.exp(s - top)
        total = jnp.sum(e, axis=1, keepdims=True)
        soft = (e * (1.0 / total)).astype(LOW)
        mixed.append(mm(soft, v[:, HD * h : HD * (h + 1)]))
        logs.append(top + jnp.log(total))
    return jnp.concatenate(mixed, axis=1).astype(LOW), logs


def softmax_heads_back(q, k, v, g, logs, heads, score_scale, mask):
    dq, dk, dv = [], [], []
    for h in range(heads):
        cols = slice(HD * h, HD * (h + 1))
        s = mm_nt(q[:, cols], k[:, cols]) * score_scale
        if mask is not None:
            s = jnp.where(mask, s, MASK_VALUE)
        soft = jnp.exp(s - logs[h])
        gs = mm_nt(g[:, cols], v[:, cols])
        dv.append(mm_tn(soft.astype(LOW), g[:, cols]))
        dot = jnp.sum(soft * gs, axis=1, keepdims=True)
        ds = (soft * (gs - dot)).astype(LOW)
        dq.append(mm(ds, k[:, cols]) * score_scale)
        dk.append(mm_tn(ds, q[:, cols]))
    return [jnp.concatenate(d, axis=1) for d in (dq, dk, dv)]


MESH_IDS = pl.DeviceIdType.MESH


def place():
    mp = lax.axis_index("mp")
    dp = lax.axis_index("dp")
    return mp // 2, mp % 2, dp // 2, dp % 2


def device(x, core, z, y):
    return (2 * z + y, 2 * x + core)


def meet(peers):
    barrier = pltpu.get_barrier_semaphore()
    for peer in peers:
        pl.semaphore_signal(barrier, inc=1, device_id=peer, device_id_type=MESH_IDS)
    pl.semaphore_wait(barrier, len(peers))


def chip_peers():
    x, core, z, y = place()
    along_z = [device(x, core, (z + k) % 4, y) for k in range(1, 4)]
    return device(1 - x, core, z, y), device(x, core, z, 1 - y), along_z


class Sender:
    def __init__(self, send, recv):
        self.send, self.recv, self.made = send, recv, []

    def start(self, src, dst, peer):
        k = len(self.made)
        copy = pltpu.make_async_remote_copy(
            src_ref=src, dst_ref=dst, send_sem=self.send.at[k], recv_sem=self.recv.at[k],
            device_id=peer, device_id_type=MESH_IDS,
        )
        copy.start()
        self.made.append(copy)
        return copy

    def close(self):
        for copy in self.made:
            copy.wait_send()


def padded_width(w):
    return -(-w // 128) * 128


def pack_piece(g, w_in, w_back, w_up, w_down, piece):
    n = w_in.shape[2]
    if g == 1:
        hid = w_up.shape[1]
        piece[:, :hid] = w_up[...].astype(LOW)
        piece[:, hid:] = w_down[...].astype(LOW)
        return
    ins, backs = GROUPS_OF[g]
    cols = [w_in[j] for j in ins] + [w_back[j].T for j in backs]
    spare = piece.shape[1] - n * len(cols)
    if spare:
        cols.append(jnp.zeros((piece.shape[0], spare), F32))
    for k in range(0, len(cols), 2):
        pair = cols[k : k + 2]
        both = pair[0] if len(pair) == 1 else jnp.concatenate(pair, axis=1)
        piece[:, n * k : n * k + both.shape[1]] = both.astype(LOW)


GROUPS_OF = {
    0: ([0, 1, 2], [0]),
    2: ([*range(7, 16), 3], []),
    3: ([], [*range(2, 11)]),
    4: ([4, 5, 6], [1]),
}


def row_of(values):
    lane = lax.broadcasted_iota(jnp.int32, (1, 128), 1)
    row = jnp.zeros((1, 128), F32)
    for j, v in enumerate(values):
        row = row + jnp.where(lane == j, v, 0.0)
    return row


def square_sum(v):
    return jnp.sum(jnp.sum(v * v, axis=1, keepdims=True), axis=0, keepdims=True)


class Gather:
    def __init__(self, pieces, outs, net):
        self.pieces, self.outs, self.net = pieces, outs, net
        self.x, self.core, self.z, self.y = place()
        self.to_x, self.to_y, self.to_z = chip_peers()
        self.lines, self.planes, self.corners = {}, {}, {}

    def line(self, g):
        self.lines[g] = [
            self.net.start(self.pieces[g], self.outs[g].at[0, self.z, self.y], peer)
            for peer in self.to_z
        ]

    def own(self, g):
        z, y, out = self.z, self.y, self.outs[g]
        self.planes[g] = [
            self.net.start(self.pieces[g], out.at[1, z, y], self.to_x),
            self.net.start(self.pieces[g], out.at[0, z, y], self.to_y),
        ]

    def spread(self, g, k):
        self.lines[g][k - 1].wait_recv()
        src = self.outs[g].at[0, (self.z - k) % 4, self.y]
        dst = self.outs[g].at[1, (self.z - k) % 4, self.y]
        self.planes[g] += [self.net.start(src, dst, self.to_x), self.net.start(src, src, self.to_y)]

    def turn(self, g):
        for c in self.planes[g]:
            c.wait_recv()
        out, y = self.outs[g], self.y
        self.corners[g] = [
            self.net.start(out.at[0, 0:2, 1 - y], out.at[1, 0:2, 1 - y], self.to_x),
            self.net.start(out.at[1, 2:4, y], out.at[1, 2:4, y], self.to_y),
        ]

    def ready(self, g):
        for c in self.corners[g]:
            c.wait_recv()

    def early(self, g):
        z, y, out = self.z, self.y, self.outs[g]
        self.first = [
            self.net.start(self.pieces[g], out.at[1, z, y], self.to_x),
            self.net.start(self.pieces[g], out.at[0, z, y], self.to_y),
        ]

    def late(self, g):
        self.first[0].wait_recv()
        src = self.outs[g].at[1, self.z, self.y]
        self.first.append(self.net.start(src, src, self.to_y))

    def far(self, g):
        self.first[1].wait_recv()
        self.first[2].wait_recv()
        block = self.outs[g].at[:, self.z]
        self.corners[g] = [self.net.start(block, block, peer) for peer in self.to_z]


def matrix_of(ref, i, first, last):
    block = ref[i, :, :, :, first:last]
    return block.reshape(-1, last - first)


def forward_body(
    w_in, w_back, w_up, w_down, seg_col, seg_row, norms, side, embed, level, tokens, noises, codecs,
    g0, g1, g2, g3, g4, sq, n1_o, qkv_o, mixed_o, logs_o, resid_o, n2_o, noisy_o, first_o, conv_o,
    taps_o, resid3_o, n3_o, cq_o, ckv_o, cross_o, logs_c_o, out_o,
    p0, p1, p2, p3, p4, v0, v1, v2, v3, v4, tok, noise, codec, n1, qkv, mixed, logs, resid, n2,
    noisy, first, conv, taps, resid3, n3, cq, ckv, cross, logs_c, out, pad, acc, sent, got,
    in_sem, out_sem, own_sem, send, recv,
):
    pieces, held, kept = (p0, p1, p2, p3, p4), (v0, v1, v2, v3, v4), (g0, g1, g2, g3, g4)
    n = mixed.shape[2]
    hid = w_up.shape[1]
    features = norms.shape[1]
    width = features // GROUPS
    heads = n // HD
    score_scale = HD ** (-0.5)
    net = Sender(send, recv)
    run = Gather(pieces, held, net)
    x, core, z, y = place()
    sibling = device(x, 1 - core, z, y)
    loads = [
        pltpu.make_async_copy(tokens.at[pl.ds(pl.multiple_of(x * ROWS, ROWS), ROWS), :], tok, in_sem.at[0]),
        pltpu.make_async_copy(noises.at[pl.ds(pl.multiple_of(x * ROWS, ROWS), ROWS), :], noise, in_sem.at[1]),
        pltpu.make_async_copy(codecs.at[x], codec, in_sem.at[2]),
    ]
    for c in loads:
        c.start()
    stores = []

    def store(src, dst):
        copy = pltpu.make_async_copy(src, dst, out_sem.at[len(stores)])
        copy.start()
        stores.append(copy)

    def pack(g):
        pack_piece(g, w_in, w_back, w_up, w_down, pieces[g])
        copy = pltpu.make_async_copy(pieces[g], held[g].at[0, z, y], own_sem.at[g])
        copy.start()
        return copy

    def exchange(k, total):
        sent[k] = total.astype(LOW)
        return net.start(sent.at[k], got.at[k], sibling)

    def joined(k, r):
        return sent[k, r, :].astype(F32) + got[k, r, :].astype(F32)

    local = [pack(0)]
    meet([run.to_x, run.to_y, *run.to_z, sibling])
    run.line(0)
    run.own(0)
    local.append(pack(1))
    run.own(1)
    local += [pack(2), pack(3), pack(4)]
    run.early(4)
    loads[0].wait()

    def norm_one(r):
        hat, _ = ln_stats(tok[r, :].astype(F32))
        n1[r, :] = (hat * norms[0:1, :] + norms[1:2, :]).astype(LOW)

    each_rows(norm_one)
    store(n1, n1_o)
    run.spread(0, 1)
    run.line(1)
    run.spread(0, 2)
    run.spread(0, 3)
    run.own(2)
    sq[...] = row_of(
        [square_sum(w_in[j]) for j in range(16)] + [square_sum(w_back[j]) for j in range(11)]
        + [square_sum(w_up[...]), square_sum(w_down[...])]
    )
    run.turn(0)
    run.late(4)
    local[0].wait()
    run.ready(0)
    store(v0, g0)
    for i in range(2):
        qkv[i] = mm(n1[...], matrix_of(v0, i, 0, 3 * n)).astype(LOW)
    store(qkv, qkv_o)
    run.spread(1, 1)
    run.line(2)
    run.spread(1, 2)
    run.spread(1, 3)
    run.own(3)

    def self_heads(r):
        mask = seg_col[r, :] == seg_row[...]
        found = []
        for i in range(2):
            part, logs_i = softmax_heads(
                qkv[i, r, 0:n], qkv[i, :, n : 2 * n], qkv[i, :, 2 * n : 3 * n], heads, score_scale, mask
            )
            mixed[i, r, :] = part
            found += logs_i
        logs[r, :] = jnp.concatenate(found, axis=1)

    each_rows(self_heads)
    swap = exchange(
        0,
        mm_nt(mixed[0], matrix_of(v0, 0, 3 * n, 4 * n)) + mm_nt(mixed[1], matrix_of(v0, 1, 3 * n, 4 * n)),
    )
    store(mixed, mixed_o)
    store(logs, logs_o)
    run.turn(1)
    swap.wait_recv()

    def norm_two(r):
        v = tok[r, :].astype(F32) + joined(0, r)
        resid[r, :] = v
        hat, _ = ln_stats(v)
        n2[r, :] = (hat * norms[2:3, :] + norms[3:4, :]).astype(LOW)

    each_rows(norm_two)
    store(resid, resid_o)
    store(n2, n2_o)
    run.spread(2, 1)
    run.line(3)
    run.spread(2, 2)
    run.spread(2, 3)
    local[1].wait()
    run.ready(1)
    store(v1, g1)
    block = 256
    for i in range(2):
        for b in range(hid // block):
            pre = mm(n2[...], matrix_of(v1, i, block * b, block * (b + 1)))
            low = gelu_parts(pre)[1].astype(LOW)
            term = mm_nt(low, matrix_of(v1, i, hid + block * b, hid + block * (b + 1)))
            if i == 0 and b == 0:
                acc[...] = term
            else:
                acc[...] += term
    swap = exchange(1, acc[...])
    run.turn(2)
    loads[1].wait()
    swap.wait_recv()

    def add_noise(r):
        noisy[r, :] = resid[r, :] + joined(1, r) + level[...] * noise[r, :].astype(F32)

    each_rows(add_noise)
    store(noisy, noisy_o)
    mats = group_mats(features, width)
    mats_n = group_mats(n, width)
    mean = group_average(jnp.sum(noisy[...], axis=0, keepdims=True), mats, width)
    centre = noisy[...] - mean
    var = group_average(jnp.sum(centre * centre, axis=0, keepdims=True), mats, width)
    scale = lax.rsqrt(var + NORM_EPS) * norms[4:5, :]
    pad[0:TIME, :] = jnp.zeros((TIME, features), LOW)
    pad[TIME + ROWS :, :] = jnp.zeros((TIME, features), LOW)

    def act(r):
        v = (noisy[r, :] - mean) * scale + norms[5:6, :]
        first[r, :] = (v * jax.nn.sigmoid(v)).astype(LOW)

    each_rows(act)
    pad[TIME : TIME + ROWS, :] = first[...]
    store(first, first_o)
    run.spread(3, 1)
    run.spread(3, 2)
    run.spread(3, 3)
    local[4].wait()
    run.far(4)
    local[2].wait()
    run.ready(2)
    store(v2, g2)
    for i in range(2):
        q = None
        for a in range(3):
            term = mm(
                pad[TIME * a : TIME * a + ROWS, :], matrix_of(v2, i, 3 * n * a, 3 * n * (a + 1))
            )
            q = term if q is None else q + term
        shift = mm(embed[...], matrix_of(v2, i, 9 * n, 10 * n))[0:1]
        c1 = from_left(q[:, :n]) + q[:, n : 2 * n] + from_right(q[:, 2 * n :]) + shift
        conv[i] = c1
        c1 = c1 - group_average(jnp.sum(c1, axis=0, keepdims=True), mats_n, width)
        var_n = group_average(jnp.sum(c1 * c1, axis=0, keepdims=True), mats_n, width)
        v = c1 * lax.rsqrt(var_n + NORM_EPS) * side[i, 0:1, :] + side[i, 1:2, :]
        v = v * jax.nn.sigmoid(v)
        taps[i, 0:TIME, :] = jnp.zeros((TIME, 3 * n), LOW)
        taps[i, TIME + ROWS :, :] = jnp.zeros((TIME, 3 * n), LOW)
        taps[i, TIME : TIME + ROWS, :] = jnp.concatenate(
            [from_left(v), v, from_right(v)], axis=1
        ).astype(LOW)
    store(conv, conv_o)
    store(taps, taps_o)
    run.turn(3)
    local[3].wait()
    run.ready(3)
    store(v3, g3)
    total = None
    for i in range(2):
        for a in range(3):
            term = mm_nt(
                taps[i, TIME * a : TIME * a + ROWS, :], matrix_of(v3, i, 3 * n * a, 3 * n * (a + 1))
            )
            total = term if total is None else total + term
    swap = exchange(2, total)
    loads[2].wait()
    run.ready(4)
    store(v4, g4)
    for i in range(2):
        ckv[i] = mm(codec[...], matrix_of(v4, i, n, 3 * n)).astype(LOW)
    store(ckv, ckv_o)
    swap.wait_recv()

    def norm_three(r):
        v = noisy[r, :] + joined(2, r)
        resid3[r, :] = v
        hat, _ = ln_stats(v)
        n3[r, :] = (hat * norms[8:9, :] + norms[9:10, :]).astype(LOW)

    each_rows(norm_three)
    store(resid3, resid3_o)
    store(n3, n3_o)
    for i in range(2):
        cq[i] = mm(n3[...], matrix_of(v4, i, 0, n)).astype(LOW)
    store(cq, cq_o)

    def cross_heads(r):
        found = []
        for i in range(2):
            part, logs_i = softmax_heads(
                cq[i, r, :], ckv[i, :, :n], ckv[i, :, n:], heads, score_scale, None
            )
            cross[i, r, :] = part
            found += logs_i
        logs_c[r, :] = jnp.concatenate(found, axis=1)

    each_rows(cross_heads)
    swap = exchange(
        3,
        mm_nt(cross[0], matrix_of(v4, 0, 3 * n, 4 * n)) + mm_nt(cross[1], matrix_of(v4, 1, 3 * n, 4 * n)),
    )
    store(cross, cross_o)
    store(logs_c, logs_c_o)
    swap.wait_recv()

    def finish_rows(r):
        out[r, :] = (resid3[r, :] + joined(3, r)).astype(LOW)

    each_rows(finish_rows)
    store(out, out_o)
    for c in stores:
        c.wait()
    net.close()


def forward_all(w_in, w_back, w_up, w_down, seg_col, seg_row, norms, side, embed, level, tokens, noises, codecs):
    n, hid = w_in.shape[2], w_up.shape[1]
    rows, features = w_in.shape[1], norms.shape[1]
    heads = 2 * n // HD
    ctok = codecs.shape[1]
    widths = [4 * n, 2 * hid, 10 * n, padded_width(9 * n), 4 * n]
    full = (ROWS, features)
    tall = ROWS + 2 * TIME
    kept = [
        (full, LOW), ((2, ROWS, 3 * n), LOW), ((2, ROWS, n), LOW), ((ROWS, heads), F32), (full, F32),
        (full, LOW), (full, F32), (full, LOW), ((2, ROWS, n), F32), ((2, tall, 3 * n), LOW),
        (full, F32), (full, LOW), ((2, ROWS, n), LOW), ((2, ctok, 2 * n), LOW), ((2, ROWS, n), LOW),
        ((ROWS, heads), F32), (full, LOW),
    ]
    groups = [(2, 4, 2, rows, w) for w in widths]
    dma = pltpu.SemaphoreType.DMA
    copies = 4 * 13 + 6 + 4
    res = pl.pallas_call(
        forward_body,
        name="forward",
        in_specs=[spec_vm() for _ in range(10)] + [spec_any() for _ in range(3)],
        out_specs=[spec_any() for _ in groups] + [spec_vm()] + [spec_any() for _ in kept],
        out_shape=[jax.ShapeDtypeStruct(s, LOW) for s in groups]
        + [jax.ShapeDtypeStruct((1, 128), F32)]
        + [jax.ShapeDtypeStruct(s, t) for s, t in kept],
        scratch_shapes=[
            *[VM((rows, w), LOW) for w in widths], *[VM(s, LOW) for s in groups],
            VM(full, LOW), VM(full, LOW), VM((ctok, features), LOW), *[VM(s, t) for s, t in kept],
            VM((tall, features), LOW), VM(full, F32), VM((4, *full), LOW), VM((4, *full), LOW),
            dma((3,)), dma((22,)), dma((5,)), dma((copies,)), dma((copies,)),
        ],
        compiler_params=pltpu.CompilerParams(
            collective_id=0, has_side_effects=True, vmem_limit_bytes=62 << 20
        ),
    )(w_in, w_back, w_up, w_down, seg_col, seg_row, norms, side, embed, level, tokens, noises, codecs)
    return res[:5], res[5], res[6:]


def add_rows(target, terms, step=16):
    def body(k, carry):
        r = pl.ds(pl.multiple_of(k * step, step), step)
        total = terms[0][r, :].astype(F32)
        for t in terms[1:]:
            total = total + t[r, :].astype(F32)
        target[r, :] = total.astype(target.dtype)
        return carry

    lax.fori_loop(0, target.shape[0] // step, body, 0)


class Scatter:
    def __init__(self, net, d, bufs, free=None):
        self.net, self.d, self.free = net, d, free
        self.cx, self.cy, self.lx, self.ly, self.zb = bufs
        self.x, self.core, self.z, self.y = place()
        self.to_x, self.to_y, self.to_z = chip_peers()

    def raw(self):
        if self.free is not None:
            for k in range(2):
                pl.semaphore_wait(self.free.at[k], 1)
        d, y, start = self.d, self.y, self.net.start
        self.first = (
            start(d.at[1, 0:2, 1 - y], self.cx, self.to_x),
            start(d.at[1, 2:4, 1 - y], self.cy, self.to_y),
            start(d.at[1, 0:2, y], self.lx.at[0:2], self.to_x),
            start(d.at[0, 2:4, 1 - y], self.ly.at[2:4], self.to_y),
        )

    def corners(self):
        d, y, start = self.d, self.y, self.net.start
        self.first[0].wait_recv()
        for k in range(2):
            add_rows(self.cx.at[k], [self.cx.at[k], d.at[0, k, 1 - y]])
        to_line = start(self.cx, self.ly.at[0:2], self.to_y)
        self.first[1].wait_recv()
        for k in range(2):
            add_rows(self.cy.at[k], [self.cy.at[k], d.at[1, 2 + k, y]])
        self.second = (to_line, start(self.cy, self.lx.at[2:4], self.to_x))

    def lines(self, credit=None):
        d, y, z = self.d, self.y, self.z
        for c in (self.first[2], self.first[3], *self.second):
            c.wait_recv()
        for k in range(4):
            add_rows(d.at[0, k, y], [d.at[0, k, y], self.lx.at[k], self.ly.at[k]])
        if credit is not None:
            for c in self.second:
                c.wait_send()
            for k, peer in enumerate((self.to_x, self.to_y)):
                pl.semaphore_signal(credit.at[k], inc=1, device_id=peer, device_id_type=MESH_IDS)
        if self.free is not None:
            for k in range(3):
                pl.semaphore_wait(self.free.at[2 + k], 1)
        self.ends = [
            self.net.start(d.at[0, (z + k) % 4, y], self.zb.at[k - 1], self.to_z[k - 1])
            for k in range(1, 4)
        ]

    def finish(self, target, credit=None):
        for c in self.ends:
            c.wait_recv()
        add_rows(target, [self.d.at[0, self.z, self.y], *(self.zb.at[k] for k in range(3))])
        if credit is not None:
            for k in range(1, 4):
                pl.semaphore_signal(
                    credit.at[2 + (4 - k) - 1], inc=1, device_id=self.to_z[k - 1], device_id_type=MESH_IDS
                )


def backward_body(
    seg_col, seg_row, norms, side, embed_col, tokens, cots, codecs,
    g0, g1, g2, g3, g4, n1_h, qkv_h, mixed_h, logs_h, resid_h, n2_h, noisy_h, first_h, conv_h, taps_h,
    resid3_h, n3_h, cq_h, ckv_h, cross_h, logs_c_h, out_h,
    s0, s1, s2, s3, s4, grad_x, other_x, other_out, rows,
    d_a, d_t, d_o, d_m, wv, cot, codec, cq, ckv, cross, gm, dq, logs, resid, nrm, grad, pad, taps, tapsg,
    conv, hb, acc, sent, got, cx_p, cy_p, lx_p, ly_p, zb_p, cx_q, cy_q, lx_q, ly_q, zb_q,
    far_buf, mid_buf, side_buf, stage, gsum, load_sem, out_sem, send, recv, free_p, free_q,
):
    n = cq.shape[2]
    features = norms.shape[1]
    width = features // GROUPS
    heads = n // HD
    hid = d_m.shape[4] // 2
    ctok = codec.shape[0]
    score_scale = HD ** (-0.5)
    x, core, z, y = place()
    to_x, to_y, to_z = chip_peers()
    sibling = device(x, 1 - core, z, y)
    net = Sender(send, recv)
    loads = []

    def load(src, dst):
        copy = pltpu.make_async_copy(src, dst, load_sem.at[len(loads)])
        copy.start()
        loads.append(copy)
        return copy

    def weights(ref, i):
        w = ref.shape[2]
        return load(ref.at[i], wv.at[i, :, pl.ds(0, w)])

    own = pl.ds(pl.multiple_of(x * ROWS, ROWS), ROWS)
    half = pl.ds(pl.multiple_of(core * (ROWS // 2), ROWS // 2), ROWS // 2)
    ready = [
        load(cots.at[own, :], cot), load(cross_h, cross), load(g4.at[0], wv.at[0, :, pl.ds(0, 4 * n)]),
        load(g4.at[1], wv.at[1, :, pl.ds(0, 4 * n)]), load(cq_h, cq), load(ckv_h, ckv),
        load(logs_c_h, logs), load(n3_h, nrm), load(codecs.at[x], codec),
    ]
    later = [load(resid3_h, resid), load(taps_h, taps), load(conv_h, conv)]
    meet([to_x, to_y, *to_z, sibling])
    out_far = net.start(out_h.at[half, :], other_out.at[half, :], to_x)
    sends = {}

    def exchange(k, total):
        if k >= 2:
            sends[k - 2].wait_send()
        sent[k % 2] = total.astype(LOW)
        sends[k] = net.start(sent.at[k % 2], got.at[k % 2], sibling)

    def joined(k, r):
        return sent[k % 2, r, :].astype(F32) + got[k % 2, r, :].astype(F32)

    def put(ref, i, first, value):
        w = value.shape[1]
        ref[i, :, :, :, first : first + w] = value.astype(LOW).reshape(4, 2, -1, w)

    rows[...] = jnp.zeros(rows.shape, F32)
    for c in ready:
        c.wait()
    for i in (1, 0):
        put(d_a, i, 3 * n, mm_tn(cot[...], cross[i]))
        gm[i] = mm(cot[...], wv[i, :, 3 * n : 4 * n]).astype(LOW)
    acc_kv = acc.at[0:ctok, :]
    acc_kv[...] = jnp.zeros((ctok, 4 * n), F32)

    def cross_heads(r):
        for i in range(2):
            rows_logs = [logs[r, heads * i + h : heads * i + h + 1] for h in range(heads)]
            gq, gk, gv = softmax_heads_back(
                cq[i, r, :], ckv[i, :, :n], ckv[i, :, n:], gm[i, r, :], rows_logs, heads, score_scale, None
            )
            dq[i, r, :] = gq.astype(LOW)
            acc_kv[:, 2 * n * i : 2 * n * (i + 1)] += jnp.concatenate([gk, gv], axis=1)

    each_rows(cross_heads)
    total = None
    for i in (1, 0):
        both = acc_kv[:, 2 * n * i : 2 * n * (i + 1)]
        low = jnp.concatenate([both[:, :n] * score_scale, both[:, n:]], axis=1).astype(LOW)
        put(d_a, i, 0, mm_tn(nrm[...], dq[i]))
        put(d_a, i, n, mm_tn(codec[...], low))
        term = mm_nt(dq[i], wv[i, :, :n])
        total = term if total is None else total + term
    exchange(0, total)
    far = [net.start(d_a.at[:, (z + k) % 4], far_buf.at[k - 1], to_z[k - 1]) for k in range(1, 4)]
    two_w = [weights(g3, i) for i in range(2)]
    first_load = load(first_h, nrm)
    pad[0:TIME, :] = jnp.zeros((TIME, features), LOW)
    pad[TIME + ROWS :, :] = jnp.zeros((TIME, features), LOW)
    low_grad = pad.at[TIME : TIME + ROWS, :]
    for c in later:
        c.wait()
    out_far.wait_recv()
    out_near = net.start(other_out.at[half, :], other_out.at[half, :], sibling)
    sends[0].wait_recv()

    def pull_three(r):
        back, gain, shift = ln_back(resid[r, :], norms[8:9, :], joined(0, r))
        v = cot[r, :].astype(F32) + back
        grad[r, :] = v
        low_grad[r, :] = v.astype(LOW)
        rows[8:9, :] += gain
        rows[9:10, :] += shift

    each_rows(pull_three)
    tok_load = load(tokens.at[own, :], cot)
    noisy_load = load(noisy_h, resid)
    two = Scatter(net, d_t, (cx_p, cy_p, lx_p, ly_p, zb_p))
    for i in (1, 0):
        for a in range(3):
            put(d_t, i, 3 * n * a, mm_tn(low_grad[...], taps[i, TIME * a : TIME * a + ROWS, :]))
    d_t[:, :, :, :, 9 * n :] = jnp.zeros((*d_t.shape[:4], d_t.shape[4] - 9 * n), LOW)
    two.raw()
    mats_n = group_mats(n, width)
    gn_rows = []
    one_w = []
    for i in range(2):
        two_w[i].wait()
        q = None
        for a in range(3):
            term = mm(
                pad[TIME * (2 - a) : TIME * (2 - a) + ROWS, :], wv[i, :, 3 * n * a : 3 * n * (a + 1)]
            )
            q = term if q is None else q + term
        one_w.append(weights(g2, i))
        g = from_right(q[:, :n]) + q[:, n : 2 * n] + from_left(q[:, 2 * n :])
        c1 = conv[i]
        c1 = c1 - group_average(jnp.sum(c1, axis=0, keepdims=True), mats_n, width)
        var_n = group_average(jnp.sum(c1 * c1, axis=0, keepdims=True), mats_n, width)
        scale = lax.rsqrt(var_n + NORM_EPS)
        hat = c1 * scale
        gain = side[i, 0:1, :]
        pre = hat * gain + side[i, 1:2, :]
        gate = jax.nn.sigmoid(pre)
        g = g * gate * (1.0 + pre * (1.0 - gate))
        d_gain = jnp.sum(g * hat, axis=0, keepdims=True)
        d_shift = jnp.sum(g, axis=0, keepdims=True)
        gn_rows.append(jnp.concatenate([d_gain, d_shift], axis=0))
        back = scale * (
            g * gain
            - group_average(d_shift * gain, mats_n, width)
            - hat * group_average(d_gain * gain, mats_n, width)
        )
        back = back.astype(LOW).astype(F32)
        gsum[i : i + 1, :] = jnp.sum(back, axis=0, keepdims=True)
        tapsg[i, 0:TIME, :] = jnp.zeros((TIME, 3 * n), LOW)
        tapsg[i, TIME + ROWS :, :] = jnp.zeros((TIME, 3 * n), LOW)
        tapsg[i, TIME : TIME + ROWS, :] = jnp.concatenate(
            [from_right(back), back, from_left(back)], axis=1
        ).astype(LOW)
    blocks = []
    for s in range(4):
        block = jnp.zeros((2, n), F32)
        for i in range(2):
            here = (2 * jnp.bitwise_xor(x, i) + core) == s
            block = block + jnp.where(here, gn_rows[i], 0.0)
        blocks.append(block)
    rows[6:8, :] = jnp.concatenate(blocks, axis=1)

    one = Scatter(net, d_o, (cx_q, cy_q, lx_q, ly_q, zb_q))
    first_load.wait()
    for i in (1, 0):
        for a in range(3):
            put(
                d_o, i, 3 * n * a,
                mm_tn(nrm[...], tapsg[i, TIME * (2 - a) : TIME * (2 - a) + ROWS, :]),
            )
        put(d_o, i, 9 * n, embed_col[...] * gsum[i : i + 1, :])
    one.raw()
    n2_load = load(n2_h, nrm)
    total = None
    mlp_w = []
    for i in range(2):
        one_w[i].wait()
        for a in range(3):
            term = mm_nt(
                tapsg[i, TIME * (2 - a) : TIME * (2 - a) + ROWS, :], wv[i, :, 3 * n * a : 3 * n * (a + 1)]
            )
            total = term if total is None else total + term
    exchange(1, total)
    mlp_w = [weights(g1, i) for i in range(2)]

    noisy_load.wait()
    mats = group_mats(features, width)
    mean = group_average(jnp.sum(resid[...], axis=0, keepdims=True), mats, width)
    centre = resid[...] - mean
    var = group_average(jnp.sum(centre * centre, axis=0, keepdims=True), mats, width)
    scale = lax.rsqrt(var + NORM_EPS)
    gain, shift = norms[4:5, :], norms[5:6, :]
    sends[1].wait_recv()

    def through_silu(r):
        hat = (resid[r, :] - mean) * scale
        pre = hat * gain + shift
        gate = jax.nn.sigmoid(pre)
        g = joined(1, r)
        g = g * gate * (1.0 + pre * (1.0 - gate))
        acc[r, :] = g
        rows[4:5, :] += jnp.sum(g * hat, axis=0, keepdims=True)
        rows[5:6, :] += jnp.sum(g, axis=0, keepdims=True)

    each_rows(through_silu)
    mean_shift = group_average(rows[5:6, :] * gain, mats, width)
    mean_gain = group_average(rows[4:5, :] * gain, mats, width)

    def pull_two(r):
        hat = (resid[r, :] - mean) * scale
        v = grad[r, :] + scale * (acc[r, :] * gain - mean_shift - hat * mean_gain)
        grad[r, :] = v
        low_grad[r, :] = v.astype(LOW)

    each_rows(pull_two)
    resid_load = load(resid_h, resid)
    two.corners()
    n2_load.wait()
    block = 256
    started = False
    for i in (1, 0):
        mlp_w[i].wait()
        for b in range(hid // block):
            up, down = block * b, hid + block * b
            pre = mm(nrm[...], wv[i, :, up : up + block])
            t, hidden = gelu_parts(pre)
            slope = gelu_slope(pre, t)
            put(d_m, i, down, mm_tn(low_grad[...], hidden.astype(LOW)))
            hb[...] = (mm(low_grad[...], wv[i, :, down : down + block]) * slope).astype(LOW)
            put(d_m, i, up, mm_tn(nrm[...], hb[...]))
            term = mm_nt(hb[...], wv[i, :, up : up + block])
            if started:
                acc[...] += term
            else:
                acc[...] = term
                started = True
    exchange(2, acc[...])
    attn_w = [weights(g0, i) for i in range(2)]
    tail_loads = [
        load(n1_h, nrm), load(qkv_h, tapsg.at[:, pl.ds(0, ROWS), :]), load(mixed_h, cross), load(logs_h, logs),
    ]
    for c in far:
        c.wait_recv()
    for i in range(2):
        for j in range(2):
            add_rows(mid_buf.at[i, j], [d_a.at[i, z, j], *(far_buf.at[k, i, j] for k in range(3))])
    halves = net.start(mid_buf.at[:, 1 - y], side_buf.at[0:2], to_y)
    resid_load.wait()
    sends[2].wait_recv()

    def pull_one(r):
        back, g_gain, g_shift = ln_back(resid[r, :], norms[2:3, :], joined(2, r))
        v = grad[r, :] + back
        grad[r, :] = v
        low_grad[r, :] = v.astype(LOW)
        rows[2:3, :] += g_gain
        rows[3:4, :] += g_shift

    each_rows(pull_one)
    two.lines(free_p)
    mlp = Scatter(
        net, d_m, (cx_p.at[:, :, pl.ds(0, 2 * hid)], cy_p.at[:, :, pl.ds(0, 2 * hid)],
                   lx_p.at[:, :, pl.ds(0, 2 * hid)], ly_p.at[:, :, pl.ds(0, 2 * hid)],
                   zb_p.at[:, :, pl.ds(0, 2 * hid)]), free_p,
    )
    mlp.raw()
    for c in (*attn_w, *tail_loads):
        c.wait()
    for i in range(2):
        gm[i] = mm(low_grad[...], wv[i, :, 3 * n : 4 * n]).astype(LOW)
    acc[...] = jnp.zeros(acc.shape, F32)

    def self_heads(r):
        mask = seg_col[r, :] == seg_row[...]
        for i in range(2):
            rows_logs = [logs[r, heads * i + h : heads * i + h + 1] for h in range(heads)]
            gq, gk, gv = softmax_heads_back(
                tapsg[i, r, :n], tapsg[i, 0:ROWS, n : 2 * n], tapsg[i, 0:ROWS, 2 * n :], gm[i, r, :],
                rows_logs, heads, score_scale, mask,
            )
            taps[i, r, :n] = gq.astype(LOW)
            acc[:, 2 * n * i : 2 * n * (i + 1)] += jnp.concatenate([gk, gv], axis=1)

    each_rows(self_heads)
    one.corners()
    for c in far:
        c.wait_send()
    attn = Scatter(
        net, d_a, (cx_q.at[:, :, pl.ds(0, 4 * n)], cy_q.at[:, :, pl.ds(0, 4 * n)],
                   lx_q.at[:, :, pl.ds(0, 4 * n)], ly_q.at[:, :, pl.ds(0, 4 * n)],
                   zb_q.at[:, :, pl.ds(0, 4 * n)]), free_q,
    )
    total = None
    for i in (1, 0):
        both = acc[:, 2 * n * i : 2 * n * (i + 1)]
        taps[i, 0:ROWS, n:] = jnp.concatenate([both[:, :n] * score_scale, both[:, n:]], axis=1).astype(LOW)
        put(d_a, i, 3 * n, mm_tn(low_grad[...], cross[i]))
        put(d_a, i, 0, mm_tn(nrm[...], taps[i, 0:ROWS, :]))
        term = mm_nt(taps[i, 0:ROWS, :], wv[i, :, : 3 * n])
        total = term if total is None else total + term
    exchange(3, total)
    halves.wait_recv()
    for i in (1, 0):
        add_rows(mid_buf.at[i, y], [mid_buf.at[i, y], side_buf.at[i]])
    last = net.start(mid_buf.at[1, y], side_buf.at[2], to_x)
    tok_load.wait()
    sends[3].wait_recv()

    def pull_zero(r):
        back, g_gain, g_shift = ln_back(cot[r, :].astype(F32), norms[0:1, :], joined(3, r))
        low_grad[r, :] = (grad[r, :] + back).astype(LOW)
        rows[0:1, :] += g_gain
        rows[1:2, :] += g_shift

    each_rows(pull_zero)
    store_x = pltpu.make_async_copy(low_grad, grad_x, out_sem.at[5])
    store_x.start()
    middle = pl.ds(pl.multiple_of(TIME + core * (ROWS // 2), TIME), ROWS // 2)
    x_far = net.start(pad.at[middle, :], other_x.at[half, :], to_x)
    rows[0:6, :] = jnp.where(core == 0, rows[0:6, :], 0.0)
    rows[8:10, :] = jnp.where(core == 0, rows[8:10, :], 0.0)

    def deliver(group, k, out, credit=None):
        w = out.shape[1]
        part = stage.at[:, pl.ds(0, w)]
        group.finish(part, credit)
        copy = pltpu.make_async_copy(part, out, out_sem.at[k])
        copy.start()
        return copy

    out_two = deliver(two, 0, s3, free_p)
    one.lines(free_q)
    attn.raw()
    x_far.wait_recv()
    x_near = net.start(other_x.at[half, :], other_x.at[half, :], sibling)
    mlp.corners()
    last.wait_recv()
    out_two.wait()
    part = stage.at[:, pl.ds(0, 4 * n)]
    add_rows(part, [mid_buf.at[0, y], side_buf.at[2]])
    out_cross = pltpu.make_async_copy(part, s4, out_sem.at[1])
    out_cross.start()
    out_cross.wait()
    out_one = deliver(one, 2, s2, free_q)
    mlp.lines()
    attn.corners()
    attn.lines()
    out_one.wait()
    out_mlp = deliver(mlp, 3, s1)
    out_mlp.wait()
    out_attn = deliver(attn, 4, s0)
    out_attn.wait()
    out_near.wait_recv()
    x_near.wait_recv()
    store_x.wait()
    wait_sends(net, [*far, sends[0], sends[1], *two.second, *one.second])


def wait_sends(net, done):
    for copy in net.made:
        if all(copy is not d for d in done):
            copy.wait_send()


def backward_all(seg_col, seg_row, norms, side, embed_col, tokens, cots, codecs, gathered, kept):
    features = norms.shape[1]
    n = side.shape[2]
    rows = gathered[0].shape[3]
    widths = [g.shape[4] for g in gathered]
    hid = widths[1] // 2
    heads = 2 * n // HD
    ctok = codecs.shape[1]
    full = (ROWS, features)
    tall = ROWS + 2 * TIME
    ins = [
        seg_col, seg_row, norms, side, embed_col, tokens, cots, codecs,
        *[g.reshape(2, features, -1) for g in gathered], *kept,
    ]
    dma = pltpu.SemaphoreType.DMA
    regular = pltpu.SemaphoreType.REGULAR

    def receive(w):
        return [VM((k, rows, w), LOW) for k in (2, 2, 4, 4, 3)]

    copies = 2 + 4 + 2 + 3 + 1 + 1 + 4 * 9
    res = pl.pallas_call(
        backward_body,
        name="backward",
        in_specs=[spec_vm() for _ in range(5)] + [spec_any() for _ in ins[5:]],
        out_specs=[spec_any() for _ in range(8)] + [spec_vm()],
        out_shape=[jax.ShapeDtypeStruct((rows, w), F32) for w in widths]
        + [jax.ShapeDtypeStruct(full, LOW)] * 3
        + [jax.ShapeDtypeStruct((10, features), F32)],
        scratch_shapes=[
            VM((2, 4, 2, rows, 4 * n), LOW), VM((2, 4, 2, rows, widths[3]), LOW),
            VM((2, 4, 2, rows, 10 * n), LOW), VM((2, 4, 2, rows, 2 * hid), LOW),
            VM((2, features, 10 * n), LOW), VM(full, LOW), VM((ctok, features), LOW),
            VM((2, ROWS, n), LOW), VM((2, ctok, 2 * n), LOW), VM((2, ROWS, n), LOW), VM((2, ROWS, n), LOW),
            VM((2, ROWS, n), LOW), VM((ROWS, heads), F32), VM(full, F32), VM(full, LOW), VM(full, F32),
            VM((tall, features), LOW), VM((2, tall, 3 * n), LOW), VM((2, tall, 3 * n), LOW),
            VM((2, ROWS, n), F32), VM((ROWS, 256), LOW), VM(full, F32), VM((2, *full), LOW), VM((2, *full), LOW),
            *receive(widths[3]), *receive(10 * n),
            VM((3, 2, 2, rows, 4 * n), LOW), VM((2, 2, rows, 4 * n), LOW), VM((3, rows, 4 * n), LOW),
            VM((rows, 10 * n), F32), VM((2, n), F32),
            dma((30,)), dma((6,)), dma((copies,)), dma((copies,)), regular((5,)), regular((5,)),
        ],
        compiler_params=pltpu.CompilerParams(
            collective_id=1, has_side_effects=True, vmem_limit_bytes=64 << 20
        ),
    )(*ins)
    return res[:5], res[5], res[6], res[7], res[8]


def adam_rows(w, g, m, v, decay_rate):
    m_new = MOMENT_DECAY * m + (1.0 - MOMENT_DECAY) * g
    v_new = MOMENT_DECAY * v + (1.0 - MOMENT_DECAY) * g * g
    correct = 1.0 - MOMENT_DECAY**STEP
    update = m_new / correct / (jnp.sqrt(v_new / correct) + ADAM_EPS) + decay_rate * w
    return m_new, v_new, update


def moments_body(*refs):
    sums, refs = refs[:5], refs[5:]
    w_in, w_back, w_up, w_down, m_in, m_back, m_up, m_down, v_in, v_back, v_up, v_down = refs[:12]
    nm_in, nm_back, nm_up, nm_down, nv_in, nv_back, nv_up, nv_down = refs[12:20]
    u_in, u_back, u_up, u_down, usq = refs[20:]
    n = w_in.shape[2]
    squares = [None] * 29

    def place_in(j, g):
        m, v, u = adam_rows(w_in[j], g, m_in[j], v_in[j], WEIGHT_DECAY)
        nm_in[j], nv_in[j], u_in[j] = m, v, u
        squares[j] = square_sum(u)

    def place_back(j, g):
        m, v, u = adam_rows(w_back[j], g.T, m_back[j], v_back[j], WEIGHT_DECAY)
        nm_back[j], nv_back[j], u_back[j] = m, v, u
        squares[16 + j] = square_sum(u)

    for g, (ins, backs) in GROUPS_OF.items():
        for k, j in enumerate(ins):
            place_in(j, sums[g][:, n * k : n * (k + 1)])
        for k, j in enumerate(backs, len(ins)):
            place_back(j, sums[g][:, n * k : n * (k + 1)])
    hid = w_up.shape[1]
    m, v, u = adam_rows(w_up[...], sums[1][:, :hid], m_up[...], v_up[...], WEIGHT_DECAY)
    nm_up[...], nv_up[...], u_up[...] = m, v, u
    squares[27] = square_sum(u)
    m, v, u = adam_rows(w_down[...], sums[1][:, hid:], m_down[...], v_down[...], WEIGHT_DECAY)
    nm_down[...], nv_down[...], u_down[...] = m, v, u
    squares[28] = square_sum(u)
    usq[...] = row_of(squares)


def totals_body(rows, sq, usq, out, ring, ring_b, send, recv):
    mp, dp = lax.axis_index("mp"), lax.axis_index("dp")
    dp_peers = [((dp + k) % 8, mp) for k in range(1, 8)]
    mp_peers = [(dp, (mp + k) % 4) for k in range(1, 4)]
    ring[dp] = jnp.zeros(ring.shape[1:], F32)
    ring[dp, 0:10, :] = rows[...]
    ring[dp, 10:11, 0:128] = sq[...]
    ring[dp, 11:12, 0:128] = usq[...]
    meet(dp_peers + mp_peers)
    net = Sender(send, recv)
    copies = [net.start(ring.at[dp], ring.at[dp], p) for p in dp_peers]
    for c in copies:
        c.wait_recv()
    total = ring[0]
    for k in range(1, 8):
        total = total + ring[k]
    ring_b[mp] = total
    copies = [net.start(ring_b.at[mp], ring_b.at[mp], p) for p in mp_peers]
    for c in copies:
        c.wait_recv()
    out[...] = ring_b[0] + ring_b[1] + ring_b[2] + ring_b[3]
    net.close()


def apply_body(total, w_in, w_back, w_up, w_down, u_in, u_back, u_up, u_down, norms, norm_m, norm_v, *outs):
    nw_in, nw_back, nw_up, nw_down, new_norm, new_nm, new_nv, lens = outs
    both = jnp.sqrt(total[10:12, 0:128])
    lens[...] = both[:, 0:29]
    trust = LEARN_RATE * (both[0:1, :] / jnp.where(both[1:2, :] == 0.0, 1.0, both[1:2, :]))
    lane = lax.broadcasted_iota(jnp.int32, (1, 128), 1)

    def trust_of(j):
        return jnp.sum(jnp.where(lane == j, trust, 0.0), axis=1, keepdims=True)

    for j in range(16):
        nw_in[j] = w_in[j] - trust_of(j) * u_in[j]
    for j in range(11):
        nw_back[j] = w_back[j] - trust_of(16 + j) * u_back[j]
    nw_up[...] = w_up[...] - trust_of(27) * u_up[...]
    nw_down[...] = w_down[...] - trust_of(28) * u_down[...]
    m, v, u = adam_rows(norms[...], total[0:10, :], norm_m[...], norm_v[...], 0.0)
    w = norms[...]
    row_trust = jnp.sqrt(jnp.sum(w * w, axis=1, keepdims=True)) / jnp.sqrt(
        jnp.sum(u * u, axis=1, keepdims=True)
    )
    new_norm[...] = w - LEARN_RATE * row_trust * u
    new_nm[...] = m
    new_nv[...] = v


def lamb_all(sums, sq, rows, masters, moments, squares, norms, norm_m, norm_v):
    shapes = [(v.shape, F32) for v in masters]
    *mvu, usq = run_kernel(
        moments_body, "lamb_moments", [*sums, *masters, *moments, *squares],
        [*shapes, *shapes, *shapes, ((1, 128), F32)], [],
    )
    dma = pltpu.SemaphoreType.DMA
    wide = norms.shape[1]
    total = pl.pallas_call(
        totals_body,
        name="norm_totals",
        in_specs=[spec_vm() for _ in range(3)],
        out_specs=spec_vm(),
        out_shape=jax.ShapeDtypeStruct((16, wide), F32),
        scratch_shapes=[VM((8, 16, wide), F32), VM((4, 16, wide), F32), dma((10,)), dma((10,))],
        compiler_params=pltpu.CompilerParams(collective_id=2, has_side_effects=True),
    )(rows, sq, usq)
    *weights, new_norm, new_nm, new_nv, lens = run_kernel(
        apply_body, "lamb_apply", [total, *masters, *mvu[8:], norms, norm_m, norm_v],
        [*shapes, *[(norms.shape, F32)] * 3, ((2, 29), F32)], [],
    )
    return (*weights, *mvu[:8], new_norm, new_nm, new_nv, lens)


def fast_device(
    tokens,
    noise_field,
    codec_tokens,
    timesteps,
    segments,
    cotangent,
    w_in,
    w_back,
    w_up,
    w_down,
    m_in,
    m_back,
    m_up,
    m_down,
    v_in,
    v_back,
    v_up,
    v_down,
    norm_params,
    norm_m,
    norm_v,
):
    features = tokens.shape[1]
    n = w_in.shape[2]
    mp = lax.axis_index("mp")
    dp = lax.axis_index("dp")
    x, core, z, y = mp // 2, mp % 2, dp // 2, dp % 2
    slices = [2 * x + core, 2 * (1 - x) + core]

    step = pick(timesteps, x, 0)
    seg = pick(segments, x, 0)
    seg_col, seg_row = seg[:, None], seg[None, :]
    noise_level = jnp.sqrt((step.astype(F32) + 1.0) / TSTEPS).reshape(1, 1)
    embed = jax.nn.silu(time_embedding(step[None], features)).astype(LOW)
    embed_rows = jnp.broadcast_to(embed, (8, features))
    embed_col = embed.astype(F32).reshape(features, 1)
    side = jnp.stack(
        [lax.dynamic_slice(norm_params, (6, s * n), (2, n)) for s in slices]
    )
    norms = norm_params

    gathered, weight_sq, kept = forward_all(
        w_in, w_back, w_up, w_down.T, seg_col, seg_row, norms, side, embed_rows, noise_level,
        tokens, noise_field, codec_tokens,
    )
    sums, own_x, other_x, other_out, rows = backward_all(
        seg_col, seg_row, norms, side, embed_col, tokens, cotangent, codec_tokens, gathered, kept
    )
    out_rows = by_parity(x, kept[-1], other_out, 0).reshape(-1, features)
    grad_rows = by_parity(x, own_x, other_x, 0).reshape(-1, features).astype(F32)
    stepped = lamb_all(
        sums, weight_sq, rows, (w_in, w_back, w_up, w_down.T), (m_in, m_back, m_up, m_down.T),
        (v_in, v_back, v_up, v_down.T), norm_params, norm_m, norm_v,
    )
    stepped = [v.T if k in (3, 7, 11) else v for k, v in enumerate(stepped)]
    return (out_rows, grad_rows, *stepped)


def solution(mesh):
    per_device = fast_device if dict(mesh.shape) == {"dp": 8, "mp": 4} else generic_device
    placed = (
        P("dp", None),
        P("dp", None),
        P("dp", None, None),
        P("dp"),
        P("dp", None),
        P("dp", None),
        P(None, "dp", "mp"),
        P(None, "mp", "dp"),
        P("dp", "mp"),
        P("mp", "dp"),
        P(None, "dp", "mp"),
        P(None, "mp", "dp"),
        P("dp", "mp"),
        P("mp", "dp"),
        P(None, "dp", "mp"),
        P(None, "mp", "dp"),
        P("dp", "mp"),
        P("mp", "dp"),
        P(),
        P(),
        P(),
    )
    return jax.shard_map(
        per_device,
        mesh=mesh,
        in_specs=placed,
        out_specs=(
            P("dp", None),
            P("dp", None),
            P(None, "dp", "mp"),
            P(None, "mp", "dp"),
            P("dp", "mp"),
            P("mp", "dp"),
            P(None, "dp", "mp"),
            P(None, "mp", "dp"),
            P("dp", "mp"),
            P("mp", "dp"),
            P(None, "dp", "mp"),
            P(None, "mp", "dp"),
            P("dp", "mp"),
            P("mp", "dp"),
            P(),
            P(),
            P(),
            P(),
        ),
        check_vma=False,
    )
```

```python
from functools import partial
import math

import jax
import jax.numpy as jnp
from jax import lax
from jax.experimental import pallas as pl
from jax.experimental.pallas import tpu as pltpu
from jax.sharding import PartitionSpec as P

HD = 64
GROUPS = 32
FREQ = 8
TIME = 64
TSTEPS = 1000
STEP = 5


NORM_EPS = 1e-05
MOMENT_DECAY = 0.5
LEARN_RATE = 0.5
WEIGHT_DECAY = 0.01
ADAM_EPS = 1e-06
MASK_VALUE = -1e30
HIGHEST_PRECISION = lax.Precision.HIGHEST


def layer_norm(value_tensor, gain_row, shift_row):
    centre = value_tensor - jnp.mean(value_tensor, axis=-1, keepdims=True)
    spread = jnp.mean(centre * centre, axis=-1, keepdims=True)
    return centre * lax.rsqrt(spread + NORM_EPS) * gain_row + shift_row


def group_norm(value_tensor, gain_row, shift_row, group_width):
    seqs_here, length, channels = value_tensor.shape
    grouped = value_tensor.reshape(seqs_here, length, channels // group_width, group_width)
    centre = grouped - jnp.mean(grouped, axis=(1, 3), keepdims=True)
    spread = jnp.mean(centre * centre, axis=(1, 3), keepdims=True)
    normed = (centre * lax.rsqrt(spread + NORM_EPS)).reshape(seqs_here, length, channels)
    return normed * gain_row + shift_row


def norm_silu(value_tensor, gain_row, shift_row, group_width):
    return jax.nn.silu(group_norm(value_tensor, gain_row, shift_row, group_width))


def time_embedding(timesteps, features):
    half_width = features // 2
    freq_rates = jnp.exp(
        -math.log(10000.0) * jnp.arange(half_width, dtype=jnp.float32) / half_width
    )
    angles = timesteps.astype(jnp.float32)[:, None] * freq_rates[None, :]
    return jnp.concatenate([jnp.sin(angles), jnp.cos(angles)], axis=1)


def flatten_rows(value_tensor):
    return value_tensor.reshape(-1, value_tensor.shape[-1])


def project(values_low, weight_matrix):
    summed = jnp.dot(flatten_rows(values_low), weight_matrix, preferred_element_type=jnp.float32)
    return summed.reshape(values_low.shape[0], values_low.shape[1], weight_matrix.shape[1])


def back_project(grad_low, weight_matrix):
    summed = jnp.einsum(
        "ne,ce->nc", flatten_rows(grad_low), weight_matrix, preferred_element_type=jnp.float32
    )
    return summed.reshape(grad_low.shape[0], grad_low.shape[1], weight_matrix.shape[0])


def weight_grad(left_low, right_low):
    return jnp.einsum(
        "nc,ne->ce",
        flatten_rows(left_low),
        flatten_rows(right_low),
        preferred_element_type=jnp.float32,
    )


def padded_grid(grid_rows):
    seqs_here = grid_rows.shape[0]
    return jnp.pad(grid_rows.reshape(seqs_here, FREQ, TIME, -1), ((0, 0), (1, 1), (1, 1), (0, 0)))


def grid_window(padded, tap_index):
    row_off = tap_index // 3
    col_off = tap_index % 3
    return padded[:, row_off : row_off + FREQ, col_off : col_off + TIME, :].reshape(
        -1, padded.shape[3]
    )


def conv_grid(grid_rows, tap_weights, backward):
    seqs_here = grid_rows.shape[0]
    padded = padded_grid(grid_rows)
    out_width = tap_weights.shape[1] if backward else tap_weights.shape[2]
    summed = jnp.zeros((seqs_here * FREQ * TIME, out_width), jnp.float32)
    for tap_index in range(9):
        window = grid_window(padded, tap_index)
        if backward:
            summed = summed + jnp.einsum(
                "nc,dc->nd", window, tap_weights[8 - tap_index], preferred_element_type=jnp.float32
            )
        else:
            summed = summed + jnp.dot(
                window, tap_weights[tap_index], preferred_element_type=jnp.float32
            )
    return summed.reshape(seqs_here, FREQ * TIME, out_width)


def conv_weight_grad(grid_low, grad_low):
    padded = padded_grid(grid_low)
    grad_flat = flatten_rows(grad_low)
    tap_grads = []
    for tap_index in range(9):
        window = grid_window(padded, tap_index)
        tap_grads.append(
            jnp.einsum("nc,ne->ce", window, grad_flat, preferred_element_type=jnp.float32)
        )
    return jnp.stack(tap_grads)


def split_heads(rows_low):
    return rows_low.reshape(rows_low.shape[0], rows_low.shape[1], rows_low.shape[2] // HD, HD)


def head_scores(queries, key_rows, allowed, score_scale):
    scores = (
        jnp.einsum(
            "sqhd,skhd->shqk",
            split_heads(queries),
            split_heads(key_rows),
            preferred_element_type=jnp.float32,
        )
        * score_scale
    )
    if allowed is not None:
        scores = jnp.where(allowed[:, None], scores, MASK_VALUE)
    return scores


def attend(queries, key_rows, value_rows, allowed, score_scale):
    scores = head_scores(queries, key_rows, allowed, score_scale)
    highest = jnp.max(scores, axis=-1, keepdims=True)
    raised = jnp.exp(scores - highest)
    totals = jnp.sum(raised, axis=-1, keepdims=True)
    soft_low = (raised / totals).astype(jnp.bfloat16)
    mixed_rows = jnp.einsum(
        "shqk,skhd->sqhd", soft_low, split_heads(value_rows), preferred_element_type=jnp.float32
    )
    return (mixed_rows.reshape(queries.shape), highest + jnp.log(totals))


def attend_back(queries, key_rows, value_rows, allowed, score_scale, log_total, grad_mixed):
    scores = head_scores(queries, key_rows, allowed, score_scale)
    soft = jnp.exp(scores - log_total)
    grad_heads = split_heads(grad_mixed)
    grad_soft = jnp.einsum(
        "sqhd,skhd->shqk", grad_heads, split_heads(value_rows), preferred_element_type=jnp.float32
    )
    grad_values = jnp.einsum(
        "shqk,sqhd->skhd", soft.astype(jnp.bfloat16), grad_heads, preferred_element_type=jnp.float32
    )
    row_dot = jnp.sum(soft * grad_soft, axis=-1, keepdims=True)
    grad_scores = (soft * (grad_soft - row_dot)).astype(jnp.bfloat16)
    grad_queries = (
        jnp.einsum(
            "shqk,skhd->sqhd",
            grad_scores,
            split_heads(key_rows),
            preferred_element_type=jnp.float32,
        )
        * score_scale
    )
    grad_keys = (
        jnp.einsum(
            "shqk,sqhd->skhd", grad_scores, split_heads(queries), preferred_element_type=jnp.float32
        )
        * score_scale
    )
    return (
        grad_queries.reshape(queries.shape).astype(jnp.bfloat16),
        grad_keys.reshape(key_rows.shape).astype(jnp.bfloat16),
        grad_values.reshape(value_rows.shape).astype(jnp.bfloat16),
    )


def tensor_parallel_sum(term_rows):
    return lax.psum(term_rows, "mp")


def matrix_squares(first_stack, second_stack, up_rows, down_rows):
    return jnp.concatenate(
        [
            jnp.sum(first_stack * first_stack, axis=(1, 2)),
            jnp.sum(second_stack * second_stack, axis=(1, 2)),
            jnp.sum(up_rows * up_rows)[None],
            jnp.sum(down_rows * down_rows)[None],
        ]
    )


def adam_update(master, grad_rows, first_moment, second_moment, decay_rate):
    first_new = MOMENT_DECAY * first_moment + (1.0 - MOMENT_DECAY) * grad_rows
    second_new = MOMENT_DECAY * second_moment + (1.0 - MOMENT_DECAY) * grad_rows * grad_rows
    correct = 1.0 - MOMENT_DECAY**STEP
    update = first_new / correct / (jnp.sqrt(second_new / correct) + ADAM_EPS) + decay_rate * master
    return (first_new, second_new, update)


def generic_device(
    tokens,
    noise_field,
    codec_tokens,
    timesteps,
    segments,
    cotangent,
    w_in,
    w_back,
    w_up,
    w_down,
    m_in,
    m_back,
    m_up,
    m_down,
    v_in,
    v_back,
    v_up,
    v_down,
    norm_params,
    norm_m,
    norm_v,
):
    seqs_here, length = segments.shape
    features = tokens.shape[1]
    chans_here = w_in.shape[2]
    group_width = features // GROUPS
    score_scale = HD ** (-0.5)
    channel_start = lax.axis_index("mp") * chans_here
    lead_device = (lax.axis_index("mp") == 0).astype(jnp.float32)
    weight_sq = matrix_squares(w_in, w_back, w_up, w_down)
    full_in, full_back, complete_up_weight, full_down = (
        lax.all_gather(w_in.astype(jnp.bfloat16), "dp", axis=1, tiled=True),
        lax.all_gather(w_back.astype(jnp.bfloat16), "dp", axis=2, tiled=True),
        lax.all_gather(w_up.astype(jnp.bfloat16), "dp", axis=0, tiled=True),
        lax.all_gather(w_down.astype(jnp.bfloat16), "dp", axis=1, tiled=True),
    )
    resid_in = tokens.astype(jnp.float32).reshape(seqs_here, length, features)
    allowed = segments[:, :, None] == segments[:, None, :]
    normed_one_low = layer_norm(resid_in, norm_params[0], norm_params[1]).astype(jnp.bfloat16)
    queries = project(normed_one_low, full_in[0]).astype(jnp.bfloat16)
    key_rows = project(normed_one_low, full_in[1]).astype(jnp.bfloat16)
    value_rows = project(normed_one_low, full_in[2]).astype(jnp.bfloat16)
    mixed_rows, log_self = attend(queries, key_rows, value_rows, allowed, score_scale)
    mixed_low = mixed_rows.astype(jnp.bfloat16)
    resid_one = resid_in + tensor_parallel_sum(project(mixed_low, full_back[0]))
    normed_two_low = layer_norm(resid_one, norm_params[2], norm_params[3]).astype(jnp.bfloat16)
    hidden_pre = project(normed_two_low, complete_up_weight)
    hidden_low = jax.nn.gelu(hidden_pre).astype(jnp.bfloat16)
    resid_two = resid_one + tensor_parallel_sum(project(hidden_low, full_down))
    noise_level = jnp.sqrt((timesteps.astype(jnp.float32) + 1.0) / TSTEPS)
    noisy = resid_two + noise_level[:, None, None] * noise_field.astype(jnp.float32).reshape(
        seqs_here, length, features
    )
    first_low = norm_silu(noisy, norm_params[4], norm_params[5], group_width).astype(jnp.bfloat16)
    embed_low = jax.nn.silu(time_embedding(timesteps, features)).astype(jnp.bfloat16)
    time_shift = jnp.dot(embed_low, full_in[3], preferred_element_type=jnp.float32)
    conv_one = conv_grid(first_low, full_in[7:16], False) + time_shift[:, None, :]
    gain_six = lax.dynamic_slice_in_dim(norm_params[6], channel_start, chans_here)
    shift_six = lax.dynamic_slice_in_dim(norm_params[7], channel_start, chans_here)
    second_low = norm_silu(conv_one, gain_six, shift_six, group_width).astype(jnp.bfloat16)
    resid_three = noisy + tensor_parallel_sum(conv_grid(second_low, full_back[2:11], False))
    normed_three_low = layer_norm(resid_three, norm_params[8], norm_params[9]).astype(jnp.bfloat16)
    cross_queries = project(normed_three_low, full_in[4]).astype(jnp.bfloat16)
    cross_keys = project(codec_tokens, full_in[5]).astype(jnp.bfloat16)
    cross_values = project(codec_tokens, full_in[6]).astype(jnp.bfloat16)
    cross_mixed, log_cross = attend(cross_queries, cross_keys, cross_values, None, score_scale)
    cross_low = cross_mixed.astype(jnp.bfloat16)
    result = resid_three + tensor_parallel_sum(project(cross_low, full_back[1]))
    out_low = result.astype(jnp.bfloat16)
    grad_out = cotangent.astype(jnp.float32).reshape(seqs_here, length, features)
    grad_cross_low = grad_out.astype(jnp.bfloat16)
    grad_w_co = weight_grad(cross_low, grad_cross_low)
    grad_cross_mixed = back_project(grad_cross_low, full_back[1]).astype(jnp.bfloat16)
    grad_cq, grad_ck, grad_cv = attend_back(
        cross_queries, cross_keys, cross_values, None, score_scale, log_cross, grad_cross_mixed
    )
    grad_w_cq = weight_grad(normed_three_low, grad_cq)
    grad_w_ck = weight_grad(codec_tokens, grad_ck)
    grad_w_cv = weight_grad(codec_tokens, grad_cv)
    grad_normed_three = tensor_parallel_sum(back_project(grad_cq, full_in[4]))
    pull_three = jax.vjp(layer_norm, resid_three, norm_params[8], norm_params[9])[1]
    grad_part, grad_gain_eight, grad_shift_eight = pull_three(grad_normed_three)
    grad_three = grad_out + grad_part
    grad_conv_low = grad_three.astype(jnp.bfloat16)
    grad_w_conv_two = conv_weight_grad(second_low, grad_conv_low)
    grad_second = conv_grid(grad_conv_low, full_back[2:11], True)
    gather_second_moment = jax.vjp(
        partial(norm_silu, group_width=group_width), conv_one, gain_six, shift_six
    )[1]
    grad_conv_one, grad_gain_six, grad_shift_six = gather_second_moment(grad_second)
    grad_conv_one_low = grad_conv_one.astype(jnp.bfloat16)
    grad_w_time = jnp.einsum(
        "sd,sc->dc",
        embed_low.astype(jnp.float32),
        jnp.sum(grad_conv_one_low.astype(jnp.float32), axis=1),
        precision=HIGHEST_PRECISION,
    )
    grad_w_conv_one = conv_weight_grad(first_low, grad_conv_one_low)
    grad_first = tensor_parallel_sum(conv_grid(grad_conv_one_low, full_in[7:16], True))
    gather_first_moment = jax.vjp(
        partial(norm_silu, group_width=group_width), noisy, norm_params[4], norm_params[5]
    )[1]
    grad_part, grad_gain_four, grad_shift_four = gather_first_moment(grad_first)
    grad_two = grad_three + grad_part
    grad_mlp_low = grad_two.astype(jnp.bfloat16)
    grad_w_down = weight_grad(hidden_low, grad_mlp_low)
    grad_hidden = back_project(grad_mlp_low, full_down)
    grad_pre_low = jax.vjp(jax.nn.gelu, hidden_pre)[1](grad_hidden)[0].astype(jnp.bfloat16)
    up_weight_gradient = weight_grad(normed_two_low, grad_pre_low)
    grad_normed_two = tensor_parallel_sum(back_project(grad_pre_low, complete_up_weight))
    pull_two = jax.vjp(layer_norm, resid_one, norm_params[2], norm_params[3])[1]
    grad_part, grad_gain_two, grad_shift_two = pull_two(grad_normed_two)
    grad_one = grad_two + grad_part
    grad_attn_low = grad_one.astype(jnp.bfloat16)
    grad_w_out = weight_grad(mixed_low, grad_attn_low)
    grad_mixed = back_project(grad_attn_low, full_back[0]).astype(jnp.bfloat16)
    grad_q, grad_k, grad_v = attend_back(
        queries, key_rows, value_rows, allowed, score_scale, log_self, grad_mixed
    )
    grad_w_q = weight_grad(normed_one_low, grad_q)
    grad_w_k = weight_grad(normed_one_low, grad_k)
    grad_w_v = weight_grad(normed_one_low, grad_v)
    grad_normed_one = tensor_parallel_sum(
        back_project(grad_q, full_in[0])
        + back_project(grad_k, full_in[1])
        + back_project(grad_v, full_in[2])
    )
    pull_one = jax.vjp(layer_norm, resid_in, norm_params[0], norm_params[1])[1]
    grad_part, grad_gain_zero, grad_shift_zero = pull_one(grad_normed_one)
    grad_input = grad_one + grad_part
    grad_in_stack = jnp.concatenate(
        [
            jnp.stack([grad_w_q, grad_w_k, grad_w_v, grad_w_time, grad_w_cq, grad_w_ck, grad_w_cv]),
            grad_w_conv_one,
        ]
    )
    grad_back_stack = jnp.concatenate([jnp.stack([grad_w_out, grad_w_co]), grad_w_conv_two])
    summed_in, summed_back, summed_up, summed_down = (
        lax.psum_scatter(grad_in_stack, "dp", scatter_dimension=1, tiled=True),
        lax.psum_scatter(grad_back_stack, "dp", scatter_dimension=2, tiled=True),
        lax.psum_scatter(up_weight_gradient, "dp", scatter_dimension=0, tiled=True),
        lax.psum_scatter(grad_w_down, "dp", scatter_dimension=1, tiled=True),
    )
    shared_rows = (
        jnp.stack(
            [
                grad_gain_zero,
                grad_shift_zero,
                grad_gain_two,
                grad_shift_two,
                grad_gain_four,
                grad_shift_four,
            ]
        )
        * lead_device
    )
    group_rows = lax.dynamic_update_slice(
        jnp.zeros((2, features), jnp.float32),
        jnp.stack([grad_gain_six, grad_shift_six]),
        (0, channel_start),
    )
    last_rows = jnp.stack([grad_gain_eight, grad_shift_eight]) * lead_device
    norm_grad = lax.psum(jnp.concatenate([shared_rows, group_rows, last_rows]), ("dp", "mp"))
    m_in_new, v_in_new, upd_in = adam_update(w_in, summed_in, m_in, v_in, WEIGHT_DECAY)
    m_back_new, v_back_new, upd_back = adam_update(
        w_back, summed_back, m_back, v_back, WEIGHT_DECAY
    )
    m_up_new, v_up_new, upd_up = adam_update(w_up, summed_up, m_up, v_up, WEIGHT_DECAY)
    m_down_new, v_down_new, upd_down = adam_update(
        w_down, summed_down, m_down, v_down, WEIGHT_DECAY
    )
    update_sq = matrix_squares(upd_in, upd_back, upd_up, upd_down)
    weight_total, update_total = lax.psum((weight_sq, update_sq), ("dp", "mp"))
    weight_len = jnp.sqrt(weight_total)
    update_len = jnp.sqrt(update_total)
    trust = weight_len / update_len
    new_in = w_in - LEARN_RATE * trust[0:16, None, None] * upd_in
    new_back = w_back - LEARN_RATE * trust[16:27, None, None] * upd_back
    new_up = w_up - LEARN_RATE * trust[27] * upd_up
    new_down = w_down - LEARN_RATE * trust[28] * upd_down
    norm_m_new, norm_v_new, upd_norm = adam_update(norm_params, norm_grad, norm_m, norm_v, 0.0)
    row_trust = jnp.sqrt(jnp.sum(norm_params * norm_params, axis=1)) / jnp.sqrt(
        jnp.sum(upd_norm * upd_norm, axis=1)
    )
    new_norm = norm_params - LEARN_RATE * row_trust[:, None] * upd_norm
    matrix_norms = jnp.stack([weight_len, update_len])
    out_rows = out_low.reshape(seqs_here * length, features)
    grad_rows = grad_input.reshape(seqs_here * length, features)
    return (
        out_rows,
        grad_rows,
        new_in,
        new_back,
        new_up,
        new_down,
        m_in_new,
        m_back_new,
        m_up_new,
        m_down_new,
        v_in_new,
        v_back_new,
        v_up_new,
        v_down_new,
        new_norm,
        norm_m_new,
        norm_v_new,
        matrix_norms,
    )


CORE_SWAP = [(i, i ^ 1) for i in range(4)]
X_SWAP = [(i, i ^ 2) for i in range(4)]
LOW = jnp.bfloat16
F32 = jnp.float32


def swap_core(v):
    return lax.ppermute(v, "mp", CORE_SWAP)


def swap_x(v):
    return lax.ppermute(v, "mp", X_SWAP)


def by_parity(flag, own, other, axis):
    first = jnp.where(flag == 0, own, other)
    second = jnp.where(flag == 0, other, own)
    return jnp.stack([first, second], axis=axis)


def pick(v, index, axis):
    return lax.dynamic_index_in_dim(v, index, axis, keepdims=False)


def ln_stats(v):
    centre = v - jnp.mean(v, axis=-1, keepdims=True)
    scale = lax.rsqrt(jnp.mean(centre * centre, axis=-1, keepdims=True) + NORM_EPS)
    return centre * scale, scale


def ln_back(v, gain, grad):
    hat, scale = ln_stats(v)
    pulled = grad * gain
    back = scale * (
        pulled
        - jnp.mean(pulled, axis=-1, keepdims=True)
        - hat * jnp.mean(pulled * hat, axis=-1, keepdims=True)
    )
    return back, jnp.sum(grad * hat, axis=0, keepdims=True), jnp.sum(grad, axis=0, keepdims=True)


def mm(a, b):
    return lax.dot_general(a, b, (((1,), (0,)), ((), ())), preferred_element_type=F32)


def mm_nt(a, b):
    return lax.dot_general(a, b, (((1,), (1,)), ((), ())), preferred_element_type=F32)


def mm_tn(a, b):
    return lax.dot_general(a, b, (((0,), (0,)), ((), ())), preferred_element_type=F32)


ANY = pl.ANY
VM = pltpu.VMEM
ROWS = 512
STEP_ROWS = 128


def spec_any():
    return pl.BlockSpec(memory_space=pl.ANY)


def spec_vm():
    return pl.BlockSpec(memory_space=pltpu.VMEM)


def run_kernel(body, name, ins, outs, scratch, hbm=(), flops=0):
    in_specs = [spec_any() if k in hbm else spec_vm() for k in range(len(ins))]
    moved = sum(v.size * v.dtype.itemsize for v in ins) + sum(
        math.prod(s) * jnp.dtype(t).itemsize for s, t in outs
    )
    return pl.pallas_call(
        body,
        name=name,
        in_specs=in_specs,
        out_specs=[spec_vm() for _ in outs],
        out_shape=[jax.ShapeDtypeStruct(s, t) for s, t in outs],
        scratch_shapes=scratch,
        compiler_params=pltpu.CompilerParams(vmem_limit_bytes=56 << 20),
        cost_estimate=pl.CostEstimate(flops=flops, bytes_accessed=moved, transcendentals=0),
    )(*ins)


def each_rows(fn, total=ROWS, step=STEP_ROWS):
    def body(k, carry):
        fn(pl.ds(pl.multiple_of(k * step, step), step))
        return carry

    lax.fori_loop(0, total // step, body, 0)


def start_copies(pairs, sems):
    copies = [pltpu.make_async_copy(a, b, sems.at[k]) for k, (a, b) in enumerate(pairs)]
    for c in copies:
        c.start()
    return copies


def group_mats(channels, width):
    count = channels // width
    r = lax.broadcasted_iota(jnp.int32, (channels, count), 0)
    c = lax.broadcasted_iota(jnp.int32, (channels, count), 1) * width
    down = ((r >= c) & (r < c + width)).astype(F32)
    r = lax.broadcasted_iota(jnp.int32, (count, channels), 1)
    c = lax.broadcasted_iota(jnp.int32, (count, channels), 0) * width
    up = ((r >= c) & (r < c + width)).astype(F32)
    return down, up


def exact_dot(a, b):
    return jnp.dot(a, b, precision=HIGHEST_PRECISION, preferred_element_type=F32)


def group_average(row, mats, width):
    wide = jnp.broadcast_to(row, (8, row.shape[1]))
    return exact_dot(exact_dot(wide, mats[0]) * (1.0 / (width * ROWS)), mats[1])[0:1]


def gelu_parts(v):
    k = math.sqrt(2.0 / math.pi)
    t = jnp.tanh(k * (v + 0.044715 * (v * v * v)))
    return t, 0.5 * v * (1.0 + t)


def gelu_slope(v, t):
    k = math.sqrt(2.0 / math.pi)
    return 0.5 * (1.0 + t) + 0.5 * v * (1.0 - t * t) * (k * (1.0 + 3 * 0.044715 * (v * v)))


def column_of(shape):
    return lax.broadcasted_iota(jnp.int32, shape, 0) % TIME


def from_left(v):
    return jnp.where(column_of(v.shape) == 0, 0.0, pltpu.roll(v, 1, 0))


def from_right(v):
    return jnp.where(column_of(v.shape) == TIME - 1, 0.0, pltpu.roll(v, v.shape[0] - 1, 0))


def softmax_heads(q, k, v, heads, score_scale, mask):
    mixed, logs = [], []
    for h in range(heads):
        s = mm_nt(q[:, HD * h : HD * (h + 1)], k[:, HD * h : HD * (h + 1)]) * score_scale
        if mask is not None:
            s = jnp.where(mask, s, MASK_VALUE)
        top = jnp.max(s, axis=1, keepdims=True)
        e = jnp.exp(s - top)
        total = jnp.sum(e, axis=1, keepdims=True)
        soft = (e * (1.0 / total)).astype(LOW)
        mixed.append(mm(soft, v[:, HD * h : HD * (h + 1)]))
        logs.append(top + jnp.log(total))
    return jnp.concatenate(mixed, axis=1).astype(LOW), logs


def softmax_heads_back(q, k, v, g, logs, heads, score_scale, mask):
    dq, dk, dv = [], [], []
    for h in range(heads):
        cols = slice(HD * h, HD * (h + 1))
        s = mm_nt(q[:, cols], k[:, cols]) * score_scale
        if mask is not None:
            s = jnp.where(mask, s, MASK_VALUE)
        soft = jnp.exp(s - logs[h])
        gs = mm_nt(g[:, cols], v[:, cols])
        dv.append(mm_tn(soft.astype(LOW), g[:, cols]))
        dot = jnp.sum(soft * gs, axis=1, keepdims=True)
        ds = (soft * (gs - dot)).astype(LOW)
        dq.append(mm(ds, k[:, cols]) * score_scale)
        dk.append(mm_tn(ds, q[:, cols]))
    return [jnp.concatenate(d, axis=1) for d in (dq, dk, dv)]


MESH_IDS = pl.DeviceIdType.MESH


def place():
    mp = lax.axis_index("mp")
    dp = lax.axis_index("dp")
    return mp // 2, mp % 2, dp // 2, dp % 2


def device(x, core, z, y):
    return (2 * z + y, 2 * x + core)


def meet(peers):
    barrier = pltpu.get_barrier_semaphore()
    for peer in peers:
        pl.semaphore_signal(barrier, inc=1, device_id=peer, device_id_type=MESH_IDS)
    pl.semaphore_wait(barrier, len(peers))


def chip_peers():
    x, core, z, y = place()
    along_z = [device(x, core, (z + k) % 4, y) for k in range(1, 4)]
    return device(1 - x, core, z, y), device(x, core, z, 1 - y), along_z


class Sender:
    def __init__(self, send, recv):
        self.send, self.recv, self.made = send, recv, []

    def start(self, src, dst, peer):
        k = len(self.made)
        copy = pltpu.make_async_remote_copy(
            src_ref=src, dst_ref=dst, send_sem=self.send.at[k], recv_sem=self.recv.at[k],
            device_id=peer, device_id_type=MESH_IDS,
        )
        copy.start()
        self.made.append(copy)
        return copy

    def close(self):
        for copy in self.made:
            copy.wait_send()


def padded_width(w):
    return -(-w // 128) * 128


def pack_piece(g, w_in, w_back, w_up, w_down, piece):
    n = w_in.shape[2]
    if g == 1:
        hid = w_up.shape[1]
        piece[:, :hid] = w_up[...].astype(LOW)
        piece[:, hid:] = w_down[...].astype(LOW)
        return
    ins, backs = GROUPS_OF[g]
    cols = [w_in[j] for j in ins] + [w_back[j].T for j in backs]
    spare = piece.shape[1] - n * len(cols)
    if spare:
        cols.append(jnp.zeros((piece.shape[0], spare), F32))
    for k in range(0, len(cols), 2):
        pair = cols[k : k + 2]
        both = pair[0] if len(pair) == 1 else jnp.concatenate(pair, axis=1)
        piece[:, n * k : n * k + both.shape[1]] = both.astype(LOW)


GROUPS_OF = {
    0: ([0, 1, 2], [0]),
    2: ([*range(7, 16), 3], []),
    3: ([], [*range(2, 11)]),
    4: ([4, 5, 6], [1]),
}


def row_of(values):
    lane = lax.broadcasted_iota(jnp.int32, (1, 128), 1)
    row = jnp.zeros((1, 128), F32)
    for j, v in enumerate(values):
        row = row + jnp.where(lane == j, v, 0.0)
    return row


def square_sum(v):
    return jnp.sum(jnp.sum(v * v, axis=1, keepdims=True), axis=0, keepdims=True)


def add_rows(target, terms, step=16):
    def body(k, carry):
        r = pl.ds(pl.multiple_of(k * step, step), step)
        total = terms[0][r, :].astype(F32)
        for t in terms[1:]:
            total = total + t[r, :].astype(F32)
        target[r, :] = total.astype(target.dtype)
        return carry

    lax.fori_loop(0, target.shape[0] // step, body, 0)


def z_peers():
    x, core, z, y = place()
    return device(x, core, z + 1 - 2 * (z % 2), y), device(x, core, (z + 2) % 4, y)


class Gather:
    def __init__(self, pieces, outs, over_x, y_first, net):
        self.pieces, self.outs, self.over_x, self.y_first, self.net = pieces, outs, over_x, y_first, net
        self.x, self.core, self.z, self.y = place()
        self.to_x, self.to_y, _ = chip_peers()
        self.to_z1, self.to_z2 = z_peers()
        near = self.z + 1 - 2 * (self.z % 2)
        self.sources = (near, (self.z + 2) % 4, (near + 2) % 4)
        self.lines, self.planes, self.corners = {}, {}, {}

    def line(self, g):
        if g in self.y_first:
            self.planes[g][0].wait_recv()
            src = dst = self.outs[g].at[0, self.z]
        else:
            src, dst = self.pieces[g], self.outs[g].at[0, self.z, self.y]
        self.lines[g] = [self.net.start(src, dst, peer) for peer in (self.to_z1, self.to_z2)]

    def relay(self, g):
        self.lines[g][1].wait_recv()
        out, far = self.outs[g], self.sources[1]
        src = out.at[0, far] if g in self.y_first else out.at[0, far, self.y]
        self.lines[g].append(self.net.start(src, src, self.to_z1))

    def own(self, g):
        z, y, out = self.z, self.y, self.outs[g]
        self.planes[g] = [self.net.start(self.pieces[g], out.at[0, z, y], self.to_y)]
        if out.shape[0] == 2:
            self.planes[g].append(self.net.start(self.pieces[g], out.at[1, z, y], self.to_x))

    def spread(self, g, k):
        if k != 2:
            self.lines[g][k - 1].wait_recv()
        out, far = self.outs[g], self.sources[k - 1]
        src = out.at[0, far, self.y]
        self.planes[g].append(self.net.start(src, src, self.to_y))
        if out.shape[0] == 2:
            self.planes[g].append(self.net.start(src, out.at[1, far, self.y], self.to_x))

    def turn(self, g):
        for c in self.planes[g]:
            c.wait_recv()
        out, y, k = self.outs[g], self.y, self.over_x[g]
        self.corners[g] = []
        if k > 0:
            self.corners[g].append(
                self.net.start(out.at[0, 0:k, 1 - y], out.at[1, 0:k, 1 - y], self.to_x)
            )
        if k < 4:
            self.corners[g].append(
                self.net.start(out.at[1, k:4, y], out.at[1, k:4, y], self.to_y)
            )

    def ready(self, g):
        if g in self.y_first:
            last = (self.lines[g][0], self.lines[g][2])
        else:
            last = self.corners[g] if self.outs[g].shape[0] == 2 else self.planes[g]
        for c in last:
            c.wait_recv()


class FourSum:
    def __init__(self, net, part, near, far_out, far_in, done):
        self.net, self.part, self.near, self.done = net, part, near, done
        self.far_out, self.far_in = far_out, far_in
        x, core, z, y = place()
        count = ROWS // 2
        self.mine = pl.ds(pl.multiple_of(core * count, count), count)
        self.theirs = pl.ds(pl.multiple_of((1 - core) * count, count), count)
        self.sibling, self.across = device(x, 1 - core, z, y), device(1 - x, core, z, y)

    def begin(self, i):
        copy = self.net.start(self.part.at[i, self.theirs, :], self.near.at[i], self.sibling)
        if i == 1:
            self.other = copy
        else:
            self.own = copy

    def cross(self):
        self.other.wait_recv()
        add_rows(self.far_out, [self.part.at[1, self.mine, :], self.near.at[1]], 64)
        self.far = self.net.start(self.far_out, self.far_in, self.across)

    def end(self):
        self.own.wait_recv()
        self.far.wait_recv()
        mine = self.done.at[self.mine, :]
        add_rows(mine, [self.part.at[0, self.mine, :], self.near.at[0], self.far_in], 64)
        self.last = self.net.start(mine, mine, self.sibling)
        self.last.wait_recv()


class Share:
    def __init__(self, net, both, first):
        self.net, self.both = net, both
        x, core, z, y = place()
        count = ROWS // 2
        self.mine = pl.ds(pl.multiple_of(first + core * count, TIME), count)
        self.sibling, self.across = device(x, 1 - core, z, y), device(1 - x, core, z, y)

    def begin(self):
        self.far = self.net.start(
            self.both.at[0, self.mine, :], self.both.at[1, self.mine, :], self.across
        )

    def pass_on(self):
        self.far.wait_recv()
        rows = self.both.at[1, self.mine, :]
        self.near = self.net.start(rows, rows, self.sibling)

    def end(self):
        self.near.wait_recv()


def matrix_of(ref, i, first, last):
    block = ref[i, :, :, :, first:last]
    return block.reshape(-1, last - first)


def forward_body(
    w_in, w_back, w_up, w_down, seg_col, seg_row, norms, side, embed, level, tokens, noises, codecs,
    g0, g1, g2, g3, g4, sq, n1_o, qkv_o, mixed_o, logs_o, resid_o, n2_o, noisy_o, first_o, conv_o,
    taps_o, resid3_o, n3_o, cq_o, ckv_o, cross_o, logs_c_o, out_o,
    p0, p1, p2, p3, p4, v0, v1, v2, v3, v4, tok, noise, codec, n1, qkv, mixed, logs, resid, n2,
    noisy, conv, taps, resid3, n3, cq, ckv, cross, logs_c, out, pad, acc, sent, got,
    part, near, far_out, far_in, summed,
    in_sem, out_sem, own_sem, send, recv,
):
    pieces, held, kept = (p0, p1, p2, p3, p4), (v0, v1, v2, v3, v4), (g0, g1, g2, g3, g4)
    n = mixed.shape[2]
    hid = w_up.shape[1]
    features = norms.shape[1]
    width = features // GROUPS
    heads = n // HD
    score_scale = HD ** (-0.5)
    net = Sender(send, recv)
    run = Gather(pieces, held, (2, 4, 0, 0, 2), (3,), net)
    share = Share(net, pad, TIME)
    total_sum = FourSum(net, part, near, far_out, far_in, summed)
    x, core, z, y = place()
    sibling = device(x, 1 - core, z, y)
    loads = [
        pltpu.make_async_copy(tokens.at[pl.ds(pl.multiple_of(x * ROWS, ROWS), ROWS), :], tok, in_sem.at[0]),
        pltpu.make_async_copy(noises.at[pl.ds(pl.multiple_of(x * ROWS, ROWS), ROWS), :], noise, in_sem.at[1]),
        pltpu.make_async_copy(codecs.at[x], codec, in_sem.at[2]),
    ]
    for c in loads:
        c.start()
    stores = []

    def store(src, dst):
        copy = pltpu.make_async_copy(src, dst, out_sem.at[len(stores)])
        copy.start()
        stores.append(copy)

    def pack(g):
        pack_piece(g, w_in, w_back, w_up, w_down, pieces[g])
        copy = pltpu.make_async_copy(pieces[g], held[g].at[0, z, y], own_sem.at[g])
        copy.start()
        return copy

    def exchange(k, total):
        sent[k] = total.astype(LOW)
        return net.start(sent.at[k], got.at[k], sibling)

    def joined(k, r):
        return sent[k, r, :].astype(F32) + got[k, r, :].astype(F32)

    local = [pack(0)]
    meet([run.to_x, run.to_y, *z_peers(), sibling])
    run.line(0)
    run.own(0)
    local.append(pack(1))
    run.line(1)
    run.own(1)
    local += [pack(2), pack(3), pack(4)]
    loads[0].wait()

    def norm_one(r):
        hat, _ = ln_stats(tok[r, :].astype(F32))
        n1[r, :] = (hat * norms[0:1, :] + norms[1:2, :]).astype(LOW)

    each_rows(norm_one)
    store(n1, n1_o)
    run.relay(0)
    run.spread(0, 1)
    run.spread(0, 2)
    run.line(2)
    run.own(3)
    run.spread(0, 3)
    run.own(2)
    sq[...] = row_of(
        [square_sum(w_in[j]) for j in range(16)] + [square_sum(w_back[j]) for j in range(11)]
        + [square_sum(w_up[...]), square_sum(w_down[...])]
    )
    run.relay(1)
    run.spread(1, 1)
    run.spread(1, 2)
    run.turn(0)
    local[0].wait()
    local[3].wait()
    run.line(3)
    run.ready(0)
    store(v0, g0)
    for i in range(2):
        qkv[i] = mm(n1[...], matrix_of(v0, i, 0, 3 * n)).astype(LOW)
    store(qkv, qkv_o)
    run.spread(1, 3)

    def self_heads(r):
        mask = seg_col[r, :] == seg_row[...]
        found = []
        for i in range(2):
            part, logs_i = softmax_heads(
                qkv[i, r, 0:n], qkv[i, :, n : 2 * n], qkv[i, :, 2 * n : 3 * n], heads, score_scale, mask
            )
            mixed[i, r, :] = part
            found += logs_i
        logs[r, :] = jnp.concatenate(found, axis=1)

    each_rows(self_heads)
    swap = exchange(
        0,
        mm_nt(mixed[0], matrix_of(v0, 0, 3 * n, 4 * n)) + mm_nt(mixed[1], matrix_of(v0, 1, 3 * n, 4 * n)),
    )
    store(mixed, mixed_o)
    store(logs, logs_o)
    run.relay(2)
    run.spread(2, 1)
    run.spread(2, 2)
    run.turn(1)
    run.own(4)
    run.line(4)
    swap.wait_recv()

    def norm_two(r):
        v = tok[r, :].astype(F32) + joined(0, r)
        resid[r, :] = v
        hat, _ = ln_stats(v)
        n2[r, :] = (hat * norms[2:3, :] + norms[3:4, :]).astype(LOW)

    each_rows(norm_two)
    store(resid, resid_o)
    store(n2, n2_o)
    run.spread(2, 3)
    run.relay(3)
    local[1].wait()
    run.ready(1)
    store(v1, g1)
    block = 256
    for i in range(2):
        for b in range(hid // block):
            pre = mm(n2[...], matrix_of(v1, i, block * b, block * (b + 1)))
            low = gelu_parts(pre)[1].astype(LOW)
            term = mm_nt(low, matrix_of(v1, i, hid + block * b, hid + block * (b + 1)))
            if i == 0 and b == 0:
                acc[...] = term
            else:
                acc[...] += term
    swap = exchange(1, acc[...])
    loads[1].wait()
    swap.wait_recv()

    def add_noise(r):
        noisy[r, :] = resid[r, :] + joined(1, r) + level[...] * noise[r, :].astype(F32)

    each_rows(add_noise)
    store(noisy, noisy_o)
    mats = group_mats(features, width)
    mats_n = group_mats(n, width)
    mean = group_average(jnp.sum(noisy[...], axis=0, keepdims=True), mats, width)
    centre = noisy[...] - mean
    var = group_average(jnp.sum(centre * centre, axis=0, keepdims=True), mats, width)
    scale = lax.rsqrt(var + NORM_EPS) * norms[4:5, :]
    for i in range(2):
        pad[i, 0:TIME, :] = jnp.zeros((TIME, features), LOW)
        pad[i, TIME + ROWS :, :] = jnp.zeros((TIME, features), LOW)

    def act(k, carry):
        r = pl.ds(pl.multiple_of(k * STEP_ROWS, STEP_ROWS), STEP_ROWS)
        v = (noisy[r, :] - mean) * scale + norms[5:6, :]
        moved = pl.ds(pl.multiple_of(TIME + k * STEP_ROWS, TIME), STEP_ROWS)
        pad[0, moved, :] = (v * jax.nn.sigmoid(v)).astype(LOW)
        return carry

    lax.fori_loop(0, ROWS // STEP_ROWS, act, 0)
    share.begin()
    run.relay(4)
    run.spread(4, 1)
    run.spread(4, 2)
    local[2].wait()
    run.ready(2)
    store(v2, g2)

    def conv_layer(i):
        q = None
        for a in range(3):
            term = mm(
                pad[i, TIME * a : TIME * a + ROWS, :], matrix_of(v2, 0, 3 * n * a, 3 * n * (a + 1))
            )
            q = term if q is None else q + term
        shift = mm(embed[i], matrix_of(v2, 0, 9 * n, 10 * n))[0:1]
        c1 = from_left(q[:, :n]) + q[:, n : 2 * n] + from_right(q[:, 2 * n :]) + shift
        conv[i] = c1
        c1 = c1 - group_average(jnp.sum(c1, axis=0, keepdims=True), mats_n, width)
        var_n = group_average(jnp.sum(c1 * c1, axis=0, keepdims=True), mats_n, width)
        v = c1 * lax.rsqrt(var_n + NORM_EPS) * side[0:1, :] + side[1:2, :]
        v = v * jax.nn.sigmoid(v)
        taps[i, 0:TIME, :] = jnp.zeros((TIME, 3 * n), LOW)
        taps[i, TIME + ROWS :, :] = jnp.zeros((TIME, 3 * n), LOW)
        taps[i, TIME : TIME + ROWS, :] = jnp.concatenate(
            [from_left(v), v, from_right(v)], axis=1
        ).astype(LOW)

    def conv_back_layer(i):
        total = None
        for a in range(3):
            term = mm_nt(
                taps[i, TIME * a : TIME * a + ROWS, :], matrix_of(v3, 0, 3 * n * a, 3 * n * (a + 1))
            )
            total = term if total is None else total + term
        part[i] = total.astype(LOW)
        total_sum.begin(i)

    conv_layer(0)
    share.pass_on()
    run.spread(4, 3)
    share.end()
    store(pad.at[:, pl.ds(TIME, ROWS), :], first_o)
    conv_layer(1)
    store(conv, conv_o)
    store(taps, taps_o)
    run.ready(3)
    store(v3, g3)
    conv_back_layer(1)
    conv_back_layer(0)
    total_sum.cross()
    local[4].wait()
    run.turn(4)
    loads[2].wait()
    run.ready(4)
    store(v4, g4)
    for i in range(2):
        ckv[i] = mm(codec[...], matrix_of(v4, i, n, 3 * n)).astype(LOW)
    store(ckv, ckv_o)
    total_sum.end()

    def norm_three(r):
        v = noisy[r, :] + summed[r, :].astype(F32)
        resid3[r, :] = v
        hat, _ = ln_stats(v)
        n3[r, :] = (hat * norms[8:9, :] + norms[9:10, :]).astype(LOW)

    each_rows(norm_three)
    store(resid3, resid3_o)
    store(n3, n3_o)
    for i in range(2):
        cq[i] = mm(n3[...], matrix_of(v4, i, 0, n)).astype(LOW)
    store(cq, cq_o)

    def cross_heads(r):
        found = []
        for i in range(2):
            part, logs_i = softmax_heads(
                cq[i, r, :], ckv[i, :, :n], ckv[i, :, n:], heads, score_scale, None
            )
            cross[i, r, :] = part
            found += logs_i
        logs_c[r, :] = jnp.concatenate(found, axis=1)

    each_rows(cross_heads)
    swap = exchange(
        2,
        mm_nt(cross[0], matrix_of(v4, 0, 3 * n, 4 * n)) + mm_nt(cross[1], matrix_of(v4, 1, 3 * n, 4 * n)),
    )
    store(cross, cross_o)
    store(logs_c, logs_c_o)
    swap.wait_recv()

    def finish_rows(r):
        out[r, :] = (resid3[r, :] + joined(2, r)).astype(LOW)

    each_rows(finish_rows)
    store(out, out_o)
    for c in stores:
        c.wait()
    net.close()


def forward_all(w_in, w_back, w_up, w_down, seg_col, seg_row, norms, side, embed, level, tokens, noises, codecs):
    n, hid = w_in.shape[2], w_up.shape[1]
    rows, features = w_in.shape[1], norms.shape[1]
    heads = 2 * n // HD
    ctok = codecs.shape[1]
    widths = [4 * n, 2 * hid, 10 * n, padded_width(9 * n), 4 * n]
    full = (ROWS, features)
    tall = ROWS + 2 * TIME
    kept = [
        (full, LOW), ((2, ROWS, 3 * n), LOW), ((2, ROWS, n), LOW), ((ROWS, heads), F32), (full, F32),
        (full, LOW), (full, F32), ((2, *full), LOW), ((2, ROWS, n), F32), ((2, tall, 3 * n), LOW),
        (full, F32), (full, LOW), ((2, ROWS, n), LOW), ((2, ctok, 2 * n), LOW), ((2, ROWS, n), LOW),
        ((ROWS, heads), F32), (full, LOW),
    ]
    groups = [(2 - (g in (2, 3)), 4, 2, rows, w) for g, w in enumerate(widths)]
    dma = pltpu.SemaphoreType.DMA
    copies = 3 * 13 + 7 + 4 + 3 + 2 + 4
    res = pl.pallas_call(
        forward_body,
        name="forward",
        in_specs=[spec_vm() for _ in range(10)] + [spec_any() for _ in range(3)],
        out_specs=[spec_any() for _ in groups] + [spec_vm()] + [spec_any() for _ in kept],
        out_shape=[jax.ShapeDtypeStruct(s, LOW) for s in groups]
        + [jax.ShapeDtypeStruct((1, 128), F32)]
        + [jax.ShapeDtypeStruct(s, t) for s, t in kept],
        scratch_shapes=[
            *[VM((rows, w), LOW) for w in widths], *[VM(s, LOW) for s in groups],
            VM(full, LOW), VM(full, LOW), VM((ctok, features), LOW), *[VM(s, t) for k, (s, t) in enumerate(kept) if k != 7],
            VM((2, tall, features), LOW), VM(full, F32), VM((3, *full), LOW), VM((3, *full), LOW),
            VM((2, *full), LOW), VM((2, ROWS // 2, features), LOW), VM((ROWS // 2, features), LOW),
            VM((ROWS // 2, features), LOW), VM(full, LOW),
            dma((3,)), dma((22,)), dma((5,)), dma((copies,)), dma((copies,)),
        ],
        compiler_params=pltpu.CompilerParams(
            collective_id=0, has_side_effects=True, vmem_limit_bytes=62 << 20
        ),
    )(w_in, w_back, w_up, w_down, seg_col, seg_row, norms, side, embed, level, tokens, noises, codecs)
    return res[:5], res[5], res[6:]


class Scatter:
    def __init__(self, net, d, over_x, bufs):
        self.net, self.d, self.k = net, d, over_x
        self.both = d.shape[0] == 2
        self.ly, self.r1, self.r2 = bufs[:3]
        if self.both:
            self.lx, self.corner = bufs[3:]
        self.x, self.core, self.z, self.y = place()
        self.to_x, self.to_y, _ = chip_peers()
        self.to_z1, self.to_z2 = z_peers()

    def raw(self):
        d, y, k, start = self.d, self.y, self.k, self.net.start
        if not self.both:
            self.first = [start(d.at[0, :, 1 - y], self.ly, self.to_y)]
            return
        self.first, self.turned = [], []
        if k > 0:
            self.turned.append(start(d.at[1, 0:k, 1 - y], self.corner.at[0:k], self.to_x))
        if k < 4:
            self.turned.append(start(d.at[1, k:4, 1 - y], self.corner.at[k:4], self.to_y))
        if k > 0:
            self.first.append(start(d.at[1, 0:k, y], self.lx.at[0:k], self.to_x))
        if k < 4:
            self.first.append(start(d.at[0, k:4, 1 - y], self.ly.at[k:4], self.to_y))

    def corners(self):
        d, y, k, start = self.d, self.y, self.k, self.net.start
        for c in self.turned:
            c.wait_recv()
        for r in range(4):
            mine = d.at[0, r, 1 - y] if r < k else d.at[1, r, y]
            add_rows(self.corner.at[r], [self.corner.at[r], mine])
        if k > 0:
            self.first.append(start(self.corner.at[0:k], self.ly.at[0:k], self.to_y))
        if k < 4:
            self.first.append(start(self.corner.at[k:4], self.lx.at[k:4], self.to_x))

    def lines(self):
        d, y, low = self.d, self.y, self.z % 2
        for c in self.first:
            c.wait_recv()
        for k in range(4):
            mine = d.at[0, k, y]
            add_rows(mine, [mine, self.ly.at[k]] + ([self.lx.at[k]] if self.both else []))
        self.ends = [
            self.net.start(d.at[0, 1 - low + 2 * h, y], self.r1.at[h], self.to_z1) for h in range(2)
        ]

    def half(self):
        d, y, z = self.d, self.y, self.z
        for h in range(2):
            self.ends[h].wait_recv()
            mine = d.at[0, z % 2 + 2 * h, y]
            add_rows(mine, [mine, self.r1.at[h]])
        self.last = self.net.start(d.at[0, (z + 2) % 4, y], self.r2, self.to_z2)

    def finish(self, target):
        self.last.wait_recv()
        add_rows(target, [self.d.at[0, self.z, self.y], self.r2])


class ScatterZ:
    def __init__(self, net, d, bufs):
        self.net, self.d, self.halves = net, d, d.shape[0]
        self.f1, self.f2, self.fy = bufs[:3]
        if self.halves == 2:
            self.pair, self.fx = bufs[3:]
        self.x, self.core, self.z, self.y = place()
        self.to_x, self.to_y, _ = chip_peers()
        self.to_z1, self.to_z2 = z_peers()

    def raw(self):
        low = self.z % 2
        self.ends = [
            self.net.start(self.d.at[:, 1 - low + 2 * h], self.f1.at[h], self.to_z1) for h in range(2)
        ]

    def half(self):
        low = self.z % 2
        for h in range(2):
            self.ends[h].wait_recv()
            for i in range(self.halves):
                for j in range(2):
                    mine = self.d.at[i, low + 2 * h, j]
                    add_rows(mine, [mine, self.f1.at[h, i, j]])
        self.next = self.net.start(self.d.at[:, (self.z + 2) % 4], self.f2, self.to_z2)

    def mid(self):
        self.next.wait_recv()
        for i in range(self.halves):
            for j in range(2):
                mine = self.d.at[i, self.z, j]
                add_rows(mine, [mine, self.f2.at[i, j]])
        self.over = self.net.start(self.d.at[:, self.z, 1 - self.y], self.fy, self.to_y)

    def turn(self):
        self.over.wait_recv()
        for i in range(2):
            add_rows(self.pair.at[i], [self.d.at[i, self.z, self.y], self.fy.at[i]])
        self.last = self.net.start(self.pair.at[1], self.fx, self.to_x)
        self.sent = [*self.ends, self.next, self.over]
        for c in self.sent:
            c.wait_send()

    def finish(self, target):
        if self.halves == 2:
            self.last.wait_recv()
            add_rows(target, [self.pair.at[0], self.fx])
        else:
            self.over.wait_recv()
            add_rows(target, [self.d.at[0, self.z, self.y], self.fy.at[0]])


class Totals:
    def __init__(self, net, values, got):
        self.net, self.values, self.got = net, values, got
        x, core, z, y = place()
        to_x, to_y, _ = chip_peers()
        self.peers = [device(x, 1 - core, z, y), to_x, to_y, *z_peers()]

    def start(self, k):
        self.copy = self.net.start(self.values.at[k], self.got.at[k], self.peers[k])

    def step(self, k):
        self.copy.wait_recv()
        self.values[k + 1] = self.values[k] + self.got[k]
        if k < 4:
            self.start(k + 1)


def backward_body(
    seg_col, seg_row, norms, side, embed_rows, sq, tokens, cots, codecs,
    g0, g1, g2, g3, g4, n1_h, qkv_h, mixed_h, logs_h, resid_h, n2_h, noisy_h, first_h, conv_h, taps_h,
    resid3_h, n3_h, cq_h, ckv_h, cross_h, logs_c_h, out_h,
    s0, s1, s2, s3, s4, grad_x, other_x, other_out, rows_o,
    d_c, d_t, d_o, d_m, wv, cot, codec, cq, ckv, cross, gm, logs, resid, nrm, grad, pad, taps, tapsg,
    conv, first, hb, hb2, acc, sent, got, part, near, far_out, far_in, summed,
    f1_c, f2_c, fy_c, pair_c, fx_c, ly_t, r1_t, r2_t, f1_o, f2_o, fy_o,
    ly_m, r1_m, r2_m, lx_m, co_m, ly_a, r1_a, r2_a, lx_a, co_a, values, values_in,
    stage, gsum, load_sem, out_sem, send, recv,
):
    n = cq.shape[2]
    features = norms.shape[1]
    width = features // GROUPS
    heads = n // HD
    hid = g1.shape[2] // 2
    block = d_m.shape[5] // 2
    ctok = codec.shape[0]
    score_scale = HD ** (-0.5)
    x, core, z, y = place()
    to_x, to_y, _ = chip_peers()
    sibling = device(x, 1 - core, z, y)
    net = Sender(send, recv)
    loads = []

    def load(src, dst):
        copy = pltpu.make_async_copy(src, dst, load_sem.at[len(loads)])
        copy.start()
        loads.append(copy)
        return copy

    def weights(ref, i):
        w = ref.shape[2]
        return load(ref.at[i], wv.at[i, :, pl.ds(0, w)])

    own = pl.ds(pl.multiple_of(x * ROWS, ROWS), ROWS)
    half = pl.ds(pl.multiple_of(core * (ROWS // 2), ROWS // 2), ROWS // 2)
    ready = [
        load(cots.at[own, :], cot), load(cross_h, cross), load(g4.at[0], wv.at[0, :, pl.ds(0, 4 * n)]),
        load(g4.at[1], wv.at[1, :, pl.ds(0, 4 * n)]), load(cq_h, cq), load(ckv_h, ckv),
        load(logs_c_h, logs), load(n3_h, nrm), load(codecs.at[x], codec),
    ]
    later = [load(resid3_h, resid), load(taps_h, taps), load(conv_h, conv), load(first_h, first)]
    meet([to_x, to_y, *z_peers(), sibling])
    out_far = net.start(out_h.at[half, :], other_out.at[half, :], to_x)
    sends = {}
    cro = ScatterZ(net, d_c, (f1_c, f2_c, fy_c, pair_c, fx_c))
    two = Scatter(net, d_t, 0, (ly_t, r1_t, r2_t))
    one = ScatterZ(net, d_o, (f1_o, f2_o, fy_o))
    mlp = [
        Scatter(net, d_m.at[q], 3, (ly_m.at[q], r1_m.at[q], r2_m.at[q], lx_m.at[q], co_m.at[q]))
        for q in range(hid // block)
    ]
    attn = Scatter(net, d_c, 2, (ly_a, r1_a, r2_a, lx_a, co_a))
    rows = values.at[0]
    totals = Totals(net, values, values_in)
    share = Share(net, pad, TIME)
    total_sum = FourSum(net, part, near, far_out, far_in, summed)

    def exchange(k, total):
        if k >= 2:
            sends[k - 2].wait_send()
        sent[k % 2] = total.astype(LOW)
        sends[k] = net.start(sent.at[k % 2], got.at[k % 2], sibling)

    def joined(k, r):
        return sent[k % 2, r, :].astype(F32) + got[k % 2, r, :].astype(F32)

    def put(ref, i, first, value):
        w = value.shape[1]
        ref[i, :, :, :, first : first + w] = value.astype(LOW).reshape(4, 2, -1, w)

    values[0] = jnp.zeros(values.shape[1:], F32)
    rows[10:11, 0:128] = sq[...]
    gsum[...] = jnp.zeros(gsum.shape, F32)
    for c in ready:
        c.wait()
    for i in (1, 0):
        gm[i] = mm(cot[...], wv[i, :, 3 * n : 4 * n]).astype(LOW)
    acc_kv = acc.at[0:ctok, :]
    acc_kv[...] = jnp.zeros((ctok, 4 * n), F32)

    def cross_heads(r):
        for i in range(2):
            rows_logs = [logs[r, heads * i + h : heads * i + h + 1] for h in range(heads)]
            gq, gk, gv = softmax_heads_back(
                cq[i, r, :], ckv[i, :, :n], ckv[i, :, n:], gm[i, r, :], rows_logs, heads, score_scale, None
            )
            cq[i, r, :] = gq.astype(LOW)
            acc_kv[:, 2 * n * i : 2 * n * (i + 1)] += jnp.concatenate([gk, gv], axis=1)

    each_rows(cross_heads)
    exchange(0, mm_nt(cq[1], wv[1, :, :n]) + mm_nt(cq[0], wv[0, :, :n]))
    for i in (1, 0):
        both = acc_kv[:, 2 * n * i : 2 * n * (i + 1)]
        low = jnp.concatenate([both[:, :n] * score_scale, both[:, n:]], axis=1).astype(LOW)
        put(d_c, i, 3 * n, mm_tn(cot[...], cross[i]))
        put(d_c, i, 0, mm_tn(nrm[...], cq[i]))
        put(d_c, i, n, mm_tn(codec[...], low))
    cro.raw()
    two_w = load(g3.at[0], wv.at[0, :, pl.ds(0, g3.shape[2])])
    one_w = load(g2.at[0], wv.at[1, :, pl.ds(0, g2.shape[2])])
    for i in range(2):
        pad[i, 0:TIME, :] = jnp.zeros((TIME, features), LOW)
        pad[i, TIME + ROWS :, :] = jnp.zeros((TIME, features), LOW)
    low_grad = pad.at[0, TIME : TIME + ROWS, :]
    other_grad = pad.at[1, TIME : TIME + ROWS, :]
    for c in later:
        c.wait()
    sends[0].wait_recv()

    def pull_three(r):
        back, gain, shift = ln_back(resid[r, :], norms[8:9, :], joined(0, r))
        v = cot[r, :].astype(F32) + back
        grad[r, :] = v
        low_grad[r, :] = v.astype(LOW)
        rows[8:9, :] += gain
        rows[9:10, :] += shift

    each_rows(pull_three)
    share.begin()
    tok_load = load(tokens.at[own, :], cot)
    noisy_load = load(noisy_h, resid)
    n2_load = load(n2_h, nrm)
    mats_n = group_mats(n, width)
    gn_rows = [None, None]
    two_w.wait()

    def conv_pull(i):
        q = None
        for a in range(3):
            term = mm(
                pad[i, TIME * (2 - a) : TIME * (2 - a) + ROWS, :], wv[0, :, 3 * n * a : 3 * n * (a + 1)]
            )
            q = term if q is None else q + term
        g = from_right(q[:, :n]) + q[:, n : 2 * n] + from_left(q[:, 2 * n :])
        c1 = conv[i]
        c1 = c1 - group_average(jnp.sum(c1, axis=0, keepdims=True), mats_n, width)
        var_n = group_average(jnp.sum(c1 * c1, axis=0, keepdims=True), mats_n, width)
        scale = lax.rsqrt(var_n + NORM_EPS)
        hat = c1 * scale
        gain = side[0:1, :]
        pre = hat * gain + side[1:2, :]
        gate = jax.nn.sigmoid(pre)
        g = g * gate * (1.0 + pre * (1.0 - gate))
        d_gain = jnp.sum(g * hat, axis=0, keepdims=True)
        d_shift = jnp.sum(g, axis=0, keepdims=True)
        gn_rows[i] = jnp.concatenate([d_gain, d_shift], axis=0)
        back = scale * (
            g * gain
            - group_average(d_shift * gain, mats_n, width)
            - hat * group_average(d_gain * gain, mats_n, width)
        )
        back = back.astype(LOW).astype(F32)
        gsum[i : i + 1, :] = jnp.sum(back, axis=0, keepdims=True)
        tapsg[i, 0:TIME, :] = jnp.zeros((TIME, 3 * n), LOW)
        tapsg[i, TIME + ROWS :, :] = jnp.zeros((TIME, 3 * n), LOW)
        tapsg[i, TIME : TIME + ROWS, :] = jnp.concatenate(
            [from_right(back), back, from_left(back)], axis=1
        ).astype(LOW)

    def first_pull(i):
        total = None
        for a in range(3):
            term = mm_nt(
                tapsg[i, TIME * (2 - a) : TIME * (2 - a) + ROWS, :], wv[1, :, 3 * n * a : 3 * n * (a + 1)]
            )
            total = term if total is None else total + term
        part[i] = total.astype(LOW)
        total_sum.begin(i)

    conv_pull(0)
    out_far.wait_recv()
    out_near = net.start(other_out.at[half, :], other_out.at[half, :], sibling)
    share.pass_on()
    share.end()
    conv_pull(1)
    one_w.wait()
    first_pull(1)
    first_pull(0)
    cro.half()
    total_sum.cross()
    for a in range(3):
        put(
            d_t, 0, 3 * n * a,
            mm_tn(low_grad[...], taps[0, TIME * a : TIME * a + ROWS, :])
            + mm_tn(other_grad[...], taps[1, TIME * a : TIME * a + ROWS, :]),
        )
    d_t[:, :, :, :, 9 * n :] = jnp.zeros((*d_t.shape[:4], d_t.shape[4] - 9 * n), LOW)
    two.raw()
    gn_both = gn_rows[0] + gn_rows[1]
    rows[6:8, :] = jnp.concatenate(
        [jnp.where(2 * x + core == s, gn_both, 0.0) for s in range(4)], axis=1
    )
    for a in range(3):
        window = pl.ds(TIME * (2 - a), ROWS)
        put(
            d_o, 0, 3 * n * a,
            mm_tn(first[0], tapsg[0, window, :]) + mm_tn(first[1], tapsg[1, window, :]),
        )
    put(
        d_o, 0, 9 * n,
        lax.dot_general(
            embed_rows[...], gsum[...], (((0,), (0,)), ((), ())), precision=HIGHEST_PRECISION,
            preferred_element_type=F32,
        ),
    )
    mlp_w = [weights(g1, i) for i in range(2)]
    total_sum.end()
    one.raw()

    noisy_load.wait()
    mats = group_mats(features, width)
    mean = group_average(jnp.sum(resid[...], axis=0, keepdims=True), mats, width)
    centre = resid[...] - mean
    var = group_average(jnp.sum(centre * centre, axis=0, keepdims=True), mats, width)
    scale = lax.rsqrt(var + NORM_EPS)
    gain, shift = norms[4:5, :], norms[5:6, :]

    def through_silu(r):
        hat = (resid[r, :] - mean) * scale
        pre = hat * gain + shift
        gate = jax.nn.sigmoid(pre)
        g = summed[r, :].astype(F32)
        g = g * gate * (1.0 + pre * (1.0 - gate))
        acc[r, :] = g
        rows[4:5, :] += jnp.sum(g * hat, axis=0, keepdims=True)
        rows[5:6, :] += jnp.sum(g, axis=0, keepdims=True)

    each_rows(through_silu)
    mean_shift = group_average(rows[5:6, :] * gain, mats, width)
    mean_gain = group_average(rows[4:5, :] * gain, mats, width)

    def pull_two(r):
        hat = (resid[r, :] - mean) * scale
        v = grad[r, :] + scale * (acc[r, :] * gain - mean_shift - hat * mean_gain)
        grad[r, :] = v
        low_grad[r, :] = v.astype(LOW)

    share.far.wait_send()
    each_rows(pull_two)
    resid_load = load(resid_h, resid)
    n2_load.wait()
    for c in mlp_w:
        c.wait()
    for q, group in enumerate(mlp):
        up, down = block * q, hid + block * q
        for i in (1, 0):
            pre = mm(nrm[...], wv[i, :, up : up + block])
            t, hidden = gelu_parts(pre)
            slope = gelu_slope(pre, t)
            hb[i] = hidden.astype(LOW)
            hb2[i] = (mm(low_grad[...], wv[i, :, down : down + block]) * slope).astype(LOW)
            term = mm_nt(hb2[i], wv[i, :, up : up + block])
            if q == 0 and i == 1:
                acc[...] = term
            else:
                acc[...] += term
        if q == len(mlp) - 1:
            exchange(1, acc[...])
        for i in (1, 0):
            put(d_m.at[q], i, block, mm_tn(low_grad[...], hb[i]))
            put(d_m.at[q], i, 0, mm_tn(nrm[...], hb2[i]))
        group.raw()
        if q == 1:
            cro.mid()
    attn_w = [weights(g0, i) for i in range(2)]
    tail_loads = [
        load(n1_h, nrm), load(qkv_h, tapsg.at[:, pl.ds(0, ROWS), :]), load(mixed_h, cross), load(logs_h, logs),
    ]
    resid_load.wait()
    sends[1].wait_recv()

    def pull_one(r):
        back, g_gain, g_shift = ln_back(resid[r, :], norms[2:3, :], joined(1, r))
        v = grad[r, :] + back
        grad[r, :] = v
        low_grad[r, :] = v.astype(LOW)
        rows[2:3, :] += g_gain
        rows[3:4, :] += g_shift

    each_rows(pull_one)
    for c in (*attn_w, *tail_loads):
        c.wait()
    for i in range(2):
        gm[i] = mm(low_grad[...], wv[i, :, 3 * n : 4 * n]).astype(LOW)
    acc[...] = jnp.zeros(acc.shape, F32)

    def self_heads(r):
        mask = seg_col[r, :] == seg_row[...]
        for i in range(2):
            rows_logs = [logs[r, heads * i + h : heads * i + h + 1] for h in range(heads)]
            gq, gk, gv = softmax_heads_back(
                tapsg[i, r, :n], tapsg[i, 0:ROWS, n : 2 * n], tapsg[i, 0:ROWS, 2 * n :], gm[i, r, :],
                rows_logs, heads, score_scale, mask,
            )
            taps[i, r, :n] = gq.astype(LOW)
            acc[:, 2 * n * i : 2 * n * (i + 1)] += jnp.concatenate([gk, gv], axis=1)

    each_rows(self_heads)
    one.half()
    cro.turn()
    mlp[0].corners()
    for i in (1, 0):
        both = acc[:, 2 * n * i : 2 * n * (i + 1)]
        taps[i, 0:ROWS, n:] = jnp.concatenate([both[:, :n] * score_scale, both[:, n:]], axis=1).astype(LOW)
        put(d_c, i, 3 * n, mm_tn(low_grad[...], cross[i]))
        put(d_c, i, 0, mm_tn(nrm[...], taps[i, 0:ROWS, :]))
    attn.raw()
    exchange(
        2, mm_nt(taps[1, 0:ROWS, :], wv[1, :, : 3 * n]) + mm_nt(taps[0, 0:ROWS, :], wv[0, :, : 3 * n])
    )
    two.lines()
    tok_load.wait()
    sends[2].wait_recv()

    def pull_zero(r):
        back, g_gain, g_shift = ln_back(cot[r, :].astype(F32), norms[0:1, :], joined(2, r))
        low_grad[r, :] = (grad[r, :] + back).astype(LOW)
        rows[0:1, :] += g_gain
        rows[1:2, :] += g_shift

    each_rows(pull_zero)
    store_x = pltpu.make_async_copy(low_grad, grad_x, out_sem.at[5])
    store_x.start()
    middle = pl.ds(pl.multiple_of(TIME + core * (ROWS // 2), TIME), ROWS // 2)
    x_far = net.start(pad.at[0, middle, :], other_x.at[half, :], to_x)
    rows[0:6, :] = jnp.where(core == 0, rows[0:6, :], 0.0)
    rows[8:10, :] = jnp.where(core == 0, rows[8:10, :], 0.0)
    totals.start(0)

    def deliver(group, k, out):
        w = out.shape[1]
        part = stage.at[:, pl.ds(0, w)]
        group.finish(part)
        copy = pltpu.make_async_copy(part, out, out_sem.at[k])
        copy.start()
        copy.wait()

    mlp[1].corners()
    mlp[0].lines()
    totals.step(0)
    mlp[2].corners()
    deliver(cro, 0, s4)
    totals.step(1)
    mlp[0].half()
    one.mid()
    mlp[1].lines()
    totals.step(2)
    deliver(mlp[0], 1, s1.at[0])
    mlp[2].lines()
    two.half()
    attn.corners()
    totals.step(3)
    x_far.wait_recv()
    x_near = net.start(other_x.at[half, :], other_x.at[half, :], sibling)
    mlp[1].half()
    deliver(one, 2, s2)
    attn.lines()
    mlp[2].half()
    totals.step(4)
    rows_o[...] = values[5]
    deliver(mlp[1], 3, s1.at[1])
    deliver(mlp[2], 4, s1.at[2])
    attn.half()
    deliver(two, 6, s3)
    deliver(attn, 7, s0)
    out_near.wait_recv()
    x_near.wait_recv()
    store_x.wait()
    wait_sends(net, [sends[0], share.far, *cro.sent])


def wait_sends(net, done):
    for copy in net.made:
        if all(copy is not d for d in done):
            copy.wait_send()


def backward_all(seg_col, seg_row, norms, side, embed_rows, sq, tokens, cots, codecs, gathered, kept):
    features = norms.shape[1]
    n = side.shape[1]
    rows = gathered[0].shape[3]
    widths = [g.shape[4] for g in gathered]
    hid = widths[1] // 2
    heads = 2 * n // HD
    ctok = codecs.shape[1]
    full = (ROWS, features)
    tall = ROWS + 2 * TIME
    ins = [
        seg_col, seg_row, norms, side, embed_rows, sq, tokens, cots, codecs,
        *[g.reshape(g.shape[0], features, -1) for g in gathered], *kept,
    ]
    dma = pltpu.SemaphoreType.DMA

    block = 256
    parts = hid // block

    def pieces(width, *counts):
        return [VM((*(k if isinstance(k, tuple) else (k,)), rows, width), LOW) for k in counts]

    copies = 2 + 3 + 2 + 2 + 4 + 5 + 5 + 4 + 4 + parts * 9 + 9
    res = pl.pallas_call(
        backward_body,
        name="backward",
        in_specs=[spec_vm() for _ in range(6)] + [spec_any() for _ in ins[6:]],
        out_specs=[spec_any() for _ in range(8)] + [spec_vm()],
        out_shape=[
            jax.ShapeDtypeStruct((parts, rows, 2 * block) if g == 1 else (rows, w), F32)
            for g, w in enumerate(widths)
        ]
        + [jax.ShapeDtypeStruct(full, LOW)] * 3
        + [jax.ShapeDtypeStruct((16, features), F32)],
        scratch_shapes=[
            VM((2, 4, 2, rows, 4 * n), LOW), VM((1, 4, 2, rows, widths[3]), LOW),
            VM((1, 4, 2, rows, 10 * n), LOW), VM((parts, 2, 4, 2, rows, 2 * block), LOW),
            VM((2, features, 10 * n), LOW), VM(full, LOW), VM((ctok, features), LOW),
            VM((2, ROWS, n), LOW), VM((2, ctok, 2 * n), LOW), VM((2, ROWS, n), LOW), VM((2, ROWS, n), LOW),
            VM((ROWS, heads), F32), VM(full, F32), VM(full, LOW), VM(full, F32),
            VM((2, tall, features), LOW), VM((2, tall, 3 * n), LOW), VM((2, tall, 3 * n), LOW),
            VM((2, ROWS, n), F32), VM((2, *full), LOW), VM((2, ROWS, 256), LOW), VM((2, ROWS, 256), LOW), VM(full, F32),
            VM((2, *full), LOW), VM((2, *full), LOW), VM((2, *full), LOW),
            VM((2, ROWS // 2, features), LOW), VM((ROWS // 2, features), LOW),
            VM((ROWS // 2, features), LOW), VM(full, LOW),
            *pieces(4 * n, (2, 2, 2), (2, 2), 2, 2), VM((rows, 4 * n), LOW),
            *pieces(widths[3], 4, 2), VM((rows, widths[3]), LOW),
            *pieces(10 * n, (2, 1, 2), (1, 2), 1),
            *pieces(2 * block, (parts, 4), (parts, 2), parts, (parts, 4), (parts, 4)),
            *pieces(4 * n, 4, 2), VM((rows, 4 * n), LOW), *pieces(4 * n, 4, 4),
            VM((6, 16, features), F32), VM((5, 16, features), F32),
            VM((rows, 10 * n), F32), VM((8, n), F32),
            dma((30,)), dma((8,)), dma((copies,)), dma((copies,)),
        ],
        compiler_params=pltpu.CompilerParams(
            collective_id=1, has_side_effects=True, vmem_limit_bytes=64 << 20
        ),
    )(*ins)
    return res[:5], res[5], res[6], res[7], res[8]


def adam_rows(w, g, m, v, decay_rate):
    m_new = MOMENT_DECAY * m + (1.0 - MOMENT_DECAY) * g
    v_new = MOMENT_DECAY * v + (1.0 - MOMENT_DECAY) * g * g
    correct = 1.0 - MOMENT_DECAY**STEP
    update = m_new / correct / (jnp.sqrt(v_new / correct) + ADAM_EPS) + decay_rate * w
    return m_new, v_new, update


def moments_body(*refs):
    sums, refs = refs[:5], refs[5:]
    w_in, w_back, w_up, w_down, m_in, m_back, m_up, m_down, v_in, v_back, v_up, v_down = refs[:12]
    nm_in, nm_back, nm_up, nm_down, nv_in, nv_back, nv_up, nv_down = refs[12:20]
    u_in, u_back, u_up, u_down, usq = refs[20:]
    n = w_in.shape[2]
    squares = [None] * 29

    def place_in(j, g):
        m, v, u = adam_rows(w_in[j], g, m_in[j], v_in[j], WEIGHT_DECAY)
        nm_in[j], nv_in[j], u_in[j] = m, v, u
        squares[j] = square_sum(u)

    def place_back(j, g):
        m, v, u = adam_rows(w_back[j], g.T, m_back[j], v_back[j], WEIGHT_DECAY)
        nm_back[j], nv_back[j], u_back[j] = m, v, u
        squares[16 + j] = square_sum(u)

    for g, (ins, backs) in GROUPS_OF.items():
        for k, j in enumerate(ins):
            place_in(j, sums[g][:, n * k : n * (k + 1)])
        for k, j in enumerate(backs, len(ins)):
            place_back(j, sums[g][:, n * k : n * (k + 1)])
    block = sums[1].shape[2] // 2
    up_sq, down_sq = [], []
    for q in range(w_up.shape[1] // block):
        cols = slice(block * q, block * (q + 1))
        m, v, u = adam_rows(w_up[:, cols], sums[1][q, :, :block], m_up[:, cols], v_up[:, cols], WEIGHT_DECAY)
        nm_up[:, cols], nv_up[:, cols], u_up[:, cols] = m, v, u
        up_sq.append(square_sum(u))
        m, v, u = adam_rows(
            w_down[:, cols], sums[1][q, :, block:], m_down[:, cols], v_down[:, cols], WEIGHT_DECAY
        )
        nm_down[:, cols], nv_down[:, cols], u_down[:, cols] = m, v, u
        down_sq.append(square_sum(u))
    squares[27] = sum(up_sq)
    squares[28] = sum(down_sq)
    usq[...] = row_of(squares)


def totals_body(usq, out, ring, ring_b, send, recv):
    mp, dp = lax.axis_index("mp"), lax.axis_index("dp")
    dp_peers = [((dp + k) % 8, mp) for k in range(1, 8)]
    mp_peers = [(dp, (mp + k) % 4) for k in range(1, 4)]
    ring[dp] = jnp.broadcast_to(usq[...], ring.shape[1:])
    meet(dp_peers + mp_peers)
    net = Sender(send, recv)
    copies = [net.start(ring.at[dp], ring.at[dp], p) for p in dp_peers]
    for c in copies:
        c.wait_recv()
    total = ring[0]
    for k in range(1, 8):
        total = total + ring[k]
    ring_b[mp] = total
    copies = [net.start(ring_b.at[mp], ring_b.at[mp], p) for p in mp_peers]
    for c in copies:
        c.wait_recv()
    out[...] = ring_b[0] + ring_b[1] + ring_b[2] + ring_b[3]
    net.close()


def apply_body(total, sums, w_in, w_back, w_up, w_down, u_in, u_back, u_up, u_down, norms, norm_m, norm_v, *outs):
    nw_in, nw_back, nw_up, nw_down, new_norm, new_nm, new_nv, lens = outs
    both = jnp.sqrt(jnp.concatenate([total[10:11, 0:128], sums[0:1, :]], axis=0))
    lens[...] = both[:, 0:29]
    trust = LEARN_RATE * (both[0:1, :] / jnp.where(both[1:2, :] == 0.0, 1.0, both[1:2, :]))
    lane = lax.broadcasted_iota(jnp.int32, (1, 128), 1)

    def trust_of(j):
        return jnp.sum(jnp.where(lane == j, trust, 0.0), axis=1, keepdims=True)

    for j in range(16):
        nw_in[j] = w_in[j] - trust_of(j) * u_in[j]
    for j in range(11):
        nw_back[j] = w_back[j] - trust_of(16 + j) * u_back[j]
    nw_up[...] = w_up[...] - trust_of(27) * u_up[...]
    nw_down[...] = w_down[...] - trust_of(28) * u_down[...]
    m, v, u = adam_rows(norms[...], total[0:10, :], norm_m[...], norm_v[...], 0.0)
    w = norms[...]
    row_trust = jnp.sqrt(jnp.sum(w * w, axis=1, keepdims=True)) / jnp.sqrt(
        jnp.sum(u * u, axis=1, keepdims=True)
    )
    new_norm[...] = w - LEARN_RATE * row_trust * u
    new_nm[...] = m
    new_nv[...] = v


def lamb_all(sums, rows, masters, moments, squares, norms, norm_m, norm_v):
    shapes = [(v.shape, F32) for v in masters]
    *mvu, usq = run_kernel(
        moments_body, "lamb_moments", [*sums, *masters, *moments, *squares],
        [*shapes, *shapes, *shapes, ((1, 128), F32)], [],
    )
    dma = pltpu.SemaphoreType.DMA
    usq_sum = pl.pallas_call(
        totals_body,
        name="norm_totals",
        in_specs=[spec_vm()],
        out_specs=spec_vm(),
        out_shape=jax.ShapeDtypeStruct((8, 128), F32),
        scratch_shapes=[VM((8, 8, 128), F32), VM((4, 8, 128), F32), dma((10,)), dma((10,))],
        compiler_params=pltpu.CompilerParams(collective_id=2, has_side_effects=True),
    )(usq)
    *weights, new_norm, new_nm, new_nv, lens = run_kernel(
        apply_body, "lamb_apply", [rows, usq_sum, *masters, *mvu[8:], norms, norm_m, norm_v],
        [*shapes, *[(norms.shape, F32)] * 3, ((2, 29), F32)], [],
    )
    return (*weights, *mvu[:8], new_norm, new_nm, new_nv, lens)


def fast_device(
    tokens,
    noise_field,
    codec_tokens,
    timesteps,
    segments,
    cotangent,
    w_in,
    w_back,
    w_up,
    w_down,
    m_in,
    m_back,
    m_up,
    m_down,
    v_in,
    v_back,
    v_up,
    v_down,
    norm_params,
    norm_m,
    norm_v,
):
    features = tokens.shape[1]
    n = w_in.shape[2]
    mp = lax.axis_index("mp")
    dp = lax.axis_index("dp")
    x, core, z, y = mp // 2, mp % 2, dp // 2, dp % 2

    steps = by_parity(x, timesteps[0], timesteps[1], 0)
    seg = pick(segments, x, 0)
    seg_col, seg_row = seg[:, None], seg[None, :]
    noise_level = jnp.sqrt((steps[0].astype(F32) + 1.0) / TSTEPS).reshape(1, 1)
    embed = jax.nn.silu(time_embedding(steps, features)).astype(LOW)
    embed_rows = jnp.broadcast_to(embed[:, None], (2, 8, features))
    embed_eight = jnp.pad(embed.astype(F32), ((0, 6), (0, 0)))
    side = lax.dynamic_slice(norm_params, (6, (2 * x + core) * n), (2, n))
    norms = norm_params

    gathered, weight_sq, kept = forward_all(
        w_in, w_back, w_up, w_down.T, seg_col, seg_row, norms, side, embed_rows, noise_level,
        tokens, noise_field, codec_tokens,
    )
    sums, own_x, other_x, other_out, rows = backward_all(
        seg_col, seg_row, norms, side, embed_eight, weight_sq, tokens, cotangent, codec_tokens, gathered, kept
    )
    out_rows = by_parity(x, kept[-1], other_out, 0).reshape(-1, features)
    grad_rows = by_parity(x, own_x, other_x, 0).reshape(-1, features).astype(F32)
    stepped = lamb_all(
        sums, rows, (w_in, w_back, w_up, w_down.T), (m_in, m_back, m_up, m_down.T),
        (v_in, v_back, v_up, v_down.T), norm_params, norm_m, norm_v,
    )
    stepped = [v.T if k in (3, 7, 11) else v for k, v in enumerate(stepped)]
    return (out_rows, grad_rows, *stepped)


def solution(mesh):
    per_device = fast_device if dict(mesh.shape) == {"dp": 8, "mp": 4} else generic_device
    placed = (
        P("dp", None),
        P("dp", None),
        P("dp", None, None),
        P("dp"),
        P("dp", None),
        P("dp", None),
        P(None, "dp", "mp"),
        P(None, "mp", "dp"),
        P("dp", "mp"),
        P("mp", "dp"),
        P(None, "dp", "mp"),
        P(None, "mp", "dp"),
        P("dp", "mp"),
        P("mp", "dp"),
        P(None, "dp", "mp"),
        P(None, "mp", "dp"),
        P("dp", "mp"),
        P("mp", "dp"),
        P(),
        P(),
        P(),
    )
    return jax.shard_map(
        per_device,
        mesh=mesh,
        in_specs=placed,
        out_specs=(
            P("dp", None),
            P("dp", None),
            P(None, "dp", "mp"),
            P(None, "mp", "dp"),
            P("dp", "mp"),
            P("mp", "dp"),
            P(None, "dp", "mp"),
            P(None, "mp", "dp"),
            P("dp", "mp"),
            P("mp", "dp"),
            P(None, "dp", "mp"),
            P(None, "mp", "dp"),
            P("dp", "mp"),
            P("mp", "dp"),
            P(),
            P(),
            P(),
            P(),
        ),
        check_vma=False,
    )
```

```python
from functools import partial
import math

import jax
import jax.numpy as jnp
from jax import lax
from jax.experimental import pallas as pl
from jax.experimental.pallas import tpu as pltpu
from jax.sharding import PartitionSpec as P

HD = 64
GROUPS = 32
FREQ = 8
TIME = 64
TSTEPS = 1000
STEP = 5


NORM_EPS = 1e-05
MOMENT_DECAY = 0.5
LEARN_RATE = 0.5
WEIGHT_DECAY = 0.01
ADAM_EPS = 1e-06
MASK_VALUE = -1e30
HIGHEST_PRECISION = lax.Precision.HIGHEST


def layer_norm(value_tensor, gain_row, shift_row):
    centre = value_tensor - jnp.mean(value_tensor, axis=-1, keepdims=True)
    spread = jnp.mean(centre * centre, axis=-1, keepdims=True)
    return centre * lax.rsqrt(spread + NORM_EPS) * gain_row + shift_row


def group_norm(value_tensor, gain_row, shift_row, group_width):
    seqs_here, length, channels = value_tensor.shape
    grouped = value_tensor.reshape(seqs_here, length, channels // group_width, group_width)
    centre = grouped - jnp.mean(grouped, axis=(1, 3), keepdims=True)
    spread = jnp.mean(centre * centre, axis=(1, 3), keepdims=True)
    normed = (centre * lax.rsqrt(spread + NORM_EPS)).reshape(seqs_here, length, channels)
    return normed * gain_row + shift_row


def norm_silu(value_tensor, gain_row, shift_row, group_width):
    return jax.nn.silu(group_norm(value_tensor, gain_row, shift_row, group_width))


def time_embedding(timesteps, features):
    half_width = features // 2
    freq_rates = jnp.exp(
        -math.log(10000.0) * jnp.arange(half_width, dtype=jnp.float32) / half_width
    )
    angles = timesteps.astype(jnp.float32)[:, None] * freq_rates[None, :]
    return jnp.concatenate([jnp.sin(angles), jnp.cos(angles)], axis=1)


def flatten_rows(value_tensor):
    return value_tensor.reshape(-1, value_tensor.shape[-1])


def project(values_low, weight_matrix):
    summed = jnp.dot(flatten_rows(values_low), weight_matrix, preferred_element_type=jnp.float32)
    return summed.reshape(values_low.shape[0], values_low.shape[1], weight_matrix.shape[1])


def back_project(grad_low, weight_matrix):
    summed = jnp.einsum(
        "ne,ce->nc", flatten_rows(grad_low), weight_matrix, preferred_element_type=jnp.float32
    )
    return summed.reshape(grad_low.shape[0], grad_low.shape[1], weight_matrix.shape[0])


def weight_grad(left_low, right_low):
    return jnp.einsum(
        "nc,ne->ce",
        flatten_rows(left_low),
        flatten_rows(right_low),
        preferred_element_type=jnp.float32,
    )


def padded_grid(grid_rows):
    seqs_here = grid_rows.shape[0]
    return jnp.pad(grid_rows.reshape(seqs_here, FREQ, TIME, -1), ((0, 0), (1, 1), (1, 1), (0, 0)))


def grid_window(padded, tap_index):
    row_off = tap_index // 3
    col_off = tap_index % 3
    return padded[:, row_off : row_off + FREQ, col_off : col_off + TIME, :].reshape(
        -1, padded.shape[3]
    )


def conv_grid(grid_rows, tap_weights, backward):
    seqs_here = grid_rows.shape[0]
    padded = padded_grid(grid_rows)
    out_width = tap_weights.shape[1] if backward else tap_weights.shape[2]
    summed = jnp.zeros((seqs_here * FREQ * TIME, out_width), jnp.float32)
    for tap_index in range(9):
        window = grid_window(padded, tap_index)
        if backward:
            summed = summed + jnp.einsum(
                "nc,dc->nd", window, tap_weights[8 - tap_index], preferred_element_type=jnp.float32
            )
        else:
            summed = summed + jnp.dot(
                window, tap_weights[tap_index], preferred_element_type=jnp.float32
            )
    return summed.reshape(seqs_here, FREQ * TIME, out_width)


def conv_weight_grad(grid_low, grad_low):
    padded = padded_grid(grid_low)
    grad_flat = flatten_rows(grad_low)
    tap_grads = []
    for tap_index in range(9):
        window = grid_window(padded, tap_index)
        tap_grads.append(
            jnp.einsum("nc,ne->ce", window, grad_flat, preferred_element_type=jnp.float32)
        )
    return jnp.stack(tap_grads)


def split_heads(rows_low):
    return rows_low.reshape(rows_low.shape[0], rows_low.shape[1], rows_low.shape[2] // HD, HD)


def head_scores(queries, key_rows, allowed, score_scale):
    scores = (
        jnp.einsum(
            "sqhd,skhd->shqk",
            split_heads(queries),
            split_heads(key_rows),
            preferred_element_type=jnp.float32,
        )
        * score_scale
    )
    if allowed is not None:
        scores = jnp.where(allowed[:, None], scores, MASK_VALUE)
    return scores


def attend(queries, key_rows, value_rows, allowed, score_scale):
    scores = head_scores(queries, key_rows, allowed, score_scale)
    highest = jnp.max(scores, axis=-1, keepdims=True)
    raised = jnp.exp(scores - highest)
    totals = jnp.sum(raised, axis=-1, keepdims=True)
    soft_low = (raised / totals).astype(jnp.bfloat16)
    mixed_rows = jnp.einsum(
        "shqk,skhd->sqhd", soft_low, split_heads(value_rows), preferred_element_type=jnp.float32
    )
    return (mixed_rows.reshape(queries.shape), highest + jnp.log(totals))


def attend_back(queries, key_rows, value_rows, allowed, score_scale, log_total, grad_mixed):
    scores = head_scores(queries, key_rows, allowed, score_scale)
    soft = jnp.exp(scores - log_total)
    grad_heads = split_heads(grad_mixed)
    grad_soft = jnp.einsum(
        "sqhd,skhd->shqk", grad_heads, split_heads(value_rows), preferred_element_type=jnp.float32
    )
    grad_values = jnp.einsum(
        "shqk,sqhd->skhd", soft.astype(jnp.bfloat16), grad_heads, preferred_element_type=jnp.float32
    )
    row_dot = jnp.sum(soft * grad_soft, axis=-1, keepdims=True)
    grad_scores = (soft * (grad_soft - row_dot)).astype(jnp.bfloat16)
    grad_queries = (
        jnp.einsum(
            "shqk,skhd->sqhd",
            grad_scores,
            split_heads(key_rows),
            preferred_element_type=jnp.float32,
        )
        * score_scale
    )
    grad_keys = (
        jnp.einsum(
            "shqk,sqhd->skhd", grad_scores, split_heads(queries), preferred_element_type=jnp.float32
        )
        * score_scale
    )
    return (
        grad_queries.reshape(queries.shape).astype(jnp.bfloat16),
        grad_keys.reshape(key_rows.shape).astype(jnp.bfloat16),
        grad_values.reshape(value_rows.shape).astype(jnp.bfloat16),
    )


def tensor_parallel_sum(term_rows):
    return lax.psum(term_rows, "mp")


def matrix_squares(first_stack, second_stack, up_rows, down_rows):
    return jnp.concatenate(
        [
            jnp.sum(first_stack * first_stack, axis=(1, 2)),
            jnp.sum(second_stack * second_stack, axis=(1, 2)),
            jnp.sum(up_rows * up_rows)[None],
            jnp.sum(down_rows * down_rows)[None],
        ]
    )


def adam_update(master, grad_rows, first_moment, second_moment, decay_rate):
    first_new = MOMENT_DECAY * first_moment + (1.0 - MOMENT_DECAY) * grad_rows
    second_new = MOMENT_DECAY * second_moment + (1.0 - MOMENT_DECAY) * grad_rows * grad_rows
    correct = 1.0 - MOMENT_DECAY**STEP
    update = first_new / correct / (jnp.sqrt(second_new / correct) + ADAM_EPS) + decay_rate * master
    return (first_new, second_new, update)


def generic_device(
    tokens,
    noise_field,
    codec_tokens,
    timesteps,
    segments,
    cotangent,
    w_in,
    w_back,
    w_up,
    w_down,
    m_in,
    m_back,
    m_up,
    m_down,
    v_in,
    v_back,
    v_up,
    v_down,
    norm_params,
    norm_m,
    norm_v,
):
    seqs_here, length = segments.shape
    features = tokens.shape[1]
    chans_here = w_in.shape[2]
    group_width = features // GROUPS
    score_scale = HD ** (-0.5)
    channel_start = lax.axis_index("mp") * chans_here
    lead_device = (lax.axis_index("mp") == 0).astype(jnp.float32)
    weight_sq = matrix_squares(w_in, w_back, w_up, w_down)
    full_in, full_back, complete_up_weight, full_down = (
        lax.all_gather(w_in.astype(jnp.bfloat16), "dp", axis=1, tiled=True),
        lax.all_gather(w_back.astype(jnp.bfloat16), "dp", axis=2, tiled=True),
        lax.all_gather(w_up.astype(jnp.bfloat16), "dp", axis=0, tiled=True),
        lax.all_gather(w_down.astype(jnp.bfloat16), "dp", axis=1, tiled=True),
    )
    resid_in = tokens.astype(jnp.float32).reshape(seqs_here, length, features)
    allowed = segments[:, :, None] == segments[:, None, :]
    normed_one_low = layer_norm(resid_in, norm_params[0], norm_params[1]).astype(jnp.bfloat16)
    queries = project(normed_one_low, full_in[0]).astype(jnp.bfloat16)
    key_rows = project(normed_one_low, full_in[1]).astype(jnp.bfloat16)
    value_rows = project(normed_one_low, full_in[2]).astype(jnp.bfloat16)
    mixed_rows, log_self = attend(queries, key_rows, value_rows, allowed, score_scale)
    mixed_low = mixed_rows.astype(jnp.bfloat16)
    resid_one = resid_in + tensor_parallel_sum(project(mixed_low, full_back[0]))
    normed_two_low = layer_norm(resid_one, norm_params[2], norm_params[3]).astype(jnp.bfloat16)
    hidden_pre = project(normed_two_low, complete_up_weight)
    hidden_low = jax.nn.gelu(hidden_pre).astype(jnp.bfloat16)
    resid_two = resid_one + tensor_parallel_sum(project(hidden_low, full_down))
    noise_level = jnp.sqrt((timesteps.astype(jnp.float32) + 1.0) / TSTEPS)
    noisy = resid_two + noise_level[:, None, None] * noise_field.astype(jnp.float32).reshape(
        seqs_here, length, features
    )
    first_low = norm_silu(noisy, norm_params[4], norm_params[5], group_width).astype(jnp.bfloat16)
    embed_low = jax.nn.silu(time_embedding(timesteps, features)).astype(jnp.bfloat16)
    time_shift = jnp.dot(embed_low, full_in[3], preferred_element_type=jnp.float32)
    conv_one = conv_grid(first_low, full_in[7:16], False) + time_shift[:, None, :]
    gain_six = lax.dynamic_slice_in_dim(norm_params[6], channel_start, chans_here)
    shift_six = lax.dynamic_slice_in_dim(norm_params[7], channel_start, chans_here)
    second_low = norm_silu(conv_one, gain_six, shift_six, group_width).astype(jnp.bfloat16)
    resid_three = noisy + tensor_parallel_sum(conv_grid(second_low, full_back[2:11], False))
    normed_three_low = layer_norm(resid_three, norm_params[8], norm_params[9]).astype(jnp.bfloat16)
    cross_queries = project(normed_three_low, full_in[4]).astype(jnp.bfloat16)
    cross_keys = project(codec_tokens, full_in[5]).astype(jnp.bfloat16)
    cross_values = project(codec_tokens, full_in[6]).astype(jnp.bfloat16)
    cross_mixed, log_cross = attend(cross_queries, cross_keys, cross_values, None, score_scale)
    cross_low = cross_mixed.astype(jnp.bfloat16)
    result = resid_three + tensor_parallel_sum(project(cross_low, full_back[1]))
    out_low = result.astype(jnp.bfloat16)
    grad_out = cotangent.astype(jnp.float32).reshape(seqs_here, length, features)
    grad_cross_low = grad_out.astype(jnp.bfloat16)
    grad_w_co = weight_grad(cross_low, grad_cross_low)
    grad_cross_mixed = back_project(grad_cross_low, full_back[1]).astype(jnp.bfloat16)
    grad_cq, grad_ck, grad_cv = attend_back(
        cross_queries, cross_keys, cross_values, None, score_scale, log_cross, grad_cross_mixed
    )
    grad_w_cq = weight_grad(normed_three_low, grad_cq)
    grad_w_ck = weight_grad(codec_tokens, grad_ck)
    grad_w_cv = weight_grad(codec_tokens, grad_cv)
    grad_normed_three = tensor_parallel_sum(back_project(grad_cq, full_in[4]))
    pull_three = jax.vjp(layer_norm, resid_three, norm_params[8], norm_params[9])[1]
    grad_part, grad_gain_eight, grad_shift_eight = pull_three(grad_normed_three)
    grad_three = grad_out + grad_part
    grad_conv_low = grad_three.astype(jnp.bfloat16)
    grad_w_conv_two = conv_weight_grad(second_low, grad_conv_low)
    grad_second = conv_grid(grad_conv_low, full_back[2:11], True)
    gather_second_moment = jax.vjp(
        partial(norm_silu, group_width=group_width), conv_one, gain_six, shift_six
    )[1]
    grad_conv_one, grad_gain_six, grad_shift_six = gather_second_moment(grad_second)
    grad_conv_one_low = grad_conv_one.astype(jnp.bfloat16)
    grad_w_time = jnp.einsum(
        "sd,sc->dc",
        embed_low.astype(jnp.float32),
        jnp.sum(grad_conv_one_low.astype(jnp.float32), axis=1),
        precision=HIGHEST_PRECISION,
    )
    grad_w_conv_one = conv_weight_grad(first_low, grad_conv_one_low)
    grad_first = tensor_parallel_sum(conv_grid(grad_conv_one_low, full_in[7:16], True))
    gather_first_moment = jax.vjp(
        partial(norm_silu, group_width=group_width), noisy, norm_params[4], norm_params[5]
    )[1]
    grad_part, grad_gain_four, grad_shift_four = gather_first_moment(grad_first)
    grad_two = grad_three + grad_part
    grad_mlp_low = grad_two.astype(jnp.bfloat16)
    grad_w_down = weight_grad(hidden_low, grad_mlp_low)
    grad_hidden = back_project(grad_mlp_low, full_down)
    grad_pre_low = jax.vjp(jax.nn.gelu, hidden_pre)[1](grad_hidden)[0].astype(jnp.bfloat16)
    up_weight_gradient = weight_grad(normed_two_low, grad_pre_low)
    grad_normed_two = tensor_parallel_sum(back_project(grad_pre_low, complete_up_weight))
    pull_two = jax.vjp(layer_norm, resid_one, norm_params[2], norm_params[3])[1]
    grad_part, grad_gain_two, grad_shift_two = pull_two(grad_normed_two)
    grad_one = grad_two + grad_part
    grad_attn_low = grad_one.astype(jnp.bfloat16)
    grad_w_out = weight_grad(mixed_low, grad_attn_low)
    grad_mixed = back_project(grad_attn_low, full_back[0]).astype(jnp.bfloat16)
    grad_q, grad_k, grad_v = attend_back(
        queries, key_rows, value_rows, allowed, score_scale, log_self, grad_mixed
    )
    grad_w_q = weight_grad(normed_one_low, grad_q)
    grad_w_k = weight_grad(normed_one_low, grad_k)
    grad_w_v = weight_grad(normed_one_low, grad_v)
    grad_normed_one = tensor_parallel_sum(
        back_project(grad_q, full_in[0])
        + back_project(grad_k, full_in[1])
        + back_project(grad_v, full_in[2])
    )
    pull_one = jax.vjp(layer_norm, resid_in, norm_params[0], norm_params[1])[1]
    grad_part, grad_gain_zero, grad_shift_zero = pull_one(grad_normed_one)
    grad_input = grad_one + grad_part
    grad_in_stack = jnp.concatenate(
        [
            jnp.stack([grad_w_q, grad_w_k, grad_w_v, grad_w_time, grad_w_cq, grad_w_ck, grad_w_cv]),
            grad_w_conv_one,
        ]
    )
    grad_back_stack = jnp.concatenate([jnp.stack([grad_w_out, grad_w_co]), grad_w_conv_two])
    summed_in, summed_back, summed_up, summed_down = (
        lax.psum_scatter(grad_in_stack, "dp", scatter_dimension=1, tiled=True),
        lax.psum_scatter(grad_back_stack, "dp", scatter_dimension=2, tiled=True),
        lax.psum_scatter(up_weight_gradient, "dp", scatter_dimension=0, tiled=True),
        lax.psum_scatter(grad_w_down, "dp", scatter_dimension=1, tiled=True),
    )
    shared_rows = (
        jnp.stack(
            [
                grad_gain_zero,
                grad_shift_zero,
                grad_gain_two,
                grad_shift_two,
                grad_gain_four,
                grad_shift_four,
            ]
        )
        * lead_device
    )
    group_rows = lax.dynamic_update_slice(
        jnp.zeros((2, features), jnp.float32),
        jnp.stack([grad_gain_six, grad_shift_six]),
        (0, channel_start),
    )
    last_rows = jnp.stack([grad_gain_eight, grad_shift_eight]) * lead_device
    norm_grad = lax.psum(jnp.concatenate([shared_rows, group_rows, last_rows]), ("dp", "mp"))
    m_in_new, v_in_new, upd_in = adam_update(w_in, summed_in, m_in, v_in, WEIGHT_DECAY)
    m_back_new, v_back_new, upd_back = adam_update(
        w_back, summed_back, m_back, v_back, WEIGHT_DECAY
    )
    m_up_new, v_up_new, upd_up = adam_update(w_up, summed_up, m_up, v_up, WEIGHT_DECAY)
    m_down_new, v_down_new, upd_down = adam_update(
        w_down, summed_down, m_down, v_down, WEIGHT_DECAY
    )
    update_sq = matrix_squares(upd_in, upd_back, upd_up, upd_down)
    weight_total, update_total = lax.psum((weight_sq, update_sq), ("dp", "mp"))
    weight_len = jnp.sqrt(weight_total)
    update_len = jnp.sqrt(update_total)
    trust = weight_len / update_len
    new_in = w_in - LEARN_RATE * trust[0:16, None, None] * upd_in
    new_back = w_back - LEARN_RATE * trust[16:27, None, None] * upd_back
    new_up = w_up - LEARN_RATE * trust[27] * upd_up
    new_down = w_down - LEARN_RATE * trust[28] * upd_down
    norm_m_new, norm_v_new, upd_norm = adam_update(norm_params, norm_grad, norm_m, norm_v, 0.0)
    row_trust = jnp.sqrt(jnp.sum(norm_params * norm_params, axis=1)) / jnp.sqrt(
        jnp.sum(upd_norm * upd_norm, axis=1)
    )
    new_norm = norm_params - LEARN_RATE * row_trust[:, None] * upd_norm
    matrix_norms = jnp.stack([weight_len, update_len])
    out_rows = out_low.reshape(seqs_here * length, features)
    grad_rows = grad_input.reshape(seqs_here * length, features)
    return (
        out_rows,
        grad_rows,
        new_in,
        new_back,
        new_up,
        new_down,
        m_in_new,
        m_back_new,
        m_up_new,
        m_down_new,
        v_in_new,
        v_back_new,
        v_up_new,
        v_down_new,
        new_norm,
        norm_m_new,
        norm_v_new,
        matrix_norms,
    )


CORE_SWAP = [(i, i ^ 1) for i in range(4)]
X_SWAP = [(i, i ^ 2) for i in range(4)]
LOW = jnp.bfloat16
F32 = jnp.float32


def swap_core(v):
    return lax.ppermute(v, "mp", CORE_SWAP)


def swap_x(v):
    return lax.ppermute(v, "mp", X_SWAP)


def by_parity(flag, own, other, axis):
    first = jnp.where(flag == 0, own, other)
    second = jnp.where(flag == 0, other, own)
    return jnp.stack([first, second], axis=axis)


def pick(v, index, axis):
    return lax.dynamic_index_in_dim(v, index, axis, keepdims=False)


def ln_stats(v):
    centre = v - jnp.mean(v, axis=-1, keepdims=True)
    scale = lax.rsqrt(jnp.mean(centre * centre, axis=-1, keepdims=True) + NORM_EPS)
    return centre * scale, scale


def ln_back(v, gain, grad):
    hat, scale = ln_stats(v)
    pulled = grad * gain
    back = scale * (
        pulled
        - jnp.mean(pulled, axis=-1, keepdims=True)
        - hat * jnp.mean(pulled * hat, axis=-1, keepdims=True)
    )
    return back, jnp.sum(grad * hat, axis=0, keepdims=True), jnp.sum(grad, axis=0, keepdims=True)


def mm(a, b):
    return lax.dot_general(a, b, (((1,), (0,)), ((), ())), preferred_element_type=F32)


def mm_nt(a, b):
    return lax.dot_general(a, b, (((1,), (1,)), ((), ())), preferred_element_type=F32)


def mm_tn(a, b):
    return lax.dot_general(a, b, (((0,), (0,)), ((), ())), preferred_element_type=F32)


ANY = pl.ANY
VM = pltpu.VMEM
ROWS = 512
STEP_ROWS = 128


def spec_any():
    return pl.BlockSpec(memory_space=pl.ANY)


def spec_vm():
    return pl.BlockSpec(memory_space=pltpu.VMEM)


def run_kernel(body, name, ins, outs, scratch, hbm=(), flops=0):
    in_specs = [spec_any() if k in hbm else spec_vm() for k in range(len(ins))]
    moved = sum(v.size * v.dtype.itemsize for v in ins) + sum(
        math.prod(s) * jnp.dtype(t).itemsize for s, t in outs
    )
    return pl.pallas_call(
        body,
        name=name,
        in_specs=in_specs,
        out_specs=[spec_vm() for _ in outs],
        out_shape=[jax.ShapeDtypeStruct(s, t) for s, t in outs],
        scratch_shapes=scratch,
        compiler_params=pltpu.CompilerParams(vmem_limit_bytes=56 << 20),
        cost_estimate=pl.CostEstimate(flops=flops, bytes_accessed=moved, transcendentals=0),
    )(*ins)


def each_rows(fn, total=ROWS, step=STEP_ROWS):
    def body(k, carry):
        fn(pl.ds(pl.multiple_of(k * step, step), step))
        return carry

    lax.fori_loop(0, total // step, body, 0)


def start_copies(pairs, sems):
    copies = [pltpu.make_async_copy(a, b, sems.at[k]) for k, (a, b) in enumerate(pairs)]
    for c in copies:
        c.start()
    return copies


def group_mats(channels, width):
    count = channels // width
    r = lax.broadcasted_iota(jnp.int32, (channels, count), 0)
    c = lax.broadcasted_iota(jnp.int32, (channels, count), 1) * width
    down = ((r >= c) & (r < c + width)).astype(F32)
    r = lax.broadcasted_iota(jnp.int32, (count, channels), 1)
    c = lax.broadcasted_iota(jnp.int32, (count, channels), 0) * width
    up = ((r >= c) & (r < c + width)).astype(F32)
    return down, up


def exact_dot(a, b):
    return jnp.dot(a, b, precision=HIGHEST_PRECISION, preferred_element_type=F32)


def group_average(row, mats, width):
    wide = jnp.broadcast_to(row, (8, row.shape[1]))
    return exact_dot(exact_dot(wide, mats[0]) * (1.0 / (width * ROWS)), mats[1])[0:1]


def gelu_parts(v):
    k = math.sqrt(2.0 / math.pi)
    t = jnp.tanh(k * (v + 0.044715 * (v * v * v)))
    return t, 0.5 * v * (1.0 + t)


def gelu_slope(v, t):
    k = math.sqrt(2.0 / math.pi)
    return 0.5 * (1.0 + t) + 0.5 * v * (1.0 - t * t) * (k * (1.0 + 3 * 0.044715 * (v * v)))


def column_of(shape):
    return lax.broadcasted_iota(jnp.int32, shape, 0) % TIME


def from_left(v):
    return jnp.where(column_of(v.shape) == 0, 0.0, pltpu.roll(v, 1, 0))


def from_right(v):
    return jnp.where(column_of(v.shape) == TIME - 1, 0.0, pltpu.roll(v, v.shape[0] - 1, 0))


def softmax_heads(q, k, v, heads, score_scale, mask):
    mixed, logs = [], []
    for h in range(heads):
        s = mm_nt(q[:, HD * h : HD * (h + 1)], k[:, HD * h : HD * (h + 1)]) * score_scale
        if mask is not None:
            s = jnp.where(mask, s, MASK_VALUE)
        top = jnp.max(s, axis=1, keepdims=True)
        e = jnp.exp(s - top)
        total = jnp.sum(e, axis=1, keepdims=True)
        soft = (e * (1.0 / total)).astype(LOW)
        mixed.append(mm(soft, v[:, HD * h : HD * (h + 1)]))
        logs.append(top + jnp.log(total))
    return jnp.concatenate(mixed, axis=1).astype(LOW), logs


def softmax_heads_back(q, k, v, g, logs, heads, score_scale, mask):
    dq, dk, dv = [], [], []
    for h in range(heads):
        cols = slice(HD * h, HD * (h + 1))
        s = mm_nt(q[:, cols], k[:, cols]) * score_scale
        if mask is not None:
            s = jnp.where(mask, s, MASK_VALUE)
        soft = jnp.exp(s - logs[h])
        gs = mm_nt(g[:, cols], v[:, cols])
        dv.append(mm_tn(soft.astype(LOW), g[:, cols]))
        dot = jnp.sum(soft * gs, axis=1, keepdims=True)
        ds = (soft * (gs - dot)).astype(LOW)
        dq.append(mm(ds, k[:, cols]) * score_scale)
        dk.append(mm_tn(ds, q[:, cols]))
    return [jnp.concatenate(d, axis=1) for d in (dq, dk, dv)]


MESH_IDS = pl.DeviceIdType.MESH


def place():
    mp = lax.axis_index("mp")
    dp = lax.axis_index("dp")
    return mp // 2, mp % 2, dp // 2, dp % 2


def device(x, core, z, y):
    return (2 * z + y, 2 * x + core)


def meet(peers):
    barrier = pltpu.get_barrier_semaphore()
    for peer in peers:
        pl.semaphore_signal(barrier, inc=1, device_id=peer, device_id_type=MESH_IDS)
    pl.semaphore_wait(barrier, len(peers))


def chip_peers():
    x, core, z, y = place()
    along_z = [device(x, core, (z + k) % 4, y) for k in range(1, 4)]
    return device(1 - x, core, z, y), device(x, core, z, 1 - y), along_z


def own_segments(segments, x, seg_col):
    row = jnp.where(x == 0, segments[0:1, :], segments[1:2, :]).astype(F32)
    seg_col[...] = jnp.broadcast_to(row, (8, row.shape[1])).T[:, 0:1]
    return row


def own_channels(norms, which, n):
    return sum(jnp.where(which == s, norms[6:8, n * s : n * (s + 1)], 0.0) for s in range(4))


class Sender:
    def __init__(self, send, recv):
        self.send, self.recv, self.made = send, recv, []

    def start(self, src, dst, peer):
        k = len(self.made)
        copy = pltpu.make_async_remote_copy(
            src_ref=src, dst_ref=dst, send_sem=self.send.at[k], recv_sem=self.recv.at[k],
            device_id=peer, device_id_type=MESH_IDS,
        )
        copy.start()
        self.made.append(copy)
        return copy

    def reserve(self, count, item):
        base = len(self.made)
        self.made += [item] + [None] * (count - 1)
        return base

    def close(self):
        for copy in self.made:
            if copy is not None:
                copy.wait_send()


class Exchange:
    def __init__(self, net, sent, got, peer):
        self.net, self.sent, self.got, self.peer = net, sent, got, peer
        self.base = net.reserve(ROWS // STEP_ROWS, self)

    def copy(self, k):
        r = pl.ds(pl.multiple_of(k * STEP_ROWS, STEP_ROWS), STEP_ROWS)
        return pltpu.make_async_remote_copy(
            src_ref=self.sent.at[r, :], dst_ref=self.got.at[r, :],
            send_sem=self.net.send.at[self.base + k], recv_sem=self.net.recv.at[self.base + k],
            device_id=self.peer, device_id_type=MESH_IDS,
        )

    def give(self, fn):
        def body(k, carry):
            r = pl.ds(pl.multiple_of(k * STEP_ROWS, STEP_ROWS), STEP_ROWS)
            self.sent[r, :] = fn(r).astype(LOW)
            self.copy(k).start()
            return carry

        lax.fori_loop(0, ROWS // STEP_ROWS, body, 0)

    def take(self, fn):
        def body(k, carry):
            r = pl.ds(pl.multiple_of(k * STEP_ROWS, STEP_ROWS), STEP_ROWS)
            self.copy(k).wait_recv()
            fn(r, self.sent[r, :].astype(F32) + self.got[r, :].astype(F32))
            return carry

        lax.fori_loop(0, ROWS // STEP_ROWS, body, 0)

    def wait_send(self):
        for k in range(ROWS // STEP_ROWS):
            self.copy(k).wait_send()


def padded_width(w):
    return -(-w // 128) * 128


def pack_piece(g, w_in, w_back, w_up, w_down, piece):
    n = w_in.shape[2]
    if g == 1:
        hid = w_up.shape[1]
        piece[:, :hid] = w_up[...].astype(LOW)
        piece[:, hid:] = w_down[...].astype(LOW)
        return
    ins, backs = GROUPS_OF[g]
    cols = [w_in[j] for j in ins] + [w_back[j].T for j in backs]
    spare = piece.shape[1] - n * len(cols)
    if spare:
        cols.append(jnp.zeros((piece.shape[0], spare), F32))
    for k in range(0, len(cols), 2):
        pair = cols[k : k + 2]
        both = pair[0] if len(pair) == 1 else jnp.concatenate(pair, axis=1)
        piece[:, n * k : n * k + both.shape[1]] = both.astype(LOW)


GROUPS_OF = {
    0: ([0, 1, 2], [0]),
    2: ([*range(7, 16), 3], []),
    3: ([], [*range(2, 11)]),
    4: ([4, 5, 6], [1]),
}


def row_of(values):
    lane = lax.broadcasted_iota(jnp.int32, (1, 128), 1)
    row = jnp.zeros((1, 128), F32)
    for j, v in enumerate(values):
        row = row + jnp.where(lane == j, v, 0.0)
    return row


def square_sum(v):
    return jnp.sum(jnp.sum(v * v, axis=1, keepdims=True), axis=0, keepdims=True)


def add_rows(target, terms, step=16):
    def body(k, carry):
        r = pl.ds(pl.multiple_of(k * step, step), step)
        total = terms[0][r, :].astype(F32)
        for t in terms[1:]:
            total = total + t[r, :].astype(F32)
        target[r, :] = total.astype(target.dtype)
        return carry

    lax.fori_loop(0, target.shape[0] // step, body, 0)


def z_peers():
    x, core, z, y = place()
    return device(x, core, z + 1 - 2 * (z % 2), y), device(x, core, (z + 2) % 4, y)


class Gather:
    def __init__(self, pieces, outs, over_x, y_first, net):
        self.pieces, self.outs, self.over_x, self.y_first, self.net = pieces, outs, over_x, y_first, net
        self.x, self.core, self.z, self.y = place()
        self.to_x, self.to_y, _ = chip_peers()
        self.to_z1, self.to_z2 = z_peers()
        near = self.z + 1 - 2 * (self.z % 2)
        self.sources = (near, (self.z + 2) % 4, (near + 2) % 4)
        self.lines, self.planes, self.corners = {}, {}, {}

    def line(self, g):
        if g in self.y_first:
            self.planes[g][0].wait_recv()
            src = dst = self.outs[g].at[0, self.z]
        else:
            src, dst = self.pieces[g], self.outs[g].at[0, self.z, self.y]
        self.lines[g] = [self.net.start(src, dst, peer) for peer in (self.to_z1, self.to_z2)]

    def relay(self, g):
        self.lines[g][1].wait_recv()
        out, far = self.outs[g], self.sources[1]
        src = out.at[0, far] if g in self.y_first else out.at[0, far, self.y]
        self.lines[g].append(self.net.start(src, src, self.to_z1))

    def own(self, g):
        z, y, out = self.z, self.y, self.outs[g]
        self.planes[g] = [self.net.start(self.pieces[g], out.at[0, z, y], self.to_y)]
        if out.shape[0] == 2:
            self.planes[g].append(self.net.start(self.pieces[g], out.at[1, z, y], self.to_x))

    def spread(self, g, k):
        if k != 2:
            self.lines[g][k - 1].wait_recv()
        out, far = self.outs[g], self.sources[k - 1]
        src = out.at[0, far, self.y]
        self.planes[g].append(self.net.start(src, src, self.to_y))
        if out.shape[0] == 2:
            self.planes[g].append(self.net.start(src, out.at[1, far, self.y], self.to_x))

    def turn(self, g):
        for c in self.planes[g]:
            c.wait_recv()
        out, y, k = self.outs[g], self.y, self.over_x[g]
        self.corners[g] = []
        if k > 0:
            self.corners[g].append(
                self.net.start(out.at[0, 0:k, 1 - y], out.at[1, 0:k, 1 - y], self.to_x)
            )
        if k < 4:
            self.corners[g].append(
                self.net.start(out.at[1, k:4, y], out.at[1, k:4, y], self.to_y)
            )

    def ready(self, g):
        if g in self.y_first:
            last = (self.lines[g][0], self.lines[g][2])
        else:
            last = self.corners[g] if self.outs[g].shape[0] == 2 else self.planes[g]
        for c in last:
            c.wait_recv()


class FourSum:
    def __init__(self, net, part, near, far_out, far_in, done):
        self.net, self.part, self.near, self.done = net, part, near, done
        self.far_out, self.far_in = far_out, far_in
        x, core, z, y = place()
        count = ROWS // 2
        self.mine = pl.ds(pl.multiple_of(core * count, count), count)
        self.theirs = pl.ds(pl.multiple_of((1 - core) * count, count), count)
        self.sibling, self.across = device(x, 1 - core, z, y), device(1 - x, core, z, y)

    def begin(self, i):
        copy = self.net.start(self.part.at[i, self.theirs, :], self.near.at[i], self.sibling)
        if i == 1:
            self.other = copy
        else:
            self.own = copy

    def cross(self):
        self.other.wait_recv()
        add_rows(self.far_out, [self.part.at[1, self.mine, :], self.near.at[1]], 64)
        self.far = self.net.start(self.far_out, self.far_in, self.across)

    def end(self):
        self.own.wait_recv()
        self.far.wait_recv()
        mine = self.done.at[self.mine, :]
        add_rows(mine, [self.part.at[0, self.mine, :], self.near.at[0], self.far_in], 64)
        self.last = self.net.start(mine, mine, self.sibling)
        self.last.wait_recv()


class Share:
    def __init__(self, net, both, first):
        self.net, self.both = net, both
        x, core, z, y = place()
        count = ROWS // 2
        self.mine = pl.ds(pl.multiple_of(first + core * count, TIME), count)
        self.sibling, self.across = device(x, 1 - core, z, y), device(1 - x, core, z, y)

    def begin(self):
        self.far = self.net.start(
            self.both.at[0, self.mine, :], self.both.at[1, self.mine, :], self.across
        )

    def pass_on(self):
        self.far.wait_recv()
        rows = self.both.at[1, self.mine, :]
        self.near = self.net.start(rows, rows, self.sibling)

    def end(self):
        self.near.wait_recv()


def matrix_of(ref, i, first, last):
    block = ref[i, :, :, :, first:last]
    return block.reshape(-1, last - first)


def forward_body(
    w_in, w_back, w_up, w_down, segments, norms, steps, tokens, noises, codecs,
    g0, g1, g2, g3, g4, sq, n1_o, qkv_o, mixed_o, logs_o, resid_o, n2_o, noisy_o, first_o, conv_o,
    taps_o, resid3_o, n3_o, cq_o, ckv_o, cross_o, logs_c_o, out_o,
    p0, p1, p2, p3, p4, v0, v1, v2, v3, v4, tok, noise, codec, n1, qkv, mixed, logs, resid, n2,
    noisy, conv, taps, resid3, n3, cq, ckv, cross, logs_c, out, pad, acc, sent, got,
    part, near, far_out, far_in, summed, seg_col,
    in_sem, out_sem, own_sem, send, recv,
):
    pieces, held, kept = (p0, p1, p2, p3, p4), (v0, v1, v2, v3, v4), (g0, g1, g2, g3, g4)
    n = mixed.shape[2]
    hid = w_up.shape[1]
    features = norms.shape[1]
    width = features // GROUPS
    heads = n // HD
    score_scale = HD ** (-0.5)
    net = Sender(send, recv)
    run = Gather(pieces, held, (2, 4, 0, 0, 0), (3,), net)
    share = Share(net, pad, TIME)
    total_sum = FourSum(net, part, near, far_out, far_in, summed)
    x, core, z, y = place()
    sibling = device(x, 1 - core, z, y)
    loads = [
        pltpu.make_async_copy(tokens.at[pl.ds(pl.multiple_of(x * ROWS, ROWS), ROWS), :], tok, in_sem.at[0]),
        pltpu.make_async_copy(noises.at[pl.ds(pl.multiple_of(x * ROWS, ROWS), ROWS), :], noise, in_sem.at[1]),
        pltpu.make_async_copy(codecs.at[x], codec, in_sem.at[2]),
    ]
    for c in loads:
        c.start()
    stores = []

    def store(src, dst):
        copy = pltpu.make_async_copy(src, dst, out_sem.at[len(stores)])
        copy.start()
        stores.append(copy)

    def pack(g):
        pack_piece(g, w_in, w_back, w_up, w_down, pieces[g])
        copy = pltpu.make_async_copy(pieces[g], held[g].at[0, z, y], own_sem.at[g])
        copy.start()
        return copy

    side = own_channels(norms, 2 * x + core, n)
    level = steps[2:3, 0:1]
    local = [pack(0)]
    meet([run.to_x, run.to_y, *z_peers(), sibling])
    run.line(0)
    run.own(0)
    local.append(pack(1))
    run.line(1)
    run.own(1)
    local += [pack(2), pack(3), pack(4)]
    loads[0].wait()

    def norm_one(r):
        hat, _ = ln_stats(tok[r, :].astype(F32))
        n1[r, :] = (hat * norms[0:1, :] + norms[1:2, :]).astype(LOW)

    each_rows(norm_one)
    store(n1, n1_o)
    run.relay(0)
    run.spread(0, 1)
    run.spread(0, 2)
    run.line(2)
    run.own(3)
    run.spread(0, 3)
    run.own(2)
    sq[...] = row_of(
        [square_sum(w_in[j]) for j in range(16)] + [square_sum(w_back[j]) for j in range(11)]
        + [square_sum(w_up[...]), square_sum(w_down[...])]
    )
    run.relay(1)
    run.spread(1, 1)
    run.spread(1, 2)
    run.turn(0)
    local[0].wait()
    local[3].wait()
    run.line(3)
    run.ready(0)
    store(v0, g0)
    for i in range(2):
        qkv[i] = mm(n1[...], matrix_of(v0, i, 0, 3 * n)).astype(LOW)
    store(qkv, qkv_o)
    run.spread(1, 3)

    seg_row = own_segments(segments, x, seg_col)

    def self_heads(r):
        mask = seg_col[r, :] == seg_row
        found = []
        for i in range(2):
            part, logs_i = softmax_heads(
                qkv[i, r, 0:n], qkv[i, :, n : 2 * n], qkv[i, :, 2 * n : 3 * n], heads, score_scale, mask
            )
            mixed[i, r, :] = part
            found += logs_i
        logs[r, :] = jnp.concatenate(found, axis=1)
        return mm_nt(mixed[0, r, :], matrix_of(v0, 0, 3 * n, 4 * n)) + mm_nt(
            mixed[1, r, :], matrix_of(v0, 1, 3 * n, 4 * n)
        )

    swap = Exchange(net, sent.at[0], got.at[0], sibling)
    swap.give(self_heads)
    store(mixed, mixed_o)
    store(logs, logs_o)
    run.relay(2)
    run.spread(2, 1)
    run.spread(2, 2)
    run.turn(1)
    run.own(4)
    run.line(4)

    def norm_two(r, both):
        v = tok[r, :].astype(F32) + both
        resid[r, :] = v
        hat, _ = ln_stats(v)
        n2[r, :] = (hat * norms[2:3, :] + norms[3:4, :]).astype(LOW)

    swap.take(norm_two)
    store(resid, resid_o)
    store(n2, n2_o)
    run.spread(2, 3)
    run.relay(3)
    local[1].wait()
    run.ready(1)
    store(v1, g1)
    block = 256
    for i in range(2):
        for b in range(hid // block):
            pre = mm(n2[...], matrix_of(v1, i, block * b, block * (b + 1)))
            low = gelu_parts(pre)[1].astype(LOW)
            term = mm_nt(low, matrix_of(v1, i, hid + block * b, hid + block * (b + 1)))
            if i == 0 and b == 0:
                acc[...] = term
            else:
                acc[...] += term
    swap = Exchange(net, sent.at[1], got.at[1], sibling)
    swap.give(lambda r: acc[r, :])
    loads[1].wait()

    def add_noise(r, both):
        noisy[r, :] = resid[r, :] + both + level * noise[r, :].astype(F32)

    swap.take(add_noise)
    store(noisy, noisy_o)
    mats = group_mats(features, width)
    mats_n = group_mats(n, width)
    mean = group_average(jnp.sum(noisy[...], axis=0, keepdims=True), mats, width)
    centre = noisy[...] - mean
    var = group_average(jnp.sum(centre * centre, axis=0, keepdims=True), mats, width)
    scale = lax.rsqrt(var + NORM_EPS) * norms[4:5, :]
    for i in range(2):
        pad[i, 0:TIME, :] = jnp.zeros((TIME, features), LOW)
        pad[i, TIME + ROWS :, :] = jnp.zeros((TIME, features), LOW)

    def act(k, carry):
        r = pl.ds(pl.multiple_of(k * STEP_ROWS, STEP_ROWS), STEP_ROWS)
        v = (noisy[r, :] - mean) * scale + norms[5:6, :]
        moved = pl.ds(pl.multiple_of(TIME + k * STEP_ROWS, TIME), STEP_ROWS)
        pad[0, moved, :] = (v * jax.nn.sigmoid(v)).astype(LOW)
        return carry

    lax.fori_loop(0, ROWS // STEP_ROWS, act, 0)
    share.begin()
    run.relay(4)
    local[2].wait()
    run.ready(2)
    store(v2, g2)

    def conv_layer(i):
        q = None
        for a in range(3):
            term = mm(
                pad[i, TIME * a : TIME * a + ROWS, :], matrix_of(v2, 0, 3 * n * a, 3 * n * (a + 1))
            )
            q = term if q is None else q + term
        embed = jnp.broadcast_to(steps[i : i + 1, :], (8, features)).astype(LOW)
        shift = mm(embed, matrix_of(v2, 0, 9 * n, 10 * n))[0:1]
        c1 = from_left(q[:, :n]) + q[:, n : 2 * n] + from_right(q[:, 2 * n :]) + shift
        conv[i] = c1
        c1 = c1 - group_average(jnp.sum(c1, axis=0, keepdims=True), mats_n, width)
        var_n = group_average(jnp.sum(c1 * c1, axis=0, keepdims=True), mats_n, width)
        v = c1 * lax.rsqrt(var_n + NORM_EPS) * side[0:1, :] + side[1:2, :]
        v = v * jax.nn.sigmoid(v)
        taps[i, 0:TIME, :] = jnp.zeros((TIME, 3 * n), LOW)
        taps[i, TIME + ROWS :, :] = jnp.zeros((TIME, 3 * n), LOW)
        taps[i, TIME : TIME + ROWS, :] = jnp.concatenate(
            [from_left(v), v, from_right(v)], axis=1
        ).astype(LOW)

    def conv_back_layer(i):
        total = None
        for a in range(3):
            term = mm_nt(
                taps[i, TIME * a : TIME * a + ROWS, :], matrix_of(v3, 0, 3 * n * a, 3 * n * (a + 1))
            )
            total = term if total is None else total + term
        part[i] = total.astype(LOW)
        total_sum.begin(i)

    conv_layer(0)
    share.pass_on()
    run.spread(4, 1)
    run.spread(4, 2)
    run.spread(4, 3)
    share.end()
    store(pad.at[:, pl.ds(TIME, ROWS), :], first_o)
    conv_layer(1)
    store(conv, conv_o)
    store(taps, taps_o)
    run.ready(3)
    store(v3, g3)
    conv_back_layer(1)
    conv_back_layer(0)
    total_sum.cross()
    local[4].wait()
    run.turn(4)
    loads[2].wait()
    run.ready(4)
    store(v4, g4)
    for i in range(2):
        ckv[i] = mm(codec[...], matrix_of(v4, i, n, 3 * n)).astype(LOW)
    store(ckv, ckv_o)
    total_sum.end()

    def norm_three(r):
        v = noisy[r, :] + summed[r, :].astype(F32)
        resid3[r, :] = v
        hat, _ = ln_stats(v)
        n3[r, :] = (hat * norms[8:9, :] + norms[9:10, :]).astype(LOW)

    each_rows(norm_three)
    store(resid3, resid3_o)
    store(n3, n3_o)
    for i in range(2):
        cq[i] = mm(n3[...], matrix_of(v4, i, 0, n)).astype(LOW)
    store(cq, cq_o)

    def cross_heads(r):
        found = []
        for i in range(2):
            part, logs_i = softmax_heads(
                cq[i, r, :], ckv[i, :, :n], ckv[i, :, n:], heads, score_scale, None
            )
            cross[i, r, :] = part
            found += logs_i
        logs_c[r, :] = jnp.concatenate(found, axis=1)
        return mm_nt(cross[0, r, :], matrix_of(v4, 0, 3 * n, 4 * n)) + mm_nt(
            cross[1, r, :], matrix_of(v4, 1, 3 * n, 4 * n)
        )

    swap = Exchange(net, sent.at[2], got.at[2], sibling)
    swap.give(cross_heads)
    store(cross, cross_o)
    store(logs_c, logs_c_o)

    def finish_rows(r, both):
        out[r, :] = (resid3[r, :] + both).astype(LOW)

    swap.take(finish_rows)
    store(out, out_o)
    for c in stores:
        c.wait()
    net.close()


def forward_all(w_in, w_back, w_up, w_down, segments, norms, steps, tokens, noises, codecs):
    n, hid = w_in.shape[2], w_up.shape[1]
    rows, features = w_in.shape[1], norms.shape[1]
    heads = 2 * n // HD
    ctok = codecs.shape[1]
    widths = [4 * n, 2 * hid, 10 * n, padded_width(9 * n), 4 * n]
    full = (ROWS, features)
    tall = ROWS + 2 * TIME
    kept = [
        (full, LOW), ((2, ROWS, 3 * n), LOW), ((2, ROWS, n), LOW), ((ROWS, heads), F32), (full, F32),
        (full, LOW), (full, F32), ((2, *full), LOW), ((2, ROWS, n), F32), ((2, tall, 3 * n), LOW),
        (full, F32), (full, LOW), ((2, ROWS, n), LOW), ((2, ctok, 2 * n), LOW), ((2, ROWS, n), LOW),
        ((ROWS, heads), F32), (full, LOW),
    ]
    groups = [(2 - (g in (2, 3)), 4, 2, rows, w) for g, w in enumerate(widths)]
    dma = pltpu.SemaphoreType.DMA
    copies = 3 * 13 + 7 + 4 + 12 + 2 + 4
    res = pl.pallas_call(
        forward_body,
        name="forward",
        in_specs=[spec_vm() for _ in range(7)] + [spec_any() for _ in range(3)],
        out_specs=[spec_any() for _ in groups] + [spec_vm()] + [spec_any() for _ in kept],
        out_shape=[jax.ShapeDtypeStruct(s, LOW) for s in groups]
        + [jax.ShapeDtypeStruct((1, 128), F32)]
        + [jax.ShapeDtypeStruct(s, t) for s, t in kept],
        scratch_shapes=[
            *[VM((rows, w), LOW) for w in widths], *[VM(s, LOW) for s in groups],
            VM(full, LOW), VM(full, LOW), VM((ctok, features), LOW), *[VM(s, t) for k, (s, t) in enumerate(kept) if k != 7],
            VM((2, tall, features), LOW), VM(full, F32), VM((3, *full), LOW), VM((3, *full), LOW),
            VM((2, *full), LOW), VM((2, ROWS // 2, features), LOW), VM((ROWS // 2, features), LOW),
            VM((ROWS // 2, features), LOW), VM(full, LOW), VM((ROWS, 1), F32),
            dma((3,)), dma((22,)), dma((5,)), dma((copies,)), dma((copies,)),
        ],
        compiler_params=pltpu.CompilerParams(
            collective_id=0, has_side_effects=True, vmem_limit_bytes=62 << 20
        ),
    )(w_in, w_back, w_up, w_down, segments, norms, steps, tokens, noises, codecs)
    return res[:5], res[5], res[6:]


class Scatter:
    def __init__(self, net, d, over_x, bufs):
        self.net, self.d, self.k = net, d, over_x
        self.both = d.shape[0] == 2
        self.ly, self.r1, self.r2 = bufs[:3]
        if self.both:
            self.lx, self.corner = bufs[3:]
        self.x, self.core, self.z, self.y = place()
        self.to_x, self.to_y, _ = chip_peers()
        self.to_z1, self.to_z2 = z_peers()

    def raw(self):
        d, y, k, start = self.d, self.y, self.k, self.net.start
        if not self.both:
            self.first = [start(d.at[0, :, 1 - y], self.ly, self.to_y)]
            return
        self.first, self.turned = [], []
        if k > 0:
            self.turned.append(start(d.at[1, 0:k, 1 - y], self.corner.at[0:k], self.to_x))
        if k < 4:
            self.turned.append(start(d.at[1, k:4, 1 - y], self.corner.at[k:4], self.to_y))
        if k > 0:
            self.first.append(start(d.at[1, 0:k, y], self.lx.at[0:k], self.to_x))
        if k < 4:
            self.first.append(start(d.at[0, k:4, 1 - y], self.ly.at[k:4], self.to_y))

    def corners(self):
        d, y, k, start = self.d, self.y, self.k, self.net.start
        for c in self.turned:
            c.wait_recv()
        for r in range(4):
            mine = d.at[0, r, 1 - y] if r < k else d.at[1, r, y]
            add_rows(self.corner.at[r], [self.corner.at[r], mine])
        if k > 0:
            self.first.append(start(self.corner.at[0:k], self.ly.at[0:k], self.to_y))
        if k < 4:
            self.first.append(start(self.corner.at[k:4], self.lx.at[k:4], self.to_x))

    def lines(self):
        d, y, low = self.d, self.y, self.z % 2
        for c in self.first:
            c.wait_recv()
        for k in range(4):
            mine = d.at[0, k, y]
            add_rows(mine, [mine, self.ly.at[k]] + ([self.lx.at[k]] if self.both else []))
        self.ends = [
            self.net.start(d.at[0, 1 - low + 2 * h, y], self.r1.at[h], self.to_z1) for h in range(2)
        ]

    def half(self):
        d, y, z = self.d, self.y, self.z
        for h in range(2):
            self.ends[h].wait_recv()
            mine = d.at[0, z % 2 + 2 * h, y]
            add_rows(mine, [mine, self.r1.at[h]])
        self.last = self.net.start(d.at[0, (z + 2) % 4, y], self.r2, self.to_z2)

    def finish(self, target):
        self.last.wait_recv()
        add_rows(target, [self.d.at[0, self.z, self.y], self.r2])


class ScatterZ:
    def __init__(self, net, d, bufs):
        self.net, self.d, self.halves = net, d, d.shape[0]
        self.f1, self.f2, self.fy = bufs[:3]
        if self.halves == 2:
            self.pair, self.fx = bufs[3:]
        self.x, self.core, self.z, self.y = place()
        self.to_x, self.to_y, _ = chip_peers()
        self.to_z1, self.to_z2 = z_peers()

    def raw(self):
        low = self.z % 2
        self.ends = [
            self.net.start(self.d.at[:, 1 - low + 2 * h], self.f1.at[h], self.to_z1) for h in range(2)
        ]

    def half(self):
        low = self.z % 2
        for h in range(2):
            self.ends[h].wait_recv()
            for i in range(self.halves):
                for j in range(2):
                    mine = self.d.at[i, low + 2 * h, j]
                    add_rows(mine, [mine, self.f1.at[h, i, j]])
        self.next = self.net.start(self.d.at[:, (self.z + 2) % 4], self.f2, self.to_z2)

    def mid(self):
        self.next.wait_recv()
        for i in range(self.halves):
            for j in range(2):
                mine = self.d.at[i, self.z, j]
                add_rows(mine, [mine, self.f2.at[i, j]])
        self.over = self.net.start(self.d.at[:, self.z, 1 - self.y], self.fy, self.to_y)

    def turn(self):
        self.over.wait_recv()
        for i in range(2):
            add_rows(self.pair.at[i], [self.d.at[i, self.z, self.y], self.fy.at[i]])
        self.last = self.net.start(self.pair.at[1], self.fx, self.to_x)
        self.sent = [*self.ends, self.next, self.over]
        for c in self.sent:
            c.wait_send()

    def finish(self, target):
        if self.halves == 2:
            self.last.wait_recv()
            add_rows(target, [self.pair.at[0], self.fx])
        else:
            self.over.wait_recv()
            add_rows(target, [self.d.at[0, self.z, self.y], self.fy.at[0]])


class Totals:
    def __init__(self, net, values, got):
        self.net, self.values, self.got = net, values, got
        x, core, z, y = place()
        to_x, to_y, _ = chip_peers()
        self.peers = [device(x, 1 - core, z, y), to_x, to_y, *z_peers()]

    def start(self, k):
        self.copy = self.net.start(self.values.at[k], self.got.at[k], self.peers[k])

    def step(self, k):
        self.copy.wait_recv()
        self.values[k + 1] = self.values[k] + self.got[k]
        if k < 4:
            self.start(k + 1)


def backward_body(
    segments, norms, steps, sq, tokens, cots, codecs,
    g0, g1, g2, g3, g4, n1_h, qkv_h, mixed_h, logs_h, resid_h, n2_h, noisy_h, first_h, conv_h, taps_h,
    resid3_h, n3_h, cq_h, ckv_h, cross_h, logs_c_h, out_h,
    s0, s1, s2, s3, s4, all_x, all_out, rows_o,
    d_c, d_t, d_o, d_m, wv, cot, codec, cq, ckv, cross, gm, logs, resid, nrm, grad, pad, taps, tapsg,
    conv, first, hb, hb2, acc, sent, got, part, near, far_out, far_in, summed,
    f1_c, f2_c, fy_c, pair_c, fx_c, ly_t, r1_t, r2_t, f1_o, f2_o, fy_o,
    ly_m, r1_m, r2_m, lx_m, co_m, ly_a, r1_a, r2_a, lx_a, co_a, values, values_in, seg_col,
    stage, gsum, load_sem, out_sem, send, recv,
):
    n = cq.shape[2]
    features = norms.shape[1]
    width = features // GROUPS
    heads = n // HD
    hid = g1.shape[2] // 2
    block = d_m.shape[5] // 2
    ctok = codec.shape[0]
    score_scale = HD ** (-0.5)
    x, core, z, y = place()
    to_x, to_y, _ = chip_peers()
    sibling = device(x, 1 - core, z, y)
    net = Sender(send, recv)
    loads = []

    def load(src, dst):
        copy = pltpu.make_async_copy(src, dst, load_sem.at[len(loads)])
        copy.start()
        loads.append(copy)
        return copy

    def weights(ref, i):
        w = ref.shape[2]
        return load(ref.at[i], wv.at[i, :, pl.ds(0, w)])

    own = pl.ds(pl.multiple_of(x * ROWS, ROWS), ROWS)
    half = pl.ds(pl.multiple_of(core * (ROWS // 2), ROWS // 2), ROWS // 2)
    mine = pl.ds(pl.multiple_of(x * ROWS + core * (ROWS // 2), ROWS // 2), ROWS // 2)
    brought = pl.ds(pl.multiple_of((1 - x) * ROWS + core * (ROWS // 2), ROWS // 2), ROWS // 2)
    side = own_channels(norms, 2 * x + core, n)
    ready = [
        load(cots.at[own, :], cot), load(cross_h, cross), load(g4.at[0], wv.at[0, :, pl.ds(0, 4 * n)]),
        load(g4.at[1], wv.at[1, :, pl.ds(0, 4 * n)]), load(cq_h, cq), load(ckv_h, ckv),
        load(logs_c_h, logs), load(n3_h, nrm), load(codecs.at[x], codec),
    ]
    later = [load(resid3_h, resid), load(taps_h, taps), load(conv_h, conv), load(first_h, first)]
    meet([to_x, to_y, *z_peers(), sibling])
    out_far = net.start(out_h.at[half, :], all_out.at[mine, :], to_x)
    out_own = pltpu.make_async_copy(out_h, all_out.at[own, :], out_sem.at[8])
    out_own.start()
    sends = {}
    cro = ScatterZ(net, d_c, (f1_c, f2_c, fy_c, pair_c, fx_c))
    two = Scatter(net, d_t, 0, (ly_t, r1_t, r2_t))
    one = ScatterZ(net, d_o, (f1_o, f2_o, fy_o))
    mlp = [
        Scatter(net, d_m.at[q], 3, (ly_m.at[q], r1_m.at[q], r2_m.at[q], lx_m.at[q], co_m.at[q]))
        for q in range(hid // block)
    ]
    attn = Scatter(net, d_c, 2, (ly_a, r1_a, r2_a, lx_a, co_a))
    rows = values.at[0]
    totals = Totals(net, values, values_in)
    share = Share(net, pad, TIME)
    total_sum = FourSum(net, part, near, far_out, far_in, summed)

    def exchange(k):
        if k >= 2:
            sends[k - 2].wait_send()
        sends[k] = Exchange(net, sent.at[k % 2], got.at[k % 2], sibling)
        return sends[k]

    def put(ref, i, first, value):
        w = value.shape[1]
        ref[i, :, :, :, first : first + w] = value.astype(LOW).reshape(4, 2, -1, w)

    values[0] = jnp.zeros(values.shape[1:], F32)
    rows[10:11, 0:128] = sq[...]
    gsum[...] = jnp.zeros(gsum.shape, F32)
    for c in ready:
        c.wait()
    for i in (1, 0):
        gm[i] = mm(cot[...], wv[i, :, 3 * n : 4 * n]).astype(LOW)
    acc_kv = acc.at[0:ctok, :]
    acc_kv[...] = jnp.zeros((ctok, 4 * n), F32)

    def cross_heads(r):
        for i in range(2):
            rows_logs = [logs[r, heads * i + h : heads * i + h + 1] for h in range(heads)]
            gq, gk, gv = softmax_heads_back(
                cq[i, r, :], ckv[i, :, :n], ckv[i, :, n:], gm[i, r, :], rows_logs, heads, score_scale, None
            )
            cq[i, r, :] = gq.astype(LOW)
            acc_kv[:, 2 * n * i : 2 * n * (i + 1)] += jnp.concatenate([gk, gv], axis=1)
        return mm_nt(cq[1, r, :], wv[1, :, :n]) + mm_nt(cq[0, r, :], wv[0, :, :n])

    exchange(0).give(cross_heads)
    for i in (1, 0):
        both = acc_kv[:, 2 * n * i : 2 * n * (i + 1)]
        low = jnp.concatenate([both[:, :n] * score_scale, both[:, n:]], axis=1).astype(LOW)
        put(d_c, i, 3 * n, mm_tn(cot[...], cross[i]))
        put(d_c, i, 0, mm_tn(nrm[...], cq[i]))
        put(d_c, i, n, mm_tn(codec[...], low))
    cro.raw()
    two_w = load(g3.at[0], wv.at[0, :, pl.ds(0, g3.shape[2])])
    one_w = load(g2.at[0], wv.at[1, :, pl.ds(0, g2.shape[2])])
    for i in range(2):
        pad[i, 0:TIME, :] = jnp.zeros((TIME, features), LOW)
        pad[i, TIME + ROWS :, :] = jnp.zeros((TIME, features), LOW)
    low_grad = pad.at[0, TIME : TIME + ROWS, :]
    other_grad = pad.at[1, TIME : TIME + ROWS, :]
    for c in later:
        c.wait()

    def pull_three(r, both):
        back, gain, shift = ln_back(resid[r, :], norms[8:9, :], both)
        v = cot[r, :].astype(F32) + back
        grad[r, :] = v
        low_grad[r, :] = v.astype(LOW)
        rows[8:9, :] += gain
        rows[9:10, :] += shift

    sends[0].take(pull_three)
    share.begin()
    tok_load = load(tokens.at[own, :], cot)
    noisy_load = load(noisy_h, resid)
    n2_load = load(n2_h, nrm)
    mats_n = group_mats(n, width)
    gn_rows = [None, None]
    two_w.wait()

    def conv_pull(i):
        q = None
        for a in range(3):
            term = mm(
                pad[i, TIME * (2 - a) : TIME * (2 - a) + ROWS, :], wv[0, :, 3 * n * a : 3 * n * (a + 1)]
            )
            q = term if q is None else q + term
        g = from_right(q[:, :n]) + q[:, n : 2 * n] + from_left(q[:, 2 * n :])
        c1 = conv[i]
        c1 = c1 - group_average(jnp.sum(c1, axis=0, keepdims=True), mats_n, width)
        var_n = group_average(jnp.sum(c1 * c1, axis=0, keepdims=True), mats_n, width)
        scale = lax.rsqrt(var_n + NORM_EPS)
        hat = c1 * scale
        gain = side[0:1, :]
        pre = hat * gain + side[1:2, :]
        gate = jax.nn.sigmoid(pre)
        g = g * gate * (1.0 + pre * (1.0 - gate))
        d_gain = jnp.sum(g * hat, axis=0, keepdims=True)
        d_shift = jnp.sum(g, axis=0, keepdims=True)
        gn_rows[i] = jnp.concatenate([d_gain, d_shift], axis=0)
        back = scale * (
            g * gain
            - group_average(d_shift * gain, mats_n, width)
            - hat * group_average(d_gain * gain, mats_n, width)
        )
        back = back.astype(LOW).astype(F32)
        gsum[i : i + 1, :] = jnp.sum(back, axis=0, keepdims=True)
        tapsg[i, 0:TIME, :] = jnp.zeros((TIME, 3 * n), LOW)
        tapsg[i, TIME + ROWS :, :] = jnp.zeros((TIME, 3 * n), LOW)
        tapsg[i, TIME : TIME + ROWS, :] = jnp.concatenate(
            [from_right(back), back, from_left(back)], axis=1
        ).astype(LOW)

    def first_pull(i):
        total = None
        for a in range(3):
            term = mm_nt(
                tapsg[i, TIME * (2 - a) : TIME * (2 - a) + ROWS, :], wv[1, :, 3 * n * a : 3 * n * (a + 1)]
            )
            total = term if total is None else total + term
        part[i] = total.astype(LOW)
        total_sum.begin(i)

    conv_pull(0)
    out_far.wait_recv()
    out_near = net.start(all_out.at[brought, :], all_out.at[brought, :], sibling)
    share.pass_on()
    share.end()
    conv_pull(1)
    one_w.wait()
    first_pull(1)
    first_pull(0)
    cro.half()
    total_sum.cross()
    for a in range(3):
        put(
            d_t, 0, 3 * n * a,
            mm_tn(low_grad[...], taps[0, TIME * a : TIME * a + ROWS, :])
            + mm_tn(other_grad[...], taps[1, TIME * a : TIME * a + ROWS, :]),
        )
    d_t[:, :, :, :, 9 * n :] = jnp.zeros((*d_t.shape[:4], d_t.shape[4] - 9 * n), LOW)
    two.raw()
    gn_both = gn_rows[0] + gn_rows[1]
    rows[6:8, :] = jnp.concatenate(
        [jnp.where(2 * x + core == s, gn_both, 0.0) for s in range(4)], axis=1
    )
    for a in range(3):
        window = pl.ds(TIME * (2 - a), ROWS)
        put(
            d_o, 0, 3 * n * a,
            mm_tn(first[0], tapsg[0, window, :]) + mm_tn(first[1], tapsg[1, window, :]),
        )
    put(
        d_o, 0, 9 * n,
        lax.dot_general(
            steps[...], gsum[...], (((0,), (0,)), ((), ())), precision=HIGHEST_PRECISION,
            preferred_element_type=F32,
        ),
    )
    mlp_w = [weights(g1, i) for i in range(2)]
    total_sum.end()
    one.raw()

    noisy_load.wait()
    mats = group_mats(features, width)
    mean = group_average(jnp.sum(resid[...], axis=0, keepdims=True), mats, width)
    centre = resid[...] - mean
    var = group_average(jnp.sum(centre * centre, axis=0, keepdims=True), mats, width)
    scale = lax.rsqrt(var + NORM_EPS)
    gain, shift = norms[4:5, :], norms[5:6, :]

    def through_silu(r):
        hat = (resid[r, :] - mean) * scale
        pre = hat * gain + shift
        gate = jax.nn.sigmoid(pre)
        g = summed[r, :].astype(F32)
        g = g * gate * (1.0 + pre * (1.0 - gate))
        acc[r, :] = g
        rows[4:5, :] += jnp.sum(g * hat, axis=0, keepdims=True)
        rows[5:6, :] += jnp.sum(g, axis=0, keepdims=True)

    each_rows(through_silu)
    mean_shift = group_average(rows[5:6, :] * gain, mats, width)
    mean_gain = group_average(rows[4:5, :] * gain, mats, width)

    def pull_two(r):
        hat = (resid[r, :] - mean) * scale
        v = grad[r, :] + scale * (acc[r, :] * gain - mean_shift - hat * mean_gain)
        grad[r, :] = v
        low_grad[r, :] = v.astype(LOW)

    share.far.wait_send()
    each_rows(pull_two)
    resid_load = load(resid_h, resid)
    n2_load.wait()
    for c in mlp_w:
        c.wait()
    for q, group in enumerate(mlp):
        up, down = block * q, hid + block * q
        for i in (1, 0):
            pre = mm(nrm[...], wv[i, :, up : up + block])
            t, hidden = gelu_parts(pre)
            slope = gelu_slope(pre, t)
            hb[i] = hidden.astype(LOW)
            hb2[i] = (mm(low_grad[...], wv[i, :, down : down + block]) * slope).astype(LOW)
            term = mm_nt(hb2[i], wv[i, :, up : up + block])
            if q == 0 and i == 1:
                acc[...] = term
            else:
                acc[...] += term
        if q == len(mlp) - 1:
            exchange(1).give(lambda r: acc[r, :])
        for i in (1, 0):
            put(d_m.at[q], i, block, mm_tn(low_grad[...], hb[i]))
            put(d_m.at[q], i, 0, mm_tn(nrm[...], hb2[i]))
        group.raw()
        if q == 1:
            cro.mid()
    attn_w = [weights(g0, i) for i in range(2)]
    tail_loads = [
        load(n1_h, nrm), load(qkv_h, tapsg.at[:, pl.ds(0, ROWS), :]), load(mixed_h, cross), load(logs_h, logs),
    ]
    resid_load.wait()

    def pull_one(r, both):
        back, g_gain, g_shift = ln_back(resid[r, :], norms[2:3, :], both)
        v = grad[r, :] + back
        grad[r, :] = v
        low_grad[r, :] = v.astype(LOW)
        rows[2:3, :] += g_gain
        rows[3:4, :] += g_shift

    sends[1].take(pull_one)
    for c in (*attn_w, *tail_loads):
        c.wait()
    for i in range(2):
        gm[i] = mm(low_grad[...], wv[i, :, 3 * n : 4 * n]).astype(LOW)
    acc[...] = jnp.zeros(acc.shape, F32)

    seg_row = own_segments(segments, x, seg_col)

    def self_heads(r):
        mask = seg_col[r, :] == seg_row
        for i in range(2):
            rows_logs = [logs[r, heads * i + h : heads * i + h + 1] for h in range(heads)]
            gq, gk, gv = softmax_heads_back(
                tapsg[i, r, :n], tapsg[i, 0:ROWS, n : 2 * n], tapsg[i, 0:ROWS, 2 * n :], gm[i, r, :],
                rows_logs, heads, score_scale, mask,
            )
            taps[i, r, :n] = gq.astype(LOW)
            acc[:, 2 * n * i : 2 * n * (i + 1)] += jnp.concatenate([gk, gv], axis=1)

    each_rows(self_heads)
    one.half()
    cro.turn()
    mlp[0].corners()
    for i in (1, 0):
        both = acc[:, 2 * n * i : 2 * n * (i + 1)]
        taps[i, 0:ROWS, n:] = jnp.concatenate([both[:, :n] * score_scale, both[:, n:]], axis=1).astype(LOW)
        put(d_c, i, 3 * n, mm_tn(low_grad[...], cross[i]))
        put(d_c, i, 0, mm_tn(nrm[...], taps[i, 0:ROWS, :]))
    attn.raw()
    exchange(2).give(
        lambda r: mm_nt(taps[1, r, :], wv[1, :, : 3 * n]) + mm_nt(taps[0, r, :], wv[0, :, : 3 * n])
    )
    two.lines()
    tok_load.wait()

    def pull_zero(r, both):
        back, g_gain, g_shift = ln_back(cot[r, :].astype(F32), norms[0:1, :], both)
        low_grad[r, :] = (grad[r, :] + back).astype(LOW)
        rows[0:1, :] += g_gain
        rows[1:2, :] += g_shift

    sends[2].take(pull_zero)
    store_x = pltpu.make_async_copy(low_grad, all_x.at[own, :], out_sem.at[5])
    store_x.start()
    middle = pl.ds(pl.multiple_of(TIME + core * (ROWS // 2), TIME), ROWS // 2)
    x_far = net.start(pad.at[0, middle, :], all_x.at[mine, :], to_x)
    rows[0:6, :] = jnp.where(core == 0, rows[0:6, :], 0.0)
    rows[8:10, :] = jnp.where(core == 0, rows[8:10, :], 0.0)
    totals.start(0)

    def deliver(group, k, out):
        w = out.shape[1]
        part = stage.at[:, pl.ds(0, w)]
        group.finish(part)
        copy = pltpu.make_async_copy(part, out, out_sem.at[k])
        copy.start()
        copy.wait()

    mlp[1].corners()
    mlp[0].lines()
    totals.step(0)
    mlp[2].corners()
    deliver(cro, 0, s4)
    totals.step(1)
    mlp[0].half()
    one.mid()
    mlp[1].lines()
    totals.step(2)
    deliver(mlp[0], 1, s1.at[0])
    mlp[2].lines()
    two.half()
    attn.corners()
    totals.step(3)
    x_far.wait_recv()
    x_near = net.start(all_x.at[brought, :], all_x.at[brought, :], sibling)
    mlp[1].half()
    deliver(one, 2, s2)
    attn.lines()
    mlp[2].half()
    totals.step(4)
    rows_o[...] = values[5]
    deliver(mlp[1], 3, s1.at[1])
    deliver(mlp[2], 4, s1.at[2])
    attn.half()
    deliver(two, 6, s3)
    deliver(attn, 7, s0)
    out_near.wait_recv()
    x_near.wait_recv()
    store_x.wait()
    out_own.wait()
    wait_sends(net, [sends[0], share.far, *cro.sent])


def wait_sends(net, done):
    for copy in net.made:
        if copy is not None and all(copy is not d for d in done):
            copy.wait_send()


def backward_all(segments, norms, steps, sq, tokens, cots, codecs, gathered, kept):
    features = norms.shape[1]
    n = kept[2].shape[2]
    rows = gathered[0].shape[3]
    widths = [g.shape[4] for g in gathered]
    hid = widths[1] // 2
    heads = 2 * n // HD
    ctok = codecs.shape[1]
    full = (ROWS, features)
    tall = ROWS + 2 * TIME
    ins = [
        segments, norms, steps, sq, tokens, cots, codecs,
        *[g.reshape(g.shape[0], features, -1) for g in gathered], *kept,
    ]
    dma = pltpu.SemaphoreType.DMA

    block = 256
    parts = hid // block

    def pieces(width, *counts):
        return [VM((*(k if isinstance(k, tuple) else (k,)), rows, width), LOW) for k in counts]

    copies = 2 + 12 + 2 + 2 + 4 + 5 + 5 + 4 + 4 + parts * 9 + 9
    res = pl.pallas_call(
        backward_body,
        name="backward",
        in_specs=[spec_vm() for _ in range(4)] + [spec_any() for _ in ins[4:]],
        out_specs=[spec_any() for _ in range(7)] + [spec_vm()],
        out_shape=[
            jax.ShapeDtypeStruct((parts, rows, 2 * block) if g == 1 else (rows, w), F32)
            for g, w in enumerate(widths)
        ]
        + [jax.ShapeDtypeStruct((2 * ROWS, features), LOW)] * 2
        + [jax.ShapeDtypeStruct((16, features), F32)],
        scratch_shapes=[
            VM((2, 4, 2, rows, 4 * n), LOW), VM((1, 4, 2, rows, widths[3]), LOW),
            VM((1, 4, 2, rows, 10 * n), LOW), VM((parts, 2, 4, 2, rows, 2 * block), LOW),
            VM((2, features, 10 * n), LOW), VM(full, LOW), VM((ctok, features), LOW),
            VM((2, ROWS, n), LOW), VM((2, ctok, 2 * n), LOW), VM((2, ROWS, n), LOW), VM((2, ROWS, n), LOW),
            VM((ROWS, heads), F32), VM(full, F32), VM(full, LOW), VM(full, F32),
            VM((2, tall, features), LOW), VM((2, tall, 3 * n), LOW), VM((2, tall, 3 * n), LOW),
            VM((2, ROWS, n), F32), VM((2, *full), LOW), VM((2, ROWS, 256), LOW), VM((2, ROWS, 256), LOW), VM(full, F32),
            VM((2, *full), LOW), VM((2, *full), LOW), VM((2, *full), LOW),
            VM((2, ROWS // 2, features), LOW), VM((ROWS // 2, features), LOW),
            VM((ROWS // 2, features), LOW), VM(full, LOW),
            *pieces(4 * n, (2, 2, 2), (2, 2), 2, 2), VM((rows, 4 * n), LOW),
            *pieces(widths[3], 4, 2), VM((rows, widths[3]), LOW),
            *pieces(10 * n, (2, 1, 2), (1, 2), 1),
            *pieces(2 * block, (parts, 4), (parts, 2), parts, (parts, 4), (parts, 4)),
            *pieces(4 * n, 4, 2), VM((rows, 4 * n), LOW), *pieces(4 * n, 4, 4),
            VM((6, 16, features), F32), VM((5, 16, features), F32), VM((ROWS, 1), F32),
            VM((rows, 10 * n), F32), VM((8, n), F32),
            dma((30,)), dma((9,)), dma((copies,)), dma((copies,)),
        ],
        compiler_params=pltpu.CompilerParams(
            collective_id=1, has_side_effects=True, vmem_limit_bytes=64 << 20
        ),
    )(*ins)
    return res[:5], res[5], res[6], res[7]


def adam_rows(w, g, m, v, decay_rate):
    m_new = MOMENT_DECAY * m + (1.0 - MOMENT_DECAY) * g
    v_new = MOMENT_DECAY * v + (1.0 - MOMENT_DECAY) * g * g
    correct = 1.0 - MOMENT_DECAY**STEP
    update = m_new / correct / (jnp.sqrt(v_new / correct) + ADAM_EPS) + decay_rate * w
    return m_new, v_new, update


def moment_chunks(masters):
    chunks = []
    for a, size in ((0, 4), (1, 4)):
        count = masters[a].shape[0]
        chunks += [(a, k, min(k + size, count)) for k in range(0, count, size)]
    return chunks + [(2, 0, 1), (3, 0, 1)]


def moments_body(*refs):
    sums_h, refs = refs[:5], refs[5:]
    w_h, m_h, v_h, refs = refs[:4], refs[4:8], refs[8:12], refs[12:]
    nm_h, nv_h, u_h, usq, refs = refs[:4], refs[4:8], refs[8:12], refs[12], refs[13:]
    sums, refs = refs[:5], refs[5:]
    w, m, v, nm, nv, u, (in_sem, out_sem) = (
        refs[:4], refs[4:8], refs[8:12], refs[12:16], refs[16:20], refs[20:24], refs[24:]
    )
    n = w[0].shape[2]
    chunks = moment_chunks(w)
    copies = []

    def part(ref, chunk):
        return ref.at[chunk[1] : chunk[2]] if chunk[0] < 2 else ref

    def load(src, dst):
        copy = pltpu.make_async_copy(src, dst, in_sem.at[len(copies)])
        copy.start()
        copies.append(copy)
        return copy

    sum_loads = [load(sums_h[g], sums[g]) for g in range(5)]
    loads = [
        [load(part(h[c[0]], c), part(r[c[0]], c)) for h, r in ((w_h, w), (m_h, m), (v_h, v))]
        for c in chunks
    ]
    where_in, where_back = {}, {}
    for g, (ins, backs) in GROUPS_OF.items():
        where_in.update({j: (g, k) for k, j in enumerate(ins)})
        where_back.update({j: (g, k) for k, j in enumerate(backs, len(ins))})
    squares = [None] * 29
    for s in sum_loads:
        s.wait()
    stores = []
    for c, waits in zip(chunks, loads):
        for s in waits:
            s.wait()
        a = c[0]
        if a < 2:
            for j in range(c[1], c[2]):
                g, k = (where_back if a else where_in)[j]
                grad = sums[g][:, n * k : n * (k + 1)]
                grad = grad.T if a else grad
                nm[a][j], nv[a][j], u[a][j] = adam_rows(w[a][j], grad, m[a][j], v[a][j], WEIGHT_DECAY)
                squares[16 * a + j] = square_sum(u[a][j])
        else:
            block = sums[1].shape[2] // 2
            found = []
            for q in range(w[a].shape[1] // block):
                cols = slice(block * q, block * (q + 1))
                grad = sums[1][q, :, block * (a - 2) : block * (a - 1)]
                nm[a][:, cols], nv[a][:, cols], u[a][:, cols] = adam_rows(
                    w[a][:, cols], grad, m[a][:, cols], v[a][:, cols], WEIGHT_DECAY
                )
                found.append(square_sum(u[a][:, cols]))
            squares[25 + a] = sum(found)
        for r, h in ((nm, nm_h), (nv, nv_h), (u, u_h)):
            copy = pltpu.make_async_copy(part(r[a], c), part(h[a], c), out_sem.at[len(stores)])
            copy.start()
            stores.append(copy)
    usq[...] = row_of(squares)
    for copy in stores:
        copy.wait()


def totals_body(usq, out, ring, ring_b, send, recv):
    mp, dp = lax.axis_index("mp"), lax.axis_index("dp")
    dp_peers = [((dp + k) % 8, mp) for k in range(1, 8)]
    mp_peers = [(dp, (mp + k) % 4) for k in range(1, 4)]
    ring[dp] = jnp.broadcast_to(usq[...], ring.shape[1:])
    meet(dp_peers + mp_peers)
    net = Sender(send, recv)
    copies = [net.start(ring.at[dp], ring.at[dp], p) for p in dp_peers]
    for c in copies:
        c.wait_recv()
    total = ring[0]
    for k in range(1, 8):
        total = total + ring[k]
    ring_b[mp] = total
    copies = [net.start(ring_b.at[mp], ring_b.at[mp], p) for p in mp_peers]
    for c in copies:
        c.wait_recv()
    out[...] = ring_b[0] + ring_b[1] + ring_b[2] + ring_b[3]
    net.close()


def apply_body(total, sums, w_in, w_back, w_up, w_down, u_in, u_back, u_up, u_down, norms, norm_m, norm_v, *outs):
    nw_in, nw_back, nw_up, nw_down, new_norm, new_nm, new_nv, lens = outs
    both = jnp.sqrt(jnp.concatenate([total[10:11, 0:128], sums[0:1, :]], axis=0))
    lens[...] = both[:, 0:29]
    trust = LEARN_RATE * (both[0:1, :] / jnp.where(both[1:2, :] == 0.0, 1.0, both[1:2, :]))
    lane = lax.broadcasted_iota(jnp.int32, (1, 128), 1)

    def trust_of(j):
        return jnp.sum(jnp.where(lane == j, trust, 0.0), axis=1, keepdims=True)

    for j in range(16):
        nw_in[j] = w_in[j] - trust_of(j) * u_in[j]
    for j in range(11):
        nw_back[j] = w_back[j] - trust_of(16 + j) * u_back[j]
    nw_up[...] = w_up[...] - trust_of(27) * u_up[...]
    nw_down[...] = w_down[...] - trust_of(28) * u_down[...]
    m, v, u = adam_rows(norms[...], total[0:10, :], norm_m[...], norm_v[...], 0.0)
    w = norms[...]
    row_trust = jnp.sqrt(jnp.sum(w * w, axis=1, keepdims=True)) / jnp.sqrt(
        jnp.sum(u * u, axis=1, keepdims=True)
    )
    new_norm[...] = w - LEARN_RATE * row_trust * u
    new_nm[...] = m
    new_nv[...] = v


def lamb_all(sums, rows, masters, moments, squares, norms, norm_m, norm_v):
    shapes = [(v.shape, F32) for v in masters]
    dma = pltpu.SemaphoreType.DMA
    ins = [*sums, *masters, *moments, *squares]
    runs = len(moment_chunks(masters))
    *mvu, usq = pl.pallas_call(
        moments_body,
        name="lamb_moments",
        in_specs=[spec_any() for _ in ins],
        out_specs=[spec_any() for _ in range(12)] + [spec_vm()],
        out_shape=[jax.ShapeDtypeStruct(v.shape, F32) for v in masters * 3]
        + [jax.ShapeDtypeStruct((1, 128), F32)],
        scratch_shapes=[
            *[VM(v.shape, F32) for v in sums], *[VM(v.shape, F32) for v in masters * 6],
            dma((5 + 3 * runs,)), dma((3 * runs,)),
        ],
        compiler_params=pltpu.CompilerParams(vmem_limit_bytes=50 << 20),
        cost_estimate=pl.CostEstimate(flops=2 * 10**7, bytes_accessed=21 * 10**6, transcendentals=10**6),
    )(*ins)
    dma = pltpu.SemaphoreType.DMA
    usq_sum = pl.pallas_call(
        totals_body,
        name="norm_totals",
        in_specs=[spec_vm()],
        out_specs=spec_vm(),
        out_shape=jax.ShapeDtypeStruct((8, 128), F32),
        scratch_shapes=[VM((8, 8, 128), F32), VM((4, 8, 128), F32), dma((10,)), dma((10,))],
        compiler_params=pltpu.CompilerParams(collective_id=2, has_side_effects=True),
    )(usq)
    *weights, new_norm, new_nm, new_nv, lens = run_kernel(
        apply_body, "lamb_apply", [rows, usq_sum, *masters, *mvu[8:], norms, norm_m, norm_v],
        [*shapes, *[(norms.shape, F32)] * 3, ((2, 29), F32)], [],
    )
    return (*weights, *mvu[:8], new_norm, new_nm, new_nv, lens)


def fast_device(
    tokens,
    noise_field,
    codec_tokens,
    timesteps,
    segments,
    cotangent,
    w_in,
    w_back,
    w_up,
    w_down,
    m_in,
    m_back,
    m_up,
    m_down,
    v_in,
    v_back,
    v_up,
    v_down,
    norm_params,
    norm_m,
    norm_v,
):
    features = tokens.shape[1]
    mp = lax.axis_index("mp")
    x = mp // 2

    both = jnp.where(x == 0, timesteps, timesteps[::-1])
    embed = jax.nn.silu(time_embedding(both, features)).astype(LOW).astype(F32)
    level = jnp.sqrt((both[:1].astype(F32) + 1.0) / TSTEPS)
    row = lax.broadcasted_iota(jnp.int32, (8, features), 0)
    steps = jnp.where(row == 0, embed[0:1], jnp.where(row == 1, embed[1:2], level))
    gathered, weight_sq, kept = forward_all(
        w_in, w_back, w_up, w_down.T, segments, norm_params, steps, tokens, noise_field, codec_tokens
    )
    gsteps = jnp.where(row < 2, steps, 0.0)
    sums, all_x, out_rows, rows = backward_all(
        segments, norm_params, gsteps, weight_sq, tokens, cotangent, codec_tokens, gathered, kept
    )
    grad_rows = all_x.astype(F32)
    stepped = lamb_all(
        sums, rows, (w_in, w_back, w_up, w_down.T), (m_in, m_back, m_up, m_down.T),
        (v_in, v_back, v_up, v_down.T), norm_params, norm_m, norm_v,
    )
    stepped = [v.T if k in (3, 7, 11) else v for k, v in enumerate(stepped)]
    return (out_rows, grad_rows, *stepped)


def solution(mesh):
    per_device = fast_device if dict(mesh.shape) == {"dp": 8, "mp": 4} else generic_device
    placed = (
        P("dp", None),
        P("dp", None),
        P("dp", None, None),
        P("dp"),
        P("dp", None),
        P("dp", None),
        P(None, "dp", "mp"),
        P(None, "mp", "dp"),
        P("dp", "mp"),
        P("mp", "dp"),
        P(None, "dp", "mp"),
        P(None, "mp", "dp"),
        P("dp", "mp"),
        P("mp", "dp"),
        P(None, "dp", "mp"),
        P(None, "mp", "dp"),
        P("dp", "mp"),
        P("mp", "dp"),
        P(),
        P(),
        P(),
    )
    return jax.shard_map(
        per_device,
        mesh=mesh,
        in_specs=placed,
        out_specs=(
            P("dp", None),
            P("dp", None),
            P(None, "dp", "mp"),
            P(None, "mp", "dp"),
            P("dp", "mp"),
            P("mp", "dp"),
            P(None, "dp", "mp"),
            P(None, "mp", "dp"),
            P("dp", "mp"),
            P("mp", "dp"),
            P(None, "dp", "mp"),
            P(None, "mp", "dp"),
            P("dp", "mp"),
            P("mp", "dp"),
            P(),
            P(),
            P(),
            P(),
        ),
        check_vma=False,
    )
```

```python
from functools import partial
import math

import jax
import jax.numpy as jnp
from jax import lax
from jax.experimental import pallas as pl
from jax.experimental.pallas import tpu as pltpu
from jax.sharding import PartitionSpec as P

HD = 64
GROUPS = 32
FREQ = 8
TIME = 64
TSTEPS = 1000
STEP = 5


NORM_EPS = 1e-05
MOMENT_DECAY = 0.5
LEARN_RATE = 0.5
WEIGHT_DECAY = 0.01
ADAM_EPS = 1e-06
MASK_VALUE = -1e30
HIGHEST_PRECISION = lax.Precision.HIGHEST


def layer_norm(value_tensor, gain_row, shift_row):
    centre = value_tensor - jnp.mean(value_tensor, axis=-1, keepdims=True)
    spread = jnp.mean(centre * centre, axis=-1, keepdims=True)
    return centre * lax.rsqrt(spread + NORM_EPS) * gain_row + shift_row


def group_norm(value_tensor, gain_row, shift_row, group_width):
    seqs_here, length, channels = value_tensor.shape
    grouped = value_tensor.reshape(seqs_here, length, channels // group_width, group_width)
    centre = grouped - jnp.mean(grouped, axis=(1, 3), keepdims=True)
    spread = jnp.mean(centre * centre, axis=(1, 3), keepdims=True)
    normed = (centre * lax.rsqrt(spread + NORM_EPS)).reshape(seqs_here, length, channels)
    return normed * gain_row + shift_row


def norm_silu(value_tensor, gain_row, shift_row, group_width):
    return jax.nn.silu(group_norm(value_tensor, gain_row, shift_row, group_width))


def time_embedding(timesteps, features):
    half_width = features // 2
    freq_rates = jnp.exp(
        -math.log(10000.0) * jnp.arange(half_width, dtype=jnp.float32) / half_width
    )
    angles = timesteps.astype(jnp.float32)[:, None] * freq_rates[None, :]
    return jnp.concatenate([jnp.sin(angles), jnp.cos(angles)], axis=1)


def flatten_rows(value_tensor):
    return value_tensor.reshape(-1, value_tensor.shape[-1])


def project(values_low, weight_matrix):
    summed = jnp.dot(flatten_rows(values_low), weight_matrix, preferred_element_type=jnp.float32)
    return summed.reshape(values_low.shape[0], values_low.shape[1], weight_matrix.shape[1])


def back_project(grad_low, weight_matrix):
    summed = jnp.einsum(
        "ne,ce->nc", flatten_rows(grad_low), weight_matrix, preferred_element_type=jnp.float32
    )
    return summed.reshape(grad_low.shape[0], grad_low.shape[1], weight_matrix.shape[0])


def weight_grad(left_low, right_low):
    return jnp.einsum(
        "nc,ne->ce",
        flatten_rows(left_low),
        flatten_rows(right_low),
        preferred_element_type=jnp.float32,
    )


def padded_grid(grid_rows):
    seqs_here = grid_rows.shape[0]
    return jnp.pad(grid_rows.reshape(seqs_here, FREQ, TIME, -1), ((0, 0), (1, 1), (1, 1), (0, 0)))


def grid_window(padded, tap_index):
    row_off = tap_index // 3
    col_off = tap_index % 3
    return padded[:, row_off : row_off + FREQ, col_off : col_off + TIME, :].reshape(
        -1, padded.shape[3]
    )


def conv_grid(grid_rows, tap_weights, backward):
    seqs_here = grid_rows.shape[0]
    padded = padded_grid(grid_rows)
    out_width = tap_weights.shape[1] if backward else tap_weights.shape[2]
    summed = jnp.zeros((seqs_here * FREQ * TIME, out_width), jnp.float32)
    for tap_index in range(9):
        window = grid_window(padded, tap_index)
        if backward:
            summed = summed + jnp.einsum(
                "nc,dc->nd", window, tap_weights[8 - tap_index], preferred_element_type=jnp.float32
            )
        else:
            summed = summed + jnp.dot(
                window, tap_weights[tap_index], preferred_element_type=jnp.float32
            )
    return summed.reshape(seqs_here, FREQ * TIME, out_width)


def conv_weight_grad(grid_low, grad_low):
    padded = padded_grid(grid_low)
    grad_flat = flatten_rows(grad_low)
    tap_grads = []
    for tap_index in range(9):
        window = grid_window(padded, tap_index)
        tap_grads.append(
            jnp.einsum("nc,ne->ce", window, grad_flat, preferred_element_type=jnp.float32)
        )
    return jnp.stack(tap_grads)


def split_heads(rows_low):
    return rows_low.reshape(rows_low.shape[0], rows_low.shape[1], rows_low.shape[2] // HD, HD)


def head_scores(queries, key_rows, allowed, score_scale):
    scores = (
        jnp.einsum(
            "sqhd,skhd->shqk",
            split_heads(queries),
            split_heads(key_rows),
            preferred_element_type=jnp.float32,
        )
        * score_scale
    )
    if allowed is not None:
        scores = jnp.where(allowed[:, None], scores, MASK_VALUE)
    return scores


def attend(queries, key_rows, value_rows, allowed, score_scale):
    scores = head_scores(queries, key_rows, allowed, score_scale)
    highest = jnp.max(scores, axis=-1, keepdims=True)
    raised = jnp.exp(scores - highest)
    totals = jnp.sum(raised, axis=-1, keepdims=True)
    soft_low = (raised / totals).astype(jnp.bfloat16)
    mixed_rows = jnp.einsum(
        "shqk,skhd->sqhd", soft_low, split_heads(value_rows), preferred_element_type=jnp.float32
    )
    return (mixed_rows.reshape(queries.shape), highest + jnp.log(totals))


def attend_back(queries, key_rows, value_rows, allowed, score_scale, log_total, grad_mixed):
    scores = head_scores(queries, key_rows, allowed, score_scale)
    soft = jnp.exp(scores - log_total)
    grad_heads = split_heads(grad_mixed)
    grad_soft = jnp.einsum(
        "sqhd,skhd->shqk", grad_heads, split_heads(value_rows), preferred_element_type=jnp.float32
    )
    grad_values = jnp.einsum(
        "shqk,sqhd->skhd", soft.astype(jnp.bfloat16), grad_heads, preferred_element_type=jnp.float32
    )
    row_dot = jnp.sum(soft * grad_soft, axis=-1, keepdims=True)
    grad_scores = (soft * (grad_soft - row_dot)).astype(jnp.bfloat16)
    grad_queries = (
        jnp.einsum(
            "shqk,skhd->sqhd",
            grad_scores,
            split_heads(key_rows),
            preferred_element_type=jnp.float32,
        )
        * score_scale
    )
    grad_keys = (
        jnp.einsum(
            "shqk,sqhd->skhd", grad_scores, split_heads(queries), preferred_element_type=jnp.float32
        )
        * score_scale
    )
    return (
        grad_queries.reshape(queries.shape).astype(jnp.bfloat16),
        grad_keys.reshape(key_rows.shape).astype(jnp.bfloat16),
        grad_values.reshape(value_rows.shape).astype(jnp.bfloat16),
    )


def tensor_parallel_sum(term_rows):
    return lax.psum(term_rows, "mp")


def matrix_squares(first_stack, second_stack, up_rows, down_rows):
    return jnp.concatenate(
        [
            jnp.sum(first_stack * first_stack, axis=(1, 2)),
            jnp.sum(second_stack * second_stack, axis=(1, 2)),
            jnp.sum(up_rows * up_rows)[None],
            jnp.sum(down_rows * down_rows)[None],
        ]
    )


def adam_update(master, grad_rows, first_moment, second_moment, decay_rate):
    first_new = MOMENT_DECAY * first_moment + (1.0 - MOMENT_DECAY) * grad_rows
    second_new = MOMENT_DECAY * second_moment + (1.0 - MOMENT_DECAY) * grad_rows * grad_rows
    correct = 1.0 - MOMENT_DECAY**STEP
    update = first_new / correct / (jnp.sqrt(second_new / correct) + ADAM_EPS) + decay_rate * master
    return (first_new, second_new, update)


def generic_device(
    tokens,
    noise_field,
    codec_tokens,
    timesteps,
    segments,
    cotangent,
    w_in,
    w_back,
    w_up,
    w_down,
    m_in,
    m_back,
    m_up,
    m_down,
    v_in,
    v_back,
    v_up,
    v_down,
    norm_params,
    norm_m,
    norm_v,
):
    seqs_here, length = segments.shape
    features = tokens.shape[1]
    chans_here = w_in.shape[2]
    group_width = features // GROUPS
    score_scale = HD ** (-0.5)
    channel_start = lax.axis_index("mp") * chans_here
    lead_device = (lax.axis_index("mp") == 0).astype(jnp.float32)
    weight_sq = matrix_squares(w_in, w_back, w_up, w_down)
    full_in, full_back, complete_up_weight, full_down = (
        lax.all_gather(w_in.astype(jnp.bfloat16), "dp", axis=1, tiled=True),
        lax.all_gather(w_back.astype(jnp.bfloat16), "dp", axis=2, tiled=True),
        lax.all_gather(w_up.astype(jnp.bfloat16), "dp", axis=0, tiled=True),
        lax.all_gather(w_down.astype(jnp.bfloat16), "dp", axis=1, tiled=True),
    )
    resid_in = tokens.astype(jnp.float32).reshape(seqs_here, length, features)
    allowed = segments[:, :, None] == segments[:, None, :]
    normed_one_low = layer_norm(resid_in, norm_params[0], norm_params[1]).astype(jnp.bfloat16)
    queries = project(normed_one_low, full_in[0]).astype(jnp.bfloat16)
    key_rows = project(normed_one_low, full_in[1]).astype(jnp.bfloat16)
    value_rows = project(normed_one_low, full_in[2]).astype(jnp.bfloat16)
    mixed_rows, log_self = attend(queries, key_rows, value_rows, allowed, score_scale)
    mixed_low = mixed_rows.astype(jnp.bfloat16)
    resid_one = resid_in + tensor_parallel_sum(project(mixed_low, full_back[0]))
    normed_two_low = layer_norm(resid_one, norm_params[2], norm_params[3]).astype(jnp.bfloat16)
    hidden_pre = project(normed_two_low, complete_up_weight)
    hidden_low = jax.nn.gelu(hidden_pre).astype(jnp.bfloat16)
    resid_two = resid_one + tensor_parallel_sum(project(hidden_low, full_down))
    noise_level = jnp.sqrt((timesteps.astype(jnp.float32) + 1.0) / TSTEPS)
    noisy = resid_two + noise_level[:, None, None] * noise_field.astype(jnp.float32).reshape(
        seqs_here, length, features
    )
    first_low = norm_silu(noisy, norm_params[4], norm_params[5], group_width).astype(jnp.bfloat16)
    embed_low = jax.nn.silu(time_embedding(timesteps, features)).astype(jnp.bfloat16)
    time_shift = jnp.dot(embed_low, full_in[3], preferred_element_type=jnp.float32)
    conv_one = conv_grid(first_low, full_in[7:16], False) + time_shift[:, None, :]
    gain_six = lax.dynamic_slice_in_dim(norm_params[6], channel_start, chans_here)
    shift_six = lax.dynamic_slice_in_dim(norm_params[7], channel_start, chans_here)
    second_low = norm_silu(conv_one, gain_six, shift_six, group_width).astype(jnp.bfloat16)
    resid_three = noisy + tensor_parallel_sum(conv_grid(second_low, full_back[2:11], False))
    normed_three_low = layer_norm(resid_three, norm_params[8], norm_params[9]).astype(jnp.bfloat16)
    cross_queries = project(normed_three_low, full_in[4]).astype(jnp.bfloat16)
    cross_keys = project(codec_tokens, full_in[5]).astype(jnp.bfloat16)
    cross_values = project(codec_tokens, full_in[6]).astype(jnp.bfloat16)
    cross_mixed, log_cross = attend(cross_queries, cross_keys, cross_values, None, score_scale)
    cross_low = cross_mixed.astype(jnp.bfloat16)
    result = resid_three + tensor_parallel_sum(project(cross_low, full_back[1]))
    out_low = result.astype(jnp.bfloat16)
    grad_out = cotangent.astype(jnp.float32).reshape(seqs_here, length, features)
    grad_cross_low = grad_out.astype(jnp.bfloat16)
    grad_w_co = weight_grad(cross_low, grad_cross_low)
    grad_cross_mixed = back_project(grad_cross_low, full_back[1]).astype(jnp.bfloat16)
    grad_cq, grad_ck, grad_cv = attend_back(
        cross_queries, cross_keys, cross_values, None, score_scale, log_cross, grad_cross_mixed
    )
    grad_w_cq = weight_grad(normed_three_low, grad_cq)
    grad_w_ck = weight_grad(codec_tokens, grad_ck)
    grad_w_cv = weight_grad(codec_tokens, grad_cv)
    grad_normed_three = tensor_parallel_sum(back_project(grad_cq, full_in[4]))
    pull_three = jax.vjp(layer_norm, resid_three, norm_params[8], norm_params[9])[1]
    grad_part, grad_gain_eight, grad_shift_eight = pull_three(grad_normed_three)
    grad_three = grad_out + grad_part
    grad_conv_low = grad_three.astype(jnp.bfloat16)
    grad_w_conv_two = conv_weight_grad(second_low, grad_conv_low)
    grad_second = conv_grid(grad_conv_low, full_back[2:11], True)
    gather_second_moment = jax.vjp(
        partial(norm_silu, group_width=group_width), conv_one, gain_six, shift_six
    )[1]
    grad_conv_one, grad_gain_six, grad_shift_six = gather_second_moment(grad_second)
    grad_conv_one_low = grad_conv_one.astype(jnp.bfloat16)
    grad_w_time = jnp.einsum(
        "sd,sc->dc",
        embed_low.astype(jnp.float32),
        jnp.sum(grad_conv_one_low.astype(jnp.float32), axis=1),
        precision=HIGHEST_PRECISION,
    )
    grad_w_conv_one = conv_weight_grad(first_low, grad_conv_one_low)
    grad_first = tensor_parallel_sum(conv_grid(grad_conv_one_low, full_in[7:16], True))
    gather_first_moment = jax.vjp(
        partial(norm_silu, group_width=group_width), noisy, norm_params[4], norm_params[5]
    )[1]
    grad_part, grad_gain_four, grad_shift_four = gather_first_moment(grad_first)
    grad_two = grad_three + grad_part
    grad_mlp_low = grad_two.astype(jnp.bfloat16)
    grad_w_down = weight_grad(hidden_low, grad_mlp_low)
    grad_hidden = back_project(grad_mlp_low, full_down)
    grad_pre_low = jax.vjp(jax.nn.gelu, hidden_pre)[1](grad_hidden)[0].astype(jnp.bfloat16)
    up_weight_gradient = weight_grad(normed_two_low, grad_pre_low)
    grad_normed_two = tensor_parallel_sum(back_project(grad_pre_low, complete_up_weight))
    pull_two = jax.vjp(layer_norm, resid_one, norm_params[2], norm_params[3])[1]
    grad_part, grad_gain_two, grad_shift_two = pull_two(grad_normed_two)
    grad_one = grad_two + grad_part
    grad_attn_low = grad_one.astype(jnp.bfloat16)
    grad_w_out = weight_grad(mixed_low, grad_attn_low)
    grad_mixed = back_project(grad_attn_low, full_back[0]).astype(jnp.bfloat16)
    grad_q, grad_k, grad_v = attend_back(
        queries, key_rows, value_rows, allowed, score_scale, log_self, grad_mixed
    )
    grad_w_q = weight_grad(normed_one_low, grad_q)
    grad_w_k = weight_grad(normed_one_low, grad_k)
    grad_w_v = weight_grad(normed_one_low, grad_v)
    grad_normed_one = tensor_parallel_sum(
        back_project(grad_q, full_in[0])
        + back_project(grad_k, full_in[1])
        + back_project(grad_v, full_in[2])
    )
    pull_one = jax.vjp(layer_norm, resid_in, norm_params[0], norm_params[1])[1]
    grad_part, grad_gain_zero, grad_shift_zero = pull_one(grad_normed_one)
    grad_input = grad_one + grad_part
    grad_in_stack = jnp.concatenate(
        [
            jnp.stack([grad_w_q, grad_w_k, grad_w_v, grad_w_time, grad_w_cq, grad_w_ck, grad_w_cv]),
            grad_w_conv_one,
        ]
    )
    grad_back_stack = jnp.concatenate([jnp.stack([grad_w_out, grad_w_co]), grad_w_conv_two])
    summed_in, summed_back, summed_up, summed_down = (
        lax.psum_scatter(grad_in_stack, "dp", scatter_dimension=1, tiled=True),
        lax.psum_scatter(grad_back_stack, "dp", scatter_dimension=2, tiled=True),
        lax.psum_scatter(up_weight_gradient, "dp", scatter_dimension=0, tiled=True),
        lax.psum_scatter(grad_w_down, "dp", scatter_dimension=1, tiled=True),
    )
    shared_rows = (
        jnp.stack(
            [
                grad_gain_zero,
                grad_shift_zero,
                grad_gain_two,
                grad_shift_two,
                grad_gain_four,
                grad_shift_four,
            ]
        )
        * lead_device
    )
    group_rows = lax.dynamic_update_slice(
        jnp.zeros((2, features), jnp.float32),
        jnp.stack([grad_gain_six, grad_shift_six]),
        (0, channel_start),
    )
    last_rows = jnp.stack([grad_gain_eight, grad_shift_eight]) * lead_device
    norm_grad = lax.psum(jnp.concatenate([shared_rows, group_rows, last_rows]), ("dp", "mp"))
    m_in_new, v_in_new, upd_in = adam_update(w_in, summed_in, m_in, v_in, WEIGHT_DECAY)
    m_back_new, v_back_new, upd_back = adam_update(
        w_back, summed_back, m_back, v_back, WEIGHT_DECAY
    )
    m_up_new, v_up_new, upd_up = adam_update(w_up, summed_up, m_up, v_up, WEIGHT_DECAY)
    m_down_new, v_down_new, upd_down = adam_update(
        w_down, summed_down, m_down, v_down, WEIGHT_DECAY
    )
    update_sq = matrix_squares(upd_in, upd_back, upd_up, upd_down)
    weight_total, update_total = lax.psum((weight_sq, update_sq), ("dp", "mp"))
    weight_len = jnp.sqrt(weight_total)
    update_len = jnp.sqrt(update_total)
    trust = weight_len / update_len
    new_in = w_in - LEARN_RATE * trust[0:16, None, None] * upd_in
    new_back = w_back - LEARN_RATE * trust[16:27, None, None] * upd_back
    new_up = w_up - LEARN_RATE * trust[27] * upd_up
    new_down = w_down - LEARN_RATE * trust[28] * upd_down
    norm_m_new, norm_v_new, upd_norm = adam_update(norm_params, norm_grad, norm_m, norm_v, 0.0)
    row_trust = jnp.sqrt(jnp.sum(norm_params * norm_params, axis=1)) / jnp.sqrt(
        jnp.sum(upd_norm * upd_norm, axis=1)
    )
    new_norm = norm_params - LEARN_RATE * row_trust[:, None] * upd_norm
    matrix_norms = jnp.stack([weight_len, update_len])
    out_rows = out_low.reshape(seqs_here * length, features)
    grad_rows = grad_input.reshape(seqs_here * length, features)
    return (
        out_rows,
        grad_rows,
        new_in,
        new_back,
        new_up,
        new_down,
        m_in_new,
        m_back_new,
        m_up_new,
        m_down_new,
        v_in_new,
        v_back_new,
        v_up_new,
        v_down_new,
        new_norm,
        norm_m_new,
        norm_v_new,
        matrix_norms,
    )


CORE_SWAP = [(i, i ^ 1) for i in range(4)]
X_SWAP = [(i, i ^ 2) for i in range(4)]
LOW = jnp.bfloat16
F32 = jnp.float32


def swap_core(v):
    return lax.ppermute(v, "mp", CORE_SWAP)


def swap_x(v):
    return lax.ppermute(v, "mp", X_SWAP)


def by_parity(flag, own, other, axis):
    first = jnp.where(flag == 0, own, other)
    second = jnp.where(flag == 0, other, own)
    return jnp.stack([first, second], axis=axis)


def pick(v, index, axis):
    return lax.dynamic_index_in_dim(v, index, axis, keepdims=False)


def ln_stats(v):
    centre = v - jnp.mean(v, axis=-1, keepdims=True)
    scale = lax.rsqrt(jnp.mean(centre * centre, axis=-1, keepdims=True) + NORM_EPS)
    return centre * scale, scale


def ln_back(v, gain, grad):
    hat, scale = ln_stats(v)
    pulled = grad * gain
    back = scale * (
        pulled
        - jnp.mean(pulled, axis=-1, keepdims=True)
        - hat * jnp.mean(pulled * hat, axis=-1, keepdims=True)
    )
    return back, jnp.sum(grad * hat, axis=0, keepdims=True), jnp.sum(grad, axis=0, keepdims=True)


def mm(a, b):
    return lax.dot_general(a, b, (((1,), (0,)), ((), ())), preferred_element_type=F32)


def mm_nt(a, b):
    return lax.dot_general(a, b, (((1,), (1,)), ((), ())), preferred_element_type=F32)


def mm_tn(a, b):
    return lax.dot_general(a, b, (((0,), (0,)), ((), ())), preferred_element_type=F32)


ANY = pl.ANY
VM = pltpu.VMEM
ROWS = 512
STEP_ROWS = 128


def spec_any():
    return pl.BlockSpec(memory_space=pl.ANY)


def spec_vm():
    return pl.BlockSpec(memory_space=pltpu.VMEM)


def run_kernel(body, name, ins, outs, scratch, hbm=(), flops=0):
    in_specs = [spec_any() if k in hbm else spec_vm() for k in range(len(ins))]
    moved = sum(v.size * v.dtype.itemsize for v in ins) + sum(
        math.prod(s) * jnp.dtype(t).itemsize for s, t in outs
    )
    return pl.pallas_call(
        body,
        name=name,
        in_specs=in_specs,
        out_specs=[spec_vm() for _ in outs],
        out_shape=[jax.ShapeDtypeStruct(s, t) for s, t in outs],
        scratch_shapes=scratch,
        compiler_params=pltpu.CompilerParams(vmem_limit_bytes=56 << 20),
        cost_estimate=pl.CostEstimate(flops=flops, bytes_accessed=moved, transcendentals=0),
    )(*ins)


def each_rows(fn, total=ROWS, step=STEP_ROWS):
    def body(k, carry):
        fn(pl.ds(pl.multiple_of(k * step, step), step))
        return carry

    lax.fori_loop(0, total // step, body, 0)


def start_copies(pairs, sems):
    copies = [pltpu.make_async_copy(a, b, sems.at[k]) for k, (a, b) in enumerate(pairs)]
    for c in copies:
        c.start()
    return copies


def group_mats(channels, width):
    count = channels // width
    r = lax.broadcasted_iota(jnp.int32, (channels, count), 0)
    c = lax.broadcasted_iota(jnp.int32, (channels, count), 1) * width
    down = ((r >= c) & (r < c + width)).astype(F32)
    r = lax.broadcasted_iota(jnp.int32, (count, channels), 1)
    c = lax.broadcasted_iota(jnp.int32, (count, channels), 0) * width
    up = ((r >= c) & (r < c + width)).astype(F32)
    return down, up


def exact_dot(a, b):
    return jnp.dot(a, b, precision=HIGHEST_PRECISION, preferred_element_type=F32)


def group_average(row, mats, width):
    wide = jnp.broadcast_to(row, (8, row.shape[1]))
    return exact_dot(exact_dot(wide, mats[0]) * (1.0 / (width * ROWS)), mats[1])[0:1]


def gelu_parts(v):
    k = math.sqrt(2.0 / math.pi)
    t = jnp.tanh(k * (v + 0.044715 * (v * v * v)))
    return t, 0.5 * v * (1.0 + t)


def gelu_slope(v, t):
    k = math.sqrt(2.0 / math.pi)
    return 0.5 * (1.0 + t) + 0.5 * v * (1.0 - t * t) * (k * (1.0 + 3 * 0.044715 * (v * v)))


def column_of(shape):
    return lax.broadcasted_iota(jnp.int32, shape, 0) % TIME


def from_left(v):
    return jnp.where(column_of(v.shape) == 0, 0.0, pltpu.roll(v, 1, 0))


def from_right(v):
    return jnp.where(column_of(v.shape) == TIME - 1, 0.0, pltpu.roll(v, v.shape[0] - 1, 0))


def softmax_heads(q, k, v, heads, score_scale, mask):
    mixed, logs = [], []
    for h in range(heads):
        s = mm_nt(q[:, HD * h : HD * (h + 1)], k[:, HD * h : HD * (h + 1)]) * score_scale
        if mask is not None:
            s = jnp.where(mask, s, MASK_VALUE)
        top = jnp.max(s, axis=1, keepdims=True)
        e = jnp.exp(s - top)
        total = jnp.sum(e, axis=1, keepdims=True)
        soft = (e * (1.0 / total)).astype(LOW)
        mixed.append(mm(soft, v[:, HD * h : HD * (h + 1)]))
        logs.append(top + jnp.log(total))
    return jnp.concatenate(mixed, axis=1).astype(LOW), logs


def softmax_heads_back(q, k, v, g, logs, heads, score_scale, mask):
    dq, dk, dv = [], [], []
    for h in range(heads):
        cols = slice(HD * h, HD * (h + 1))
        s = mm_nt(q[:, cols], k[:, cols]) * score_scale
        if mask is not None:
            s = jnp.where(mask, s, MASK_VALUE)
        soft = jnp.exp(s - logs[h])
        gs = mm_nt(g[:, cols], v[:, cols])
        dv.append(mm_tn(soft.astype(LOW), g[:, cols]))
        dot = jnp.sum(soft * gs, axis=1, keepdims=True)
        ds = (soft * (gs - dot)).astype(LOW)
        dq.append(mm(ds, k[:, cols]) * score_scale)
        dk.append(mm_tn(ds, q[:, cols]))
    return [jnp.concatenate(d, axis=1) for d in (dq, dk, dv)]


MESH_IDS = pl.DeviceIdType.MESH


def place():
    mp = lax.axis_index("mp")
    dp = lax.axis_index("dp")
    return mp // 2, mp % 2, dp // 2, dp % 2


def device(x, core, z, y):
    return (2 * z + y, 2 * x + core)


def meet(peers):
    barrier = pltpu.get_barrier_semaphore()
    for peer in peers:
        pl.semaphore_signal(barrier, inc=1, device_id=peer, device_id_type=MESH_IDS)
    pl.semaphore_wait(barrier, len(peers))


def chip_peers():
    x, core, z, y = place()
    along_z = [device(x, core, (z + k) % 4, y) for k in range(1, 4)]
    return device(1 - x, core, z, y), device(x, core, z, 1 - y), along_z


def own_segments(segments, x, seg_col):
    row = jnp.where(x == 0, segments[0:1, :], segments[1:2, :]).astype(F32)
    seg_col[...] = jnp.broadcast_to(row, (8, row.shape[1])).T[:, 0:1]
    return row


def own_channels(norms, which, n):
    return sum(jnp.where(which == s, norms[6:8, n * s : n * (s + 1)], 0.0) for s in range(4))


class Sender:
    def __init__(self, send, recv):
        self.send, self.recv, self.made = send, recv, []

    def start(self, src, dst, peer):
        k = len(self.made)
        copy = pltpu.make_async_remote_copy(
            src_ref=src, dst_ref=dst, send_sem=self.send.at[k], recv_sem=self.recv.at[k],
            device_id=peer, device_id_type=MESH_IDS,
        )
        copy.start()
        self.made.append(copy)
        return copy

    def reserve(self, count, item):
        base = len(self.made)
        self.made += [item] + [None] * (count - 1)
        return base

    def close(self):
        for copy in self.made:
            if copy is not None:
                copy.wait_send()


class Exchange:
    def __init__(self, net, sent, got, peer):
        self.net, self.sent, self.got, self.peer = net, sent, got, peer
        self.base = net.reserve(ROWS // STEP_ROWS, self)

    def copy(self, k):
        r = pl.ds(pl.multiple_of(k * STEP_ROWS, STEP_ROWS), STEP_ROWS)
        return pltpu.make_async_remote_copy(
            src_ref=self.sent.at[r, :], dst_ref=self.got.at[r, :],
            send_sem=self.net.send.at[self.base + k], recv_sem=self.net.recv.at[self.base + k],
            device_id=self.peer, device_id_type=MESH_IDS,
        )

    def give(self, fn):
        def body(k, carry):
            r = pl.ds(pl.multiple_of(k * STEP_ROWS, STEP_ROWS), STEP_ROWS)
            self.sent[r, :] = fn(r).astype(LOW)
            self.copy(k).start()
            return carry

        lax.fori_loop(0, ROWS // STEP_ROWS, body, 0)

    def take(self, fn, first=0, last=ROWS // STEP_ROWS):
        def body(k, carry):
            r = pl.ds(pl.multiple_of(k * STEP_ROWS, STEP_ROWS), STEP_ROWS)
            self.copy(k).wait_recv()
            fn(r, self.sent[r, :].astype(F32) + self.got[r, :].astype(F32))
            return carry

        lax.fori_loop(first, last, body, 0)

    def wait_send(self):
        for k in range(ROWS // STEP_ROWS):
            self.copy(k).wait_send()


def padded_width(w):
    return -(-w // 128) * 128


def pack_piece(g, w_in, w_back, w_up, w_down, piece):
    n = w_in.shape[2]
    if g == 1:
        hid = w_up.shape[1]
        piece[:, :hid] = w_up[...].astype(LOW)
        piece[:, hid:] = w_down[...].astype(LOW)
        return
    ins, backs = GROUPS_OF[g]
    cols = [w_in[j] for j in ins] + [w_back[j].T for j in backs]
    spare = piece.shape[1] - n * len(cols)
    if spare:
        cols.append(jnp.zeros((piece.shape[0], spare), F32))
    for k in range(0, len(cols), 2):
        pair = cols[k : k + 2]
        both = pair[0] if len(pair) == 1 else jnp.concatenate(pair, axis=1)
        piece[:, n * k : n * k + both.shape[1]] = both.astype(LOW)


GROUPS_OF = {
    0: ([0, 1, 2], [0]),
    2: ([*range(7, 16), 3], []),
    3: ([], [*range(2, 11)]),
    4: ([4, 5, 6], [1]),
}


def row_of(values):
    lane = lax.broadcasted_iota(jnp.int32, (1, 128), 1)
    row = jnp.zeros((1, 128), F32)
    for j, v in enumerate(values):
        row = row + jnp.where(lane == j, v, 0.0)
    return row


def square_sum(v):
    return jnp.sum(jnp.sum(v * v, axis=1, keepdims=True), axis=0, keepdims=True)


def add_rows(target, terms, step=16):
    def body(k, carry):
        r = pl.ds(pl.multiple_of(k * step, step), step)
        total = terms[0][r, :].astype(F32)
        for t in terms[1:]:
            total = total + t[r, :].astype(F32)
        target[r, :] = total.astype(target.dtype)
        return carry

    lax.fori_loop(0, target.shape[0] // step, body, 0)


def z_peers():
    x, core, z, y = place()
    return device(x, core, z + 1 - 2 * (z % 2), y), device(x, core, (z + 2) % 4, y)


class Gather:
    def __init__(self, pieces, outs, over_x, y_first, net):
        self.pieces, self.outs, self.over_x, self.y_first, self.net = pieces, outs, over_x, y_first, net
        self.x, self.core, self.z, self.y = place()
        self.to_x, self.to_y, _ = chip_peers()
        self.to_z1, self.to_z2 = z_peers()
        near = self.z + 1 - 2 * (self.z % 2)
        self.sources = (near, (self.z + 2) % 4, (near + 2) % 4)
        self.lines, self.planes, self.corners = {}, {}, {}

    def line(self, g):
        if g in self.y_first:
            self.planes[g][0].wait_recv()
            src = dst = self.outs[g].at[0, self.z]
        else:
            src, dst = self.pieces[g], self.outs[g].at[0, self.z, self.y]
        self.lines[g] = [self.net.start(src, dst, peer) for peer in (self.to_z1, self.to_z2)]

    def relay(self, g):
        self.lines[g][1].wait_recv()
        out, far = self.outs[g], self.sources[1]
        src = out.at[0, far] if g in self.y_first else out.at[0, far, self.y]
        self.lines[g].append(self.net.start(src, src, self.to_z1))

    def own(self, g):
        z, y, out = self.z, self.y, self.outs[g]
        self.planes[g] = [self.net.start(self.pieces[g], out.at[0, z, y], self.to_y)]
        if out.shape[0] == 2:
            self.planes[g].append(self.net.start(self.pieces[g], out.at[1, z, y], self.to_x))

    def spread(self, g, k):
        if k != 2:
            self.lines[g][k - 1].wait_recv()
        out, far = self.outs[g], self.sources[k - 1]
        src = out.at[0, far, self.y]
        self.planes[g].append(self.net.start(src, src, self.to_y))
        if out.shape[0] == 2:
            self.planes[g].append(self.net.start(src, out.at[1, far, self.y], self.to_x))

    def turn(self, g):
        for c in self.planes[g]:
            c.wait_recv()
        out, y, k = self.outs[g], self.y, self.over_x[g]
        self.corners[g] = []
        if k > 0:
            self.corners[g].append(
                self.net.start(out.at[0, 0:k, 1 - y], out.at[1, 0:k, 1 - y], self.to_x)
            )
        if k < 4:
            self.corners[g].append(
                self.net.start(out.at[1, k:4, y], out.at[1, k:4, y], self.to_y)
            )

    def ready(self, g):
        if g in self.y_first:
            last = (self.lines[g][0], self.lines[g][2])
        else:
            last = self.corners[g] if self.outs[g].shape[0] == 2 else self.planes[g]
        for c in last:
            c.wait_recv()


class FourSum:
    def __init__(self, net, part, near, far_out, far_in, done):
        self.net, self.part, self.near, self.done = net, part, near, done
        self.far_out, self.far_in = far_out, far_in
        x, core, z, y = place()
        count = ROWS // 2
        self.theirs = pl.ds(pl.multiple_of((1 - core) * count, count), count)
        self.sibling, self.across = device(x, 1 - core, z, y), device(1 - x, core, z, y)

    def begin(self, i):
        copy = self.net.start(self.part.at[i, self.theirs, :], self.near.at[i], self.sibling)
        if i == 1:
            self.other = copy
        else:
            self.own = copy

    def block(self, j):
        count = ROWS // 4
        core = place()[1]
        return pl.ds(pl.multiple_of(2 * count * core + count * j, count), count), pl.ds(count * j, count)

    def cross(self):
        self.other.wait_recv()
        self.far = []
        for j in range(2):
            mine, here = self.block(j)
            add_rows(self.far_out.at[here, :], [self.part.at[1, mine, :], self.near.at[1, here, :]], 64)
            self.far.append(
                self.net.start(self.far_out.at[here, :], self.far_in.at[here, :], self.across)
            )

    def end(self):
        self.own.wait_recv()
        last = []
        for j in range(2):
            mine, here = self.block(j)
            self.far[j].wait_recv()
            target = self.done.at[mine, :]
            add_rows(
                target, [self.part.at[0, mine, :], self.near.at[0, here, :], self.far_in.at[here, :]], 64
            )
            last.append(self.net.start(target, target, self.sibling))
        for copy in last:
            copy.wait_recv()


class Share:
    def __init__(self, net, both, first):
        self.net, self.both, self.far, self.near = net, both, [], []
        x, core, z, y = place()
        count = ROWS // 4
        self.rows = [
            pl.ds(pl.multiple_of(first + count * (2 * j + core), TIME), count) for j in range(2)
        ]
        self.sibling, self.across = device(x, 1 - core, z, y), device(1 - x, core, z, y)

    def begin(self, j):
        r = self.rows[j]
        self.far.append(self.net.start(self.both.at[0, r, :], self.both.at[1, r, :], self.across))

    def pass_on(self):
        for j in range(2):
            self.far[j].wait_recv()
            rows = self.both.at[1, self.rows[j], :]
            self.near.append(self.net.start(rows, rows, self.sibling))

    def end(self):
        for copy in self.near:
            copy.wait_recv()


def matrix_of(ref, i, first, last):
    block = ref[i, :, :, :, first:last]
    return block.reshape(-1, last - first)


def forward_body(
    w_in, w_back, w_up, w_down, segments, norms, steps, tokens, noises, codecs,
    g0, g1, g2, g3, g4, sq, n1_o, qkv_o, mixed_o, logs_o, resid_o, n2_o, noisy_o, first_o, conv_o,
    taps_o, resid3_o, n3_o, cq_o, ckv_o, cross_o, logs_c_o, out_o,
    p0, p1, p2, p3, p4, v0, v1, v2, v3, v4, tok, noise, codec, n1, qkv, mixed, logs, resid, n2,
    noisy, conv, taps, resid3, n3, cq, ckv, cross, logs_c, out, pad, acc, sent, got,
    part, near, far_out, far_in, summed, seg_col,
    in_sem, out_sem, own_sem, send, recv,
):
    pieces, held, kept = (p0, p1, p2, p3, p4), (v0, v1, v2, v3, v4), (g0, g1, g2, g3, g4)
    n = mixed.shape[2]
    hid = w_up.shape[1]
    features = norms.shape[1]
    width = features // GROUPS
    heads = n // HD
    score_scale = HD ** (-0.5)
    net = Sender(send, recv)
    run = Gather(pieces, held, (2, 3, 0, 0, 0), (3,), net)
    share = Share(net, pad, TIME)
    total_sum = FourSum(net, part, near, far_out, far_in, summed)
    x, core, z, y = place()
    sibling = device(x, 1 - core, z, y)
    loads = [
        pltpu.make_async_copy(tokens.at[pl.ds(pl.multiple_of(x * ROWS, ROWS), ROWS), :], tok, in_sem.at[0]),
        pltpu.make_async_copy(noises.at[pl.ds(pl.multiple_of(x * ROWS, ROWS), ROWS), :], noise, in_sem.at[1]),
        pltpu.make_async_copy(codecs.at[x], codec, in_sem.at[2]),
    ]
    for c in loads:
        c.start()
    stores = []

    def store(src, dst):
        copy = pltpu.make_async_copy(src, dst, out_sem.at[len(stores)])
        copy.start()
        stores.append(copy)

    def pack(g):
        pack_piece(g, w_in, w_back, w_up, w_down, pieces[g])
        copy = pltpu.make_async_copy(pieces[g], held[g].at[0, z, y], own_sem.at[g])
        copy.start()
        return copy

    side = own_channels(norms, 2 * x + core, n)
    level = steps[2:3, 0:1]
    local = [pack(0)]
    meet([run.to_x, run.to_y, *z_peers(), sibling])
    run.line(0)
    run.own(0)
    local.append(pack(1))
    run.line(1)
    run.own(1)
    local += [pack(2), pack(3), pack(4)]
    loads[0].wait()

    def norm_one(r):
        hat, _ = ln_stats(tok[r, :].astype(F32))
        n1[r, :] = (hat * norms[0:1, :] + norms[1:2, :]).astype(LOW)

    each_rows(norm_one)
    store(n1, n1_o)
    run.relay(0)
    run.spread(0, 1)
    run.spread(0, 2)
    run.line(2)
    run.own(3)
    run.spread(0, 3)
    run.own(2)
    sq[...] = row_of(
        [square_sum(w_in[j]) for j in range(16)] + [square_sum(w_back[j]) for j in range(11)]
        + [square_sum(w_up[...]), square_sum(w_down[...])]
    )
    run.relay(1)
    run.spread(1, 1)
    run.spread(1, 2)
    run.turn(0)
    local[0].wait()
    local[3].wait()
    run.line(3)
    run.ready(0)
    store(v0, g0)
    for i in range(2):
        qkv[i] = mm(n1[...], matrix_of(v0, i, 0, 3 * n)).astype(LOW)
    store(qkv, qkv_o)
    run.spread(1, 3)

    seg_row = own_segments(segments, x, seg_col)

    def self_heads(r):
        mask = seg_col[r, :] == seg_row
        found = []
        for i in range(2):
            part, logs_i = softmax_heads(
                qkv[i, r, 0:n], qkv[i, :, n : 2 * n], qkv[i, :, 2 * n : 3 * n], heads, score_scale, mask
            )
            mixed[i, r, :] = part
            found += logs_i
        logs[r, :] = jnp.concatenate(found, axis=1)
        return mm_nt(mixed[0, r, :], matrix_of(v0, 0, 3 * n, 4 * n)) + mm_nt(
            mixed[1, r, :], matrix_of(v0, 1, 3 * n, 4 * n)
        )

    swap = Exchange(net, sent.at[0], got.at[0], sibling)
    swap.give(self_heads)
    store(mixed, mixed_o)
    store(logs, logs_o)
    run.relay(2)
    run.spread(2, 1)
    run.spread(2, 2)
    run.turn(1)
    run.own(4)
    run.line(4)

    def norm_two(r, both):
        v = tok[r, :].astype(F32) + both
        resid[r, :] = v
        hat, _ = ln_stats(v)
        n2[r, :] = (hat * norms[2:3, :] + norms[3:4, :]).astype(LOW)

    swap.take(norm_two)
    store(resid, resid_o)
    store(n2, n2_o)
    run.spread(2, 3)
    run.relay(3)
    local[1].wait()
    run.ready(1)
    store(v1, g1)
    block = 256
    for i in range(2):
        for b in range(hid // block):
            pre = mm(n2[...], matrix_of(v1, i, block * b, block * (b + 1)))
            low = gelu_parts(pre)[1].astype(LOW)
            term = mm_nt(low, matrix_of(v1, i, hid + block * b, hid + block * (b + 1)))
            if i == 0 and b == 0:
                acc[...] = term
            else:
                acc[...] += term
    swap = Exchange(net, sent.at[1], got.at[1], sibling)
    swap.give(lambda r: acc[r, :])
    loads[1].wait()

    def add_noise(r, both):
        noisy[r, :] = resid[r, :] + both + level * noise[r, :].astype(F32)

    swap.take(add_noise)
    store(noisy, noisy_o)
    mats = group_mats(features, width)
    mats_n = group_mats(n, width)
    mean = group_average(jnp.sum(noisy[...], axis=0, keepdims=True), mats, width)
    centre = noisy[...] - mean
    var = group_average(jnp.sum(centre * centre, axis=0, keepdims=True), mats, width)
    scale = lax.rsqrt(var + NORM_EPS) * norms[4:5, :]
    for i in range(2):
        pad[i, 0:TIME, :] = jnp.zeros((TIME, features), LOW)
        pad[i, TIME + ROWS :, :] = jnp.zeros((TIME, features), LOW)

    def act(k, carry):
        r = pl.ds(pl.multiple_of(k * STEP_ROWS, STEP_ROWS), STEP_ROWS)
        v = (noisy[r, :] - mean) * scale + norms[5:6, :]
        moved = pl.ds(pl.multiple_of(TIME + k * STEP_ROWS, TIME), STEP_ROWS)
        pad[0, moved, :] = (v * jax.nn.sigmoid(v)).astype(LOW)
        return carry

    for j in range(2):
        lax.fori_loop(2 * j, 2 * j + 2, act, 0)
        share.begin(j)
    run.relay(4)
    local[2].wait()
    run.ready(2)
    store(v2, g2)

    def conv_layer(i):
        q = None
        for a in range(3):
            term = mm(
                pad[i, TIME * a : TIME * a + ROWS, :], matrix_of(v2, 0, 3 * n * a, 3 * n * (a + 1))
            )
            q = term if q is None else q + term
        embed = jnp.broadcast_to(steps[i : i + 1, :], (8, features)).astype(LOW)
        shift = mm(embed, matrix_of(v2, 0, 9 * n, 10 * n))[0:1]
        c1 = from_left(q[:, :n]) + q[:, n : 2 * n] + from_right(q[:, 2 * n :]) + shift
        conv[i] = c1
        c1 = c1 - group_average(jnp.sum(c1, axis=0, keepdims=True), mats_n, width)
        var_n = group_average(jnp.sum(c1 * c1, axis=0, keepdims=True), mats_n, width)
        v = c1 * lax.rsqrt(var_n + NORM_EPS) * side[0:1, :] + side[1:2, :]
        v = v * jax.nn.sigmoid(v)
        taps[i, 0:TIME, :] = jnp.zeros((TIME, 3 * n), LOW)
        taps[i, TIME + ROWS :, :] = jnp.zeros((TIME, 3 * n), LOW)
        taps[i, TIME : TIME + ROWS, :] = jnp.concatenate(
            [from_left(v), v, from_right(v)], axis=1
        ).astype(LOW)

    def conv_back_layer(i):
        total = None
        for a in range(3):
            term = mm_nt(
                taps[i, TIME * a : TIME * a + ROWS, :], matrix_of(v3, 0, 3 * n * a, 3 * n * (a + 1))
            )
            total = term if total is None else total + term
        part[i] = total.astype(LOW)
        total_sum.begin(i)

    conv_layer(0)
    share.pass_on()
    run.spread(4, 1)
    run.spread(4, 2)
    run.spread(4, 3)
    share.end()
    store(pad.at[:, pl.ds(TIME, ROWS), :], first_o)
    conv_layer(1)
    store(conv, conv_o)
    store(taps, taps_o)
    run.ready(3)
    store(v3, g3)
    conv_back_layer(1)
    conv_back_layer(0)
    total_sum.cross()
    local[4].wait()
    run.turn(4)
    loads[2].wait()
    run.ready(4)
    store(v4, g4)
    for i in range(2):
        ckv[i] = mm(codec[...], matrix_of(v4, i, n, 3 * n)).astype(LOW)
    store(ckv, ckv_o)
    total_sum.end()

    def norm_three(r):
        v = noisy[r, :] + summed[r, :].astype(F32)
        resid3[r, :] = v
        hat, _ = ln_stats(v)
        n3[r, :] = (hat * norms[8:9, :] + norms[9:10, :]).astype(LOW)

    each_rows(norm_three)
    store(resid3, resid3_o)
    store(n3, n3_o)
    for i in range(2):
        cq[i] = mm(n3[...], matrix_of(v4, i, 0, n)).astype(LOW)
    store(cq, cq_o)

    def cross_heads(r):
        found = []
        for i in range(2):
            part, logs_i = softmax_heads(
                cq[i, r, :], ckv[i, :, :n], ckv[i, :, n:], heads, score_scale, None
            )
            cross[i, r, :] = part
            found += logs_i
        logs_c[r, :] = jnp.concatenate(found, axis=1)
        return mm_nt(cross[0, r, :], matrix_of(v4, 0, 3 * n, 4 * n)) + mm_nt(
            cross[1, r, :], matrix_of(v4, 1, 3 * n, 4 * n)
        )

    swap = Exchange(net, sent.at[2], got.at[2], sibling)
    swap.give(cross_heads)
    store(cross, cross_o)
    store(logs_c, logs_c_o)

    def finish_rows(r, both):
        out[r, :] = (resid3[r, :] + both).astype(LOW)

    swap.take(finish_rows)
    store(out, out_o)
    for c in stores:
        c.wait()
    net.close()


def forward_all(w_in, w_back, w_up, w_down, segments, norms, steps, tokens, noises, codecs):
    n, hid = w_in.shape[2], w_up.shape[1]
    rows, features = w_in.shape[1], norms.shape[1]
    heads = 2 * n // HD
    ctok = codecs.shape[1]
    widths = [4 * n, 2 * hid, 10 * n, padded_width(9 * n), 4 * n]
    full = (ROWS, features)
    tall = ROWS + 2 * TIME
    kept = [
        (full, LOW), ((2, ROWS, 3 * n), LOW), ((2, ROWS, n), LOW), ((ROWS, heads), F32), (full, F32),
        (full, LOW), (full, F32), ((2, *full), LOW), ((2, ROWS, n), F32), ((2, tall, 3 * n), LOW),
        (full, F32), (full, LOW), ((2, ROWS, n), LOW), ((2, ctok, 2 * n), LOW), ((2, ROWS, n), LOW),
        ((ROWS, heads), F32), (full, LOW),
    ]
    groups = [(2 - (g in (2, 3)), 4, 2, rows, w) for g, w in enumerate(widths)]
    dma = pltpu.SemaphoreType.DMA
    copies = 3 * 13 + 7 + 4 + 12 + 4 + 6
    res = pl.pallas_call(
        forward_body,
        name="forward",
        in_specs=[spec_vm() for _ in range(7)] + [spec_any() for _ in range(3)],
        out_specs=[spec_any() for _ in groups] + [spec_vm()] + [spec_any() for _ in kept],
        out_shape=[jax.ShapeDtypeStruct(s, LOW) for s in groups]
        + [jax.ShapeDtypeStruct((1, 128), F32)]
        + [jax.ShapeDtypeStruct(s, t) for s, t in kept],
        scratch_shapes=[
            *[VM((rows, w), LOW) for w in widths], *[VM(s, LOW) for s in groups],
            VM(full, LOW), VM(full, LOW), VM((ctok, features), LOW), *[VM(s, t) for k, (s, t) in enumerate(kept) if k != 7],
            VM((2, tall, features), LOW), VM(full, F32), VM((3, *full), LOW), VM((3, *full), LOW),
            VM((2, *full), LOW), VM((2, ROWS // 2, features), LOW), VM((ROWS // 2, features), LOW),
            VM((ROWS // 2, features), LOW), VM(full, LOW), VM((ROWS, 1), F32),
            dma((3,)), dma((22,)), dma((5,)), dma((copies,)), dma((copies,)),
        ],
        compiler_params=pltpu.CompilerParams(
            collective_id=0, has_side_effects=True, vmem_limit_bytes=62 << 20
        ),
    )(w_in, w_back, w_up, w_down, segments, norms, steps, tokens, noises, codecs)
    return res[:5], res[5], res[6:]


class Scatter:
    def __init__(self, net, d, over_x, bufs):
        self.net, self.d, self.k = net, d, over_x
        self.both = d.shape[0] == 2
        self.ly, self.r1, self.r2 = bufs[:3]
        if self.both:
            self.lx, self.corner = bufs[3:]
        self.x, self.core, self.z, self.y = place()
        self.to_x, self.to_y, _ = chip_peers()
        self.to_z1, self.to_z2 = z_peers()

    def raw(self):
        d, y, k, start = self.d, self.y, self.k, self.net.start
        if not self.both:
            self.first = [start(d.at[0, :, 1 - y], self.ly, self.to_y)]
            return
        self.first, self.turned = [], []
        if k > 0:
            self.turned.append(start(d.at[1, 0:k, 1 - y], self.corner.at[0:k], self.to_x))
        if k < 4:
            self.turned.append(start(d.at[1, k:4, 1 - y], self.corner.at[k:4], self.to_y))
        if k > 0:
            self.first.append(start(d.at[1, 0:k, y], self.lx.at[0:k], self.to_x))
        if k < 4:
            self.first.append(start(d.at[0, k:4, 1 - y], self.ly.at[k:4], self.to_y))

    def corners(self):
        d, y, k, start = self.d, self.y, self.k, self.net.start
        for c in self.turned:
            c.wait_recv()
        for r in range(4):
            mine = d.at[0, r, 1 - y] if r < k else d.at[1, r, y]
            add_rows(self.corner.at[r], [self.corner.at[r], mine])
        if k > 0:
            self.first.append(start(self.corner.at[0:k], self.ly.at[0:k], self.to_y))
        if k < 4:
            self.first.append(start(self.corner.at[k:4], self.lx.at[k:4], self.to_x))

    def lines(self):
        d, y, low = self.d, self.y, self.z % 2
        for c in self.first:
            c.wait_recv()
        for k in range(4):
            mine = d.at[0, k, y]
            add_rows(mine, [mine, self.ly.at[k]] + ([self.lx.at[k]] if self.both else []))
        self.ends = [
            self.net.start(d.at[0, 1 - low + 2 * h, y], self.r1.at[h], self.to_z1) for h in range(2)
        ]

    def half(self):
        d, y, z = self.d, self.y, self.z
        for h in range(2):
            self.ends[h].wait_recv()
            mine = d.at[0, z % 2 + 2 * h, y]
            add_rows(mine, [mine, self.r1.at[h]])
        self.last = self.net.start(d.at[0, (z + 2) % 4, y], self.r2, self.to_z2)

    def finish(self, target):
        self.last.wait_recv()
        add_rows(target, [self.d.at[0, self.z, self.y], self.r2])


class ScatterZ:
    def __init__(self, net, d, bufs):
        self.net, self.d, self.halves = net, d, d.shape[0]
        self.f1, self.f2, self.fy = bufs[:3]
        if self.halves == 2:
            self.pair, self.fx = bufs[3:]
        self.x, self.core, self.z, self.y = place()
        self.to_x, self.to_y, _ = chip_peers()
        self.to_z1, self.to_z2 = z_peers()

    def raw(self):
        low = self.z % 2
        self.ends = [
            self.net.start(self.d.at[:, 1 - low + 2 * h], self.f1.at[h], self.to_z1) for h in range(2)
        ]

    def half(self):
        low = self.z % 2
        for h in range(2):
            self.ends[h].wait_recv()
            for i in range(self.halves):
                for j in range(2):
                    mine = self.d.at[i, low + 2 * h, j]
                    add_rows(mine, [mine, self.f1.at[h, i, j]])
        self.next = self.net.start(self.d.at[:, (self.z + 2) % 4], self.f2, self.to_z2)

    def mid(self):
        self.next.wait_recv()
        for i in range(self.halves):
            for j in range(2):
                mine = self.d.at[i, self.z, j]
                add_rows(mine, [mine, self.f2.at[i, j]])
        self.over = self.net.start(self.d.at[:, self.z, 1 - self.y], self.fy, self.to_y)

    def turn(self):
        self.over.wait_recv()
        for i in range(2):
            add_rows(self.pair.at[i], [self.d.at[i, self.z, self.y], self.fy.at[i]])
        self.last = self.net.start(self.pair.at[1], self.fx, self.to_x)
        self.sent = [*self.ends, self.next, self.over]
        for c in self.sent:
            c.wait_send()

    def finish(self, target):
        if self.halves == 2:
            self.last.wait_recv()
            add_rows(target, [self.pair.at[0], self.fx])
        else:
            self.over.wait_recv()
            add_rows(target, [self.d.at[0, self.z, self.y], self.fy.at[0]])


class Totals:
    def __init__(self, net, values, got):
        self.net, self.values, self.got = net, values, got
        x, core, z, y = place()
        to_x, to_y, _ = chip_peers()
        self.peers = [device(x, 1 - core, z, y), to_x, to_y, *z_peers()]

    def start(self, k):
        self.copy = self.net.start(self.values.at[k], self.got.at[k], self.peers[k])

    def step(self, k):
        self.copy.wait_recv()
        self.values[k + 1] = self.values[k] + self.got[k]
        if k < 4:
            self.start(k + 1)


def backward_body(
    segments, norms, steps, sq, tokens, cots, codecs,
    g0, g1, g2, g3, g4, n1_h, qkv_h, mixed_h, logs_h, resid_h, n2_h, noisy_h, first_h, conv_h, taps_h,
    resid3_h, n3_h, cq_h, ckv_h, cross_h, logs_c_h, out_h,
    s0, s1, s2, s3, s4, all_x, all_out, rows_o,
    d_c, d_t, d_o, d_m, wv, cot, codec, cq, ckv, cross, gm, logs, resid, nrm, grad, pad, taps, tapsg,
    conv, first, hb, hb2, acc, sent, got, part, near, far_out, far_in, summed,
    f1_c, f2_c, fy_c, pair_c, fx_c, ly_t, r1_t, r2_t, f1_o, f2_o, fy_o,
    ly_m, r1_m, r2_m, lx_m, co_m, ly_a, r1_a, r2_a, lx_a, co_a, values, values_in, seg_col,
    stage, gsum, load_sem, out_sem, send, recv,
):
    n = cq.shape[2]
    features = norms.shape[1]
    width = features // GROUPS
    heads = n // HD
    hid = g1.shape[2] // 2
    block = d_m.shape[5] // 2
    ctok = codec.shape[0]
    score_scale = HD ** (-0.5)
    x, core, z, y = place()
    to_x, to_y, _ = chip_peers()
    sibling = device(x, 1 - core, z, y)
    net = Sender(send, recv)
    loads = []

    def load(src, dst):
        copy = pltpu.make_async_copy(src, dst, load_sem.at[len(loads)])
        copy.start()
        loads.append(copy)
        return copy

    def weights(ref, i):
        w = ref.shape[2]
        return load(ref.at[i], wv.at[i, :, pl.ds(0, w)])

    own = pl.ds(pl.multiple_of(x * ROWS, ROWS), ROWS)
    half = pl.ds(pl.multiple_of(core * (ROWS // 2), ROWS // 2), ROWS // 2)
    mine = pl.ds(pl.multiple_of(x * ROWS + core * (ROWS // 2), ROWS // 2), ROWS // 2)
    brought = pl.ds(pl.multiple_of((1 - x) * ROWS + core * (ROWS // 2), ROWS // 2), ROWS // 2)
    side = own_channels(norms, 2 * x + core, n)
    ready = [
        load(cots.at[own, :], cot), load(cross_h, cross), load(g4.at[0], wv.at[0, :, pl.ds(0, 4 * n)]),
        load(g4.at[1], wv.at[1, :, pl.ds(0, 4 * n)]), load(cq_h, cq), load(ckv_h, ckv),
        load(logs_c_h, logs), load(n3_h, nrm), load(codecs.at[x], codec),
    ]
    later = [load(resid3_h, resid), load(taps_h, taps), load(conv_h, conv), load(first_h, first)]
    meet([to_x, to_y, *z_peers(), sibling])
    out_far = net.start(out_h.at[half, :], all_out.at[mine, :], to_x)
    out_own = pltpu.make_async_copy(out_h, all_out.at[own, :], out_sem.at[8])
    out_own.start()
    sends = {}
    cro = ScatterZ(net, d_c, (f1_c, f2_c, fy_c, pair_c, fx_c))
    two = Scatter(net, d_t, 0, (ly_t, r1_t, r2_t))
    one = ScatterZ(net, d_o, (f1_o, f2_o, fy_o))
    mlp = [
        Scatter(net, d_m.at[q], 3, (ly_m.at[q], r1_m.at[q], r2_m.at[q], lx_m.at[q], co_m.at[q]))
        for q in range(hid // block)
    ]
    attn = Scatter(net, d_c, 2, (ly_a, r1_a, r2_a, lx_a, co_a))
    rows = values.at[0]
    totals = Totals(net, values, values_in)
    share = Share(net, pad, TIME)
    total_sum = FourSum(net, part, near, far_out, far_in, summed)

    def exchange(k):
        if k >= 2:
            sends[k - 2].wait_send()
        sends[k] = Exchange(net, sent.at[k % 2], got.at[k % 2], sibling)
        return sends[k]

    def put(ref, i, first, value):
        w = value.shape[1]
        ref[i, :, :, :, first : first + w] = value.astype(LOW).reshape(4, 2, -1, w)

    values[0] = jnp.zeros(values.shape[1:], F32)
    rows[10:11, 0:128] = sq[...]
    gsum[...] = jnp.zeros(gsum.shape, F32)
    for c in ready:
        c.wait()
    for i in (1, 0):
        gm[i] = mm(cot[...], wv[i, :, 3 * n : 4 * n]).astype(LOW)
    acc_kv = acc.at[0:ctok, :]
    acc_kv[...] = jnp.zeros((ctok, 4 * n), F32)

    def cross_heads(r):
        for i in range(2):
            rows_logs = [logs[r, heads * i + h : heads * i + h + 1] for h in range(heads)]
            gq, gk, gv = softmax_heads_back(
                cq[i, r, :], ckv[i, :, :n], ckv[i, :, n:], gm[i, r, :], rows_logs, heads, score_scale, None
            )
            cq[i, r, :] = gq.astype(LOW)
            acc_kv[:, 2 * n * i : 2 * n * (i + 1)] += jnp.concatenate([gk, gv], axis=1)
        return mm_nt(cq[1, r, :], wv[1, :, :n]) + mm_nt(cq[0, r, :], wv[0, :, :n])

    exchange(0).give(cross_heads)
    for i in (1, 0):
        both = acc_kv[:, 2 * n * i : 2 * n * (i + 1)]
        low = jnp.concatenate([both[:, :n] * score_scale, both[:, n:]], axis=1).astype(LOW)
        put(d_c, i, 3 * n, mm_tn(cot[...], cross[i]))
        put(d_c, i, 0, mm_tn(nrm[...], cq[i]))
        put(d_c, i, n, mm_tn(codec[...], low))
    cro.raw()
    two_w = load(g3.at[0], wv.at[0, :, pl.ds(0, g3.shape[2])])
    one_w = load(g2.at[0], wv.at[1, :, pl.ds(0, g2.shape[2])])
    for i in range(2):
        pad[i, 0:TIME, :] = jnp.zeros((TIME, features), LOW)
        pad[i, TIME + ROWS :, :] = jnp.zeros((TIME, features), LOW)
    low_grad = pad.at[0, TIME : TIME + ROWS, :]
    other_grad = pad.at[1, TIME : TIME + ROWS, :]
    for c in later:
        c.wait()

    def pull_three(r, both):
        back, gain, shift = ln_back(resid[r, :], norms[8:9, :], both)
        v = cot[r, :].astype(F32) + back
        grad[r, :] = v
        low_grad[r, :] = v.astype(LOW)
        rows[8:9, :] += gain
        rows[9:10, :] += shift

    for j in range(2):
        sends[0].take(pull_three, 2 * j, 2 * j + 2)
        share.begin(j)
    tok_load = load(tokens.at[own, :], cot)
    noisy_load = load(noisy_h, resid)
    n2_load = load(n2_h, nrm)
    mats_n = group_mats(n, width)
    gn_rows = [None, None]
    two_w.wait()

    def conv_pull(i):
        q = None
        for a in range(3):
            term = mm(
                pad[i, TIME * (2 - a) : TIME * (2 - a) + ROWS, :], wv[0, :, 3 * n * a : 3 * n * (a + 1)]
            )
            q = term if q is None else q + term
        g = from_right(q[:, :n]) + q[:, n : 2 * n] + from_left(q[:, 2 * n :])
        c1 = conv[i]
        c1 = c1 - group_average(jnp.sum(c1, axis=0, keepdims=True), mats_n, width)
        var_n = group_average(jnp.sum(c1 * c1, axis=0, keepdims=True), mats_n, width)
        scale = lax.rsqrt(var_n + NORM_EPS)
        hat = c1 * scale
        gain = side[0:1, :]
        pre = hat * gain + side[1:2, :]
        gate = jax.nn.sigmoid(pre)
        g = g * gate * (1.0 + pre * (1.0 - gate))
        d_gain = jnp.sum(g * hat, axis=0, keepdims=True)
        d_shift = jnp.sum(g, axis=0, keepdims=True)
        gn_rows[i] = jnp.concatenate([d_gain, d_shift], axis=0)
        back = scale * (
            g * gain
            - group_average(d_shift * gain, mats_n, width)
            - hat * group_average(d_gain * gain, mats_n, width)
        )
        back = back.astype(LOW).astype(F32)
        gsum[i : i + 1, :] = jnp.sum(back, axis=0, keepdims=True)
        tapsg[i, 0:TIME, :] = jnp.zeros((TIME, 3 * n), LOW)
        tapsg[i, TIME + ROWS :, :] = jnp.zeros((TIME, 3 * n), LOW)
        tapsg[i, TIME : TIME + ROWS, :] = jnp.concatenate(
            [from_right(back), back, from_left(back)], axis=1
        ).astype(LOW)

    def first_pull(i):
        total = None
        for a in range(3):
            term = mm_nt(
                tapsg[i, TIME * (2 - a) : TIME * (2 - a) + ROWS, :], wv[1, :, 3 * n * a : 3 * n * (a + 1)]
            )
            total = term if total is None else total + term
        part[i] = total.astype(LOW)
        total_sum.begin(i)

    conv_pull(0)
    out_far.wait_recv()
    out_near = net.start(all_out.at[brought, :], all_out.at[brought, :], sibling)
    share.pass_on()
    share.end()
    conv_pull(1)
    one_w.wait()
    first_pull(1)
    first_pull(0)
    cro.half()
    total_sum.cross()
    for a in range(3):
        put(
            d_t, 0, 3 * n * a,
            mm_tn(low_grad[...], taps[0, TIME * a : TIME * a + ROWS, :])
            + mm_tn(other_grad[...], taps[1, TIME * a : TIME * a + ROWS, :]),
        )
    d_t[:, :, :, :, 9 * n :] = jnp.zeros((*d_t.shape[:4], d_t.shape[4] - 9 * n), LOW)
    two.raw()
    gn_both = gn_rows[0] + gn_rows[1]
    rows[6:8, :] = jnp.concatenate(
        [jnp.where(2 * x + core == s, gn_both, 0.0) for s in range(4)], axis=1
    )
    for a in range(3):
        window = pl.ds(TIME * (2 - a), ROWS)
        put(
            d_o, 0, 3 * n * a,
            mm_tn(first[0], tapsg[0, window, :]) + mm_tn(first[1], tapsg[1, window, :]),
        )
    put(
        d_o, 0, 9 * n,
        lax.dot_general(
            steps[...], gsum[...], (((0,), (0,)), ((), ())), precision=HIGHEST_PRECISION,
            preferred_element_type=F32,
        ),
    )
    mlp_w = [weights(g1, i) for i in range(2)]
    total_sum.end()
    one.raw()

    noisy_load.wait()
    mats = group_mats(features, width)
    mean = group_average(jnp.sum(resid[...], axis=0, keepdims=True), mats, width)
    centre = resid[...] - mean
    var = group_average(jnp.sum(centre * centre, axis=0, keepdims=True), mats, width)
    scale = lax.rsqrt(var + NORM_EPS)
    gain, shift = norms[4:5, :], norms[5:6, :]

    def through_silu(r):
        hat = (resid[r, :] - mean) * scale
        pre = hat * gain + shift
        gate = jax.nn.sigmoid(pre)
        g = summed[r, :].astype(F32)
        g = g * gate * (1.0 + pre * (1.0 - gate))
        acc[r, :] = g
        rows[4:5, :] += jnp.sum(g * hat, axis=0, keepdims=True)
        rows[5:6, :] += jnp.sum(g, axis=0, keepdims=True)

    each_rows(through_silu)
    mean_shift = group_average(rows[5:6, :] * gain, mats, width)
    mean_gain = group_average(rows[4:5, :] * gain, mats, width)

    def pull_two(r):
        hat = (resid[r, :] - mean) * scale
        v = grad[r, :] + scale * (acc[r, :] * gain - mean_shift - hat * mean_gain)
        grad[r, :] = v
        low_grad[r, :] = v.astype(LOW)

    for c in share.far:
        c.wait_send()
    each_rows(pull_two)
    resid_load = load(resid_h, resid)
    n2_load.wait()
    for c in mlp_w:
        c.wait()
    for q, group in enumerate(mlp):
        up, down = block * q, hid + block * q
        for i in (1, 0):
            pre = mm(nrm[...], wv[i, :, up : up + block])
            t, hidden = gelu_parts(pre)
            slope = gelu_slope(pre, t)
            hb[i] = hidden.astype(LOW)
            hb2[i] = (mm(low_grad[...], wv[i, :, down : down + block]) * slope).astype(LOW)
            term = mm_nt(hb2[i], wv[i, :, up : up + block])
            if q == 0 and i == 1:
                acc[...] = term
            else:
                acc[...] += term
        if q == len(mlp) - 1:
            exchange(1).give(lambda r: acc[r, :])
        for i in (1, 0):
            put(d_m.at[q], i, block, mm_tn(low_grad[...], hb[i]))
            put(d_m.at[q], i, 0, mm_tn(nrm[...], hb2[i]))
        group.raw()
        if q == 1:
            cro.mid()
    attn_w = [weights(g0, i) for i in range(2)]
    tail_loads = [
        load(n1_h, nrm), load(qkv_h, tapsg.at[:, pl.ds(0, ROWS), :]), load(mixed_h, cross), load(logs_h, logs),
    ]
    resid_load.wait()

    def pull_one(r, both):
        back, g_gain, g_shift = ln_back(resid[r, :], norms[2:3, :], both)
        v = grad[r, :] + back
        grad[r, :] = v
        low_grad[r, :] = v.astype(LOW)
        rows[2:3, :] += g_gain
        rows[3:4, :] += g_shift

    sends[1].take(pull_one)
    for c in (*attn_w, *tail_loads):
        c.wait()
    for i in range(2):
        gm[i] = mm(low_grad[...], wv[i, :, 3 * n : 4 * n]).astype(LOW)
    acc[...] = jnp.zeros(acc.shape, F32)

    seg_row = own_segments(segments, x, seg_col)

    def self_heads(r):
        mask = seg_col[r, :] == seg_row
        for i in range(2):
            rows_logs = [logs[r, heads * i + h : heads * i + h + 1] for h in range(heads)]
            gq, gk, gv = softmax_heads_back(
                tapsg[i, r, :n], tapsg[i, 0:ROWS, n : 2 * n], tapsg[i, 0:ROWS, 2 * n :], gm[i, r, :],
                rows_logs, heads, score_scale, mask,
            )
            taps[i, r, :n] = gq.astype(LOW)
            acc[:, 2 * n * i : 2 * n * (i + 1)] += jnp.concatenate([gk, gv], axis=1)

    each_rows(self_heads)
    one.half()
    cro.turn()
    mlp[0].corners()
    for i in (1, 0):
        both = acc[:, 2 * n * i : 2 * n * (i + 1)]
        taps[i, 0:ROWS, n:] = jnp.concatenate([both[:, :n] * score_scale, both[:, n:]], axis=1).astype(LOW)
        put(d_c, i, 3 * n, mm_tn(low_grad[...], cross[i]))
        put(d_c, i, 0, mm_tn(nrm[...], taps[i, 0:ROWS, :]))
    attn.raw()
    exchange(2).give(
        lambda r: mm_nt(taps[1, r, :], wv[1, :, : 3 * n]) + mm_nt(taps[0, r, :], wv[0, :, : 3 * n])
    )
    two.lines()
    tok_load.wait()

    def pull_zero(r, both):
        back, g_gain, g_shift = ln_back(cot[r, :].astype(F32), norms[0:1, :], both)
        low_grad[r, :] = (grad[r, :] + back).astype(LOW)
        rows[0:1, :] += g_gain
        rows[1:2, :] += g_shift

    sends[2].take(pull_zero)
    store_x = pltpu.make_async_copy(low_grad, all_x.at[own, :], out_sem.at[5])
    store_x.start()
    middle = pl.ds(pl.multiple_of(TIME + core * (ROWS // 2), TIME), ROWS // 2)
    x_far = net.start(pad.at[0, middle, :], all_x.at[mine, :], to_x)
    rows[0:6, :] = jnp.where(core == 0, rows[0:6, :], 0.0)
    rows[8:10, :] = jnp.where(core == 0, rows[8:10, :], 0.0)
    totals.start(0)

    def deliver(group, k, out):
        w = out.shape[1]
        part = stage.at[:, pl.ds(0, w)]
        group.finish(part)
        copy = pltpu.make_async_copy(part, out, out_sem.at[k])
        copy.start()
        copy.wait()

    mlp[1].corners()
    mlp[0].lines()
    totals.step(0)
    mlp[2].corners()
    deliver(cro, 0, s4)
    totals.step(1)
    mlp[0].half()
    one.mid()
    mlp[1].lines()
    totals.step(2)
    deliver(mlp[0], 1, s1.at[0])
    mlp[2].lines()
    two.half()
    attn.corners()
    totals.step(3)
    x_far.wait_recv()
    x_near = net.start(all_x.at[brought, :], all_x.at[brought, :], sibling)
    mlp[1].half()
    deliver(one, 2, s2)
    attn.lines()
    mlp[2].half()
    totals.step(4)
    rows_o[...] = values[5]
    deliver(mlp[1], 3, s1.at[1])
    deliver(mlp[2], 4, s1.at[2])
    attn.half()
    deliver(two, 6, s3)
    deliver(attn, 7, s0)
    out_near.wait_recv()
    x_near.wait_recv()
    store_x.wait()
    out_own.wait()
    wait_sends(net, [sends[0], *share.far, *cro.sent])


def wait_sends(net, done):
    for copy in net.made:
        if copy is not None and all(copy is not d for d in done):
            copy.wait_send()


def backward_all(segments, norms, steps, sq, tokens, cots, codecs, gathered, kept):
    features = norms.shape[1]
    n = kept[2].shape[2]
    rows = gathered[0].shape[3]
    widths = [g.shape[4] for g in gathered]
    hid = widths[1] // 2
    heads = 2 * n // HD
    ctok = codecs.shape[1]
    full = (ROWS, features)
    tall = ROWS + 2 * TIME
    ins = [
        segments, norms, steps, sq, tokens, cots, codecs,
        *[g.reshape(g.shape[0], features, -1) for g in gathered], *kept,
    ]
    dma = pltpu.SemaphoreType.DMA

    block = 256
    parts = hid // block

    def pieces(width, *counts):
        return [VM((*(k if isinstance(k, tuple) else (k,)), rows, width), LOW) for k in counts]

    copies = 2 + 12 + 4 + 2 + 6 + 5 + 5 + 4 + 4 + parts * 9 + 9
    res = pl.pallas_call(
        backward_body,
        name="backward",
        in_specs=[spec_vm() for _ in range(4)] + [spec_any() for _ in ins[4:]],
        out_specs=[spec_any() for _ in range(7)] + [spec_vm()],
        out_shape=[
            jax.ShapeDtypeStruct((parts, rows, 2 * block) if g == 1 else (rows, w), F32)
            for g, w in enumerate(widths)
        ]
        + [jax.ShapeDtypeStruct((2 * ROWS, features), LOW)] * 2
        + [jax.ShapeDtypeStruct((16, features), F32)],
        scratch_shapes=[
            VM((2, 4, 2, rows, 4 * n), LOW), VM((1, 4, 2, rows, widths[3]), LOW),
            VM((1, 4, 2, rows, 10 * n), LOW), VM((parts, 2, 4, 2, rows, 2 * block), LOW),
            VM((2, features, 10 * n), LOW), VM(full, LOW), VM((ctok, features), LOW),
            VM((2, ROWS, n), LOW), VM((2, ctok, 2 * n), LOW), VM((2, ROWS, n), LOW), VM((2, ROWS, n), LOW),
            VM((ROWS, heads), F32), VM(full, F32), VM(full, LOW), VM(full, F32),
            VM((2, tall, features), LOW), VM((2, tall, 3 * n), LOW), VM((2, tall, 3 * n), LOW),
            VM((2, ROWS, n), F32), VM((2, *full), LOW), VM((2, ROWS, 256), LOW), VM((2, ROWS, 256), LOW), VM(full, F32),
            VM((2, *full), LOW), VM((2, *full), LOW), VM((2, *full), LOW),
            VM((2, ROWS // 2, features), LOW), VM((ROWS // 2, features), LOW),
            VM((ROWS // 2, features), LOW), VM(full, LOW),
            *pieces(4 * n, (2, 2, 2), (2, 2), 2, 2), VM((rows, 4 * n), LOW),
            *pieces(widths[3], 4, 2), VM((rows, widths[3]), LOW),
            *pieces(10 * n, (2, 1, 2), (1, 2), 1),
            *pieces(2 * block, (parts, 4), (parts, 2), parts, (parts, 4), (parts, 4)),
            *pieces(4 * n, 4, 2), VM((rows, 4 * n), LOW), *pieces(4 * n, 4, 4),
            VM((6, 16, features), F32), VM((5, 16, features), F32), VM((ROWS, 1), F32),
            VM((rows, 10 * n), F32), VM((8, n), F32),
            dma((30,)), dma((9,)), dma((copies,)), dma((copies,)),
        ],
        compiler_params=pltpu.CompilerParams(
            collective_id=1, has_side_effects=True, vmem_limit_bytes=64 << 20
        ),
    )(*ins)
    return res[:5], res[5], res[6], res[7]


def adam_rows(w, g, m, v, decay_rate):
    m_new = MOMENT_DECAY * m + (1.0 - MOMENT_DECAY) * g
    v_new = MOMENT_DECAY * v + (1.0 - MOMENT_DECAY) * g * g
    correct = 1.0 - MOMENT_DECAY**STEP
    update = m_new / correct / (jnp.sqrt(v_new / correct) + ADAM_EPS) + decay_rate * w
    return m_new, v_new, update


def moment_chunks(masters):
    chunks = []
    for a, size in ((0, 4), (1, 4)):
        count = masters[a].shape[0]
        chunks += [(a, k, min(k + size, count)) for k in range(0, count, size)]
    return chunks + [(2, 0, 1), (3, 0, 1)]


def moments_body(*refs):
    sums_h, refs = refs[:5], refs[5:]
    w_h, m_h, v_h, refs = refs[:4], refs[4:8], refs[8:12], refs[12:]
    nm_h, nv_h, u_h, usq, refs = refs[:4], refs[4:8], refs[8:12], refs[12], refs[13:]
    sums, refs = refs[:5], refs[5:]
    w, m, v, nm, nv, u, (in_sem, out_sem) = (
        refs[:4], refs[4:8], refs[8:12], refs[12:16], refs[16:20], refs[20:24], refs[24:]
    )
    n = w[0].shape[2]
    chunks = moment_chunks(w)
    copies = []

    def part(ref, chunk):
        return ref.at[chunk[1] : chunk[2]] if chunk[0] < 2 else ref

    def load(src, dst):
        copy = pltpu.make_async_copy(src, dst, in_sem.at[len(copies)])
        copy.start()
        copies.append(copy)
        return copy

    sum_loads = [load(sums_h[g], sums[g]) for g in range(5)]
    loads = [
        [load(part(h[c[0]], c), part(r[c[0]], c)) for h, r in ((w_h, w), (m_h, m), (v_h, v))]
        for c in chunks
    ]
    where_in, where_back = {}, {}
    for g, (ins, backs) in GROUPS_OF.items():
        where_in.update({j: (g, k) for k, j in enumerate(ins)})
        where_back.update({j: (g, k) for k, j in enumerate(backs, len(ins))})
    squares = [None] * 29
    for s in sum_loads:
        s.wait()
    stores = []
    for c, waits in zip(chunks, loads):
        for s in waits:
            s.wait()
        a = c[0]
        if a < 2:
            for j in range(c[1], c[2]):
                g, k = (where_back if a else where_in)[j]
                grad = sums[g][:, n * k : n * (k + 1)]
                grad = grad.T if a else grad
                nm[a][j], nv[a][j], u[a][j] = adam_rows(w[a][j], grad, m[a][j], v[a][j], WEIGHT_DECAY)
                squares[16 * a + j] = square_sum(u[a][j])
        else:
            block = sums[1].shape[2] // 2
            found = []
            for q in range(w[a].shape[1] // block):
                cols = slice(block * q, block * (q + 1))
                grad = sums[1][q, :, block * (a - 2) : block * (a - 1)]
                nm[a][:, cols], nv[a][:, cols], u[a][:, cols] = adam_rows(
                    w[a][:, cols], grad, m[a][:, cols], v[a][:, cols], WEIGHT_DECAY
                )
                found.append(square_sum(u[a][:, cols]))
            squares[25 + a] = sum(found)
        for r, h in ((nm, nm_h), (nv, nv_h), (u, u_h)):
            copy = pltpu.make_async_copy(part(r[a], c), part(h[a], c), out_sem.at[len(stores)])
            copy.start()
            stores.append(copy)
    usq[...] = row_of(squares)
    for copy in stores:
        copy.wait()


def totals_body(usq, out, ring, ring_b, send, recv):
    mp, dp = lax.axis_index("mp"), lax.axis_index("dp")
    dp_peers = [((dp + k) % 8, mp) for k in range(1, 8)]
    mp_peers = [(dp, (mp + k) % 4) for k in range(1, 4)]
    ring[dp] = jnp.broadcast_to(usq[...], ring.shape[1:])
    meet(dp_peers + mp_peers)
    net = Sender(send, recv)
    copies = [net.start(ring.at[dp], ring.at[dp], p) for p in dp_peers]
    for c in copies:
        c.wait_recv()
    total = ring[0]
    for k in range(1, 8):
        total = total + ring[k]
    ring_b[mp] = total
    copies = [net.start(ring_b.at[mp], ring_b.at[mp], p) for p in mp_peers]
    for c in copies:
        c.wait_recv()
    out[...] = ring_b[0] + ring_b[1] + ring_b[2] + ring_b[3]
    net.close()


def apply_body(total, sums, w_in, w_back, w_up, w_down, u_in, u_back, u_up, u_down, norms, norm_m, norm_v, *outs):
    nw_in, nw_back, nw_up, nw_down, new_norm, new_nm, new_nv, lens = outs
    both = jnp.sqrt(jnp.concatenate([total[10:11, 0:128], sums[0:1, :]], axis=0))
    lens[...] = both[:, 0:29]
    trust = LEARN_RATE * (both[0:1, :] / jnp.where(both[1:2, :] == 0.0, 1.0, both[1:2, :]))
    lane = lax.broadcasted_iota(jnp.int32, (1, 128), 1)

    def trust_of(j):
        return jnp.sum(jnp.where(lane == j, trust, 0.0), axis=1, keepdims=True)

    for j in range(16):
        nw_in[j] = w_in[j] - trust_of(j) * u_in[j]
    for j in range(11):
        nw_back[j] = w_back[j] - trust_of(16 + j) * u_back[j]
    nw_up[...] = w_up[...] - trust_of(27) * u_up[...]
    nw_down[...] = w_down[...] - trust_of(28) * u_down[...]
    m, v, u = adam_rows(norms[...], total[0:10, :], norm_m[...], norm_v[...], 0.0)
    w = norms[...]
    row_trust = jnp.sqrt(jnp.sum(w * w, axis=1, keepdims=True)) / jnp.sqrt(
        jnp.sum(u * u, axis=1, keepdims=True)
    )
    new_norm[...] = w - LEARN_RATE * row_trust * u
    new_nm[...] = m
    new_nv[...] = v


def lamb_all(sums, rows, masters, moments, squares, norms, norm_m, norm_v):
    shapes = [(v.shape, F32) for v in masters]
    dma = pltpu.SemaphoreType.DMA
    ins = [*sums, *masters, *moments, *squares]
    runs = len(moment_chunks(masters))
    *mvu, usq = pl.pallas_call(
        moments_body,
        name="lamb_moments",
        in_specs=[spec_any() for _ in ins],
        out_specs=[spec_any() for _ in range(12)] + [spec_vm()],
        out_shape=[jax.ShapeDtypeStruct(v.shape, F32) for v in masters * 3]
        + [jax.ShapeDtypeStruct((1, 128), F32)],
        scratch_shapes=[
            *[VM(v.shape, F32) for v in sums], *[VM(v.shape, F32) for v in masters * 6],
            dma((5 + 3 * runs,)), dma((3 * runs,)),
        ],
        compiler_params=pltpu.CompilerParams(vmem_limit_bytes=50 << 20),
        cost_estimate=pl.CostEstimate(flops=2 * 10**7, bytes_accessed=21 * 10**6, transcendentals=10**6),
    )(*ins)
    dma = pltpu.SemaphoreType.DMA
    usq_sum = pl.pallas_call(
        totals_body,
        name="norm_totals",
        in_specs=[spec_vm()],
        out_specs=spec_vm(),
        out_shape=jax.ShapeDtypeStruct((8, 128), F32),
        scratch_shapes=[VM((8, 8, 128), F32), VM((4, 8, 128), F32), dma((10,)), dma((10,))],
        compiler_params=pltpu.CompilerParams(collective_id=2, has_side_effects=True),
    )(usq)
    *weights, new_norm, new_nm, new_nv, lens = run_kernel(
        apply_body, "lamb_apply", [rows, usq_sum, *masters, *mvu[8:], norms, norm_m, norm_v],
        [*shapes, *[(norms.shape, F32)] * 3, ((2, 29), F32)], [],
    )
    return (*weights, *mvu[:8], new_norm, new_nm, new_nv, lens)


def fast_device(
    tokens,
    noise_field,
    codec_tokens,
    timesteps,
    segments,
    cotangent,
    w_in,
    w_back,
    w_up,
    w_down,
    m_in,
    m_back,
    m_up,
    m_down,
    v_in,
    v_back,
    v_up,
    v_down,
    norm_params,
    norm_m,
    norm_v,
):
    features = tokens.shape[1]
    mp = lax.axis_index("mp")
    x = mp // 2

    both = jnp.where(x == 0, timesteps, timesteps[::-1])
    embed = jax.nn.silu(time_embedding(both, features)).astype(LOW).astype(F32)
    level = jnp.sqrt((both[:1].astype(F32) + 1.0) / TSTEPS)
    row = lax.broadcasted_iota(jnp.int32, (8, features), 0)
    steps = jnp.where(row == 0, embed[0:1], jnp.where(row == 1, embed[1:2], level))
    gathered, weight_sq, kept = forward_all(
        w_in, w_back, w_up, w_down.T, segments, norm_params, steps, tokens, noise_field, codec_tokens
    )
    gsteps = jnp.where(row < 2, steps, 0.0)
    sums, all_x, out_rows, rows = backward_all(
        segments, norm_params, gsteps, weight_sq, tokens, cotangent, codec_tokens, gathered, kept
    )
    grad_rows = all_x.astype(F32)
    stepped = lamb_all(
        sums, rows, (w_in, w_back, w_up, w_down.T), (m_in, m_back, m_up, m_down.T),
        (v_in, v_back, v_up, v_down.T), norm_params, norm_m, norm_v,
    )
    stepped = [v.T if k in (3, 7, 11) else v for k, v in enumerate(stepped)]
    return (out_rows, grad_rows, *stepped)


def solution(mesh):
    per_device = fast_device if dict(mesh.shape) == {"dp": 8, "mp": 4} else generic_device
    placed = (
        P("dp", None),
        P("dp", None),
        P("dp", None, None),
        P("dp"),
        P("dp", None),
        P("dp", None),
        P(None, "dp", "mp"),
        P(None, "mp", "dp"),
        P("dp", "mp"),
        P("mp", "dp"),
        P(None, "dp", "mp"),
        P(None, "mp", "dp"),
        P("dp", "mp"),
        P("mp", "dp"),
        P(None, "dp", "mp"),
        P(None, "mp", "dp"),
        P("dp", "mp"),
        P("mp", "dp"),
        P(),
        P(),
        P(),
    )
    return jax.shard_map(
        per_device,
        mesh=mesh,
        in_specs=placed,
        out_specs=(
            P("dp", None),
            P("dp", None),
            P(None, "dp", "mp"),
            P(None, "mp", "dp"),
            P("dp", "mp"),
            P("mp", "dp"),
            P(None, "dp", "mp"),
            P(None, "mp", "dp"),
            P("dp", "mp"),
            P("mp", "dp"),
            P(None, "dp", "mp"),
            P(None, "mp", "dp"),
            P("dp", "mp"),
            P("mp", "dp"),
            P(),
            P(),
            P(),
            P(),
        ),
        check_vma=False,
    )
```
